32 devices in a mesh: groups: 2 (over y), tm: 16 (over z, x, core).
Axes of the slice: x: 2, y: 2, z: 4, core: 2. Of those that a mesh axis runs over, the one named last changes fastest.
Arguments:
- frames: bfloat16 [128, 2, 4, 64, 128], P(('groups', 'tm')), parts along dimension 0, may hold values from -6 to 6
- row_halo: bfloat16 [128, 2, 2, 64, 128], P(('groups', 'tm')), parts along dimension 0, may hold values from -6 to 6
- clip_start: int32 [128], P(('groups', 'tm')), parts along dimension 0, may hold values from 0 to 1
- slab_counts: int32 [32], P(('groups', 'tm')), parts along dimension 0, may hold values from 0 to 4, as said below
- conv_weight: bfloat16 [3, 3, 3, 128, 128], replicated, may hold values from -0.109375 to 0.109375
- conv_bias: float32 [128], replicated, may hold values from -3 to 3
- stride_weight: bfloat16 [2, 128, 128], replicated, may hold values from -0.375 to 0.375
- stride_bias: float32 [128], replicated, may hold values from -3 to 3
- cotangent: bfloat16 [128, 1, 4, 64, 128], P(('groups', 'tm')), parts along dimension 0, may hold values from -6 to 6
Outputs:
- latents: bfloat16 [128, 1, 4, 64, 128], P(('groups', 'tm')), parts along dimension 0
- frames_grad: bfloat16 [128, 2, 4, 64, 128], P(('groups', 'tm')), parts along dimension 0
- conv_weight_grad: float32 [6, 3, 3, 128, 128], P('groups'), parts along dimension 0
- conv_bias_grad: float32 [256], P('groups'), parts along dimension 0
- stride_weight_grad: float32 [4, 128, 128], P('groups'), parts along dimension 0
- stride_bias_grad: float32 [256], P('groups'), parts along dimension 0
The draws below stay inside these ranges and needn't reach their ends.
There are 2 independent parts, one for each index of `groups`. The reference program is written for one: setup_inputs(seed, part) draws one part's arguments, and reference() takes and returns one part's arrays. A program takes and returns all parts, laid end to end along the dimension named above; an argument that names none is the same for every part. Nothing has to cross between parts.
Inputs may be any that keep to these rules, and one draw needn't show every extreme that they name: `slab_counts`: the filled slots of a device are its first ones. In every draw some device has all 4 slots filled and some device has none.
All inputs are finite; a program needn't handle non-finite values.
Results may differ from the reference program's by a relative error of at most 0.0055.
Values may be sent and summed in bfloat16 or wider, within the bound.
No kernel may reach another device: no remote copies, remote signals or barrier semaphores. Data moves between devices by JAX's collectives and lax.ppermute only.
A program may use at most 192 MiB of HBM per device.

```python
import jax
import jax.numpy as jnp
from jax import lax

C = 128
H = 4
W = 64
F = 2
SLOTS = 4
OWNERS = 16
SLABS = 64


def plan(key):
    base_key = jax.random.fold_in(key, 7)
    count_key, anchor_key, source_key = jax.random.split(base_key, 3)
    reach = OWNERS // 4
    counts = jax.random.randint(count_key, (OWNERS,), 0, SLOTS + 1)
    anchor = jax.random.randint(anchor_key, (), 0, OWNERS - reach - 1)
    source_count = jax.random.randint(source_key, (), 1, SLOTS + 1)
    index = jnp.arange(OWNERS, dtype=jnp.int32)
    counts = jnp.where(index == anchor, source_count, counts)
    counts = jnp.where((index > anchor) & (index <= anchor + reach), 0, counts)
    target = anchor + reach + 1
    counts = jnp.where(index == target, SLOTS, counts)
    return (counts.astype(jnp.int32), target.astype(jnp.int32))


def draw_slab_counts(key, part):
    counts, target = plan(key)
    return counts


def draw_clip_start(key, part):
    counts, target = plan(key)
    start_key = jax.random.fold_in(key, 11)
    starts = (jax.random.randint(start_key, (SLABS,), 0, 4) == 0).astype(jnp.int32)
    position = jnp.arange(SLABS, dtype=jnp.int32)
    starts = jnp.where(position == target * SLOTS, 0, starts)
    return starts.astype(jnp.int32)


def level_of(stream_key, dims, shards, least, largest):
    level = 1.0
    for dim, shards_of in shards:
        draws = jax.random.uniform(jax.random.fold_in(jax.random.fold_in(stream_key, 6), dim), (shards_of,), jnp.float32, least / len(shards), largest / len(shards))
        level = level * jnp.repeat(jnp.exp(draws), dims[dim] // shards_of).reshape((-1,) + (1,) * (len(dims) - 1 - dim))
    return level


def centred(rng, shape, deviation, limit, shards=(), kind=jnp.bfloat16):
    entries = deviation * jax.random.normal(rng, shape, jnp.float32)
    if shards:
        entries = entries * level_of(rng, shape, shards, -0.22, 0.18)
    return jnp.clip(entries, -limit, limit).astype(kind)


def setup_inputs(seed: int = 0, part: int = 0) -> dict:
    keys = jax.random.split(jax.random.key(seed), 10)
    part_keys = jax.random.split(jax.random.fold_in(keys[9], part), 10)
    frames = centred(part_keys[0], (SLABS, F, H, W, C), 1.0, 6.0, ((0, 16),))
    row_halo = centred(part_keys[1], (SLABS, F, 2, W, C), 1.0, 6.0, ((0, 16),))
    clip_start = draw_clip_start(jax.random.fold_in(jax.random.fold_in(keys[9], part), 71), part)
    slab_counts = draw_slab_counts(jax.random.fold_in(jax.random.fold_in(keys[9], part), 71), part)
    conv_weight = centred(keys[4], (3, 3, 3, C, C), (27 * C) ** -0.5, 0.109375)
    conv_bias = centred(keys[5], (C,), 0.5, 3.0, (), jnp.float32)
    stride_weight = centred(keys[6], (2, C, C), (2 * C) ** -0.5, 0.375)
    stride_bias = centred(keys[7], (C,), 0.5, 3.0, (), jnp.float32)
    cotangent = centred(part_keys[8], (SLABS, F // 2, H, W, C), 1.0, 6.0, ((0, 16),))
    return dict(frames=frames, row_halo=row_halo, clip_start=clip_start, slab_counts=slab_counts, conv_weight=conv_weight, conv_bias=conv_bias, stride_weight=stride_weight, stride_bias=stride_bias, cotangent=cotangent)


def forward_conv(extended, weight):
    return lax.conv_general_dilated(extended, weight, (1, 1, 1), ((0, 0), (0, 0), (1, 1)), dimension_numbers=('NDHWC', 'DHWIO', 'NDHWC'), preferred_element_type=jnp.float32)

def input_grad(grad_pre, weight):
    flipped = jnp.transpose(weight[::-1, ::-1, ::-1], (0, 1, 2, 4, 3))
    return lax.conv_general_dilated(grad_pre, flipped, (1, 1, 1), ((2, 2), (2, 2), (1, 1)), dimension_numbers=('NDHWC', 'DHWIO', 'NDHWC'), preferred_element_type=jnp.float32)

def weight_grad(extended, grad_pre):
    return lax.conv_general_dilated(extended, grad_pre, (1, 1, 1), ((0, 0), (0, 0), (1, 1)), dimension_numbers=('CDHWN', 'IDHWO', 'DHWNC'), preferred_element_type=jnp.float32)

def reference(frames, row_halo, clip_start, slab_counts, conv_weight, conv_bias, stride_weight, stride_bias, cotangent):
    slab_total = frames.shape[0]
    position = jnp.arange(slab_total, dtype=jnp.int32)
    owner = (position // SLOTS).astype(jnp.int32)
    filled = position % SLOTS < slab_counts[owner]
    marked = jnp.where(filled, position, -1).astype(jnp.int32)
    running = lax.cummax(marked, axis=0)
    prior = jnp.concatenate([jnp.full((1,), -1, jnp.int32), running[:-1].astype(jnp.int32)]).astype(jnp.int32)
    carried = (prior >= 0) & (clip_start == 0)
    source = jnp.maximum(prior, 0).astype(jnp.int32)
    carried_mask = carried[:, None, None, None, None]
    filled_mask = filled[:, None, None, None, None]
    bordered = jnp.concatenate([row_halo[:, :, :1], frames, row_halo[:, :, 1:]], axis=2)
    tails = bordered[:, F - 2:]
    previous = jnp.where(carried_mask, tails[source], jnp.zeros_like(tails))
    extended = jnp.concatenate([previous, bordered], axis=1)
    extended_wide = extended.astype(jnp.float32)
    pre_act = forward_conv(extended_wide, conv_weight.astype(jnp.float32)) + conv_bias
    squash = jax.nn.sigmoid(pre_act)
    hidden = (pre_act * squash).astype(jnp.bfloat16)
    paired = hidden.reshape(slab_total, F // 2, 2, H, W, C).astype(jnp.float32)
    stride_wide = stride_weight.astype(jnp.float32)
    outputs = jnp.einsum('stkhwc,kcd->sthwd', paired, stride_wide) + stride_bias
    latents = jnp.where(filled_mask, outputs, jnp.zeros_like(outputs)).astype(jnp.bfloat16)
    grad_out = jnp.where(filled_mask, cotangent, jnp.zeros_like(cotangent))
    grad_wide = grad_out.astype(jnp.float32)
    grad_hidden = jnp.einsum('sthwd,kcd->stkhwc', grad_wide, stride_wide).reshape(slab_total, F, H, W, C)
    stride_weight_grad = jnp.einsum('stkhwc,sthwd->kcd', paired, grad_wide)
    stride_bias_grad = lax.optimization_barrier(jnp.sum(grad_wide, axis=(0, 1, 2, 3)))
    grad_pre = (grad_hidden * squash * (1.0 + pre_act * (1.0 - squash))).astype(jnp.bfloat16)
    grad_pre_wide = grad_pre.astype(jnp.float32)
    conv_bias_grad = lax.optimization_barrier(jnp.sum(grad_pre_wide, axis=(0, 1, 2, 3)))
    conv_weight_grad = weight_grad(extended_wide, grad_pre_wide)
    extended_grad = input_grad(grad_pre_wide, conv_weight.astype(jnp.float32))[:, :, 1:H + 1]
    cache_grad = jnp.where(carried_mask, extended_grad[:, :2], jnp.zeros_like(extended_grad[:, :2]))
    returned = jnp.zeros((slab_total, 2, H, W, C), jnp.float32).at[source].add(cache_grad)
    head_zeros = jnp.zeros((slab_total, F - 2, H, W, C), jnp.float32)
    frame_grad = extended_grad[:, 2:] + jnp.concatenate([head_zeros, returned], axis=1)
    frames_grad = jnp.where(filled_mask, frame_grad, jnp.zeros_like(frame_grad)).astype(jnp.bfloat16)
    return (latents, frames_grad, conv_weight_grad, conv_bias_grad, stride_weight_grad, stride_bias_grad)
```

```python
import functools

import jax
import jax.numpy as jnp
from jax import lax
from jax.experimental import pallas as pl
from jax.experimental.pallas import tpu as pltpu
from jax.sharding import PartitionSpec as P

BF = jnp.bfloat16
F32 = jnp.float32
EMPTY_FRAME = 100.0
EMPTY_GRAD = 1e30

_VMEM = pl.BlockSpec(memory_space=pltpu.VMEM)
_SMEM = pl.BlockSpec(memory_space=pltpu.SMEM)


def _call(kernel, out_shape, in_specs, scratch=(), flops=0, moved=0):
    return pl.pallas_call(
        kernel,
        out_shape=out_shape,
        in_specs=in_specs,
        out_specs=jax.tree.map(lambda _: _VMEM, out_shape),
        scratch_shapes=list(scratch),
        compiler_params=pltpu.CompilerParams(vmem_limit_bytes=56 << 20),
        cost_estimate=pl.CostEstimate(flops=flops, bytes_accessed=moved, transcendentals=0),
    )


def _put(xk, at, rows, value):
    n, w, c = value.shape
    flat = value.astype(F32).reshape(n * w, c)
    col = lax.broadcasted_iota(jnp.int32, (n * w, c), 0) % w
    right = jnp.where(col == 0, 0.0, pltpu.roll(flat, 1, 0))
    left = jnp.where(col == w - 1, 0.0, pltpu.roll(flat, n * w - 1, 0))
    for kw, shifted in enumerate((right, flat, left)):
        xk[(kw, *at, rows)] = shifted.astype(BF).reshape(n, w, c)


def _window(xk, kw, j, kh, h):
    v = xk[kw, :, j, kh : kh + h]
    return v.reshape(v.shape[0] * v.shape[1] * v.shape[2], v.shape[3])


def _wide(xk, j, h):
    return jnp.concatenate(
        [_window(xk, kw, j, kh, h) for kh in range(3) for kw in range(3)], axis=1
    )


def _conv(xk, w_ref, h):
    c = w_ref.shape[-1]
    zero = jnp.zeros((c, c), BF)
    lhs = jnp.concatenate([_wide(xk, j, h) for j in range(4)], axis=1)
    rhs = []
    for j in range(4):
        for tap in range(9):
            rhs.append(
                jnp.concatenate(
                    [w_ref[(j - t) * 9 + tap] if 0 <= j - t <= 2 else zero for t in range(2)],
                    axis=1,
                )
            )
    return jnp.dot(lhs, jnp.concatenate(rhs, axis=0), preferred_element_type=F32)


def _conv_back(xk, w_ref, h):
    c = w_ref.shape[-1]
    zero = jnp.zeros((c, c), BF)
    lhs = jnp.concatenate([_wide(xk, j, h) for j in range(4)], axis=1)
    rhs = []
    for f in range(2):
        row = []
        for j in range(4):
            for tap in range(9):
                kt = 2 - (j - f)
                row.append(w_ref[kt * 9 + 8 - tap] if 0 <= kt <= 2 else zero)
        rhs.append(jnp.concatenate(row, axis=1))
    return lax.dot_general(
        lhs, jnp.concatenate(rhs, axis=0), (((1,), (1,)), ((), ())), preferred_element_type=F32
    )


def _head(xk, gout, w_ref, cb_ref, sw_ref, sb_ref, h):
    pre = _conv(xk, w_ref, h) + jnp.concatenate([cb_ref[...], cb_ref[...]], axis=1)
    s = 1.0 / (1.0 + jnp.exp(-pre))
    hidden = (pre * s).astype(BF)
    sw = jnp.concatenate([sw_ref[0], sw_ref[1]], axis=0)
    lat = jnp.dot(hidden, sw, preferred_element_type=F32) + sb_ref[...]
    gh = lax.dot_general(gout, sw, (((1,), (1,)), ((), ())), preferred_element_type=F32)
    g = (gh * s * (1.0 + pre * (1.0 - s))).astype(BF)
    return lat, g, hidden


def _weight_grads(xk, g, hidden, gout, h, add):
    c = gout.shape[-1]
    parts = []
    for j in range(4):
        lhs = _wide(xk, j, h)
        parts.append(
            lax.dot_general(lhs, g, (((0,), (0,)), ((), ())), preferred_element_type=F32)
        )
    for kt in range(3):
        add(kt, parts[kt][:, :c] + parts[kt + 1][:, c:])
    sg = lax.dot_general(hidden, gout, (((0,), (0,)), ((), ())), preferred_element_type=F32)
    g32 = jnp.sum(g.astype(F32), axis=0, keepdims=True)
    add(3, sg)
    add(4, g32[:, :c] + g32[:, c:])
    add(5, jnp.sum(gout.astype(F32), axis=0, keepdims=True))


def _store_g(g_ref, g, slots, h, w):
    c = g_ref.shape[-1]
    for t in range(2):
        g_ref[:, t] = g[:, t * c : (t + 1) * c].reshape(slots, h, w, c)


def _early_kernel(sc, fr, ha, co, w_ref, cb, sw, sb, lat_ref, g_ref, acc, xk):
    slots, _, h, w, c = fr.shape
    for s in range(slots):
        for f in range(2):
            mine = fr[s, f], ha[s, f]
            spots = [(s - 1, f + 2, None)] if s > 0 else []
            if s + 1 < slots:
                spots.append((s, f, sc[1 + s + 1] == 0))
            for slot, j, keep in spots:
                a, b = mine
                if keep is not None:
                    a = jnp.where(keep, a, jnp.zeros_like(a))
                    b = jnp.where(keep, b, jnp.zeros_like(b))
                _put(xk, (slot, j), slice(1, 1 + h), a)
                _put(xk, (slot, j), slice(0, 1), b[:1])
                _put(xk, (slot, j), slice(h + 1, h + 2), b[1:])
    gout = jnp.concatenate(
        [
            jnp.where(s < sc[0], co[s, 0], jnp.zeros_like(co[s, 0])).reshape(h * w, c)
            for s in range(1, slots)
        ],
        axis=0,
    )
    lat, g, hidden = _head(xk, gout, w_ref, cb, sw, sb, h)
    for s in range(1, slots):
        part = lat[(s - 1) * h * w : s * h * w]
        lat_ref[s - 1] = (
            jnp.where(s < sc[0], part, jnp.zeros_like(part)).astype(BF).reshape(h, w, c)
        )
    _store_g(g_ref, g, slots - 1, h, w)
    n9 = 9 * c

    def add(kind, value):
        if kind < 3:
            acc[kind * n9 : (kind + 1) * n9] = value
        elif kind == 3:
            acc[3 * n9 : 3 * n9 + 2 * c] = value
        else:
            at = 3 * n9 + 2 * c + (kind - 4)
            acc[at : at + 1] = value

    acc[3 * n9 + 2 * c :] = jnp.zeros((acc.shape[0] - 3 * n9 - 2 * c, c), F32)
    _weight_grads(xk, g, hidden, gout, h, add)


def _late_kernel(
    sc, fr, ha, tail, co, w_ref, cb, sw, sb, early, lat_ref, g_ref, send, keep, xk, acc
):
    _, h, w, c = fr.shape
    on = sc[1] == 0
    for f in range(2):
        _put(xk, (0, f + 2), slice(1, 1 + h), fr[f])
        _put(xk, (0, f + 2), slice(0, 1), ha[f, :1])
        _put(xk, (0, f + 2), slice(h + 1, h + 2), ha[f, 1:])
        a = tail[f * h : (f + 1) * h]
        b = tail[2 * h + 2 * f : 2 * h + 2 * f + 2]
        a = jnp.where(on, a, jnp.zeros_like(a))
        b = jnp.where(on, b, jnp.zeros_like(b))
        _put(xk, (0, f), slice(1, 1 + h), a)
        _put(xk, (0, f), slice(0, 1), b[:1])
        _put(xk, (0, f), slice(h + 1, h + 2), b[1:])
    filled = sc[0] > 0
    gout = jnp.where(filled, co[0], jnp.zeros_like(co[0])).reshape(h * w, c)
    lat, g, hidden = _head(xk, gout, w_ref, cb, sw, sb, h)
    lat_ref[...] = jnp.where(filled, lat, jnp.zeros_like(lat)).astype(BF).reshape(h, w, c)
    for t in range(2):
        g_ref[t] = g[:, t * c : (t + 1) * c].reshape(h, w, c)
    n9 = 9 * c

    def add(kind, value):
        if kind < 3:
            rows = slice(kind * n9, (kind + 1) * n9)
        elif kind == 3:
            rows = slice(3 * n9, 3 * n9 + 2 * c)
        else:
            at = 3 * n9 + 2 * c + (kind - 4)
            rows = slice(at, at + 1)
        acc[rows] = early[rows] + value

    tail_rows = slice(3 * n9 + 2 * c, acc.shape[0])
    acc[tail_rows] = early[tail_rows]
    _weight_grads(xk, g, hidden, gout, h, add)
    half = send.shape[0]
    core = sc[sc.shape[0] - 1]
    send[...] = acc[pl.ds(pl.multiple_of((1 - core) * half, 16), half)].astype(BF)
    keep[...] = acc[pl.ds(pl.multiple_of(core * half, 16), half)]


def _back_kernel(sc, g0, g1, w_ref, out_ref, cache_ref, xk):
    _, h, w, c = g0.shape
    slots = g1.shape[0] + 1
    zero = jnp.zeros((1, w, c), BF)
    for kw in range(3):
        for j in range(4):
            for s in range(slots + 1):
                xk[kw, s, j, 0:1] = zero
                xk[kw, s, j, h + 1 : h + 2] = zero
    blank = jnp.zeros((h, w, c), BF)
    for f in range(2):
        for kw in range(3):
            xk[kw, 0, f, 1 : 1 + h] = blank
            xk[kw, slots, f + 2, 1 : 1 + h] = blank
        for s in range(slots):
            v = g0[f] if s == 0 else g1[s - 1, f]
            _put(xk, (s + 1, f), slice(1, 1 + h), v)
            _put(
                xk, (s, f + 2), slice(1, 1 + h), jnp.where(sc[1 + s] == 0, v, jnp.zeros_like(v))
            )
    out = _conv_back(xk, w_ref, h)
    hw = h * w
    live = sc[0] > 0
    for f in range(2):
        lanes = slice(f * c, (f + 1) * c)
        cache = out[:hw, lanes]
        cache = jnp.where(live, cache, jnp.full_like(cache, EMPTY_GRAD))
        cache_ref[f * h : (f + 1) * h] = cache.astype(BF).reshape(h, w, c)
        out_ref[:, f] = out[hw:, lanes].reshape(slots, h, w, c)


def _cut_kernel(sc, keep, got, own, *sends):
    rows = own.shape[0]
    chip = sc[sc.shape[0] - 2]

    def piece(p):
        at = pl.ds(pl.multiple_of(p * rows, 16), rows)
        return keep[at] + got[at].astype(F32)

    own[...] = piece(chip)
    for k, ref in enumerate(sends):
        ref[...] = piece(lax.bitwise_xor(chip, k + 1)).astype(BF)


def _join_kernel(sc, own, *refs):
    half = refs[-1]
    rows = own.shape[0]
    chip = sc[sc.shape[0] - 2]
    for k, ref in enumerate((own,) + refs[:-1]):
        half[pl.ds(pl.multiple_of(lax.bitwise_xor(chip, k) * rows, 16), rows)] = ref[...]


def _xor(x, k, n, axis):
    return lax.ppermute(x, axis, [(i, i ^ k) for i in range(n)])


def _latest_before(x, empty, axis, n, reverse=False):
    index = lax.axis_index(axis)
    index = n - 1 - index if reverse else index
    core, pair = index & 1, (index >> 1) & 1

    def shift(v, k):
        pairs = [(i, i + k) for i in range(n - k)]
        return lax.ppermute(v, axis, [(b, a) for a, b in pairs] if reverse else pairs)

    def newest(early, late):
        return jnp.where(late > empty / 2, early, late)

    def part(v, at):
        half = v.shape[0] // 2
        return jnp.where(at == 0, v[:half], v[half:])

    def join(mine, other, at):
        return jnp.concatenate(
            [jnp.where(at == 0, mine, other), jnp.where(at == 0, other, mine)], axis=0
        )

    other = _xor(x, 1, n, axis)
    chip = part(jnp.where(core == 0, newest(x, other), newest(other, x)), core)
    beside = _xor(chip, 2, n, axis)
    quad = part(jnp.where(pair == 0, newest(chip, beside), newest(beside, chip)), pair)
    blocks = n // 4
    before = None
    for k in range(min(3, blocks - 1), 0, -1):
        came = shift(quad, 4 * k)
        before = came if before is None else newest(before, came)
    reach = min(3, blocks - 1)
    while reach < blocks - 1:
        before = newest(shift(before, 4 * reach), before)
        reach *= 2
    before = join(before, _xor(before, 2, n, axis), pair)
    before = jnp.where(pair == 0, before, newest(before, beside))
    before = join(before, _xor(before, 1, n, axis), core)
    before = jnp.where(core == 0, before, newest(before, other))
    return jnp.where(before > empty / 2, jnp.zeros_like(before), before)


def _sum_over(send, keep, sc, axis, n):
    rows, c = keep.shape
    chips = min(8, n // 2)
    piece = rows // chips
    got = _xor(send, 1, n, axis)
    outs = _call(
        _cut_kernel,
        [jax.ShapeDtypeStruct((piece, c), F32)]
        + [jax.ShapeDtypeStruct((piece, c), BF)] * (chips - 1),
        [_SMEM, _VMEM, _VMEM],
    )(sc, keep, got)
    total = outs[0]
    for k in range(1, chips):
        total = total + _xor(outs[k], 2 * k, n, axis).astype(F32)
    mine = total.astype(BF)
    k = 2 * chips
    while k < n:
        total = mine.astype(F32) + _xor(mine, k, n, axis).astype(F32)
        mine = total.astype(BF)
        k *= 2
    others = [_xor(mine, 2 * k, n, axis) for k in range(1, chips)]
    half = _call(
        _join_kernel, jax.ShapeDtypeStruct((rows, c), BF), [_SMEM] + [_VMEM] * chips
    )(sc, mine, *others)
    other = _xor(half, 1, n, axis)
    core = sc[-1]
    low = jnp.where(core == 0, half, other)
    high = jnp.where(core == 0, other, half)
    return jnp.concatenate([low, high], axis=0).astype(F32)


def body(
    n,
    frames,
    row_halo,
    clip_start,
    slab_counts,
    conv_weight,
    conv_bias,
    stride_weight,
    stride_bias,
    cotangent,
):
    axis = "tm"
    slots, _, h, w, c = frames.shape
    count = slab_counts[0]
    index = lax.axis_index(axis)
    chips = min(8, n // 2)
    sc = jnp.concatenate(
        [
            slab_counts,
            clip_start,
            ((index >> 1) & (chips - 1)).reshape(1).astype(jnp.int32),
            (index & 1).reshape(1).astype(jnp.int32),
        ]
    )
    wt = conv_weight.reshape(27, c, c)
    cb, sb = conv_bias.reshape(1, c), stride_bias.reshape(1, c)

    last = jnp.maximum(count - 1, 0)
    tail = jnp.concatenate(
        [
            lax.dynamic_index_in_dim(frames, last, 0, False).reshape(2 * h, w, c),
            lax.dynamic_index_in_dim(row_halo, last, 0, False).reshape(4, w, c),
        ],
        axis=0,
    )
    tail = jnp.where(count > 0, tail, jnp.asarray(EMPTY_FRAME, BF))
    arrived = _latest_before(tail, EMPTY_FRAME, axis, n)

    unit = 16 * 2 * chips
    rows = -(-(29 * c + 2) // unit) * unit
    m = h * w
    lat1, g1, early = _call(
        _early_kernel,
        [
            jax.ShapeDtypeStruct((slots - 1, h, w, c), BF),
            jax.ShapeDtypeStruct((slots - 1, 2, h, w, c), BF),
            jax.ShapeDtypeStruct((rows, c), F32),
        ],
        [_SMEM] + [_VMEM] * 7,
        [pltpu.VMEM((3, slots - 1, 4, h + 2, w, c), BF)],
        flops=2 * 2 * (slots - 1) * m * 36 * c * 2 * c,
        moved=6 << 20,
    )(sc, frames, row_halo, cotangent, wt, cb, stride_weight, sb)

    lat0, g0, send, keep = _call(
        _late_kernel,
        [
            jax.ShapeDtypeStruct((h, w, c), BF),
            jax.ShapeDtypeStruct((2, h, w, c), BF),
            jax.ShapeDtypeStruct((rows // 2, c), BF),
            jax.ShapeDtypeStruct((rows // 2, c), F32),
        ],
        [_SMEM] + [_VMEM] * 9,
        [pltpu.VMEM((3, 1, 4, h + 2, w, c), BF), pltpu.VMEM((rows, c), F32)],
        flops=2 * 2 * m * 36 * c * 2 * c,
        moved=6 << 20,
    )(sc, frames[0], row_halo[0], arrived, cotangent[0], wt, cb, stride_weight, sb, early)

    total = _sum_over(send, keep, sc, axis, n)

    grad, cache = _call(
        _back_kernel,
        [
            jax.ShapeDtypeStruct((slots, 2, h, w, c), F32),
            jax.ShapeDtypeStruct((2 * h, w, c), BF),
        ],
        [_SMEM] + [_VMEM] * 3,
        [pltpu.VMEM((3, slots + 1, 4, h + 2, w, c), BF)],
        flops=2 * (slots + 1) * m * 36 * c * 2 * c,
        moved=6 << 20,
    )(sc, g0, g1, wt)
    returned = _latest_before(cache, EMPTY_GRAD, axis, n, reverse=True)
    newest = (jnp.arange(slots, dtype=jnp.int32) == count - 1)[:, None, None, None, None]
    back = returned.reshape(1, 2, h, w, c).astype(F32)
    frames_grad = (grad + jnp.where(newest, back, jnp.zeros_like(back))).astype(BF)
    latents = jnp.concatenate([lat0[None], lat1], axis=0)[:, None]
    return (
        latents,
        frames_grad,
        total[: 27 * c].reshape(3, 3, 3, c, c),
        total[29 * c],
        total[27 * c : 29 * c].reshape(2, c, c),
        total[29 * c + 1],
    )


def solution(mesh):
    split = P(("groups", "tm"))
    return jax.shard_map(
        functools.partial(body, mesh.shape["tm"]),
        mesh=mesh,
        in_specs=(split, split, split, split, P(), P(), P(), P(), split),
        out_specs=(split, split, P("groups"), P("groups"), P("groups"), P("groups")),
        check_vma=False,
    )
```

```python
import functools

import jax
import jax.numpy as jnp
from jax import lax
from jax.experimental import pallas as pl
from jax.experimental.pallas import tpu as pltpu
from jax.sharding import PartitionSpec as P

BF = jnp.bfloat16
F32 = jnp.float32
EMPTY_FRAME = 100.0
EMPTY_GRAD = 1e30

_VMEM = pl.BlockSpec(memory_space=pltpu.VMEM)
_SMEM = pl.BlockSpec(memory_space=pltpu.SMEM)


def _call(kernel, out_shape, in_specs, scratch=(), flops=0, moved=0, room=16, grid=()):
    return pl.pallas_call(
        kernel,
        out_shape=out_shape,
        grid=grid,
        in_specs=in_specs,
        out_specs=jax.tree.map(lambda _: _VMEM, out_shape),
        scratch_shapes=list(scratch),
        compiler_params=pltpu.CompilerParams(vmem_limit_bytes=room << 20),
        cost_estimate=pl.CostEstimate(flops=flops, bytes_accessed=moved, transcendentals=0),
    )


def _put(xk, at, rows, value):
    n, w, c = value.shape
    flat = value.astype(F32).reshape(n * w, c)
    col = lax.broadcasted_iota(jnp.int32, (n * w, c), 0) % w
    right = jnp.where(col == 0, 0.0, pltpu.roll(flat, 1, 0))
    left = jnp.where(col == w - 1, 0.0, pltpu.roll(flat, n * w - 1, 0))
    for kw, shifted in enumerate((right, flat, left)):
        xk[(kw, *at, rows)] = shifted.astype(BF).reshape(n, w, c)


def _window(xk, kw, j, kh, h):
    v = xk[kw, :, j, kh : kh + h]
    return v.reshape(v.shape[0] * v.shape[1] * v.shape[2], v.shape[3])


def _wide(xk, j, h):
    return jnp.concatenate(
        [_window(xk, kw, j, kh, h) for kh in range(3) for kw in range(3)], axis=1
    )


def _conv(xk, w_ref, h):
    c = w_ref.shape[-1]
    zero = jnp.zeros((c, c), BF)
    lhs = jnp.concatenate([_wide(xk, j, h) for j in range(4)], axis=1)
    rhs = []
    for j in range(4):
        for tap in range(9):
            rhs.append(
                jnp.concatenate(
                    [w_ref[(j - t) * 9 + tap] if 0 <= j - t <= 2 else zero for t in range(2)],
                    axis=1,
                )
            )
    return jnp.dot(lhs, jnp.concatenate(rhs, axis=0), preferred_element_type=F32)


def _conv_back(xk, w_ref, h):
    c = w_ref.shape[-1]
    zero = jnp.zeros((c, c), BF)
    lhs = jnp.concatenate([_wide(xk, j, h) for j in range(4)], axis=1)
    rhs = []
    for f in range(2):
        row = []
        for j in range(4):
            for tap in range(9):
                kt = 2 - (j - f)
                row.append(w_ref[kt * 9 + 8 - tap] if 0 <= kt <= 2 else zero)
        rhs.append(jnp.concatenate(row, axis=1))
    return lax.dot_general(
        lhs, jnp.concatenate(rhs, axis=0), (((1,), (1,)), ((), ())), preferred_element_type=F32
    )


def _head(xk, gout, w_ref, cb_ref, sw_ref, sb_ref, h):
    pre = _conv(xk, w_ref, h) + jnp.concatenate([cb_ref[...], cb_ref[...]], axis=1)
    s = 1.0 / (1.0 + jnp.exp(-pre))
    hidden = (pre * s).astype(BF)
    sw = jnp.concatenate([sw_ref[0], sw_ref[1]], axis=0)
    lat = jnp.dot(hidden, sw, preferred_element_type=F32) + sb_ref[...]
    gh = lax.dot_general(gout, sw, (((1,), (1,)), ((), ())), preferred_element_type=F32)
    g = (gh * s * (1.0 + pre * (1.0 - s))).astype(BF)
    return lat, g, hidden


def _weight_grads(xk, g, hidden, gout, h, add):
    c = gout.shape[-1]
    parts = []
    for j in range(4):
        lhs = _wide(xk, j, h)
        parts.append(
            lax.dot_general(lhs, g, (((0,), (0,)), ((), ())), preferred_element_type=F32)
        )
    for kt in range(3):
        add(kt, parts[kt][:, :c] + parts[kt + 1][:, c:])
    sg = lax.dot_general(hidden, gout, (((0,), (0,)), ((), ())), preferred_element_type=F32)
    g32 = jnp.sum(g.astype(F32), axis=0, keepdims=True)
    add(3, sg)
    add(4, g32[:, :c] + g32[:, c:])
    add(5, jnp.sum(gout.astype(F32), axis=0, keepdims=True))


def _fill_early(sc, fr, ha, xk):
    slots, _, h, w, c = fr.shape
    for s in range(slots):
        for f in range(2):
            spots = [(s - 1, f + 2, None)] if s > 0 else []
            if s + 1 < slots:
                spots.append((s, f, sc[1 + s + 1] == 0))
            for slot, j, keep in spots:
                a, b = fr[s, f], ha[s, f]
                if keep is not None:
                    a = jnp.where(keep, a, jnp.zeros_like(a))
                    b = jnp.where(keep, b, jnp.zeros_like(b))
                _put(xk, (slot, j), slice(1, 1 + h), a)
                _put(xk, (slot, j), slice(0, 1), b[:1])
                _put(xk, (slot, j), slice(h + 1, h + 2), b[1:])


def _early_gout(sc, co):
    slots, _, h, w, c = co.shape
    return jnp.concatenate(
        [
            jnp.where(s < sc[0], co[s, 0], jnp.zeros_like(co[s, 0])).reshape(h * w, c)
            for s in range(1, slots)
        ],
        axis=0,
    )


def _early_kernel(sc, fr, ha, co, w_ref, cb, sw, sb, lat_ref, g_ref, hid_ref, xk):
    slots, _, h, w, c = fr.shape
    _fill_early(sc, fr, ha, xk)
    lat, g, hidden = _head(xk, _early_gout(sc, co), w_ref, cb, sw, sb, h)
    for s in range(1, slots):
        part = lat[(s - 1) * h * w : s * h * w]
        lat_ref[s - 1] = (
            jnp.where(s < sc[0], part, jnp.zeros_like(part)).astype(BF).reshape(h, w, c)
        )
    g_ref[...] = g
    hid_ref[...] = hidden


def _early_sums_kernel(sc, fr, ha, co, g_ref, hid_ref, acc, xk):
    _, _, h, w, c = fr.shape
    _fill_early(sc, fr, ha, xk)
    n9 = 9 * c

    def add(kind, value):
        if kind < 3:
            acc[kind * n9 : (kind + 1) * n9] = value
        elif kind == 3:
            acc[3 * n9 : 3 * n9 + 2 * c] = value
        else:
            at = 3 * n9 + 2 * c + (kind - 4)
            acc[at : at + 1] = value

    acc[3 * n9 + 2 * c :] = jnp.zeros((acc.shape[0] - 3 * n9 - 2 * c, c), F32)
    _weight_grads(xk, g_ref[...], hid_ref[...], _early_gout(sc, co), h, add)


def _late_kernel(
    sc, frs, has, tail, cos, w_ref, cb, sw, sb, early, lat_ref, g_ref, send, keep, xk, acc
):
    fr, ha, co = frs.at[0], has.at[0], cos.at[0]
    _, h, w, c = fr.shape
    on = sc[1] == 0
    for f in range(2):
        _put(xk, (0, f + 2), slice(1, 1 + h), fr[f])
        _put(xk, (0, f + 2), slice(0, 1), ha[f, :1])
        _put(xk, (0, f + 2), slice(h + 1, h + 2), ha[f, 1:])
        a = tail[f * h : (f + 1) * h]
        b = tail[2 * h + 2 * f : 2 * h + 2 * f + 2]
        a = jnp.where(on, a, jnp.zeros_like(a))
        b = jnp.where(on, b, jnp.zeros_like(b))
        _put(xk, (0, f), slice(1, 1 + h), a)
        _put(xk, (0, f), slice(0, 1), b[:1])
        _put(xk, (0, f), slice(h + 1, h + 2), b[1:])
    filled = sc[0] > 0
    gout = jnp.where(filled, co[0], jnp.zeros_like(co[0])).reshape(h * w, c)
    lat, g, hidden = _head(xk, gout, w_ref, cb, sw, sb, h)
    lat_ref[...] = jnp.where(filled, lat, jnp.zeros_like(lat)).astype(BF).reshape(h, w, c)
    g_ref[...] = g
    n9 = 9 * c

    def add(kind, value):
        if kind < 3:
            rows = slice(kind * n9, (kind + 1) * n9)
        elif kind == 3:
            rows = slice(3 * n9, 3 * n9 + 2 * c)
        else:
            at = 3 * n9 + 2 * c + (kind - 4)
            rows = slice(at, at + 1)
        acc[rows] = early[rows] + value

    tail_rows = slice(3 * n9 + 2 * c, acc.shape[0])
    acc[tail_rows] = early[tail_rows]

    @pl.when(sc[0] >= 0)
    def _():
        _weight_grads(xk, g, hidden, gout, h, add)

    half = send.shape[0]
    core = sc[sc.shape[0] - 1]
    send[...] = acc[pl.ds(pl.multiple_of((1 - core) * half, 16), half)].astype(BF)
    keep[...] = acc[pl.ds(pl.multiple_of(core * half, 16), half)]


def _back_kernel(sc, g0, g1, w_ref, out_ref, cache_ref, xk):
    slots, _, h, w, c = out_ref.shape
    m = h * w
    zero = jnp.zeros((1, w, c), BF)
    for kw in range(3):
        for j in range(4):
            for s in range(slots + 1):
                xk[kw, s, j, 0:1] = zero
                xk[kw, s, j, h + 1 : h + 2] = zero
    blank = jnp.zeros((h, w, c), BF)
    for f in range(2):
        for kw in range(3):
            xk[kw, 0, f, 1 : 1 + h] = blank
            xk[kw, slots, f + 2, 1 : 1 + h] = blank
        lanes = slice(f * c, (f + 1) * c)
        for s in range(slots):
            v = g0[:, lanes] if s == 0 else g1[(s - 1) * m : s * m, lanes]
            v = v.reshape(h, w, c)
            _put(xk, (s + 1, f), slice(1, 1 + h), v)
            _put(
                xk, (s, f + 2), slice(1, 1 + h), jnp.where(sc[1 + s] == 0, v, jnp.zeros_like(v))
            )
    out = _conv_back(xk, w_ref, h)
    hw = h * w
    live = sc[0] > 0
    for f in range(2):
        lanes = slice(f * c, (f + 1) * c)
        cache = out[:hw, lanes]
        cache = jnp.where(live, cache, jnp.full_like(cache, EMPTY_GRAD))
        cache_ref[f * h : (f + 1) * h] = cache.astype(BF).reshape(h, w, c)
        out_ref[:, f] = out[hw:, lanes].reshape(slots, h, w, c)


def _cut_kernel(sc, keep, got, own, *sends):
    rows = own.shape[0]
    chip = sc[sc.shape[0] - 2]

    def piece(p):
        at = pl.ds(pl.multiple_of(p * rows, 16), rows)
        return keep[at] + got[at].astype(F32)

    own[...] = piece(chip)
    for k, ref in enumerate(sends):
        ref[...] = piece(lax.bitwise_xor(chip, k + 1)).astype(BF)


def _tail_kernel(sc, fr, ha, out):
    h2 = fr.shape[1] * fr.shape[2]
    live = sc[0] > 0
    for ref, rows in ((fr, slice(0, h2)), (ha, slice(h2, out.shape[0]))):
        v = ref[...].reshape(rows.stop - rows.start, *out.shape[1:])
        out[rows] = jnp.where(live, v, jnp.full_like(v, EMPTY_FRAME))


def _final_kernel(sc, *refs):
    pieces, (other, cw, sw, cb, sb, acc) = refs[:-6], refs[-6:]
    rows, c = pieces[0].shape
    half = rows * len(pieces)
    chip = sc[sc.shape[0] - 2]
    core = sc[sc.shape[0] - 1]
    for k, ref in enumerate(pieces):
        at = lax.bitwise_xor(chip, k) * rows
        acc[pl.ds(pl.multiple_of(core * half + at, 16), rows)] = ref[...].astype(F32)
        acc[pl.ds(pl.multiple_of((1 - core) * half + at, 16), rows)] = other[
            k * rows : (k + 1) * rows
        ].astype(F32)
    n27, n29 = 27 * c, 29 * c
    cw[...] = acc[:n27]
    sw[...] = acc[n27:n29]
    cb[...] = acc[n29 : n29 + 1]
    sb[...] = acc[n29 + 1 : n29 + 2]


def _xor(x, k, n, axis):
    return lax.ppermute(x, axis, [(i, i ^ k) for i in range(n)])


def _latest_before(x, empty, axis, n, reverse=False, beside_first=None, beside_second=None):
    index = lax.axis_index(axis)
    index = n - 1 - index if reverse else index
    core, pair = index & 1, (index >> 1) & 1

    def shift(v, k):
        pairs = [(i, i + k) for i in range(n - k)]
        return lax.ppermute(v, axis, [(b, a) for a, b in pairs] if reverse else pairs)

    def newest(early, late):
        return jnp.where(late > empty / 2, early, late)

    def part(v, at):
        half = v.shape[0] // 2
        return jnp.where(at == 0, v[:half], v[half:])

    def join(mine, other, at):
        return jnp.concatenate(
            [jnp.where(at == 0, mine, other), jnp.where(at == 0, other, mine)], axis=0
        )

    other = _xor(x, 1, n, axis)
    chip = part(jnp.where(core == 0, newest(x, other), newest(other, x)), core)
    beside = _xor(chip, 2, n, axis)
    quad = part(jnp.where(pair == 0, newest(chip, beside), newest(beside, chip)), pair)
    if beside_first is not None:
        quad = beside_first(chip, quad)
    blocks = n // 4
    before = None
    for k in range(min(3, blocks - 1), 0, -1):
        came = shift(quad, 4 * k)
        before = came if before is None else newest(before, came)
    reach = min(3, blocks - 1)
    while reach < blocks - 1:
        before = newest(shift(before, 4 * reach), before)
        reach *= 2
    first = before
    before = join(before, _xor(before, 2, n, axis), pair)
    before = jnp.where(pair == 0, before, newest(before, beside))
    if beside_second is not None:
        before = beside_second(first, before)
    before = join(before, _xor(before, 1, n, axis), core)
    before = jnp.where(core == 0, before, newest(before, other))
    return jnp.where(before > empty / 2, jnp.zeros_like(before), before)


def _after(value, *earlier):
    return lax.optimization_barrier((value, *earlier))[0]


def body(
    n,
    frames,
    row_halo,
    clip_start,
    slab_counts,
    conv_weight,
    conv_bias,
    stride_weight,
    stride_bias,
    cotangent,
):
    axis = "tm"
    slots, _, h, w, c = frames.shape
    count = slab_counts[0]
    index = lax.axis_index(axis)
    chips = min(8, n // 2)
    sc = jnp.concatenate(
        [
            slab_counts,
            clip_start,
            ((index >> 1) & (chips - 1)).reshape(1).astype(jnp.int32),
            (index & 1).reshape(1).astype(jnp.int32),
        ]
    )
    wt = conv_weight.reshape(27, c, c)
    cb, sb = conv_bias.reshape(1, c), stride_bias.reshape(1, c)
    unit = 16 * 2 * chips
    rows = -(-(29 * c + 2) // unit) * unit
    m = h * w
    conv_flops = 2 * m * 36 * c * 2 * c

    def newest_slot(i, sc):
        return (jnp.maximum(sc[0] - 1, 0), 0, 0, 0, 0)

    tail = pl.pallas_call(
        _tail_kernel,
        out_shape=jax.ShapeDtypeStruct((2 * h + 4, w, c), BF),
        grid_spec=pltpu.PrefetchScalarGridSpec(
            num_scalar_prefetch=1,
            grid=(1,),
            in_specs=[
                pl.BlockSpec((1, 2, h, w, c), newest_slot),
                pl.BlockSpec((1, 2, 2, w, c), newest_slot),
            ],
            out_specs=pl.BlockSpec((2 * h + 4, w, c), lambda i, sc: (0, 0, 0)),
        ),
        compiler_params=pltpu.CompilerParams(vmem_limit_bytes=60 << 20),
    )(slab_counts, frames, row_halo)

    held = {}

    def early_forward(start, follow):
        held["early"] = _call(
            _early_kernel,
            [
                jax.ShapeDtypeStruct((slots - 1, h, w, c), BF),
                jax.ShapeDtypeStruct(((slots - 1) * m, 2 * c), BF),
                jax.ShapeDtypeStruct(((slots - 1) * m, 2 * c), BF),
            ],
            [_SMEM] + [_VMEM] * 7,
            [pltpu.VMEM((3, slots - 1, 4, h + 2, w, c), BF)],
            flops=(slots - 1) * conv_flops,
            moved=4 << 20,
        )(_after(sc, start), frames, row_halo, cotangent, wt, cb, stride_weight, sb)
        return _after(follow, held["early"][1])

    def early_sums(start, follow):
        _, g1, hid1 = held["early"]
        held["sums"] = _call(
            _early_sums_kernel,
            jax.ShapeDtypeStruct((rows, c), F32),
            [_SMEM] + [_VMEM] * 5,
            [pltpu.VMEM((3, slots - 1, 4, h + 2, w, c), BF)],
            flops=(slots - 1) * conv_flops,
            moved=4 << 20,
        )(_after(sc, start), frames, row_halo, cotangent, g1, hid1)
        return _after(follow, held["sums"])

    arrived = _latest_before(
        tail, EMPTY_FRAME, axis, n, beside_first=early_forward, beside_second=early_sums
    )
    lat1, g1, _ = held["early"]

    def first(*shape):
        return pl.BlockSpec((1, *shape), lambda i: (0,) * (len(shape) + 1))

    lat0, g0, send, keep = _call(
        _late_kernel,
        [
            jax.ShapeDtypeStruct((h, w, c), BF),
            jax.ShapeDtypeStruct((m, 2 * c), BF),
            jax.ShapeDtypeStruct((rows // 2, c), BF),
            jax.ShapeDtypeStruct((rows // 2, c), F32),
        ],
        [_SMEM, first(2, h, w, c), first(2, 2, w, c), _VMEM, first(1, h, w, c)] + [_VMEM] * 5,
        [pltpu.VMEM((3, 1, 4, h + 2, w, c), BF), pltpu.VMEM((rows, c), F32)],
        flops=2 * conv_flops,
        moved=6 << 20,
        grid=(1,),
    )(sc, frames, row_halo, arrived, cotangent, wt, cb, stride_weight, sb, held["sums"])

    got = _xor(send, 1, n, axis)
    piece = rows // 2 // chips
    own, *outs = _call(
        _cut_kernel,
        [jax.ShapeDtypeStruct((piece, c), F32)]
        + [jax.ShapeDtypeStruct((piece, c), BF)] * (chips - 1),
        [_SMEM, _VMEM, _VMEM],
        room=12,
    )(sc, keep, got)

    grad, cache = _call(
        _back_kernel,
        [
            jax.ShapeDtypeStruct((slots, 2, h, w, c), F32),
            jax.ShapeDtypeStruct((2 * h, w, c), BF),
        ],
        [_SMEM] + [_VMEM] * 3,
        [pltpu.VMEM((3, slots + 1, 4, h + 2, w, c), BF)],
        flops=(slots + 1) * conv_flops,
        moved=6 << 20,
        room=24,
    )(_after(sc, own), g0, g1, wt)

    total = _after(own, cache)
    for k in range(1, chips):
        total = total + _xor(outs[k - 1], 2 * k, n, axis).astype(F32)
    mine = total.astype(BF)
    k = 2 * chips
    while k < n:
        mine = (mine.astype(F32) + _xor(mine, k, n, axis).astype(F32)).astype(BF)
        k *= 2
    pieces = [mine] + [_xor(mine, 2 * k, n, axis) for k in range(1, chips)]
    other = _xor(jnp.concatenate(pieces, axis=0), 1, n, axis)
    cwg, swg, cbg, sbg = _call(
        _final_kernel,
        [
            jax.ShapeDtypeStruct((27 * c, c), F32),
            jax.ShapeDtypeStruct((2 * c, c), F32),
            jax.ShapeDtypeStruct((1, c), F32),
            jax.ShapeDtypeStruct((1, c), F32),
        ],
        [_SMEM] + [_VMEM] * (chips + 1),
        [pltpu.VMEM((rows, c), F32)],
        room=12,
    )(sc, *pieces, other)

    returned = _latest_before(cache, EMPTY_GRAD, axis, n, reverse=True)
    newest = (jnp.arange(slots, dtype=jnp.int32) == count - 1)[:, None, None, None, None]
    back = returned.reshape(1, 2, h, w, c).astype(F32)
    frames_grad = (grad + jnp.where(newest, back, jnp.zeros_like(back))).astype(BF)
    latents = jnp.concatenate([lat0[None], lat1], axis=0)[:, None]
    return (
        latents,
        frames_grad,
        cwg.reshape(3, 3, 3, c, c),
        cbg[0],
        swg.reshape(2, c, c),
        sbg[0],
    )


def solution(mesh):
    split = P(("groups", "tm"))
    return jax.shard_map(
        functools.partial(body, mesh.shape["tm"]),
        mesh=mesh,
        in_specs=(split, split, split, split, P(), P(), P(), P(), split),
        out_specs=(split, split, P("groups"), P("groups"), P("groups"), P("groups")),
        check_vma=False,
    )
```

```python
import functools

import jax
import jax.numpy as jnp
from jax import lax
from jax.experimental import pallas as pl
from jax.experimental.pallas import tpu as pltpu
from jax.sharding import PartitionSpec as P

BF = jnp.bfloat16
F32 = jnp.float32
EMPTY_FRAME = 100.0
EMPTY_GRAD = 1e30

_VMEM = pl.BlockSpec(memory_space=pltpu.VMEM)
_SMEM = pl.BlockSpec(memory_space=pltpu.SMEM)
_HBM = pl.BlockSpec(memory_space=pltpu.HBM)


def _call(kernel, out_shape, in_specs, scratch=(), flops=0, moved=0, room=16, grid=()):
    return pl.pallas_call(
        kernel,
        out_shape=out_shape,
        grid=grid,
        in_specs=in_specs,
        out_specs=jax.tree.map(lambda _: _VMEM, out_shape),
        scratch_shapes=list(scratch),
        compiler_params=pltpu.CompilerParams(vmem_limit_bytes=room << 20),
        cost_estimate=pl.CostEstimate(flops=flops, bytes_accessed=moved, transcendentals=0),
    )


def _put(xk, at, rows, value):
    n, w, c = value.shape
    flat = value.astype(F32).reshape(n * w, c)
    col = lax.broadcasted_iota(jnp.int32, (n * w, c), 0) % w
    right = jnp.where(col == 0, 0.0, pltpu.roll(flat, 1, 0))
    left = jnp.where(col == w - 1, 0.0, pltpu.roll(flat, n * w - 1, 0))
    for kw, shifted in enumerate((right, flat, left)):
        xk[(kw, *at, rows)] = shifted.astype(BF).reshape(n, w, c)


def _window(xk, kw, j, kh, h):
    v = xk[kw, :, j, kh : kh + h]
    return v.reshape(v.shape[0] * v.shape[1] * v.shape[2], v.shape[3])


def _wide(xk, j, h):
    return jnp.concatenate(
        [_window(xk, kw, j, kh, h) for kh in range(3) for kw in range(3)], axis=1
    )


def _conv(xk, w_ref, h):
    c = w_ref.shape[-1]
    zero = jnp.zeros((c, c), BF)
    lhs = jnp.concatenate([_wide(xk, j, h) for j in range(4)], axis=1)
    rhs = []
    for j in range(4):
        for tap in range(9):
            rhs.append(
                jnp.concatenate(
                    [w_ref[(j - t) * 9 + tap] if 0 <= j - t <= 2 else zero for t in range(2)],
                    axis=1,
                )
            )
    return jnp.dot(lhs, jnp.concatenate(rhs, axis=0), preferred_element_type=F32)


def _conv_back(xk, w_ref, h, frames=range(4)):
    c = w_ref.shape[-1]
    zero = jnp.zeros((c, c), BF)
    lhs = jnp.concatenate([_wide(xk, j, h) for j in frames], axis=1)
    rhs = []
    for f in range(2):
        row = []
        for j in frames:
            for tap in range(9):
                kt = 2 - (j - f)
                row.append(w_ref[kt * 9 + 8 - tap] if 0 <= kt <= 2 else zero)
        rhs.append(jnp.concatenate(row, axis=1))
    return lax.dot_general(
        lhs, jnp.concatenate(rhs, axis=0), (((1,), (1,)), ((), ())), preferred_element_type=F32
    )


def _head(xk, gout, w_ref, cb_ref, sw_ref, sb_ref, h):
    pre = _conv(xk, w_ref, h) + jnp.concatenate([cb_ref[...], cb_ref[...]], axis=1)
    s = 1.0 / (1.0 + jnp.exp(-pre))
    hidden = (pre * s).astype(BF)
    sw = jnp.concatenate([sw_ref[0], sw_ref[1]], axis=0)
    lat = jnp.dot(hidden, sw, preferred_element_type=F32) + sb_ref[...]
    gh = lax.dot_general(gout, sw, (((1,), (1,)), ((), ())), preferred_element_type=F32)
    g = (gh * s * (1.0 + pre * (1.0 - s))).astype(BF)
    return lat, g, hidden


def _weight_grads(xk, g, hidden, gout, h, add):
    c = gout.shape[-1]
    parts = []
    for j in range(4):
        lhs = _wide(xk, j, h)
        parts.append(
            lax.dot_general(lhs, g, (((0,), (0,)), ((), ())), preferred_element_type=F32)
        )
    for kt in range(3):
        add(kt, parts[kt][:, :c] + parts[kt + 1][:, c:])
    sg = lax.dot_general(hidden, gout, (((0,), (0,)), ((), ())), preferred_element_type=F32)
    g32 = jnp.sum(g.astype(F32), axis=0, keepdims=True)
    add(3, sg)
    add(4, g32[:, :c] + g32[:, c:])
    add(5, jnp.sum(gout.astype(F32), axis=0, keepdims=True))


def _fill_early(sc, fr, ha, xk):
    slots, _, h, w, c = fr.shape
    for s in range(slots):
        for f in range(2):
            spots = [(s - 1, f + 2, None)] if s > 0 else []
            if s + 1 < slots:
                spots.append((s, f, sc[1 + s + 1] == 0))
            for slot, j, keep in spots:
                a, b = fr[s, f], ha[s, f]
                if keep is not None:
                    a = jnp.where(keep, a, jnp.zeros_like(a))
                    b = jnp.where(keep, b, jnp.zeros_like(b))
                _put(xk, (slot, j), slice(1, 1 + h), a)
                _put(xk, (slot, j), slice(0, 1), b[:1])
                _put(xk, (slot, j), slice(h + 1, h + 2), b[1:])


def _early_gout(sc, co):
    slots, _, h, w, c = co.shape
    return jnp.concatenate(
        [
            jnp.where(s < sc[0], co[s, 0], jnp.zeros_like(co[s, 0])).reshape(h * w, c)
            for s in range(1, slots)
        ],
        axis=0,
    )


def _early_kernel(
    sc, frh, hah, coh, wh, cb, sw, sb, lat_ref, g_ref, hid_ref, gout_ref, xk, fr, ha, co, w_ref, sems
):
    slots, _, h, w, c = fr.shape
    pairs = ((frh, fr), (hah, ha), (coh, co), (wh, w_ref))
    copies = [pltpu.make_async_copy(a, b, sems.at[i]) for i, (a, b) in enumerate(pairs)]
    for copy in copies:
        copy.start()
    copies[0].wait()
    copies[1].wait()
    _fill_early(sc, fr, ha, xk)
    copies[2].wait()
    gout = _early_gout(sc, co)
    gout_ref[...] = gout
    copies[3].wait()
    lat, g, hidden = _head(xk, gout, w_ref, cb, sw, sb, h)
    for s in range(1, slots):
        part = lat[(s - 1) * h * w : s * h * w]
        lat_ref[s - 1] = (
            jnp.where(s < sc[0], part, jnp.zeros_like(part)).astype(BF).reshape(h, w, c)
        )
    g_ref[...] = g
    hid_ref[...] = hidden


def _early_sums_kernel(sc, g_ref, hid_ref, gout_ref, xk, acc):
    c = gout_ref.shape[-1]
    h = xk.shape[3] - 2
    n9 = 9 * c

    def add(kind, value):
        if kind < 3:
            acc[kind * n9 : (kind + 1) * n9] = value
        elif kind == 3:
            acc[3 * n9 : 3 * n9 + 2 * c] = value
        else:
            at = 3 * n9 + 2 * c + (kind - 4)
            acc[at : at + 1] = value

    acc[3 * n9 + 2 * c :] = jnp.zeros((acc.shape[0] - 3 * n9 - 2 * c, c), F32)
    _weight_grads(xk, g_ref[...], hid_ref[...], gout_ref[...], h, add)


def _late_kernel(
    sc, frs, has, tail, cos, w_ref, cb, sw, sb, early, lat_ref, g_ref, send, keep, cache_ref, xk, acc
):
    fr, ha, co = frs.at[0], has.at[0], cos.at[0]
    _, h, w, c = fr.shape
    on = sc[1] == 0
    for f in range(2):
        _put(xk, (0, f + 2), slice(1, 1 + h), fr[f])
        _put(xk, (0, f + 2), slice(0, 1), ha[f, :1])
        _put(xk, (0, f + 2), slice(h + 1, h + 2), ha[f, 1:])
        a = tail[f * h : (f + 1) * h]
        b = tail[2 * h + 2 * f : 2 * h + 2 * f + 2]
        a = jnp.where(on, a, jnp.zeros_like(a))
        b = jnp.where(on, b, jnp.zeros_like(b))
        _put(xk, (0, f), slice(1, 1 + h), a)
        _put(xk, (0, f), slice(0, 1), b[:1])
        _put(xk, (0, f), slice(h + 1, h + 2), b[1:])
    filled = sc[0] > 0
    gout = jnp.where(filled, co[0], jnp.zeros_like(co[0])).reshape(h * w, c)
    lat, g, hidden = _head(xk, gout, w_ref, cb, sw, sb, h)
    lat_ref[...] = jnp.where(filled, lat, jnp.zeros_like(lat)).astype(BF).reshape(h, w, c)
    g_ref[...] = g
    n9 = 9 * c

    def add(kind, value):
        if kind < 3:
            rows = slice(kind * n9, (kind + 1) * n9)
        elif kind == 3:
            rows = slice(3 * n9, 3 * n9 + 2 * c)
        else:
            at = 3 * n9 + 2 * c + (kind - 4)
            rows = slice(at, at + 1)
        acc[rows] = early[rows] + value

    tail_rows = slice(3 * n9 + 2 * c, acc.shape[0])
    acc[tail_rows] = early[tail_rows]

    @pl.when(sc[0] >= 0)
    def _():
        _weight_grads(xk, g, hidden, gout, h, add)

        for t in range(2):
            for kw in range(3):
                xk[kw, 0, 2 + t, 0:1] = jnp.zeros((1, w, c), BF)
                xk[kw, 0, 2 + t, h + 1 : h + 2] = jnp.zeros((1, w, c), BF)
            v = g[:, t * c : (t + 1) * c].reshape(h, w, c)
            _put(xk, (0, 2 + t), slice(1, 1 + h), jnp.where(on, v, jnp.zeros_like(v)))
        back = _conv_back(xk, w_ref, h, (2, 3))
        back = jnp.where(filled, back, jnp.full_like(back, EMPTY_GRAD)).astype(BF)
        half = keep.shape[0]
        for t in range(2):
            lanes = slice(t * c, (t + 1) * c)
            cache_ref[t * h * w : (t + 1) * h * w] = back[:, lanes]
            send[half + t * h * w : half + (t + 1) * h * w] = back[:, lanes]
        core = sc[sc.shape[0] - 1]
        send[:half] = acc[pl.ds(pl.multiple_of((1 - core) * half, 16), half)].astype(BF)
        keep[...] = acc[pl.ds(pl.multiple_of(core * half, 16), half)]


def _back_kernel(sc, g0, g1, w_ref, out_ref, xk):
    slots, _, h, w, c = out_ref.shape
    m = h * w
    zero = jnp.zeros((1, w, c), BF)
    for kw in range(3):
        for j in range(4):
            for s in range(slots):
                xk[kw, s, j, 0:1] = zero
                xk[kw, s, j, h + 1 : h + 2] = zero
    for f in range(2):
        for kw in range(3):
            xk[kw, slots - 1, f + 2, 1 : 1 + h] = jnp.zeros((h, w, c), BF)
        lanes = slice(f * c, (f + 1) * c)
        for s in range(slots):
            v = g0[:, lanes] if s == 0 else g1[(s - 1) * m : s * m, lanes]
            v = v.reshape(h, w, c)
            _put(xk, (s, f), slice(1, 1 + h), v)
            if s > 0:
                on = sc[1 + s] == 0
                _put(xk, (s - 1, f + 2), slice(1, 1 + h), jnp.where(on, v, jnp.zeros_like(v)))
    out = _conv_back(xk, w_ref, h)
    for f in range(2):
        out_ref[:, f] = out[:, f * c : (f + 1) * c].reshape(slots, h, w, c)


def _first_live(a, b):
    return jnp.where(a.astype(F32) < EMPTY_GRAD / 2, a, b)


def _place(sc):
    chip, core = sc[sc.shape[0] - 2], sc[sc.shape[0] - 1]
    return lax.shift_right_logical(chip, 1), lax.bitwise_and(chip, 1), core


def _across_x_kernel(sc, keep, got, cache, send, kept):
    z, x, core = _place(sc)
    del z
    half = keep.shape[0]
    blocks = 4
    rows = half // (2 * blocks)

    def piece(p):
        at = pl.ds(pl.multiple_of(p * rows, 16), rows)
        return keep[at] + got[at].astype(F32)

    for b in range(blocks):
        kept[b * rows : (b + 1) * rows] = piece(2 * b + x)
        send[b * rows : (b + 1) * rows] = piece(2 * b + 1 - x).astype(BF)
    part = cache.shape[0] // 2
    at = pl.multiple_of(core * part, 16)
    mine, theirs = cache[pl.ds(at, part)], got[pl.ds(half + at, part)]
    first = jnp.where(core == 0, _first_live(mine, theirs), _first_live(theirs, mine))
    send[blocks * rows :] = first


def _across_z_kernel(sc, kept, got, sent, own, *sends):
    z, x, core = _place(sc)
    del core
    rows = own.shape[0]
    below = kept.shape[0]
    part = (sent.shape[0] - below) // 2

    def piece(b):
        at = pl.ds(pl.multiple_of(b * rows, 16), rows)
        return kept[at] + got[at].astype(F32)

    at = pl.ds(pl.multiple_of(below + x * part, 16), part)
    first = jnp.where(x == 0, _first_live(sent[at], got[at]), _first_live(got[at], sent[at]))
    own[...] = piece(z)
    for j, ref in enumerate(sends):
        ref[:rows] = piece(lax.bitwise_xor(z, j + 1)).astype(BF)
        ref[rows:] = first


def _sum_kernel(sc, own, *refs):
    gots, (mine, after) = refs[:-2], refs[-2:]
    z, _, _ = _place(sc)
    rows = own.shape[0]
    total = own[...]
    for ref in gots:
        total = total + ref[:rows].astype(F32)
    mine[...] = total.astype(BF)
    best = jnp.full(after.shape, EMPTY_GRAD, F32)
    for target in range(len(gots), 0, -1):
        for j, ref in enumerate(gots):
            here = jnp.logical_and(lax.bitwise_xor(z, j + 1) == target, target > z)
            value = ref[rows:].astype(F32)
            use = jnp.where(here, value, jnp.full_like(value, EMPTY_GRAD))
            best = _first_live(use, best)
    after[...] = best.astype(BF)


def _tail_kernel(sc, fr, ha, out):
    h2 = fr.shape[1] * fr.shape[2]
    live = sc[0] > 0
    for ref, rows in ((fr, slice(0, h2)), (ha, slice(h2, out.shape[0]))):
        v = ref[...].reshape(rows.stop - rows.start, *out.shape[1:])
        out[rows] = jnp.where(live, v, jnp.full_like(v, EMPTY_FRAME))


def _final_kernel(sc, mine, other, got, grad, cw, sw, cb, sb, fg, acc):
    c = mine.shape[1]
    half = acc.shape[0] // 2
    z, x, core = _place(sc)
    blocks = 4
    rows = half // (2 * blocks)
    for ref, at_core in ((mine, core), (other, 1 - core)):
        for k in range(2 * blocks):
            side = x if k < blocks else 1 - x
            chip = 2 * lax.bitwise_xor(z, k % blocks) + side
            at = pl.multiple_of(at_core * half + chip * rows, 16)
            acc[pl.ds(at, rows)] = ref[k * rows : (k + 1) * rows].astype(F32)
    n27, n29 = 27 * c, 29 * c
    cw[...] = acc[:n27]
    sw[...] = acc[n27:n29]
    cb[...] = acc[n29 : n29 + 1]
    sb[...] = acc[n29 + 1 : n29 + 2]
    slots, frames, h, w, _ = grad.shape
    part = mine.shape[0] - half
    for s in range(slots):
        here = sc[0] - 1 == s
        for f in range(frames):
            low = f == 0
            a, b = mine[half:].astype(F32), other[half:].astype(F32)
            beyond = jnp.where(core == 0, a, b) if low else jnp.where(core == 0, b, a)
            beside = got[half + f * part : half + (f + 1) * part].astype(F32)
            came = jnp.where(core == 0, _first_live(beside, beyond), beyond)
            came = jnp.where(came < EMPTY_GRAD / 2, came, jnp.zeros_like(came)).reshape(h, w, c)
            fg[s, f] = (grad[s, f] + jnp.where(here, came, jnp.zeros_like(came))).astype(BF)


def _xor(x, k, n, axis):
    return lax.ppermute(x, axis, [(i, i ^ k) for i in range(n)])


def _latest_before(x, empty, axis, n, beside_x, beside_z):
    index = lax.axis_index(axis)
    core, pair = index & 1, (index >> 1) & 1

    def shift(v, k):
        return lax.ppermute(v, axis, [(i, i + k) for i in range(n - k)])

    def newest(early, late):
        return jnp.where(late > empty / 2, early, late)

    def half(v):
        rows = v.shape[0] // 2
        return jnp.where(core == 0, v[:rows], v[rows:])

    other = _xor(x, 1, n, axis)
    a, b = half(x), half(other)
    chip = jnp.where(core == 0, newest(a, b), newest(b, a))
    beside = _xor(chip, 2, n, axis)
    quad = jnp.where(pair == 0, newest(chip, beside), newest(beside, chip))
    quad = beside_x(chip, quad)
    before, reach = None, 0
    while reach < n // 4 - 1:
        start = quad if before is None else newest(before, quad)
        came = shift(start, 4 * (reach + 1))
        before = came if before is None else newest(came, before)
        reach = 2 * reach + 1
        if reach == 3:
            before = beside_z(start, before)
    before = jnp.where(pair == 0, before, newest(before, beside))
    across = _xor(before, 1, n, axis)
    before = jnp.concatenate(
        [jnp.where(core == 0, before, across), jnp.where(core == 0, across, before)], axis=0
    )
    before = jnp.where(core == 0, before, newest(before, other))
    return jnp.where(before > empty / 2, jnp.zeros_like(before), before)


def _after(value, *earlier):
    return lax.optimization_barrier((value, *earlier))[0]


def body(
    n,
    frames,
    row_halo,
    clip_start,
    slab_counts,
    conv_weight,
    conv_bias,
    stride_weight,
    stride_bias,
    cotangent,
):
    axis = "tm"
    slots, _, h, w, c = frames.shape
    count = slab_counts[0]
    index = lax.axis_index(axis)
    chips = 8
    assert n % (2 * chips) == 0
    sc = jnp.concatenate(
        [
            slab_counts,
            clip_start,
            ((index >> 1) & (chips - 1)).reshape(1).astype(jnp.int32),
            (index & 1).reshape(1).astype(jnp.int32),
        ]
    )
    wt = conv_weight.reshape(27, c, c)
    cb, sb = conv_bias.reshape(1, c), stride_bias.reshape(1, c)
    unit = 16 * 2 * chips
    rows = -(-(29 * c + 2) // unit) * unit
    m = h * w
    conv_flops = 2 * m * 36 * c * 2 * c

    def newest_slot(i, sc):
        return (jnp.maximum(sc[0] - 1, 0), 0, 0, 0, 0)

    tail = pl.pallas_call(
        _tail_kernel,
        out_shape=jax.ShapeDtypeStruct((2 * h + 4, w, c), BF),
        grid_spec=pltpu.PrefetchScalarGridSpec(
            num_scalar_prefetch=1,
            grid=(1,),
            in_specs=[
                pl.BlockSpec((1, 2, h, w, c), newest_slot),
                pl.BlockSpec((1, 2, 2, w, c), newest_slot),
            ],
            out_specs=pl.BlockSpec((2 * h + 4, w, c), lambda i, sc: (0, 0, 0)),
        ),
        compiler_params=pltpu.CompilerParams(vmem_limit_bytes=60 << 20),
    )(slab_counts, frames, row_halo)

    held = {}
    wide = ((slots - 1) * m, 2 * c)
    windows = (3, slots - 1, 4, h + 2, w, c)

    def early_forward(start, follow):
        held["early"] = _call(
            _early_kernel,
            [
                jax.ShapeDtypeStruct((slots - 1, h, w, c), BF),
                jax.ShapeDtypeStruct(wide, BF),
                jax.ShapeDtypeStruct(wide, BF),
                jax.ShapeDtypeStruct((wide[0], c), BF),
                jax.ShapeDtypeStruct(windows, BF),
            ],
            [_SMEM] + [_HBM] * 4 + [_VMEM] * 3,
            [pltpu.VMEM(v.shape, BF) for v in (frames, row_halo, cotangent, wt)]
            + [pltpu.SemaphoreType.DMA((4,))],
            flops=(slots - 1) * conv_flops,
            moved=4 << 20,
        )(_after(sc, start), frames, row_halo, cotangent, wt, cb, stride_weight, sb)
        return _after(follow, held["early"][1])

    def early_sums(start, follow):
        _, g1, hid1, gout1, xk1 = held["early"]
        held["sums"] = _call(
            _early_sums_kernel,
            jax.ShapeDtypeStruct((rows, c), F32),
            [_SMEM] + [_VMEM] * 4,
            flops=(slots - 1) * conv_flops,
            moved=4 << 20,
        )(_after(sc, start), g1, hid1, gout1, xk1)
        return _after(follow, held["sums"])

    arrived = _latest_before(tail, EMPTY_FRAME, axis, n, early_forward, early_sums)
    lat1, g1 = held["early"][:2]

    def first(*shape):
        return pl.BlockSpec((1, *shape), lambda i: (0,) * (len(shape) + 1))

    half, carried = rows // 2, 2 * m
    lat0, g0, send, keep, cache = _call(
        _late_kernel,
        [
            jax.ShapeDtypeStruct((h, w, c), BF),
            jax.ShapeDtypeStruct((m, 2 * c), BF),
            jax.ShapeDtypeStruct((half + carried, c), BF),
            jax.ShapeDtypeStruct((half, c), F32),
            jax.ShapeDtypeStruct((carried, c), BF),
        ],
        [_SMEM, first(2, h, w, c), first(2, 2, w, c), _VMEM, first(1, h, w, c)] + [_VMEM] * 5,
        [pltpu.VMEM((3, 1, 4, h + 2, w, c), BF), pltpu.VMEM((rows, c), F32)],
        flops=2 * conv_flops,
        moved=6 << 20,
        grid=(1,),
    )(sc, frames, row_halo, arrived, cotangent, wt, cb, stride_weight, sb, held["sums"])

    blocks = chips // 2
    piece = half // chips
    got = _xor(send, 1, n, axis)
    send_x, keep_x = _call(
        _across_x_kernel,
        [
            jax.ShapeDtypeStruct((blocks * piece + carried // 2, c), BF),
            jax.ShapeDtypeStruct((blocks * piece, c), F32),
        ],
        [_SMEM] + [_VMEM] * 3,
        room=8,
    )(sc, keep, got, cache)
    got_x = _xor(send_x, 2, n, axis)
    grad = _call(
        _back_kernel,
        jax.ShapeDtypeStruct((slots, 2, h, w, c), F32),
        [_SMEM] + [_VMEM] * 3,
        [pltpu.VMEM((3, slots, 4, h + 2, w, c), BF)],
        flops=slots * conv_flops,
        moved=6 << 20,
        room=24,
    )(_after(sc, keep_x), g0, g1, wt)
    own, *sends = _call(
        _across_z_kernel,
        [jax.ShapeDtypeStruct((piece, c), F32)]
        + [jax.ShapeDtypeStruct((piece + carried // 4, c), BF)] * (blocks - 1),
        [_SMEM] + [_VMEM] * 3,
        room=8,
    )(_after(sc, grad), keep_x, got_x, send_x)
    gots = [_xor(v, 4 * (j + 1), n, axis) for j, v in enumerate(sends)]
    mine, after = _call(
        _sum_kernel,
        [jax.ShapeDtypeStruct((piece, c), BF), jax.ShapeDtypeStruct((carried // 4, c), BF)],
        [_SMEM] + [_VMEM] * blocks,
        room=8,
    )(sc, own, *gots)
    k = 2 * chips
    if k < n:
        z = (index >> 2) & (blocks - 1)
        lead = sends[0][piece:]
        for target in range(blocks - 1, -1, -1):
            for j, v in enumerate(gots):
                lead = jnp.where((z ^ (j + 1)) == target, _first_live(v[piece:], lead), lead)
            lead = jnp.where(z == target, _first_live(sends[0][piece:], lead), lead)
        beyond, reach = None, 0
        while reach < n // k - 1:
            start = lead if beyond is None else _first_live(lead, beyond)
            step = k * (reach + 1)
            came = lax.ppermute(start, axis, [(i + step, i) for i in range(n - step)])
            beyond = came if beyond is None else _first_live(beyond, came)
            reach = 2 * reach + 1
        after = _first_live(after, beyond)
    while k < n:
        mine = (mine.astype(F32) + _xor(mine, k, n, axis).astype(F32)).astype(BF)
        k *= 2
    pieces = [mine] + [_xor(mine, 4 * (j + 1), n, axis) for j in range(blocks - 1)]
    back_x = jnp.concatenate(pieces + [after], axis=0)
    got_back = _xor(back_x, 2, n, axis)
    pair, below = (index >> 1) & 1, blocks * piece
    theirs = got_back[below:]
    beyond = jnp.concatenate(
        [jnp.where(pair == 0, after, theirs), jnp.where(pair == 0, theirs, after)], axis=0
    )
    beyond = jnp.where(pair == 0, _first_live(got_x[below:], beyond), beyond)
    ours = jnp.concatenate([*pieces, got_back[:below], beyond], axis=0)
    other = _xor(ours, 1, n, axis)
    cwg, swg, cbg, sbg, frames_grad = _call(
        _final_kernel,
        [
            jax.ShapeDtypeStruct((27 * c, c), F32),
            jax.ShapeDtypeStruct((2 * c, c), F32),
            jax.ShapeDtypeStruct((1, c), F32),
            jax.ShapeDtypeStruct((1, c), F32),
            jax.ShapeDtypeStruct((slots, 2, h, w, c), BF),
        ],
        [_SMEM] + [_VMEM] * 4,
        [pltpu.VMEM((rows, c), F32)],
        room=12,
    )(sc, ours, other, got, grad)
    latents = jnp.concatenate([lat0[None], lat1], axis=0)[:, None]
    return (
        latents,
        frames_grad,
        cwg.reshape(3, 3, 3, c, c),
        cbg[0],
        swg.reshape(2, c, c),
        sbg[0],
    )


def solution(mesh):
    split = P(("groups", "tm"))
    return jax.shard_map(
        functools.partial(body, mesh.shape["tm"]),
        mesh=mesh,
        in_specs=(split, split, split, split, P(), P(), P(), P(), split),
        out_specs=(split, split, P("groups"), P("groups"), P("groups"), P("groups")),
        check_vma=False,
    )
```

```python
import functools

import jax
import jax.numpy as jnp
from jax import lax
from jax.experimental import pallas as pl
from jax.experimental.pallas import tpu as pltpu
from jax.sharding import PartitionSpec as P

BF = jnp.bfloat16
F32 = jnp.float32
EMPTY_FRAME = 100.0
EMPTY_GRAD = 1e30

_VMEM = pl.BlockSpec(memory_space=pltpu.VMEM)
_SMEM = pl.BlockSpec(memory_space=pltpu.SMEM)
_HBM = pl.BlockSpec(memory_space=pltpu.HBM)


def _call(kernel, out_shape, in_specs, scratch=(), flops=0, moved=0, room=16, grid=()):
    return pl.pallas_call(
        kernel,
        out_shape=out_shape,
        grid=grid,
        in_specs=in_specs,
        out_specs=jax.tree.map(lambda _: _VMEM, out_shape),
        scratch_shapes=list(scratch),
        compiler_params=pltpu.CompilerParams(vmem_limit_bytes=room << 20),
        cost_estimate=pl.CostEstimate(flops=flops, bytes_accessed=moved, transcendentals=0),
    )


def _put(xk, at, rows, value):
    n, w, c = value.shape
    flat = value.astype(F32).reshape(n * w, c)
    col = lax.broadcasted_iota(jnp.int32, (n * w, c), 0) % w
    right = jnp.where(col == 0, 0.0, pltpu.roll(flat, 1, 0))
    left = jnp.where(col == w - 1, 0.0, pltpu.roll(flat, n * w - 1, 0))
    for kw, shifted in enumerate((right, flat, left)):
        xk[(kw, *at, rows)] = shifted.astype(BF).reshape(n, w, c)


def _window(xk, kw, j, kh, h):
    v = xk[kw, :, j, kh : kh + h]
    return v.reshape(v.shape[0] * v.shape[1] * v.shape[2], v.shape[3])


def _wide(xk, j, h):
    return jnp.concatenate(
        [_window(xk, kw, j, kh, h) for kh in range(3) for kw in range(3)], axis=1
    )


def _conv(xk, w_ref, h):
    c = w_ref.shape[-1]
    zero = jnp.zeros((c, c), BF)
    lhs = jnp.concatenate([_wide(xk, j, h) for j in range(4)], axis=1)
    rhs = []
    for j in range(4):
        for tap in range(9):
            rhs.append(
                jnp.concatenate(
                    [w_ref[(j - t) * 9 + tap] if 0 <= j - t <= 2 else zero for t in range(2)],
                    axis=1,
                )
            )
    return jnp.dot(lhs, jnp.concatenate(rhs, axis=0), preferred_element_type=F32)


def _conv_back(xk, w_ref, h, frames=range(4)):
    c = w_ref.shape[-1]
    zero = jnp.zeros((c, c), BF)
    lhs = jnp.concatenate([_wide(xk, j, h) for j in frames], axis=1)
    rhs = []
    for f in range(2):
        row = []
        for j in frames:
            for tap in range(9):
                kt = 2 - (j - f)
                row.append(w_ref[kt * 9 + 8 - tap] if 0 <= kt <= 2 else zero)
        rhs.append(jnp.concatenate(row, axis=1))
    return lax.dot_general(
        lhs, jnp.concatenate(rhs, axis=0), (((1,), (1,)), ((), ())), preferred_element_type=F32
    )


def _head(xk, gout, w_ref, cb_ref, sw_ref, sb_ref, h):
    pre = _conv(xk, w_ref, h) + jnp.concatenate([cb_ref[...], cb_ref[...]], axis=1)
    s = 1.0 / (1.0 + jnp.exp(-pre))
    hidden = (pre * s).astype(BF)
    sw = jnp.concatenate([sw_ref[0], sw_ref[1]], axis=0)
    lat = jnp.dot(hidden, sw, preferred_element_type=F32) + sb_ref[...]
    gh = lax.dot_general(gout, sw, (((1,), (1,)), ((), ())), preferred_element_type=F32)
    g = (gh * s * (1.0 + pre * (1.0 - s))).astype(BF)
    return lat, g, hidden


def _weight_grads(xk, g, hidden, gout, h, add):
    c = gout.shape[-1]
    parts = []
    for j in range(4):
        lhs = _wide(xk, j, h)
        parts.append(
            lax.dot_general(lhs, g, (((0,), (0,)), ((), ())), preferred_element_type=F32)
        )
    for kt in range(3):
        add(kt, parts[kt][:, :c] + parts[kt + 1][:, c:])
    sg = lax.dot_general(hidden, gout, (((0,), (0,)), ((), ())), preferred_element_type=F32)
    g32 = jnp.sum(g.astype(F32), axis=0, keepdims=True)
    add(3, sg)
    add(4, g32[:, :c] + g32[:, c:])
    add(5, jnp.sum(gout.astype(F32), axis=0, keepdims=True))


def _fill_early(sc, fr, ha, xk):
    slots, _, h, w, c = fr.shape
    for s in range(slots):
        for f in range(2):
            spots = [(s - 1, f + 2, None)] if s > 0 else []
            if s + 1 < slots:
                spots.append((s, f, sc[1 + s + 1] == 0))
            for slot, j, keep in spots:
                a, b = fr[s, f], ha[s, f]
                if keep is not None:
                    a = jnp.where(keep, a, jnp.zeros_like(a))
                    b = jnp.where(keep, b, jnp.zeros_like(b))
                _put(xk, (slot, j), slice(1, 1 + h), a)
                _put(xk, (slot, j), slice(0, 1), b[:1])
                _put(xk, (slot, j), slice(h + 1, h + 2), b[1:])


def _early_gout(sc, co):
    slots, _, h, w, c = co.shape
    return jnp.concatenate(
        [
            jnp.where(s < sc[0], co[s, 0], jnp.zeros_like(co[s, 0])).reshape(h * w, c)
            for s in range(1, slots)
        ],
        axis=0,
    )


def _early_kernel(
    sc,
    frh,
    hah,
    coh,
    wh,
    cbh,
    swh,
    sbh,
    lat_ref,
    g_ref,
    hid_ref,
    gout_ref,
    xk,
    fr,
    ha,
    co,
    w_ref,
    cb,
    sw,
    sb,
    sems,
):
    slots, _, h, w, c = fr.shape
    pairs = ((frh, fr), (hah, ha), (coh, co), (wh, w_ref), (cbh, cb), (swh, sw), (sbh, sb))
    copies = [pltpu.make_async_copy(a, b, sems.at[i]) for i, (a, b) in enumerate(pairs)]
    for copy in copies:
        copy.start()
    copies[0].wait()
    copies[1].wait()
    _fill_early(sc, fr, ha, xk)
    copies[2].wait()
    gout = _early_gout(sc, co)
    gout_ref[...] = gout
    for copy in copies[3:]:
        copy.wait()
    lat, g, hidden = _head(xk, gout, w_ref, cb, sw, sb, h)
    for s in range(1, slots):
        part = lat[(s - 1) * h * w : s * h * w]
        lat_ref[s - 1] = (
            jnp.where(s < sc[0], part, jnp.zeros_like(part)).astype(BF).reshape(h, w, c)
        )
    g_ref[...] = g
    hid_ref[...] = hidden


def _early_sums_kernel(sc, g_ref, hid_ref, gout_ref, xk, acc):
    c = gout_ref.shape[-1]
    h = xk.shape[3] - 2
    n9 = 9 * c

    def add(kind, value):
        if kind < 3:
            acc[kind * n9 : (kind + 1) * n9] = value
        elif kind == 3:
            acc[3 * n9 : 3 * n9 + 2 * c] = value
        else:
            at = 3 * n9 + 2 * c + (kind - 4)
            acc[at : at + 1] = value

    acc[3 * n9 + 2 * c :] = jnp.zeros((acc.shape[0] - 3 * n9 - 2 * c, c), F32)
    _weight_grads(xk, g_ref[...], hid_ref[...], gout_ref[...], h, add)


def _late_kernel(
    sc, frs, has, tail, cos, w_ref, cb, sw, sb, early, lat_ref, g_ref, send, keep, cache_ref, xk, acc
):
    fr, ha, co = frs.at[0], has.at[0], cos.at[0]
    _, h, w, c = fr.shape
    on = sc[1] == 0
    for f in range(2):
        _put(xk, (0, f + 2), slice(1, 1 + h), fr[f])
        _put(xk, (0, f + 2), slice(0, 1), ha[f, :1])
        _put(xk, (0, f + 2), slice(h + 1, h + 2), ha[f, 1:])
        a = tail[f * h : (f + 1) * h]
        b = tail[2 * h + 2 * f : 2 * h + 2 * f + 2]
        a = jnp.where(on, a, jnp.zeros_like(a))
        b = jnp.where(on, b, jnp.zeros_like(b))
        _put(xk, (0, f), slice(1, 1 + h), a)
        _put(xk, (0, f), slice(0, 1), b[:1])
        _put(xk, (0, f), slice(h + 1, h + 2), b[1:])
    filled = sc[0] > 0
    gout = jnp.where(filled, co[0], jnp.zeros_like(co[0])).reshape(h * w, c)
    lat, g, hidden = _head(xk, gout, w_ref, cb, sw, sb, h)
    lat_ref[...] = jnp.where(filled, lat, jnp.zeros_like(lat)).astype(BF).reshape(h, w, c)
    g_ref[...] = g
    n9 = 9 * c

    def add(kind, value):
        if kind < 3:
            rows = slice(kind * n9, (kind + 1) * n9)
        elif kind == 3:
            rows = slice(3 * n9, 3 * n9 + 2 * c)
        else:
            at = 3 * n9 + 2 * c + (kind - 4)
            rows = slice(at, at + 1)
        acc[rows] = early[rows] + value

    tail_rows = slice(3 * n9 + 2 * c, acc.shape[0])
    acc[tail_rows] = early[tail_rows]

    @pl.when(sc[0] >= 0)
    def _():
        _weight_grads(xk, g, hidden, gout, h, add)

        for t in range(2):
            for kw in range(3):
                xk[kw, 0, 2 + t, 0:1] = jnp.zeros((1, w, c), BF)
                xk[kw, 0, 2 + t, h + 1 : h + 2] = jnp.zeros((1, w, c), BF)
            v = g[:, t * c : (t + 1) * c].reshape(h, w, c)
            _put(xk, (0, 2 + t), slice(1, 1 + h), jnp.where(on, v, jnp.zeros_like(v)))
        back = _conv_back(xk, w_ref, h, (2, 3))
        back = jnp.where(filled, back, jnp.full_like(back, EMPTY_GRAD)).astype(BF)
        half = keep.shape[0]
        for t in range(2):
            lanes = slice(t * c, (t + 1) * c)
            cache_ref[t * h * w : (t + 1) * h * w] = back[:, lanes]
            send[half + t * h * w : half + (t + 1) * h * w] = back[:, lanes]
        core = sc[sc.shape[0] - 1]
        send[:half] = acc[pl.ds(pl.multiple_of((1 - core) * half, 16), half)].astype(BF)
        keep[...] = acc[pl.ds(pl.multiple_of(core * half, 16), half)]


def _back_kernel(sc, g0, g1, w_ref, out_ref, xk):
    slots, _, h, w, c = out_ref.shape
    m = h * w
    zero = jnp.zeros((1, w, c), BF)
    for kw in range(3):
        for j in range(4):
            for s in range(slots):
                xk[kw, s, j, 0:1] = zero
                xk[kw, s, j, h + 1 : h + 2] = zero
    for f in range(2):
        for kw in range(3):
            xk[kw, slots - 1, f + 2, 1 : 1 + h] = jnp.zeros((h, w, c), BF)
        lanes = slice(f * c, (f + 1) * c)
        for s in range(slots):
            v = g0[:, lanes] if s == 0 else g1[(s - 1) * m : s * m, lanes]
            v = v.reshape(h, w, c)
            _put(xk, (s, f), slice(1, 1 + h), v)
            if s > 0:
                on = sc[1 + s] == 0
                _put(xk, (s - 1, f + 2), slice(1, 1 + h), jnp.where(on, v, jnp.zeros_like(v)))
    out = _conv_back(xk, w_ref, h)
    for f in range(2):
        out_ref[:, f] = out[:, f * c : (f + 1) * c].reshape(slots, h, w, c)


def _first_live(a, b):
    return jnp.where(a.astype(F32) < EMPTY_GRAD / 2, a, b)


def _place(sc):
    chip, core = sc[sc.shape[0] - 2], sc[sc.shape[0] - 1]
    return lax.shift_right_logical(chip, 1), lax.bitwise_and(chip, 1), core


def _across_x_kernel(sc, keep, got, cache, send, kept):
    z, x, core = _place(sc)
    del z
    half = keep.shape[0]
    blocks = 4
    rows = half // (2 * blocks)

    def piece(p):
        at = pl.ds(pl.multiple_of(p * rows, 16), rows)
        return keep[at] + got[at].astype(F32)

    for b in range(blocks):
        kept[b * rows : (b + 1) * rows] = piece(2 * b + x)
        send[b * rows : (b + 1) * rows] = piece(2 * b + 1 - x).astype(BF)
    part = cache.shape[0] // 2
    at = pl.multiple_of(core * part, 16)
    mine, theirs = cache[pl.ds(at, part)], got[pl.ds(half + at, part)]
    first = jnp.where(core == 0, _first_live(mine, theirs), _first_live(theirs, mine))
    send[blocks * rows :] = first


def _across_z_kernel(sc, kept, got, sent, own, *sends):
    z, x, core = _place(sc)
    del core
    rows = own.shape[0]
    below = kept.shape[0]
    part = (sent.shape[0] - below) // 2

    def piece(b):
        at = pl.ds(pl.multiple_of(b * rows, 16), rows)
        return kept[at] + got[at].astype(F32)

    at = pl.ds(pl.multiple_of(below + x * part, 16), part)
    first = jnp.where(x == 0, _first_live(sent[at], got[at]), _first_live(got[at], sent[at]))
    own[...] = piece(z)
    for j, ref in enumerate(sends):
        ref[:rows] = piece(lax.bitwise_xor(z, j + 1)).astype(BF)
        ref[rows:] = first


def _sum_kernel(sc, own, *refs):
    gots, (mine, after) = refs[:-2], refs[-2:]
    z, _, _ = _place(sc)
    rows = own.shape[0]
    total = own[...]
    for ref in gots:
        total = total + ref[:rows].astype(F32)
    mine[...] = total.astype(BF)
    best = jnp.full(after.shape, EMPTY_GRAD, F32)
    for target in range(len(gots), 0, -1):
        for j, ref in enumerate(gots):
            here = jnp.logical_and(lax.bitwise_xor(z, j + 1) == target, target > z)
            value = ref[rows:].astype(F32)
            use = jnp.where(here, value, jnp.full_like(value, EMPTY_GRAD))
            best = _first_live(use, best)
    after[...] = best.astype(BF)


def _tail_kernel(sc, fr, ha, out):
    h2 = fr.shape[1] * fr.shape[2]
    live = sc[0] > 0
    for ref, rows in ((fr, slice(0, h2)), (ha, slice(h2, out.shape[0]))):
        v = ref[...].reshape(rows.stop - rows.start, *out.shape[1:])
        out[rows] = jnp.where(live, v, jnp.full_like(v, EMPTY_FRAME))


def _final_kernel(sc, mine, other, got, grad, cw, sw, cb, sb, fg, acc):
    c = mine.shape[1]
    half = acc.shape[0] // 2
    z, x, core = _place(sc)
    blocks = 4
    rows = half // (2 * blocks)
    for ref, at_core in ((mine, core), (other, 1 - core)):
        for k in range(2 * blocks):
            side = x if k < blocks else 1 - x
            chip = 2 * lax.bitwise_xor(z, k % blocks) + side
            at = pl.multiple_of(at_core * half + chip * rows, 16)
            acc[pl.ds(at, rows)] = ref[k * rows : (k + 1) * rows].astype(F32)
    n27, n29 = 27 * c, 29 * c
    cw[...] = acc[:n27]
    sw[...] = acc[n27:n29]
    cb[...] = acc[n29 : n29 + 1]
    sb[...] = acc[n29 + 1 : n29 + 2]
    slots, frames, h, w, _ = grad.shape
    part = mine.shape[0] - half
    for s in range(slots):
        here = sc[0] - 1 == s
        for f in range(frames):
            low = f == 0
            a, b = mine[half:].astype(F32), other[half:].astype(F32)
            beyond = jnp.where(core == 0, a, b) if low else jnp.where(core == 0, b, a)
            beside = got[half + f * part : half + (f + 1) * part].astype(F32)
            came = jnp.where(core == 0, _first_live(beside, beyond), beyond)
            came = jnp.where(came < EMPTY_GRAD / 2, came, jnp.zeros_like(came)).reshape(h, w, c)
            fg[s, f] = (grad[s, f] + jnp.where(here, came, jnp.zeros_like(came))).astype(BF)


def _xor(x, k, n, axis):
    return lax.ppermute(x, axis, [(i, i ^ k) for i in range(n)])


def _latest_before(x, empty, axis, n, beside_x, beside_z):
    index = lax.axis_index(axis)
    core, pair = index & 1, (index >> 1) & 1

    def shift(v, k):
        return lax.ppermute(v, axis, [(i, i + k) for i in range(n - k)])

    def newest(early, late):
        return jnp.where(late > empty / 2, early, late)

    def half(v):
        rows = v.shape[0] // 2
        return jnp.where(core == 0, v[:rows], v[rows:])

    other = _xor(x, 1, n, axis)
    a, b = half(x), half(other)
    chip = jnp.where(core == 0, newest(a, b), newest(b, a))
    beside = _xor(chip, 2, n, axis)
    quad = jnp.where(pair == 0, newest(chip, beside), newest(beside, chip))
    quad = beside_x(chip, quad)
    before, reach = None, 0
    while reach < n // 4 - 1:
        start = quad if before is None else newest(before, quad)
        came = shift(start, 4 * (reach + 1))
        before = came if before is None else newest(came, before)
        reach = 2 * reach + 1
        if reach == 3:
            before = beside_z(start, before)
    before = jnp.where(pair == 0, before, newest(before, beside))
    across = _xor(before, 1, n, axis)
    before = jnp.concatenate(
        [jnp.where(core == 0, before, across), jnp.where(core == 0, across, before)], axis=0
    )
    before = jnp.where(core == 0, before, newest(before, other))
    return jnp.where(before > empty / 2, jnp.zeros_like(before), before)


def _after(value, *earlier):
    return lax.optimization_barrier((value, *earlier))[0]


def body(
    n,
    frames,
    row_halo,
    clip_start,
    slab_counts,
    conv_weight,
    conv_bias,
    stride_weight,
    stride_bias,
    cotangent,
):
    axis = "tm"
    slots, _, h, w, c = frames.shape
    count = slab_counts[0]
    index = lax.axis_index(axis)
    chips = 8
    assert n % (2 * chips) == 0
    sc = jnp.concatenate(
        [
            slab_counts,
            clip_start,
            ((index >> 1) & (chips - 1)).reshape(1).astype(jnp.int32),
            (index & 1).reshape(1).astype(jnp.int32),
        ]
    )
    wt = conv_weight.reshape(27, c, c)
    cb, sb = conv_bias.reshape(1, c), stride_bias.reshape(1, c)
    unit = 16 * 2 * chips
    rows = -(-(29 * c + 2) // unit) * unit
    m = h * w
    conv_flops = 2 * m * 36 * c * 2 * c

    def newest_slot(i, sc):
        return (jnp.maximum(sc[0] - 1, 0), 0, 0, 0, 0)

    tail = pl.pallas_call(
        _tail_kernel,
        out_shape=jax.ShapeDtypeStruct((2 * h + 4, w, c), BF),
        grid_spec=pltpu.PrefetchScalarGridSpec(
            num_scalar_prefetch=1,
            grid=(1,),
            in_specs=[
                pl.BlockSpec((1, 2, h, w, c), newest_slot),
                pl.BlockSpec((1, 2, 2, w, c), newest_slot),
            ],
            out_specs=pl.BlockSpec((2 * h + 4, w, c), lambda i, sc: (0, 0, 0)),
        ),
        compiler_params=pltpu.CompilerParams(vmem_limit_bytes=8 << 20),
    )(
        slab_counts,
        *(pltpu.with_memory_space_constraint(v, pltpu.HBM) for v in (frames, row_halo)),
    )

    held = {}
    wide = ((slots - 1) * m, 2 * c)
    raw = (frames, row_halo, cotangent, wt, cb, stride_weight, sb)
    windows = (3, slots - 1, 4, h + 2, w, c)

    def early_forward(start, follow):
        held["early"] = _call(
            _early_kernel,
            [
                jax.ShapeDtypeStruct((slots - 1, h, w, c), BF),
                jax.ShapeDtypeStruct(wide, BF),
                jax.ShapeDtypeStruct(wide, BF),
                jax.ShapeDtypeStruct((wide[0], c), BF),
                jax.ShapeDtypeStruct(windows, BF),
            ],
            [_SMEM] + [_HBM] * len(raw),
            [pltpu.VMEM(v.shape, v.dtype) for v in raw] + [pltpu.SemaphoreType.DMA((len(raw),))],
            flops=(slots - 1) * conv_flops,
            moved=4 << 20,
        )(_after(sc, start), *(pltpu.with_memory_space_constraint(v, pltpu.HBM) for v in raw))
        return _after(follow, held["early"][1])

    def early_sums(start, follow):
        _, g1, hid1, gout1, xk1 = held["early"]
        held["sums"] = _call(
            _early_sums_kernel,
            jax.ShapeDtypeStruct((rows, c), F32),
            [_SMEM] + [_VMEM] * 4,
            flops=(slots - 1) * conv_flops,
            moved=4 << 20,
        )(_after(sc, start), g1, hid1, gout1, xk1)
        return _after(follow, held["sums"])

    arrived = _latest_before(tail, EMPTY_FRAME, axis, n, early_forward, early_sums)
    lat1, g1 = held["early"][:2]

    def first(*shape):
        return pl.BlockSpec((1, *shape), lambda i: (0,) * (len(shape) + 1))

    half, carried = rows // 2, 2 * m
    lat0, g0, send, keep, cache = _call(
        _late_kernel,
        [
            jax.ShapeDtypeStruct((h, w, c), BF),
            jax.ShapeDtypeStruct((m, 2 * c), BF),
            jax.ShapeDtypeStruct((half + carried, c), BF),
            jax.ShapeDtypeStruct((half, c), F32),
            jax.ShapeDtypeStruct((carried, c), BF),
        ],
        [_SMEM, first(2, h, w, c), first(2, 2, w, c), _VMEM, first(1, h, w, c)] + [_VMEM] * 5,
        [pltpu.VMEM((3, 1, 4, h + 2, w, c), BF), pltpu.VMEM((rows, c), F32)],
        flops=2 * conv_flops,
        moved=6 << 20,
        grid=(1,),
    )(sc, frames, row_halo, arrived, cotangent, wt, cb, stride_weight, sb, held["sums"])

    blocks = chips // 2
    piece = half // chips
    got = _xor(send, 1, n, axis)
    send_x, keep_x = _call(
        _across_x_kernel,
        [
            jax.ShapeDtypeStruct((blocks * piece + carried // 2, c), BF),
            jax.ShapeDtypeStruct((blocks * piece, c), F32),
        ],
        [_SMEM] + [_VMEM] * 3,
        room=8,
    )(sc, keep, got, cache)
    got_x = _xor(send_x, 2, n, axis)
    grad = _call(
        _back_kernel,
        jax.ShapeDtypeStruct((slots, 2, h, w, c), F32),
        [_SMEM] + [_VMEM] * 3,
        [pltpu.VMEM((3, slots, 4, h + 2, w, c), BF)],
        flops=slots * conv_flops,
        moved=6 << 20,
        room=24,
    )(_after(sc, keep_x), g0, g1, wt)
    own, *sends = _call(
        _across_z_kernel,
        [jax.ShapeDtypeStruct((piece, c), F32)]
        + [jax.ShapeDtypeStruct((piece + carried // 4, c), BF)] * (blocks - 1),
        [_SMEM] + [_VMEM] * 3,
        room=8,
    )(_after(sc, grad), keep_x, got_x, send_x)
    gots = [_xor(v, 4 * (j + 1), n, axis) for j, v in enumerate(sends)]
    mine, after = _call(
        _sum_kernel,
        [jax.ShapeDtypeStruct((piece, c), BF), jax.ShapeDtypeStruct((carried // 4, c), BF)],
        [_SMEM] + [_VMEM] * blocks,
        room=8,
    )(sc, own, *gots)
    k = 2 * chips
    if k < n:
        z = (index >> 2) & (blocks - 1)
        lead = sends[0][piece:]
        for target in range(blocks - 1, -1, -1):
            for j, v in enumerate(gots):
                lead = jnp.where((z ^ (j + 1)) == target, _first_live(v[piece:], lead), lead)
            lead = jnp.where(z == target, _first_live(sends[0][piece:], lead), lead)
        beyond, reach = None, 0
        while reach < n // k - 1:
            start = lead if beyond is None else _first_live(lead, beyond)
            step = k * (reach + 1)
            came = lax.ppermute(start, axis, [(i + step, i) for i in range(n - step)])
            beyond = came if beyond is None else _first_live(beyond, came)
            reach = 2 * reach + 1
        after = _first_live(after, beyond)
    while k < n:
        mine = (mine.astype(F32) + _xor(mine, k, n, axis).astype(F32)).astype(BF)
        k *= 2
    pieces = [mine] + [_xor(mine, 4 * (j + 1), n, axis) for j in range(blocks - 1)]
    back_x = jnp.concatenate(pieces + [after], axis=0)
    got_back = _xor(back_x, 2, n, axis)
    pair, below = (index >> 1) & 1, blocks * piece
    theirs = got_back[below:]
    beyond = jnp.concatenate(
        [jnp.where(pair == 0, after, theirs), jnp.where(pair == 0, theirs, after)], axis=0
    )
    beyond = jnp.where(pair == 0, _first_live(got_x[below:], beyond), beyond)
    ours = jnp.concatenate([*pieces, got_back[:below], beyond], axis=0)
    other = _xor(ours, 1, n, axis)
    cwg, swg, cbg, sbg, frames_grad = _call(
        _final_kernel,
        [
            jax.ShapeDtypeStruct((27 * c, c), F32),
            jax.ShapeDtypeStruct((2 * c, c), F32),
            jax.ShapeDtypeStruct((1, c), F32),
            jax.ShapeDtypeStruct((1, c), F32),
            jax.ShapeDtypeStruct((slots, 2, h, w, c), BF),
        ],
        [_SMEM] + [_VMEM] * 4,
        [pltpu.VMEM((rows, c), F32)],
        room=12,
    )(sc, ours, other, got, grad)
    latents = jnp.concatenate([lat0[None], lat1], axis=0)[:, None]
    return (
        latents,
        frames_grad,
        cwg.reshape(3, 3, 3, c, c),
        cbg[0],
        swg.reshape(2, c, c),
        sbg[0],
    )


def solution(mesh):
    split = P(("groups", "tm"))
    return jax.shard_map(
        functools.partial(body, mesh.shape["tm"]),
        mesh=mesh,
        in_specs=(split, split, split, split, P(), P(), P(), P(), split),
        out_specs=(split, split, P("groups"), P("groups"), P("groups"), P("groups")),
        check_vma=False,
    )
```

```python
import functools

import jax
import jax.numpy as jnp
from jax import lax
from jax.experimental import pallas as pl
from jax.experimental.pallas import tpu as pltpu
from jax.sharding import PartitionSpec as P

BF = jnp.bfloat16
F32 = jnp.float32
EMPTY_FRAME = 100.0
EMPTY_GRAD = 1e30

_VMEM = pl.BlockSpec(memory_space=pltpu.VMEM)
_SMEM = pl.BlockSpec(memory_space=pltpu.SMEM)
_HBM = pl.BlockSpec(memory_space=pltpu.HBM)


def _call(kernel, out_shape, in_specs, scratch=(), flops=0, moved=0, room=16, grid=()):
    return pl.pallas_call(
        kernel,
        out_shape=out_shape,
        grid=grid,
        in_specs=in_specs,
        out_specs=jax.tree.map(lambda _: _VMEM, out_shape),
        scratch_shapes=list(scratch),
        compiler_params=pltpu.CompilerParams(vmem_limit_bytes=room << 20),
        cost_estimate=pl.CostEstimate(flops=flops, bytes_accessed=moved, transcendentals=0),
    )


def _put(xk, at, rows, value):
    n, w, c = value.shape
    flat = value.astype(F32).reshape(n * w, c)
    col = lax.broadcasted_iota(jnp.int32, (n * w, c), 0) % w
    right = jnp.where(col == 0, 0.0, pltpu.roll(flat, 1, 0))
    left = jnp.where(col == w - 1, 0.0, pltpu.roll(flat, n * w - 1, 0))
    for kw, shifted in enumerate((right, flat, left)):
        xk[(kw, *at, rows)] = shifted.astype(BF).reshape(n, w, c)


def _window(xk, kw, j, kh, h):
    v = xk[kw, :, j, kh : kh + h]
    return v.reshape(v.shape[0] * v.shape[1] * v.shape[2], v.shape[3])


def _wide(xk, j, h):
    return jnp.concatenate(
        [_window(xk, kw, j, kh, h) for kh in range(3) for kw in range(3)], axis=1
    )


def _conv(xk, w_ref, h):
    c = w_ref.shape[-1]
    zero = jnp.zeros((c, c), BF)
    lhs = jnp.concatenate([_wide(xk, j, h) for j in range(4)], axis=1)
    rhs = []
    for j in range(4):
        for tap in range(9):
            rhs.append(
                jnp.concatenate(
                    [w_ref[(j - t) * 9 + tap] if 0 <= j - t <= 2 else zero for t in range(2)],
                    axis=1,
                )
            )
    return jnp.dot(lhs, jnp.concatenate(rhs, axis=0), preferred_element_type=F32)


def _conv_back(xk, w_ref, h, frames=range(4)):
    c = w_ref.shape[-1]
    zero = jnp.zeros((c, c), BF)
    lhs = jnp.concatenate([_wide(xk, j, h) for j in frames], axis=1)
    rhs = []
    for f in range(2):
        row = []
        for j in frames:
            for tap in range(9):
                kt = 2 - (j - f)
                row.append(w_ref[kt * 9 + 8 - tap] if 0 <= kt <= 2 else zero)
        rhs.append(jnp.concatenate(row, axis=1))
    return lax.dot_general(
        lhs, jnp.concatenate(rhs, axis=0), (((1,), (1,)), ((), ())), preferred_element_type=F32
    )


def _activate(pre, gout, sw_ref, sb_ref):
    s = 1.0 / (1.0 + jnp.exp(-pre))
    hidden = (pre * s).astype(BF)
    sw = jnp.concatenate([sw_ref[0], sw_ref[1]], axis=0)
    lat = jnp.dot(hidden, sw, preferred_element_type=F32) + sb_ref[...]
    gh = lax.dot_general(gout, sw, (((1,), (1,)), ((), ())), preferred_element_type=F32)
    g = (gh * s * (1.0 + pre * (1.0 - s))).astype(BF)
    return lat, g, hidden


def _conv_bias(xk, w_ref, cb_ref, h):
    return _conv(xk, w_ref, h) + jnp.concatenate([cb_ref[...], cb_ref[...]], axis=1)


def _weight_grads(xk, g, hidden, gout, h, add):
    c = gout.shape[-1]
    parts = []
    for j in range(4):
        lhs = _wide(xk, j, h)
        parts.append(
            lax.dot_general(lhs, g, (((0,), (0,)), ((), ())), preferred_element_type=F32)
        )
    for kt in range(3):
        add(kt, parts[kt][:, :c] + parts[kt + 1][:, c:])
    sg = lax.dot_general(hidden, gout, (((0,), (0,)), ((), ())), preferred_element_type=F32)
    g32 = jnp.sum(g.astype(F32), axis=0, keepdims=True)
    add(3, sg)
    add(4, g32[:, :c] + g32[:, c:])
    add(5, jnp.sum(gout.astype(F32), axis=0, keepdims=True))


def _fill_early(sc, fr, ha, xk):
    slots, _, h, w, c = fr.shape
    for s in range(slots):
        for f in range(2):
            spots = [(s - 1, f + 2, None)] if s > 0 else []
            if s + 1 < slots:
                spots.append((s, f, sc[1 + s + 1] == 0))
            for slot, j, keep in spots:
                a, b = fr[s, f], ha[s, f]
                if keep is not None:
                    a = jnp.where(keep, a, jnp.zeros_like(a))
                    b = jnp.where(keep, b, jnp.zeros_like(b))
                _put(xk, (slot, j), slice(1, 1 + h), a)
                _put(xk, (slot, j), slice(0, 1), b[:1])
                _put(xk, (slot, j), slice(h + 1, h + 2), b[1:])


def _early_gout(sc, co):
    slots, _, h, w, c = co.shape
    return jnp.concatenate(
        [
            jnp.where(s < sc[0], co[s, 0], jnp.zeros_like(co[s, 0])).reshape(h * w, c)
            for s in range(1, slots)
        ],
        axis=0,
    )


def _early_conv_kernel(
    sc, frh, hah, coh, wh, cbh, swh, sbh, pre_ref, gout_ref, sw, sb, xk, fr, ha, co, w_ref, cb, sems
):
    h = fr.shape[2]
    pairs = ((frh, fr), (hah, ha), (coh, co), (wh, w_ref), (cbh, cb), (swh, sw), (sbh, sb))
    copies = [pltpu.make_async_copy(a, b, sems.at[i]) for i, (a, b) in enumerate(pairs)]
    for copy in copies:
        copy.start()
    copies[0].wait()
    copies[1].wait()
    _fill_early(sc, fr, ha, xk)
    copies[2].wait()
    gout_ref[...] = _early_gout(sc, co)
    for copy in copies[3:]:
        copy.wait()
    pre_ref[...] = _conv_bias(xk, w_ref, cb, h)


def _early_act_kernel(sc, pre_ref, gout_ref, sw, sb, lat_ref, g_ref, hid_ref):
    slots, h, w, c = lat_ref.shape
    lat, g, hidden = _activate(pre_ref[...], gout_ref[...], sw, sb)
    for s in range(slots):
        part = lat[s * h * w : (s + 1) * h * w]
        filled = s + 1 < sc[0]
        lat_ref[s] = jnp.where(filled, part, jnp.zeros_like(part)).astype(BF).reshape(h, w, c)
    g_ref[...] = g
    hid_ref[...] = hidden


def _early_sums_kernel(sc, g_ref, hid_ref, gout_ref, xk, acc):
    c = gout_ref.shape[-1]
    h = xk.shape[3] - 2
    n9 = 9 * c

    def add(kind, value):
        if kind < 3:
            acc[kind * n9 : (kind + 1) * n9] = value
        elif kind == 3:
            acc[3 * n9 : 3 * n9 + 2 * c] = value
        else:
            at = 3 * n9 + 2 * c + (kind - 4)
            acc[at : at + 1] = value

    acc[3 * n9 + 2 * c :] = jnp.zeros((acc.shape[0] - 3 * n9 - 2 * c, c), F32)
    _weight_grads(xk, g_ref[...], hid_ref[...], gout_ref[...], h, add)


def _late_kernel(
    sc, frs, has, tail, cos, w_ref, cb, sw, sb, early, lat_ref, g_ref, send, keep, cache_ref, xk, acc
):
    fr, ha, co = frs.at[0], has.at[0], cos.at[0]
    _, h, w, c = fr.shape
    on = sc[1] == 0
    for f in range(2):
        _put(xk, (0, f + 2), slice(1, 1 + h), fr[f])
        _put(xk, (0, f + 2), slice(0, 1), ha[f, :1])
        _put(xk, (0, f + 2), slice(h + 1, h + 2), ha[f, 1:])
        a = tail[f * h : (f + 1) * h]
        b = tail[2 * h + 2 * f : 2 * h + 2 * f + 2]
        a = jnp.where(on, a, jnp.zeros_like(a))
        b = jnp.where(on, b, jnp.zeros_like(b))
        _put(xk, (0, f), slice(1, 1 + h), a)
        _put(xk, (0, f), slice(0, 1), b[:1])
        _put(xk, (0, f), slice(h + 1, h + 2), b[1:])
    filled = sc[0] > 0
    gout = jnp.where(filled, co[0], jnp.zeros_like(co[0])).reshape(h * w, c)
    lat, g, hidden = _activate(_conv_bias(xk, w_ref, cb, h), gout, sw, sb)
    lat_ref[...] = jnp.where(filled, lat, jnp.zeros_like(lat)).astype(BF).reshape(h, w, c)
    g_ref[...] = g
    n9 = 9 * c

    def add(kind, value):
        if kind < 3:
            rows = slice(kind * n9, (kind + 1) * n9)
        elif kind == 3:
            rows = slice(3 * n9, 3 * n9 + 2 * c)
        else:
            at = 3 * n9 + 2 * c + (kind - 4)
            rows = slice(at, at + 1)
        acc[rows] = early[rows] + value

    tail_rows = slice(3 * n9 + 2 * c, acc.shape[0])
    acc[tail_rows] = early[tail_rows]

    @pl.when(sc[0] >= 0)
    def _():
        _weight_grads(xk, g, hidden, gout, h, add)

        for t in range(2):
            for kw in range(3):
                xk[kw, 0, 2 + t, 0:1] = jnp.zeros((1, w, c), BF)
                xk[kw, 0, 2 + t, h + 1 : h + 2] = jnp.zeros((1, w, c), BF)
            v = g[:, t * c : (t + 1) * c].reshape(h, w, c)
            _put(xk, (0, 2 + t), slice(1, 1 + h), jnp.where(on, v, jnp.zeros_like(v)))
        back = _conv_back(xk, w_ref, h, (2, 3))
        back = jnp.where(filled, back, jnp.full_like(back, EMPTY_GRAD)).astype(BF)
        half = keep.shape[0]
        for t in range(2):
            lanes = slice(t * c, (t + 1) * c)
            cache_ref[t * h * w : (t + 1) * h * w] = back[:, lanes]
            send[half + t * h * w : half + (t + 1) * h * w] = back[:, lanes]
        core = sc[sc.shape[0] - 1]
        send[:half] = acc[pl.ds(pl.multiple_of((1 - core) * half, 16), half)].astype(BF)
        keep[...] = acc[pl.ds(pl.multiple_of(core * half, 16), half)]


def _back_kernel(sc, g0, g1, w_ref, out_ref, xk):
    slots, _, h, w, c = out_ref.shape
    m = h * w
    zero = jnp.zeros((1, w, c), BF)
    for kw in range(3):
        for j in range(4):
            for s in range(slots):
                xk[kw, s, j, 0:1] = zero
                xk[kw, s, j, h + 1 : h + 2] = zero
    for f in range(2):
        for kw in range(3):
            xk[kw, slots - 1, f + 2, 1 : 1 + h] = jnp.zeros((h, w, c), BF)
        lanes = slice(f * c, (f + 1) * c)
        for s in range(slots):
            v = g0[:, lanes] if s == 0 else g1[(s - 1) * m : s * m, lanes]
            v = v.reshape(h, w, c)
            _put(xk, (s, f), slice(1, 1 + h), v)
            if s > 0:
                on = sc[1 + s] == 0
                _put(xk, (s - 1, f + 2), slice(1, 1 + h), jnp.where(on, v, jnp.zeros_like(v)))
    out = _conv_back(xk, w_ref, h)
    for f in range(2):
        out_ref[:, f] = out[:, f * c : (f + 1) * c].reshape(slots, h, w, c)


def _first_live(a, b):
    return jnp.where(a.astype(F32) < EMPTY_GRAD / 2, a, b)


def _place(sc):
    chip, core = sc[sc.shape[0] - 2], sc[sc.shape[0] - 1]
    return lax.shift_right_logical(chip, 1), lax.bitwise_and(chip, 1), core


def _across_x_kernel(sc, keep, got, cache, send_far, send_near, kept):
    z, x, core = _place(sc)
    half = keep.shape[0]
    blocks = 4
    rows = half // (2 * blocks)

    def piece(j, side):
        p = 2 * lax.bitwise_xor(z, j) + side
        at = pl.ds(pl.multiple_of(p * rows, 16), rows)
        return keep[at] + got[at].astype(F32)

    for j in range(blocks):
        kept[j * rows : (j + 1) * rows] = piece(j, x)
        send, i = (send_near, j) if j < 2 else (send_far, j - 2)
        send[i * rows : (i + 1) * rows] = piece(j, 1 - x).astype(BF)
    part = cache.shape[0] // 2
    at = pl.multiple_of(core * part, 16)
    mine, theirs = cache[pl.ds(at, part)], got[pl.ds(half + at, part)]
    first = jnp.where(core == 0, _first_live(mine, theirs), _first_live(theirs, mine))
    send_far[2 * rows :] = first


def _tail_kernel(sc, fr, ha, out):
    h2 = fr.shape[1] * fr.shape[2]
    live = sc[0] > 0
    for ref, rows in ((fr, slice(0, h2)), (ha, slice(h2, out.shape[0]))):
        v = ref[...].reshape(rows.stop - rows.start, *out.shape[1:])
        out[rows] = jnp.where(live, v, jnp.full_like(v, EMPTY_FRAME))


def _final_kernel(sc, mine, other, got, grad, cw, sw, cb, sb, fg, acc):
    c = mine.shape[1]
    half = acc.shape[0] // 2
    z, x, core = _place(sc)
    blocks = 4
    rows = half // (2 * blocks)
    for ref, at_core in ((mine, core), (other, 1 - core)):
        for k in range(2 * blocks):
            side = x if k < blocks else 1 - x
            chip = 2 * lax.bitwise_xor(z, k % blocks) + side
            at = pl.multiple_of(at_core * half + chip * rows, 16)
            acc[pl.ds(at, rows)] = ref[k * rows : (k + 1) * rows].astype(F32)
    n27, n29 = 27 * c, 29 * c
    cw[...] = acc[:n27]
    sw[...] = acc[n27:n29]
    cb[...] = acc[n29 : n29 + 1]
    sb[...] = acc[n29 + 1 : n29 + 2]
    slots, frames, h, w, _ = grad.shape
    part = mine.shape[0] - half
    for s in range(slots):
        here = sc[0] - 1 == s
        for f in range(frames):
            low = f == 0
            a, b = mine[half:].astype(F32), other[half:].astype(F32)
            beyond = jnp.where(core == 0, a, b) if low else jnp.where(core == 0, b, a)
            beside = got[half + f * part : half + (f + 1) * part].astype(F32)
            came = jnp.where(core == 0, _first_live(beside, beyond), beyond)
            came = jnp.where(came < EMPTY_GRAD / 2, came, jnp.zeros_like(came)).reshape(h, w, c)
            fg[s, f] = (grad[s, f] + jnp.where(here, came, jnp.zeros_like(came))).astype(BF)


def _xor(x, k, n, axis):
    return lax.ppermute(x, axis, [(i, i ^ k) for i in range(n)])


def _latest_before(x, empty, axis, n, beside_x, beside_near, beside_far):
    index = lax.axis_index(axis)
    core, pair = index & 1, (index >> 1) & 1

    def shift(v, k):
        return lax.ppermute(v, axis, [(i, i + k) for i in range(n - k)])

    def newest(early, late):
        return jnp.where(late > empty / 2, early, late)

    def half(v):
        rows = v.shape[0] // 2
        return jnp.where(core == 0, v[:rows], v[rows:])

    other = _xor(x, 1, n, axis)
    a, b = half(x), half(other)
    chip = jnp.where(core == 0, newest(a, b), newest(b, a))
    beside = _xor(chip, 2, n, axis)
    quad = jnp.where(pair == 0, newest(chip, beside), newest(beside, chip))
    quad = beside_x(chip, quad)
    before, reach = None, 0
    while reach < n // 4 - 1:
        start = quad if before is None else newest(before, quad)
        came = shift(start, 4 * (reach + 1))
        if reach == 0:
            came = beside_near(start, came)
        before = came if before is None else newest(came, before)
        reach = 2 * reach + 1
        if reach == 3:
            before = beside_far(start, before)
    before = jnp.where(pair == 0, before, newest(before, beside))
    across = _xor(before, 1, n, axis)
    before = jnp.concatenate(
        [jnp.where(core == 0, before, across), jnp.where(core == 0, across, before)], axis=0
    )
    before = jnp.where(core == 0, before, newest(before, other))
    return jnp.where(before > empty / 2, jnp.zeros_like(before), before)


def _after(value, *earlier):
    return lax.optimization_barrier((value, *earlier))[0]


def body(
    n,
    frames,
    row_halo,
    clip_start,
    slab_counts,
    conv_weight,
    conv_bias,
    stride_weight,
    stride_bias,
    cotangent,
):
    axis = "tm"
    slots, _, h, w, c = frames.shape
    count = slab_counts[0]
    index = lax.axis_index(axis)
    chips = 8
    assert n % (2 * chips) == 0
    sc = jnp.concatenate(
        [
            slab_counts,
            clip_start,
            ((index >> 1) & (chips - 1)).reshape(1).astype(jnp.int32),
            (index & 1).reshape(1).astype(jnp.int32),
        ]
    )
    wt = conv_weight.reshape(27, c, c)
    cb, sb = conv_bias.reshape(1, c), stride_bias.reshape(1, c)
    unit = 16 * 2 * chips
    rows = -(-(29 * c + 2) // unit) * unit
    m = h * w
    conv_flops = 2 * m * 36 * c * 2 * c

    def newest_slot(i, sc):
        return (jnp.maximum(sc[0] - 1, 0), 0, 0, 0, 0)

    tail = pl.pallas_call(
        _tail_kernel,
        out_shape=jax.ShapeDtypeStruct((2 * h + 4, w, c), BF),
        grid_spec=pltpu.PrefetchScalarGridSpec(
            num_scalar_prefetch=1,
            grid=(1,),
            in_specs=[
                pl.BlockSpec((1, 2, h, w, c), newest_slot),
                pl.BlockSpec((1, 2, 2, w, c), newest_slot),
            ],
            out_specs=pl.BlockSpec((2 * h + 4, w, c), lambda i, sc: (0, 0, 0)),
        ),
        compiler_params=pltpu.CompilerParams(vmem_limit_bytes=8 << 20),
    )(
        slab_counts,
        *(pltpu.with_memory_space_constraint(v, pltpu.HBM) for v in (frames, row_halo)),
    )

    held = {}
    wide = ((slots - 1) * m, 2 * c)
    raw = (frames, row_halo, cotangent, wt, cb, stride_weight, sb)
    windows = (3, slots - 1, 4, h + 2, w, c)

    def early_conv(start, follow):
        held["conv"] = _call(
            _early_conv_kernel,
            [
                jax.ShapeDtypeStruct(wide, F32),
                jax.ShapeDtypeStruct((wide[0], c), BF),
                jax.ShapeDtypeStruct(stride_weight.shape, BF),
                jax.ShapeDtypeStruct(sb.shape, F32),
                jax.ShapeDtypeStruct(windows, BF),
            ],
            [_SMEM] + [_HBM] * len(raw),
            [pltpu.VMEM(v.shape, v.dtype) for v in raw[:5]]
            + [pltpu.SemaphoreType.DMA((len(raw),))],
            flops=(slots - 1) * conv_flops,
            moved=4 << 20,
        )(_after(sc, start), *(pltpu.with_memory_space_constraint(v, pltpu.HBM) for v in raw))
        return _after(follow, held["conv"][0])

    def early_act(start, follow):
        pre, gout1, sw1, sb1, _ = held["conv"]
        held["early"] = _call(
            _early_act_kernel,
            [
                jax.ShapeDtypeStruct((slots - 1, h, w, c), BF),
                jax.ShapeDtypeStruct(wide, BF),
                jax.ShapeDtypeStruct(wide, BF),
            ],
            [_SMEM] + [_VMEM] * 4,
            moved=2 << 20,
        )(_after(sc, start), pre, gout1, sw1, sb1)
        return _after(follow, held["early"][1])

    def early_sums(start, follow):
        _, gout1, _, _, xk1 = held["conv"]
        _, g1, hid1 = held["early"]
        held["sums"] = _call(
            _early_sums_kernel,
            jax.ShapeDtypeStruct((rows, c), F32),
            [_SMEM] + [_VMEM] * 4,
            flops=(slots - 1) * conv_flops,
            moved=4 << 20,
        )(_after(sc, start), g1, hid1, gout1, xk1)
        return _after(follow, held["sums"])

    arrived = _latest_before(tail, EMPTY_FRAME, axis, n, early_conv, early_act, early_sums)
    lat1, g1, _ = held["early"]

    def first(*shape):
        return pl.BlockSpec((1, *shape), lambda i: (0,) * (len(shape) + 1))

    half, carried = rows // 2, 2 * m
    lat0, g0, send, keep, cache = _call(
        _late_kernel,
        [
            jax.ShapeDtypeStruct((h, w, c), BF),
            jax.ShapeDtypeStruct((m, 2 * c), BF),
            jax.ShapeDtypeStruct((half + carried, c), BF),
            jax.ShapeDtypeStruct((half, c), F32),
            jax.ShapeDtypeStruct((carried, c), BF),
        ],
        [_SMEM, first(2, h, w, c), first(2, 2, w, c), _VMEM, first(1, h, w, c)] + [_VMEM] * 5,
        [pltpu.VMEM((3, 1, 4, h + 2, w, c), BF), pltpu.VMEM((rows, c), F32)],
        flops=2 * conv_flops,
        moved=6 << 20,
        grid=(1,),
    )(sc, frames, row_halo, arrived, cotangent, wt, cb, stride_weight, sb, held["sums"])

    blocks = chips // 2
    piece = half // chips
    got = _xor(send, 1, n, axis)
    send_far, send_near, kept = _call(
        _across_x_kernel,
        [
            jax.ShapeDtypeStruct((2 * piece + carried // 2, c), BF),
            jax.ShapeDtypeStruct((2 * piece, c), BF),
            jax.ShapeDtypeStruct((blocks * piece, c), F32),
        ],
        [_SMEM] + [_VMEM] * 3,
        room=8,
    )(sc, keep, got, cache)
    got_far = _xor(send_far, 2, n, axis)
    got_near = _xor(send_near, 2, n, axis)
    grad = _call(
        _back_kernel,
        jax.ShapeDtypeStruct((slots, 2, h, w, c), F32),
        [_SMEM] + [_VMEM] * 3,
        [pltpu.VMEM((3, slots, 4, h + 2, w, c), BF)],
        flops=1,
        moved=1,
        room=24,
    )(_after(sc, kept), g0, g1, wt)
    kept, send_far = _after(kept, grad), _after(send_far, grad)
    core, pair, z = index & 1, (index >> 1) & 1, (index >> 2) & (blocks - 1)
    below, quarter = 2 * piece, carried // 4

    def by_pair(a, b):
        return jnp.where(pair == 0, a, b)

    chip_first, beside_first = send_far[below:], got_far[below:]
    quad_first = by_pair(
        _first_live(chip_first[:quarter], beside_first[:quarter]),
        _first_live(beside_first[quarter:], chip_first[quarter:]),
    )

    def summed(j, came):
        i = j % 2
        return kept[j * piece : (j + 1) * piece] + came[i * piece : (i + 1) * piece].astype(F32)

    outs = {
        j: jnp.concatenate([summed(j, got_far).astype(BF), quad_first], axis=0) for j in (3, 2)
    }
    got_near = _after(got_near, outs[3], outs[2])
    outs[1] = jnp.concatenate([summed(1, got_near).astype(BF), quad_first], axis=0)
    gots = {j: _xor(outs[j], 4 * j, n, axis) for j in (3, 2, 1)}
    mine = summed(0, got_near)
    for j in (1, 2, 3):
        mine = mine + gots[j][:piece].astype(F32)
    mine = mine.astype(BF)
    after = jnp.full((quarter, c), EMPTY_GRAD, BF)
    for target in range(blocks - 1, 0, -1):
        value = gots[3][piece:]
        for j in (1, 2):
            value = jnp.where((z ^ j) == target, gots[j][piece:], value)
        after = jnp.where(target > z, _first_live(value, after), after)
    k = 2 * chips
    if k < n:
        lead = jnp.full((quarter, c), EMPTY_GRAD, BF)
        for target in range(blocks - 1, -1, -1):
            value = quad_first
            for j in (1, 2, 3):
                value = jnp.where((z ^ j) == target, gots[j][piece:], value)
            lead = _first_live(value, lead)
        beyond, reach = None, 0
        while reach < n // k - 1:
            start = lead if beyond is None else _first_live(lead, beyond)
            step = k * (reach + 1)
            came = lax.ppermute(start, axis, [(i + step, i) for i in range(n - step)])
            beyond = came if beyond is None else _first_live(beyond, came)
            reach = 2 * reach + 1
        after = _first_live(after, beyond)
    while k < n:
        mine = (mine.astype(F32) + _xor(mine, k, n, axis).astype(F32)).astype(BF)
        k *= 2
    others = {j: _xor(mine, 4 * j, n, axis) for j in (3, 2, 1)}
    x_own = _xor(jnp.concatenate([mine, after], axis=0), 2, n, axis)
    x_near = _xor(others[1], 2, n, axis)
    x_far = _xor(jnp.concatenate([others[2], others[3]], axis=0), 2, n, axis)
    theirs = x_own[piece:]
    beyond = jnp.concatenate([by_pair(after, theirs), by_pair(theirs, after)], axis=0)
    beyond = by_pair(_first_live(beside_first, beyond), beyond)
    ours = jnp.concatenate(
        [mine, others[1], others[2], others[3], x_own[:piece], x_near, x_far, beyond], axis=0
    )
    other = _xor(ours, 1, n, axis)
    cwg, swg, cbg, sbg, frames_grad = _call(
        _final_kernel,
        [
            jax.ShapeDtypeStruct((27 * c, c), F32),
            jax.ShapeDtypeStruct((2 * c, c), F32),
            jax.ShapeDtypeStruct((1, c), F32),
            jax.ShapeDtypeStruct((1, c), F32),
            jax.ShapeDtypeStruct((slots, 2, h, w, c), BF),
        ],
        [_SMEM] + [_VMEM] * 4,
        [pltpu.VMEM((rows, c), F32)],
        room=12,
    )(sc, ours, other, got, grad)
    latents = jnp.concatenate([lat0[None], lat1], axis=0)[:, None]
    return (
        latents,
        frames_grad,
        cwg.reshape(3, 3, 3, c, c),
        cbg[0],
        swg.reshape(2, c, c),
        sbg[0],
    )


def solution(mesh):
    split = P(("groups", "tm"))
    return jax.shard_map(
        functools.partial(body, mesh.shape["tm"]),
        mesh=mesh,
        in_specs=(split, split, split, split, P(), P(), P(), P(), split),
        out_specs=(split, split, P("groups"), P("groups"), P("groups"), P("groups")),
        check_vma=False,
    )
```

```python
import functools

import jax
import jax.numpy as jnp
from jax import lax
from jax.experimental import pallas as pl
from jax.experimental.pallas import tpu as pltpu
from jax.sharding import PartitionSpec as P

BF = jnp.bfloat16
F32 = jnp.float32
EMPTY_FRAME = 100.0
EMPTY_GRAD = 1e30

_VMEM = pl.BlockSpec(memory_space=pltpu.VMEM)
_SMEM = pl.BlockSpec(memory_space=pltpu.SMEM)
_HBM = pl.BlockSpec(memory_space=pltpu.HBM)


def _call(kernel, out_shape, in_specs, scratch=(), flops=0, moved=0, room=16, grid=()):
    return pl.pallas_call(
        kernel,
        out_shape=out_shape,
        grid=grid,
        in_specs=in_specs,
        out_specs=jax.tree.map(lambda _: _VMEM, out_shape),
        scratch_shapes=list(scratch),
        compiler_params=pltpu.CompilerParams(vmem_limit_bytes=room << 20),
        cost_estimate=pl.CostEstimate(flops=flops, bytes_accessed=moved, transcendentals=0),
    )


def _put(xk, at, rows, value):
    n, w, c = value.shape
    flat = value.astype(F32).reshape(n * w, c)
    col = lax.broadcasted_iota(jnp.int32, (n * w, c), 0) % w
    right = jnp.where(col == 0, 0.0, pltpu.roll(flat, 1, 0))
    left = jnp.where(col == w - 1, 0.0, pltpu.roll(flat, n * w - 1, 0))
    for kw, shifted in enumerate((right, flat, left)):
        xk[(kw, *at, rows)] = shifted.astype(BF).reshape(n, w, c)


def _window(xk, kw, j, kh, h):
    v = xk[kw, :, j, kh : kh + h]
    return v.reshape(v.shape[0] * v.shape[1] * v.shape[2], v.shape[3])


def _wide(xk, j, h):
    return jnp.concatenate(
        [_window(xk, kw, j, kh, h) for kh in range(3) for kw in range(3)], axis=1
    )


def _conv(xk, w_ref, h):
    c = w_ref.shape[-1]
    zero = jnp.zeros((c, c), BF)
    lhs = jnp.concatenate([_wide(xk, j, h) for j in range(4)], axis=1)
    rhs = []
    for j in range(4):
        for tap in range(9):
            rhs.append(
                jnp.concatenate(
                    [w_ref[(j - t) * 9 + tap] if 0 <= j - t <= 2 else zero for t in range(2)],
                    axis=1,
                )
            )
    return jnp.dot(lhs, jnp.concatenate(rhs, axis=0), preferred_element_type=F32)


def _conv_back(xk, w_ref, h, frames=range(4)):
    c = w_ref.shape[-1]
    zero = jnp.zeros((c, c), BF)
    lhs = jnp.concatenate([_wide(xk, j, h) for j in frames], axis=1)
    rhs = []
    for f in range(2):
        row = []
        for j in frames:
            for tap in range(9):
                kt = 2 - (j - f)
                row.append(w_ref[kt * 9 + 8 - tap] if 0 <= kt <= 2 else zero)
        rhs.append(jnp.concatenate(row, axis=1))
    return lax.dot_general(
        lhs, jnp.concatenate(rhs, axis=0), (((1,), (1,)), ((), ())), preferred_element_type=F32
    )


def _activate(pre, gout, sw_ref, sb_ref):
    s = 1.0 / (1.0 + jnp.exp(-pre))
    hidden = (pre * s).astype(BF)
    sw = jnp.concatenate([sw_ref[0], sw_ref[1]], axis=0)
    lat = jnp.dot(hidden, sw, preferred_element_type=F32) + sb_ref[...]
    gh = lax.dot_general(gout, sw, (((1,), (1,)), ((), ())), preferred_element_type=F32)
    g = (gh * s * (1.0 + pre * (1.0 - s))).astype(BF)
    return lat, g, hidden


def _conv_bias(xk, w_ref, cb_ref, h):
    return _conv(xk, w_ref, h) + jnp.concatenate([cb_ref[...], cb_ref[...]], axis=1)


def _weight_grads(xk, g, hidden, gout, h, add):
    c = gout.shape[-1]
    parts = []
    for j in range(4):
        lhs = _wide(xk, j, h)
        parts.append(
            lax.dot_general(lhs, g, (((0,), (0,)), ((), ())), preferred_element_type=F32)
        )
    for kt in range(3):
        add(kt, parts[kt][:, :c] + parts[kt + 1][:, c:])
    sg = lax.dot_general(hidden, gout, (((0,), (0,)), ((), ())), preferred_element_type=F32)
    g32 = jnp.sum(g.astype(F32), axis=0, keepdims=True)
    add(3, sg)
    add(4, g32[:, :c] + g32[:, c:])
    add(5, jnp.sum(gout.astype(F32), axis=0, keepdims=True))


def _fill_early(sc, fr, ha, xk):
    slots, _, h, w, c = fr.shape
    for s in range(slots):
        for f in range(2):
            spots = [(s - 1, f + 2, None)] if s > 0 else []
            if s + 1 < slots:
                spots.append((s, f, sc[1 + s + 1] == 0))
            for slot, j, keep in spots:
                a, b = fr[s, f], ha[s, f]
                if keep is not None:
                    a = jnp.where(keep, a, jnp.zeros_like(a))
                    b = jnp.where(keep, b, jnp.zeros_like(b))
                _put(xk, (slot, j), slice(1, 1 + h), a)
                _put(xk, (slot, j), slice(0, 1), b[:1])
                _put(xk, (slot, j), slice(h + 1, h + 2), b[1:])


def _early_gout(sc, co):
    slots, _, h, w, c = co.shape
    return jnp.concatenate(
        [
            jnp.where(s < sc[0], co[s, 0], jnp.zeros_like(co[s, 0])).reshape(h * w, c)
            for s in range(1, slots)
        ],
        axis=0,
    )


def _early_conv_kernel(
    sc, frh, hah, coh, wh, cbh, swh, sbh, pre_ref, gout_ref, sw, sb, fr, ha, co, w_ref, cb, xk, sems
):
    h = fr.shape[2]
    pairs = ((frh, fr), (hah, ha), (coh, co), (wh, w_ref), (cbh, cb), (swh, sw), (sbh, sb))
    copies = [pltpu.make_async_copy(a, b, sems.at[i]) for i, (a, b) in enumerate(pairs)]
    for copy in copies:
        copy.start()
    copies[0].wait()
    copies[1].wait()
    _fill_early(sc, fr, ha, xk)
    copies[2].wait()
    gout_ref[...] = _early_gout(sc, co)
    for copy in copies[3:]:
        copy.wait()
    pre_ref[...] = _conv_bias(xk, w_ref, cb, h)


def _early_act_kernel(sc, pre_ref, gout_ref, sw, sb, lat_ref, g_ref, hid_ref):
    slots, h, w, c = lat_ref.shape
    lat, g, hidden = _activate(pre_ref[...], gout_ref[...], sw, sb)
    for s in range(slots):
        part = lat[s * h * w : (s + 1) * h * w]
        filled = s + 1 < sc[0]
        lat_ref[s] = jnp.where(filled, part, jnp.zeros_like(part)).astype(BF).reshape(h, w, c)
    g_ref[...] = g
    hid_ref[...] = hidden


def _early_sums_kernel(sc, frh, hah, g_ref, hid_ref, gout_ref, acc, xk, fr, ha, sems):
    copies = [
        pltpu.make_async_copy(a, b, sems.at[i]) for i, (a, b) in enumerate(((frh, fr), (hah, ha)))
    ]
    for copy in copies:
        copy.start()
    for copy in copies:
        copy.wait()
    _fill_early(sc, fr, ha, xk)
    _, _, h, _, c = fr.shape
    n9 = 9 * c

    def add(kind, value):
        if kind < 3:
            acc[kind * n9 : (kind + 1) * n9] = value
        elif kind == 3:
            acc[3 * n9 : 3 * n9 + 2 * c] = value
        else:
            at = 3 * n9 + 2 * c + (kind - 4)
            acc[at : at + 1] = value

    acc[3 * n9 + 2 * c :] = jnp.zeros((acc.shape[0] - 3 * n9 - 2 * c, c), F32)
    _weight_grads(xk, g_ref[...], hid_ref[...], gout_ref[...], h, add)


def _late_kernel(
    sc, frs, has, tail, cos, w_ref, cb, sw, sb, early, lat_ref, g_ref, send, keep, cache_ref, xk, acc
):
    fr, ha, co = frs.at[0], has.at[0], cos.at[0]
    _, h, w, c = fr.shape
    on = sc[1] == 0
    for f in range(2):
        _put(xk, (0, f + 2), slice(1, 1 + h), fr[f])
        _put(xk, (0, f + 2), slice(0, 1), ha[f, :1])
        _put(xk, (0, f + 2), slice(h + 1, h + 2), ha[f, 1:])
        a = tail[f * h : (f + 1) * h]
        b = tail[2 * h + 2 * f : 2 * h + 2 * f + 2]
        a = jnp.where(on, a, jnp.zeros_like(a))
        b = jnp.where(on, b, jnp.zeros_like(b))
        _put(xk, (0, f), slice(1, 1 + h), a)
        _put(xk, (0, f), slice(0, 1), b[:1])
        _put(xk, (0, f), slice(h + 1, h + 2), b[1:])
    filled = sc[0] > 0
    gout = jnp.where(filled, co[0], jnp.zeros_like(co[0])).reshape(h * w, c)
    lat, g, hidden = _activate(_conv_bias(xk, w_ref, cb, h), gout, sw, sb)
    lat_ref[...] = jnp.where(filled, lat, jnp.zeros_like(lat)).astype(BF).reshape(h, w, c)
    g_ref[...] = g
    n9 = 9 * c

    def add(kind, value):
        if kind < 3:
            rows = slice(kind * n9, (kind + 1) * n9)
        elif kind == 3:
            rows = slice(3 * n9, 3 * n9 + 2 * c)
        else:
            at = 3 * n9 + 2 * c + (kind - 4)
            rows = slice(at, at + 1)
        acc[rows] = early[rows] + value

    tail_rows = slice(3 * n9 + 2 * c, acc.shape[0])
    acc[tail_rows] = early[tail_rows]

    @pl.when(sc[0] >= 0)
    def _():
        _weight_grads(xk, g, hidden, gout, h, add)

        for t in range(2):
            for kw in range(3):
                xk[kw, 0, 2 + t, 0:1] = jnp.zeros((1, w, c), BF)
                xk[kw, 0, 2 + t, h + 1 : h + 2] = jnp.zeros((1, w, c), BF)
            v = g[:, t * c : (t + 1) * c].reshape(h, w, c)
            _put(xk, (0, 2 + t), slice(1, 1 + h), jnp.where(on, v, jnp.zeros_like(v)))
        back = _conv_back(xk, w_ref, h, (2, 3))
        back = jnp.where(filled, back, jnp.full_like(back, EMPTY_GRAD)).astype(BF)
        half = keep.shape[0]
        for t in range(2):
            lanes = slice(t * c, (t + 1) * c)
            cache_ref[t * h * w : (t + 1) * h * w] = back[:, lanes]
            send[half + t * h * w : half + (t + 1) * h * w] = back[:, lanes]
        core = sc[sc.shape[0] - 1]
        send[:half] = acc[pl.ds(pl.multiple_of((1 - core) * half, 16), half)].astype(BF)
        keep[...] = acc[pl.ds(pl.multiple_of(core * half, 16), half)]


def _back_kernel(sc, g0, g1, w_ref, out_ref, xk):
    slots, _, h, w, c = out_ref.shape
    m = h * w
    zero = jnp.zeros((1, w, c), BF)
    for kw in range(3):
        for j in range(4):
            for s in range(slots):
                xk[kw, s, j, 0:1] = zero
                xk[kw, s, j, h + 1 : h + 2] = zero
    for f in range(2):
        for kw in range(3):
            xk[kw, slots - 1, f + 2, 1 : 1 + h] = jnp.zeros((h, w, c), BF)
        lanes = slice(f * c, (f + 1) * c)
        for s in range(slots):
            v = g0[:, lanes] if s == 0 else g1[(s - 1) * m : s * m, lanes]
            v = v.reshape(h, w, c)
            _put(xk, (s, f), slice(1, 1 + h), v)
            if s > 0:
                on = sc[1 + s] == 0
                _put(xk, (s - 1, f + 2), slice(1, 1 + h), jnp.where(on, v, jnp.zeros_like(v)))
    out = _conv_back(xk, w_ref, h)
    for f in range(2):
        out_ref[:, f] = out[:, f * c : (f + 1) * c].reshape(slots, h, w, c)


def _first_live(a, b):
    return jnp.where(a.astype(F32) < EMPTY_GRAD / 2, a, b)


def _place(sc):
    chip, core = sc[sc.shape[0] - 2], sc[sc.shape[0] - 1]
    return lax.shift_right_logical(chip, 1), lax.bitwise_and(chip, 1), core


def _across_x_kernel(sc, keep, got, cache, send_far, send_near, kept):
    z, x, core = _place(sc)
    half = keep.shape[0]
    blocks = 4
    rows = half // (2 * blocks)

    def piece(j, side):
        p = 2 * lax.bitwise_xor(z, j) + side
        at = pl.ds(pl.multiple_of(p * rows, 16), rows)
        return keep[at] + got[at].astype(F32)

    for j in range(blocks):
        kept[j * rows : (j + 1) * rows] = piece(j, x)
        send, i = (send_near, j) if j < 2 else (send_far, j - 2)
        send[i * rows : (i + 1) * rows] = piece(j, 1 - x).astype(BF)
    part = cache.shape[0] // 2
    at = pl.multiple_of(core * part, 16)
    mine, theirs = cache[pl.ds(at, part)], got[pl.ds(half + at, part)]
    first = jnp.where(core == 0, _first_live(mine, theirs), _first_live(theirs, mine))
    send_far[2 * rows :] = first


def _tail_kernel(sc, fr, ha, out):
    h2 = fr.shape[1] * fr.shape[2]
    live = sc[0] > 0
    for ref, rows in ((fr, slice(0, h2)), (ha, slice(h2, out.shape[0]))):
        v = ref[...].reshape(rows.stop - rows.start, *out.shape[1:])
        out[rows] = jnp.where(live, v, jnp.full_like(v, EMPTY_FRAME))


def _final_kernel(sc, mine, other, got, grad, cw, sw, cb, sb, fg, acc):
    c = mine.shape[1]
    half = acc.shape[0] // 2
    z, x, core = _place(sc)
    blocks = 4
    rows = half // (2 * blocks)
    for ref, at_core in ((mine, core), (other, 1 - core)):
        for k in range(2 * blocks):
            side = x if k < blocks else 1 - x
            chip = 2 * lax.bitwise_xor(z, k % blocks) + side
            at = pl.multiple_of(at_core * half + chip * rows, 16)
            acc[pl.ds(at, rows)] = ref[k * rows : (k + 1) * rows].astype(F32)
    n27, n29 = 27 * c, 29 * c
    cw[...] = acc[:n27]
    sw[...] = acc[n27:n29]
    cb[...] = acc[n29 : n29 + 1]
    sb[...] = acc[n29 + 1 : n29 + 2]
    slots, frames, h, w, _ = grad.shape
    part = mine.shape[0] - half
    for s in range(slots):
        here = sc[0] - 1 == s
        for f in range(frames):
            low = f == 0
            a, b = mine[half:].astype(F32), other[half:].astype(F32)
            beyond = jnp.where(core == 0, a, b) if low else jnp.where(core == 0, b, a)
            beside = got[half + f * part : half + (f + 1) * part].astype(F32)
            came = jnp.where(core == 0, _first_live(beside, beyond), beyond)
            came = jnp.where(came < EMPTY_GRAD / 2, came, jnp.zeros_like(came)).reshape(h, w, c)
            fg[s, f] = (grad[s, f] + jnp.where(here, came, jnp.zeros_like(came))).astype(BF)


def _xor(x, k, n, axis):
    return lax.ppermute(x, axis, [(i, i ^ k) for i in range(n)])


def _latest_before(x, empty, axis, n, beside_x, beside_near, beside_far):
    index = lax.axis_index(axis)
    core, pair = index & 1, (index >> 1) & 1

    def newest(early, late):
        return jnp.where(late > empty / 2, early, late)

    def half(v):
        rows = v.shape[0] // 2
        return jnp.where(core == 0, v[:rows], v[rows:])

    other = _xor(x, 1, n, axis)
    a, b = half(x), half(other)
    chip = jnp.where(core == 0, newest(a, b), newest(b, a))
    beside = _xor(chip, 2, n, axis)
    quad = jnp.where(pair == 0, newest(chip, beside), newest(beside, chip))
    quad = beside_x(chip, quad)
    block, before, k = quad, jnp.full_like(quad, empty), 4
    while k < n:
        late = (index & k) > 0
        came = _xor(block, k, n, axis)
        if k == 4:
            came = beside_near(block, came)
        before = jnp.where(late, newest(came, before), before)
        if k == 8:
            before = beside_far(block, before)
        if 2 * k < n:
            block = jnp.where(late, newest(came, block), newest(block, came))
        k *= 2
    before = jnp.where(pair == 0, before, newest(before, beside))
    across = _xor(before, 1, n, axis)
    before = jnp.concatenate(
        [jnp.where(core == 0, before, across), jnp.where(core == 0, across, before)], axis=0
    )
    before = jnp.where(core == 0, before, newest(before, other))
    return jnp.where(before > empty / 2, jnp.zeros_like(before), before)


def _after(value, *earlier):
    return lax.optimization_barrier((value, *earlier))[0]


def body(
    n,
    frames,
    row_halo,
    clip_start,
    slab_counts,
    conv_weight,
    conv_bias,
    stride_weight,
    stride_bias,
    cotangent,
):
    axis = "tm"
    slots, _, h, w, c = frames.shape
    count = slab_counts[0]
    index = lax.axis_index(axis)
    chips = 8
    assert n % (2 * chips) == 0
    sc = jnp.concatenate(
        [
            slab_counts,
            clip_start,
            ((index >> 1) & (chips - 1)).reshape(1).astype(jnp.int32),
            (index & 1).reshape(1).astype(jnp.int32),
        ]
    )
    wt = conv_weight.reshape(27, c, c)
    cb, sb = conv_bias.reshape(1, c), stride_bias.reshape(1, c)
    unit = 16 * 2 * chips
    rows = -(-(29 * c + 2) // unit) * unit
    m = h * w
    conv_flops = 2 * m * 36 * c * 2 * c

    def newest_slot(i, sc):
        return (jnp.maximum(sc[0] - 1, 0), 0, 0, 0, 0)

    tail = pl.pallas_call(
        _tail_kernel,
        out_shape=jax.ShapeDtypeStruct((2 * h + 4, w, c), BF),
        grid_spec=pltpu.PrefetchScalarGridSpec(
            num_scalar_prefetch=1,
            grid=(1,),
            in_specs=[
                pl.BlockSpec((1, 2, h, w, c), newest_slot),
                pl.BlockSpec((1, 2, 2, w, c), newest_slot),
            ],
            out_specs=pl.BlockSpec((2 * h + 4, w, c), lambda i, sc: (0, 0, 0)),
        ),
        compiler_params=pltpu.CompilerParams(vmem_limit_bytes=8 << 20),
    )(
        slab_counts,
        *(pltpu.with_memory_space_constraint(v, pltpu.HBM) for v in (frames, row_halo)),
    )

    held = {}
    wide = ((slots - 1) * m, 2 * c)
    raw = [
        pltpu.with_memory_space_constraint(v, pltpu.HBM)
        for v in (frames, row_halo, cotangent, wt, cb, stride_weight, sb)
    ]
    windows = (3, slots - 1, 4, h + 2, w, c)

    def early_conv(start, follow):
        held["conv"] = _call(
            _early_conv_kernel,
            [
                jax.ShapeDtypeStruct(wide, F32),
                jax.ShapeDtypeStruct((wide[0], c), BF),
                jax.ShapeDtypeStruct(stride_weight.shape, BF),
                jax.ShapeDtypeStruct(sb.shape, F32),
            ],
            [_SMEM] + [_HBM] * len(raw),
            [pltpu.VMEM(v.shape, v.dtype) for v in raw[:5]]
            + [pltpu.VMEM(windows, BF), pltpu.SemaphoreType.DMA((len(raw),))],
            flops=(slots - 1) * conv_flops,
            moved=4 << 20,
        )(_after(sc, start), *raw)
        return _after(follow, held["conv"][0])

    def early_act(start, follow):
        pre, gout1, sw1, sb1 = held["conv"]
        held["early"] = _call(
            _early_act_kernel,
            [
                jax.ShapeDtypeStruct((slots - 1, h, w, c), BF),
                jax.ShapeDtypeStruct(wide, BF),
                jax.ShapeDtypeStruct(wide, BF),
            ],
            [_SMEM] + [_VMEM] * 4,
            moved=2 << 20,
            room=6,
        )(_after(sc, start), pre, gout1, sw1, sb1)
        return _after(follow, held["early"][1])

    def early_sums(start, follow):
        gout1 = held["conv"][1]
        _, g1, hid1 = held["early"]
        held["sums"] = _call(
            _early_sums_kernel,
            jax.ShapeDtypeStruct((rows, c), F32),
            [_SMEM, _HBM, _HBM] + [_VMEM] * 3,
            [pltpu.VMEM(windows, BF)]
            + [pltpu.VMEM(v.shape, BF) for v in raw[:2]]
            + [pltpu.SemaphoreType.DMA((2,))],
            flops=(slots - 1) * conv_flops,
            moved=4 << 20,
        )(_after(sc, start), raw[0], raw[1], g1, hid1, gout1)
        return _after(follow, held["sums"])

    arrived = _latest_before(tail, EMPTY_FRAME, axis, n, early_conv, early_act, early_sums)
    lat1, g1, _ = held["early"]

    def first(*shape):
        return pl.BlockSpec((1, *shape), lambda i: (0,) * (len(shape) + 1))

    half, carried = rows // 2, 2 * m
    lat0, g0, send, keep, cache = _call(
        _late_kernel,
        [
            jax.ShapeDtypeStruct((h, w, c), BF),
            jax.ShapeDtypeStruct((m, 2 * c), BF),
            jax.ShapeDtypeStruct((half + carried, c), BF),
            jax.ShapeDtypeStruct((half, c), F32),
            jax.ShapeDtypeStruct((carried, c), BF),
        ],
        [_SMEM, first(2, h, w, c), first(2, 2, w, c), _VMEM, first(1, h, w, c)] + [_VMEM] * 5,
        [pltpu.VMEM((3, 1, 4, h + 2, w, c), BF), pltpu.VMEM((rows, c), F32)],
        flops=2 * conv_flops,
        moved=6 << 20,
        grid=(1,),
    )(sc, frames, row_halo, arrived, cotangent, wt, cb, stride_weight, sb, held["sums"])

    blocks = chips // 2
    piece = half // chips
    got = _xor(send, 1, n, axis)
    send_far, send_near, kept = _call(
        _across_x_kernel,
        [
            jax.ShapeDtypeStruct((2 * piece + carried // 2, c), BF),
            jax.ShapeDtypeStruct((2 * piece, c), BF),
            jax.ShapeDtypeStruct((blocks * piece, c), F32),
        ],
        [_SMEM] + [_VMEM] * 3,
        room=8,
    )(sc, keep, got, cache)
    got_far = _xor(send_far, 2, n, axis)
    got_near = _xor(send_near, 2, n, axis)
    grad = _call(
        _back_kernel,
        jax.ShapeDtypeStruct((slots, 2, h, w, c), F32),
        [_SMEM] + [_VMEM] * 3,
        [pltpu.VMEM((3, slots, 4, h + 2, w, c), BF)],
        flops=1,
        moved=1,
        room=24,
    )(_after(sc, kept), g0, g1, wt)
    kept, send_far = _after(kept, grad), _after(send_far, grad)
    core, pair, z = index & 1, (index >> 1) & 1, (index >> 2) & (blocks - 1)
    below, quarter = 2 * piece, carried // 4

    def by_pair(a, b):
        return jnp.where(pair == 0, a, b)

    chip_first, beside_first = send_far[below:], got_far[below:]
    quad_first = by_pair(
        _first_live(chip_first[:quarter], beside_first[:quarter]),
        _first_live(beside_first[quarter:], chip_first[quarter:]),
    )

    def summed(j, came):
        i = j % 2
        return kept[j * piece : (j + 1) * piece] + came[i * piece : (i + 1) * piece].astype(F32)

    outs = {
        j: jnp.concatenate([summed(j, got_far).astype(BF), quad_first], axis=0) for j in (3, 2)
    }
    got_near = _after(got_near, outs[3], outs[2])
    outs[1] = jnp.concatenate([summed(1, got_near).astype(BF), quad_first], axis=0)
    gots = {j: _xor(outs[j], 4 * j, n, axis) for j in (3, 2, 1)}
    mine = summed(0, _after(got_near, outs[1]))
    for j in (3, 2):
        mine = mine + gots[j][:piece].astype(F32)
    gots[1] = _after(gots[1], mine)
    mine = (mine + gots[1][:piece].astype(F32)).astype(BF)
    after = jnp.full((quarter, c), EMPTY_GRAD, BF)
    for target in range(blocks - 1, 0, -1):
        value = gots[3][piece:]
        for j in (1, 2):
            value = jnp.where((z ^ j) == target, gots[j][piece:], value)
        after = jnp.where(target > z, _first_live(value, after), after)
    k = 2 * chips
    if k < n:
        lead = jnp.full((quarter, c), EMPTY_GRAD, BF)
        for target in range(blocks - 1, -1, -1):
            value = quad_first
            for j in (1, 2, 3):
                value = jnp.where((z ^ j) == target, gots[j][piece:], value)
            lead = _first_live(value, lead)
        beyond, reach = None, 0
        while reach < n // k - 1:
            start = lead if beyond is None else _first_live(lead, beyond)
            step = k * (reach + 1)
            came = lax.ppermute(start, axis, [(i + step, i) for i in range(n - step)])
            beyond = came if beyond is None else _first_live(beyond, came)
            reach = 2 * reach + 1
        after = _first_live(after, beyond)
    while k < n:
        mine = (mine.astype(F32) + _xor(mine, k, n, axis).astype(F32)).astype(BF)
        k *= 2
    others = {j: _xor(mine, 4 * j, n, axis) for j in (1, 3, 2)}
    x_own = _xor(jnp.concatenate([mine, after], axis=0), 2, n, axis)
    x_near = _xor(others[1], 2, n, axis)
    others[2] = _after(others[2], x_near)
    x_far = _xor(jnp.concatenate([others[2], others[3]], axis=0), 2, n, axis)
    theirs = x_own[piece:]
    beyond = jnp.concatenate([by_pair(after, theirs), by_pair(theirs, after)], axis=0)
    beyond = by_pair(_first_live(beside_first, beyond), beyond)
    ours = jnp.concatenate(
        [mine, others[1], others[2], others[3], x_own[:piece], x_near, x_far, beyond], axis=0
    )
    other = _xor(ours, 1, n, axis)
    cwg, swg, cbg, sbg, frames_grad = _call(
        _final_kernel,
        [
            jax.ShapeDtypeStruct((27 * c, c), F32),
            jax.ShapeDtypeStruct((2 * c, c), F32),
            jax.ShapeDtypeStruct((1, c), F32),
            jax.ShapeDtypeStruct((1, c), F32),
            jax.ShapeDtypeStruct((slots, 2, h, w, c), BF),
        ],
        [_SMEM] + [_VMEM] * 4,
        [pltpu.VMEM((rows, c), F32)],
        room=12,
    )(sc, ours, other, got, grad)
    latents = jnp.concatenate([lat0[None], lat1], axis=0)[:, None]
    return (
        latents,
        frames_grad,
        cwg.reshape(3, 3, 3, c, c),
        cbg[0],
        swg.reshape(2, c, c),
        sbg[0],
    )


def solution(mesh):
    split = P(("groups", "tm"))
    return jax.shard_map(
        functools.partial(body, mesh.shape["tm"]),
        mesh=mesh,
        in_specs=(split, split, split, split, P(), P(), P(), P(), split),
        out_specs=(split, split, P("groups"), P("groups"), P("groups"), P("groups")),
        check_vma=False,
    )
```

```python
import functools

import jax
import jax.numpy as jnp
from jax import lax
from jax.experimental import pallas as pl
from jax.experimental.pallas import tpu as pltpu
from jax.sharding import PartitionSpec as P

BF = jnp.bfloat16
F32 = jnp.float32
EMPTY_FRAME = 100.0
EMPTY_GRAD = 1e30

_VMEM = pl.BlockSpec(memory_space=pltpu.VMEM)
_SMEM = pl.BlockSpec(memory_space=pltpu.SMEM)
_HBM = pl.BlockSpec(memory_space=pltpu.HBM)


def _call(kernel, out_shape, in_specs, scratch=(), flops=0, moved=0, room=16, grid=()):
    return pl.pallas_call(
        kernel,
        out_shape=out_shape,
        grid=grid,
        in_specs=in_specs,
        out_specs=jax.tree.map(lambda _: _VMEM, out_shape),
        scratch_shapes=list(scratch),
        compiler_params=pltpu.CompilerParams(vmem_limit_bytes=room << 20),
        cost_estimate=pl.CostEstimate(flops=flops, bytes_accessed=moved, transcendentals=0),
    )


def _put(xk, at, rows, value):
    n, w, c = value.shape
    flat = value.astype(F32).reshape(n * w, c)
    col = lax.broadcasted_iota(jnp.int32, (n * w, c), 0) % w
    right = jnp.where(col == 0, 0.0, pltpu.roll(flat, 1, 0))
    left = jnp.where(col == w - 1, 0.0, pltpu.roll(flat, n * w - 1, 0))
    for kw, shifted in enumerate((right, flat, left)):
        xk[(kw, *at, rows)] = shifted.astype(BF).reshape(n, w, c)


def _window(xk, kw, j, kh, h):
    v = xk[kw, :, j, kh : kh + h]
    return v.reshape(v.shape[0] * v.shape[1] * v.shape[2], v.shape[3])


def _wide(xk, j, h):
    return jnp.concatenate(
        [_window(xk, kw, j, kh, h) for kh in range(3) for kw in range(3)], axis=1
    )


def _conv(xk, w_ref, h):
    c = w_ref.shape[-1]
    zero = jnp.zeros((c, c), BF)
    lhs = jnp.concatenate([_wide(xk, j, h) for j in range(4)], axis=1)
    rhs = []
    for j in range(4):
        for tap in range(9):
            rhs.append(
                jnp.concatenate(
                    [w_ref[(j - t) * 9 + tap] if 0 <= j - t <= 2 else zero for t in range(2)],
                    axis=1,
                )
            )
    return jnp.dot(lhs, jnp.concatenate(rhs, axis=0), preferred_element_type=F32)


def _conv_back(xk, w_ref, h, frames=range(4), base=0):
    c = w_ref.shape[-1]
    zero = jnp.zeros((c, c), BF)
    lhs = jnp.concatenate([_wide(xk, j - base, h) for j in frames], axis=1)
    rhs = []
    for f in range(2):
        row = []
        for j in frames:
            for tap in range(9):
                kt = 2 - (j - f)
                row.append(w_ref[kt * 9 + 8 - tap] if 0 <= kt <= 2 else zero)
        rhs.append(jnp.concatenate(row, axis=1))
    return lax.dot_general(
        lhs, jnp.concatenate(rhs, axis=0), (((1,), (1,)), ((), ())), preferred_element_type=F32
    )


def _activate(pre, gout, sw_ref, sb_ref):
    s = 1.0 / (1.0 + jnp.exp(-pre))
    hidden = (pre * s).astype(BF)
    sw = jnp.concatenate([sw_ref[0], sw_ref[1]], axis=0)
    lat = jnp.dot(hidden, sw, preferred_element_type=F32) + sb_ref[...]
    gh = lax.dot_general(gout, sw, (((1,), (1,)), ((), ())), preferred_element_type=F32)
    g = (gh * s * (1.0 + pre * (1.0 - s))).astype(BF)
    return lat, g, hidden


def _conv_bias(xk, w_ref, cb_ref, h):
    return _conv(xk, w_ref, h) + jnp.concatenate([cb_ref[...], cb_ref[...]], axis=1)


def _weight_grads(xk, g, hidden, gout, h, add):
    c = gout.shape[-1]
    parts = []
    for j in range(4):
        lhs = _wide(xk, j, h)
        parts.append(
            lax.dot_general(lhs, g, (((0,), (0,)), ((), ())), preferred_element_type=F32)
        )
    for kt in range(3):
        add(kt, parts[kt][:, :c] + parts[kt + 1][:, c:])
    sg = lax.dot_general(hidden, gout, (((0,), (0,)), ((), ())), preferred_element_type=F32)
    g32 = jnp.sum(g.astype(F32), axis=0, keepdims=True)
    add(3, sg)
    add(4, g32[:, :c] + g32[:, c:])
    add(5, jnp.sum(gout.astype(F32), axis=0, keepdims=True))


def _fill_early(sc, fr, ha, xk):
    slots, _, h, w, c = fr.shape
    for s in range(slots):
        for f in range(2):
            spots = [(s - 1, f + 2, None)] if s > 0 else []
            if s + 1 < slots:
                spots.append((s, f, sc[1 + s + 1] == 0))
            for slot, j, keep in spots:
                a, b = fr[s, f], ha[s, f]
                if keep is not None:
                    a = jnp.where(keep, a, jnp.zeros_like(a))
                    b = jnp.where(keep, b, jnp.zeros_like(b))
                _put(xk, (slot, j), slice(1, 1 + h), a)
                _put(xk, (slot, j), slice(0, 1), b[:1])
                _put(xk, (slot, j), slice(h + 1, h + 2), b[1:])


def _early_gout(sc, co):
    slots, _, h, w, c = co.shape
    return jnp.concatenate(
        [
            jnp.where(s < sc[0], co[s, 0], jnp.zeros_like(co[s, 0])).reshape(h * w, c)
            for s in range(1, slots)
        ],
        axis=0,
    )


def _early_conv_kernel(
    sc, frh, hah, coh, wh, cbh, swh, sbh, pre_ref, gout_ref, sw, sb, fr, ha, co, w_ref, cb, xk, sems
):
    h = fr.shape[2]
    pairs = ((frh, fr), (hah, ha), (coh, co), (wh, w_ref), (cbh, cb), (swh, sw), (sbh, sb))
    copies = [pltpu.make_async_copy(a, b, sems.at[i]) for i, (a, b) in enumerate(pairs)]
    for copy in copies:
        copy.start()
    copies[0].wait()
    copies[1].wait()
    _fill_early(sc, fr, ha, xk)
    copies[2].wait()
    gout_ref[...] = _early_gout(sc, co)
    for copy in copies[3:]:
        copy.wait()
    pre_ref[...] = _conv_bias(xk, w_ref, cb, h)


def _early_act_kernel(sc, pre_ref, gout_ref, sw, sb, lat_ref, g_ref, hid_ref):
    slots, h, w, c = lat_ref.shape
    lat, g, hidden = _activate(pre_ref[...], gout_ref[...], sw, sb)
    for s in range(slots):
        part = lat[s * h * w : (s + 1) * h * w]
        filled = s + 1 < sc[0]
        lat_ref[s] = jnp.where(filled, part, jnp.zeros_like(part)).astype(BF).reshape(h, w, c)
    g_ref[...] = g
    hid_ref[...] = hidden


def _early_sums_kernel(sc, frh, hah, g_ref, hid_ref, gout_ref, acc, xk, fr, ha, sems):
    copies = [
        pltpu.make_async_copy(a, b, sems.at[i]) for i, (a, b) in enumerate(((frh, fr), (hah, ha)))
    ]
    for copy in copies:
        copy.start()
    for copy in copies:
        copy.wait()
    _fill_early(sc, fr, ha, xk)
    _, _, h, _, c = fr.shape
    n9 = 9 * c

    def add(kind, value):
        if kind < 3:
            acc[kind * n9 : (kind + 1) * n9] = value
        elif kind == 3:
            acc[3 * n9 : 3 * n9 + 2 * c] = value
        else:
            at = 3 * n9 + 2 * c + (kind - 4)
            acc[at : at + 1] = value

    acc[3 * n9 + 2 * c :] = jnp.zeros((acc.shape[0] - 3 * n9 - 2 * c, c), F32)
    _weight_grads(xk, g_ref[...], hid_ref[...], gout_ref[...], h, add)


def _late_kernel(
    sc, frs, has, tail, cos, w_ref, cb, sw, sb, early, lat_ref, g_ref, send, keep, xk, acc
):
    fr, ha, co = frs.at[0], has.at[0], cos.at[0]
    _, h, w, c = fr.shape
    on = sc[1] == 0
    for f in range(2):
        _put(xk, (0, f + 2), slice(1, 1 + h), fr[f])
        _put(xk, (0, f + 2), slice(0, 1), ha[f, :1])
        _put(xk, (0, f + 2), slice(h + 1, h + 2), ha[f, 1:])
        a = tail[f * h : (f + 1) * h]
        b = tail[2 * h + 2 * f : 2 * h + 2 * f + 2]
        a = jnp.where(on, a, jnp.zeros_like(a))
        b = jnp.where(on, b, jnp.zeros_like(b))
        _put(xk, (0, f), slice(1, 1 + h), a)
        _put(xk, (0, f), slice(0, 1), b[:1])
        _put(xk, (0, f), slice(h + 1, h + 2), b[1:])
    filled = sc[0] > 0
    gout = jnp.where(filled, co[0], jnp.zeros_like(co[0])).reshape(h * w, c)
    lat, g, hidden = _activate(_conv_bias(xk, w_ref, cb, h), gout, sw, sb)
    lat_ref[...] = jnp.where(filled, lat, jnp.zeros_like(lat)).astype(BF).reshape(h, w, c)
    g_ref[...] = g
    n9 = 9 * c

    def add(kind, value):
        if kind < 3:
            rows = slice(kind * n9, (kind + 1) * n9)
        elif kind == 3:
            rows = slice(3 * n9, 3 * n9 + 2 * c)
        else:
            at = 3 * n9 + 2 * c + (kind - 4)
            rows = slice(at, at + 1)
        acc[rows] = early[rows] + value

    tail_rows = slice(3 * n9 + 2 * c, acc.shape[0])
    acc[tail_rows] = early[tail_rows]

    @pl.when(sc[0] >= 0)
    def _():
        _weight_grads(xk, g, hidden, gout, h, add)

        half = keep.shape[0]
        core = sc[sc.shape[0] - 1]
        send[...] = acc[pl.ds(pl.multiple_of((1 - core) * half, 16), half)].astype(BF)
        keep[...] = acc[pl.ds(pl.multiple_of(core * half, 16), half)]


def _carried_kernel(sc, g_ref, w_ref, out, xk):
    _, _, _, h, w, c = xk.shape
    h = h - 2
    on = sc[1] == 0
    for t in range(2):
        for kw in range(3):
            xk[kw, 0, t, 0:1] = jnp.zeros((1, w, c), BF)
            xk[kw, 0, t, h + 1 : h + 2] = jnp.zeros((1, w, c), BF)
        v = g_ref[:, t * c : (t + 1) * c].reshape(h, w, c)
        _put(xk, (0, t), slice(1, 1 + h), jnp.where(on, v, jnp.zeros_like(v)))
    back = _conv_back(xk, w_ref, h, (2, 3), 2)
    back = jnp.where(sc[0] > 0, back, jnp.full_like(back, EMPTY_GRAD)).astype(BF)
    for t in range(2):
        out[t * h * w : (t + 1) * h * w] = back[:, t * c : (t + 1) * c]


def _back_kernel(sc, g0, g1, w_ref, out_ref, xk):
    slots, _, h, w, c = out_ref.shape
    m = h * w
    zero = jnp.zeros((1, w, c), BF)
    for kw in range(3):
        for j in range(4):
            for s in range(slots):
                xk[kw, s, j, 0:1] = zero
                xk[kw, s, j, h + 1 : h + 2] = zero
    for f in range(2):
        for kw in range(3):
            xk[kw, slots - 1, f + 2, 1 : 1 + h] = jnp.zeros((h, w, c), BF)
        lanes = slice(f * c, (f + 1) * c)
        for s in range(slots):
            v = g0[:, lanes] if s == 0 else g1[(s - 1) * m : s * m, lanes]
            v = v.reshape(h, w, c)
            _put(xk, (s, f), slice(1, 1 + h), v)
            if s > 0:
                on = sc[1 + s] == 0
                _put(xk, (s - 1, f + 2), slice(1, 1 + h), jnp.where(on, v, jnp.zeros_like(v)))
    out = _conv_back(xk, w_ref, h)
    for f in range(2):
        out_ref[:, f] = out[:, f * c : (f + 1) * c].reshape(slots, h, w, c)


def _first_live(a, b):
    return jnp.where(a.astype(F32) < EMPTY_GRAD / 2, a, b)


def _place(sc):
    chip, core = sc[sc.shape[0] - 2], sc[sc.shape[0] - 1]
    return lax.shift_right_logical(chip, 1), lax.bitwise_and(chip, 1), core


def _across_x_kernel(sc, keep, got, send_far, send_near, kept):
    z, x, _ = _place(sc)
    half = keep.shape[0]
    blocks = 4
    rows = half // (2 * blocks)

    def piece(j, side):
        p = 2 * lax.bitwise_xor(z, j) + side
        at = pl.ds(pl.multiple_of(p * rows, 16), rows)
        return keep[at] + got[at].astype(F32)

    for j in range(blocks):
        kept[j * rows : (j + 1) * rows] = piece(j, x)
        send, i = (send_near, j) if j < 2 else (send_far, j - 2)
        send[i * rows : (i + 1) * rows] = piece(j, 1 - x).astype(BF)


def _tail_kernel(sc, fr, ha, out):
    h2 = fr.shape[1] * fr.shape[2]
    live = sc[0] > 0
    for ref, rows in ((fr, slice(0, h2)), (ha, slice(h2, out.shape[0]))):
        v = ref[...].reshape(rows.stop - rows.start, *out.shape[1:])
        out[rows] = jnp.where(live, v, jnp.full_like(v, EMPTY_FRAME))


def _final_kernel(sc, mine, other, got, grad, cw, sw, cb, sb, fg, acc):
    c = mine.shape[1]
    half = acc.shape[0] // 2
    z, x, core = _place(sc)
    blocks = 4
    rows = half // (2 * blocks)
    for ref, at_core in ((mine, core), (other, 1 - core)):
        for k in range(2 * blocks):
            side = x if k < blocks else 1 - x
            chip = 2 * lax.bitwise_xor(z, k % blocks) + side
            at = pl.multiple_of(at_core * half + chip * rows, 16)
            acc[pl.ds(at, rows)] = ref[k * rows : (k + 1) * rows].astype(F32)
    n27, n29 = 27 * c, 29 * c
    cw[...] = acc[:n27]
    sw[...] = acc[n27:n29]
    cb[...] = acc[n29 : n29 + 1]
    sb[...] = acc[n29 + 1 : n29 + 2]
    slots, frames, h, w, _ = grad.shape
    part = mine.shape[0] - half
    for s in range(slots):
        here = sc[0] - 1 == s
        for f in range(frames):
            low = f == 0
            a, b = mine[half:].astype(F32), other[half:].astype(F32)
            beyond = jnp.where(core == 0, a, b) if low else jnp.where(core == 0, b, a)
            beside = got[f * part : (f + 1) * part].astype(F32)
            came = jnp.where(core == 0, _first_live(beside, beyond), beyond)
            came = jnp.where(came < EMPTY_GRAD / 2, came, jnp.zeros_like(came)).reshape(h, w, c)
            fg[s, f] = (grad[s, f] + jnp.where(here, came, jnp.zeros_like(came))).astype(BF)


def _xor(x, k, n, axis):
    return lax.ppermute(x, axis, [(i, i ^ k) for i in range(n)])


def _latest_before(x, empty, axis, n, beside_x, beside_near, beside_far):
    index = lax.axis_index(axis)
    core, pair = index & 1, (index >> 1) & 1

    def newest(early, late):
        return jnp.where(late > empty / 2, early, late)

    def half(v):
        rows = v.shape[0] // 2
        return jnp.where(core == 0, v[:rows], v[rows:])

    other = _xor(x, 1, n, axis)
    a, b = half(x), half(other)
    chip = jnp.where(core == 0, newest(a, b), newest(b, a))
    beside = _xor(chip, 2, n, axis)
    quad = jnp.where(pair == 0, newest(chip, beside), newest(beside, chip))
    quad = beside_x(chip, quad)
    block, before, k = quad, jnp.full_like(quad, empty), 4
    while k < n:
        late = (index & k) > 0
        came = _xor(block, k, n, axis)
        if k == 4:
            came = beside_near(block, came)
        before = jnp.where(late, newest(came, before), before)
        if k == 8:
            before = beside_far(block, before)
        if 2 * k < n:
            block = jnp.where(late, newest(came, block), newest(block, came))
        k *= 2
    before = jnp.where(pair == 0, before, newest(before, beside))
    across = _xor(before, 1, n, axis)
    before = jnp.concatenate(
        [jnp.where(core == 0, before, across), jnp.where(core == 0, across, before)], axis=0
    )
    before = jnp.where(core == 0, before, newest(before, other))
    return jnp.where(before > empty / 2, jnp.zeros_like(before), before)


def _after(value, *earlier):
    return lax.optimization_barrier((value, *earlier))[0]


def body(
    n,
    frames,
    row_halo,
    clip_start,
    slab_counts,
    conv_weight,
    conv_bias,
    stride_weight,
    stride_bias,
    cotangent,
):
    axis = "tm"
    slots, _, h, w, c = frames.shape
    count = slab_counts[0]
    index = lax.axis_index(axis)
    chips = 8
    assert n % (2 * chips) == 0
    sc = jnp.concatenate(
        [
            slab_counts,
            clip_start,
            ((index >> 1) & (chips - 1)).reshape(1).astype(jnp.int32),
            (index & 1).reshape(1).astype(jnp.int32),
        ]
    )
    wt = conv_weight.reshape(27, c, c)
    cb, sb = conv_bias.reshape(1, c), stride_bias.reshape(1, c)
    unit = 16 * 2 * chips
    rows = -(-(29 * c + 2) // unit) * unit
    m = h * w
    conv_flops = 2 * m * 36 * c * 2 * c

    def newest_slot(i, sc):
        return (jnp.maximum(sc[0] - 1, 0), 0, 0, 0, 0)

    tail = pl.pallas_call(
        _tail_kernel,
        out_shape=jax.ShapeDtypeStruct((2 * h + 4, w, c), BF),
        grid_spec=pltpu.PrefetchScalarGridSpec(
            num_scalar_prefetch=1,
            grid=(1,),
            in_specs=[
                pl.BlockSpec((1, 2, h, w, c), newest_slot),
                pl.BlockSpec((1, 2, 2, w, c), newest_slot),
            ],
            out_specs=pl.BlockSpec((2 * h + 4, w, c), lambda i, sc: (0, 0, 0)),
        ),
        compiler_params=pltpu.CompilerParams(vmem_limit_bytes=8 << 20),
    )(
        slab_counts,
        *(pltpu.with_memory_space_constraint(v, pltpu.HBM) for v in (frames, row_halo)),
    )

    held = {}
    wide = ((slots - 1) * m, 2 * c)
    raw = [
        pltpu.with_memory_space_constraint(v, pltpu.HBM)
        for v in (frames, row_halo, cotangent, wt, cb, stride_weight, sb)
    ]
    windows = (3, slots - 1, 4, h + 2, w, c)

    def early_conv(start, follow):
        held["conv"] = _call(
            _early_conv_kernel,
            [
                jax.ShapeDtypeStruct(wide, F32),
                jax.ShapeDtypeStruct((wide[0], c), BF),
                jax.ShapeDtypeStruct(stride_weight.shape, BF),
                jax.ShapeDtypeStruct(sb.shape, F32),
            ],
            [_SMEM] + [_HBM] * len(raw),
            [pltpu.VMEM(v.shape, v.dtype) for v in raw[:5]]
            + [pltpu.VMEM(windows, BF), pltpu.SemaphoreType.DMA((len(raw),))],
            flops=(slots - 1) * conv_flops,
            moved=4 << 20,
        )(_after(sc, start), *raw)
        return _after(follow, held["conv"][0])

    def early_act(start, follow):
        pre, gout1, sw1, sb1 = held["conv"]
        held["early"] = _call(
            _early_act_kernel,
            [
                jax.ShapeDtypeStruct((slots - 1, h, w, c), BF),
                jax.ShapeDtypeStruct(wide, BF),
                jax.ShapeDtypeStruct(wide, BF),
            ],
            [_SMEM] + [_VMEM] * 4,
            moved=2 << 20,
            room=6,
        )(_after(sc, start), pre, gout1, sw1, sb1)
        return _after(follow, held["early"][1])

    def early_sums(start, follow):
        gout1 = held["conv"][1]
        _, g1, hid1 = held["early"]
        held["sums"] = _call(
            _early_sums_kernel,
            jax.ShapeDtypeStruct((rows, c), F32),
            [_SMEM, _HBM, _HBM] + [_VMEM] * 3,
            [pltpu.VMEM(windows, BF)]
            + [pltpu.VMEM(v.shape, BF) for v in raw[:2]]
            + [pltpu.SemaphoreType.DMA((2,))],
            flops=(slots - 1) * conv_flops,
            moved=4 << 20,
        )(_after(sc, start), raw[0], raw[1], g1, hid1, gout1)
        return _after(follow, held["sums"])

    arrived = _latest_before(tail, EMPTY_FRAME, axis, n, early_conv, early_act, early_sums)
    lat1, g1, _ = held["early"]

    def first(*shape):
        return pl.BlockSpec((1, *shape), lambda i: (0,) * (len(shape) + 1))

    half, carried = rows // 2, 2 * m
    lat0, g0, send, keep = _call(
        _late_kernel,
        [
            jax.ShapeDtypeStruct((h, w, c), BF),
            jax.ShapeDtypeStruct((m, 2 * c), BF),
            jax.ShapeDtypeStruct((half, c), BF),
            jax.ShapeDtypeStruct((half, c), F32),
        ],
        [_SMEM, first(2, h, w, c), first(2, 2, w, c), _VMEM, first(1, h, w, c)] + [_VMEM] * 5,
        [pltpu.VMEM((3, 1, 4, h + 2, w, c), BF), pltpu.VMEM((rows, c), F32)],
        flops=2 * conv_flops,
        moved=6 << 20,
        grid=(1,),
    )(sc, frames, row_halo, arrived, cotangent, wt, cb, stride_weight, sb, held["sums"])

    blocks = chips // 2
    piece = half // chips
    got = _xor(send, 1, n, axis)
    first_grad = _call(
        _carried_kernel,
        jax.ShapeDtypeStruct((carried, c), BF),
        [_SMEM, _VMEM, _VMEM],
        [pltpu.VMEM((3, 1, 2, h + 2, w, c), BF)],
        flops=conv_flops // 2,
        moved=1 << 20,
        room=8,
    )(sc, g0, wt)
    keep = _after(keep, first_grad)
    send_far, send_near, kept = _call(
        _across_x_kernel,
        [
            jax.ShapeDtypeStruct((2 * piece, c), BF),
            jax.ShapeDtypeStruct((2 * piece, c), BF),
            jax.ShapeDtypeStruct((blocks * piece, c), F32),
        ],
        [_SMEM] + [_VMEM] * 2,
        room=8,
    )(sc, keep, got)
    got_far = _xor(send_far, 2, n, axis)
    got_first = _xor(_after(first_grad, kept), 1, n, axis)
    grad = _call(
        _back_kernel,
        jax.ShapeDtypeStruct((slots, 2, h, w, c), F32),
        [_SMEM] + [_VMEM] * 3,
        [pltpu.VMEM((3, slots, 4, h + 2, w, c), BF)],
        flops=1,
        moved=1,
        room=24,
    )(_after(sc, kept), g0, g1, wt)
    kept, got_first = _after(kept, grad), _after(got_first, grad)
    core, pair = index & 1, (index >> 1) & 1
    below, quarter = 2 * piece, carried // 4

    def by(bit, a, b):
        return jnp.where(bit == 0, a, b)

    def by_half(bit, v):
        rows = v.shape[0] // 2
        return by(bit, v[:rows], v[rows:])

    def ordered(bit, ours, theirs):
        return by(bit, _first_live(ours, theirs), _first_live(theirs, ours))

    chip_first = ordered(core, by_half(core, first_grad), by_half(core, got_first))
    got_near = _xor(jnp.concatenate([send_near, chip_first], axis=0), 2, n, axis)

    def summed(j, came):
        i = j % 2
        return kept[j * piece : (j + 1) * piece] + came[i * piece : (i + 1) * piece].astype(F32)

    outs = {j: summed(j, got_far).astype(BF) for j in (3, 2)}
    got_near = _after(got_near, outs[3], outs[2])
    beside_first = got_near[below:]
    outs[1] = summed(1, got_near).astype(BF)
    gots = {j: _xor(outs[j], 4 * j, n, axis) for j in (3, 2, 1)}
    near_again = _after(got_near, outs[1])
    mine = summed(0, near_again)
    lead = ordered(pair, by_half(pair, chip_first), by_half(pair, near_again[below:]))
    beyond, k = jnp.full_like(lead, EMPTY_GRAD), 4
    while k < n:
        came = _xor(lead, k, n, axis)
        beyond = by(index & k, _first_live(beyond, came), beyond)
        if 2 * k < n:
            lead = ordered(index & k, lead, came)
        k *= 2
    for j in (3, 2):
        mine = mine + gots[j].astype(F32)
    gots[1] = _after(gots[1], mine)
    mine = (mine + gots[1].astype(F32)).astype(BF)
    k = 2 * chips
    while k < n:
        mine = (mine.astype(F32) + _xor(mine, k, n, axis).astype(F32)).astype(BF)
        k *= 2
    others = {j: _xor(mine, 4 * j, n, axis) for j in (3, 2, 1)}
    x_own = _xor(mine, 2, n, axis)
    x_near = _xor(others[1], 2, n, axis)
    x_far = _xor(jnp.concatenate([others[2], others[3], beyond], axis=0), 2, n, axis)
    theirs = x_far[below:]
    beyond = jnp.concatenate([by(pair, beyond, theirs), by(pair, theirs, beyond)], axis=0)
    beyond = by(pair, _first_live(beside_first, beyond), beyond)
    ours = jnp.concatenate(
        [mine, others[1], others[2], others[3], x_own, x_near, x_far[:below], beyond], axis=0
    )
    other = _xor(ours, 1, n, axis)
    cwg, swg, cbg, sbg, frames_grad = _call(
        _final_kernel,
        [
            jax.ShapeDtypeStruct((27 * c, c), F32),
            jax.ShapeDtypeStruct((2 * c, c), F32),
            jax.ShapeDtypeStruct((1, c), F32),
            jax.ShapeDtypeStruct((1, c), F32),
            jax.ShapeDtypeStruct((slots, 2, h, w, c), BF),
        ],
        [_SMEM] + [_VMEM] * 4,
        [pltpu.VMEM((rows, c), F32)],
        room=12,
    )(sc, ours, other, got_first, grad)
    latents = jnp.concatenate([lat0[None], lat1], axis=0)[:, None]
    return (
        latents,
        frames_grad,
        cwg.reshape(3, 3, 3, c, c),
        cbg[0],
        swg.reshape(2, c, c),
        sbg[0],
    )


def solution(mesh):
    split = P(("groups", "tm"))
    return jax.shard_map(
        functools.partial(body, mesh.shape["tm"]),
        mesh=mesh,
        in_specs=(split, split, split, split, P(), P(), P(), P(), split),
        out_specs=(split, split, P("groups"), P("groups"), P("groups"), P("groups")),
        check_vma=False,
    )
```

```python
import functools

import jax
import jax.numpy as jnp
from jax import lax
from jax.experimental import pallas as pl
from jax.experimental.pallas import tpu as pltpu
from jax.sharding import PartitionSpec as P

BF = jnp.bfloat16
F32 = jnp.float32
EMPTY_FRAME = 100.0
EMPTY_GRAD = 1e30

_VMEM = pl.BlockSpec(memory_space=pltpu.VMEM)
_SMEM = pl.BlockSpec(memory_space=pltpu.SMEM)
_HBM = pl.BlockSpec(memory_space=pltpu.HBM)


def _call(kernel, out_shape, in_specs, scratch=(), flops=0, moved=0, room=16, grid=()):
    return pl.pallas_call(
        kernel,
        out_shape=out_shape,
        grid=grid,
        in_specs=in_specs,
        out_specs=jax.tree.map(lambda _: _VMEM, out_shape),
        scratch_shapes=list(scratch),
        compiler_params=pltpu.CompilerParams(vmem_limit_bytes=room << 20),
        cost_estimate=pl.CostEstimate(flops=flops, bytes_accessed=moved, transcendentals=0),
    )


def _put(xk, at, rows, value):
    n, w, c = value.shape
    flat = value.astype(F32).reshape(n * w, c)
    col = lax.broadcasted_iota(jnp.int32, (n * w, c), 0) % w
    right = jnp.where(col == 0, 0.0, pltpu.roll(flat, 1, 0))
    left = jnp.where(col == w - 1, 0.0, pltpu.roll(flat, n * w - 1, 0))
    for kw, shifted in enumerate((right, flat, left)):
        xk[(kw, *at, rows)] = shifted.astype(BF).reshape(n, w, c)


def _window(xk, kw, j, kh, h):
    v = xk[kw, :, j, kh : kh + h]
    return v.reshape(v.shape[0] * v.shape[1] * v.shape[2], v.shape[3])


def _wide(xk, j, h):
    return jnp.concatenate(
        [_window(xk, kw, j, kh, h) for kh in range(3) for kw in range(3)], axis=1
    )


def _conv(xk, w_ref, h):
    c = w_ref.shape[-1]
    zero = jnp.zeros((c, c), BF)
    lhs = jnp.concatenate([_wide(xk, j, h) for j in range(4)], axis=1)
    rhs = []
    for j in range(4):
        for tap in range(9):
            rhs.append(
                jnp.concatenate(
                    [w_ref[(j - t) * 9 + tap] if 0 <= j - t <= 2 else zero for t in range(2)],
                    axis=1,
                )
            )
    return jnp.dot(lhs, jnp.concatenate(rhs, axis=0), preferred_element_type=F32)


def _conv_back(xk, w_ref, h, frames=range(4), base=0):
    c = w_ref.shape[-1]
    zero = jnp.zeros((c, c), BF)
    lhs = jnp.concatenate([_wide(xk, j - base, h) for j in frames], axis=1)
    rhs = []
    for f in range(2):
        row = []
        for j in frames:
            for tap in range(9):
                kt = 2 - (j - f)
                row.append(w_ref[kt * 9 + 8 - tap] if 0 <= kt <= 2 else zero)
        rhs.append(jnp.concatenate(row, axis=1))
    return lax.dot_general(
        lhs, jnp.concatenate(rhs, axis=0), (((1,), (1,)), ((), ())), preferred_element_type=F32
    )


def _activate(pre, gout, sw_ref, sb_ref):
    s = 1.0 / (1.0 + jnp.exp(-pre))
    hidden = (pre * s).astype(BF)
    sw = jnp.concatenate([sw_ref[0], sw_ref[1]], axis=0)
    lat = jnp.dot(hidden, sw, preferred_element_type=F32) + sb_ref[...]
    gh = lax.dot_general(gout, sw, (((1,), (1,)), ((), ())), preferred_element_type=F32)
    g = (gh * s * (1.0 + pre * (1.0 - s))).astype(BF)
    return lat, g, hidden


def _conv_bias(xk, w_ref, cb_ref, h):
    return _conv(xk, w_ref, h) + jnp.concatenate([cb_ref[...], cb_ref[...]], axis=1)


def _weight_grads(xk, g, hidden, gout, h, add):
    c = gout.shape[-1]
    parts = []
    for j in range(4):
        lhs = _wide(xk, j, h)
        parts.append(
            lax.dot_general(lhs, g, (((0,), (0,)), ((), ())), preferred_element_type=F32)
        )
    for kt in range(3):
        add(kt, parts[kt][:, :c] + parts[kt + 1][:, c:])
    sg = lax.dot_general(hidden, gout, (((0,), (0,)), ((), ())), preferred_element_type=F32)
    g32 = jnp.sum(g.astype(F32), axis=0, keepdims=True)
    add(3, sg)
    add(4, g32[:, :c] + g32[:, c:])
    add(5, jnp.sum(gout.astype(F32), axis=0, keepdims=True))


def _fill_early(sc, fr, ha, xk):
    slots, _, h, w, c = fr.shape
    for s in range(slots):
        for f in range(2):
            spots = [(s - 1, f + 2, None)] if s > 0 else []
            if s + 1 < slots:
                spots.append((s, f, sc[1 + s + 1] == 0))
            for slot, j, keep in spots:
                a, b = fr[s, f], ha[s, f]
                if keep is not None:
                    a = jnp.where(keep, a, jnp.zeros_like(a))
                    b = jnp.where(keep, b, jnp.zeros_like(b))
                _put(xk, (slot, j), slice(1, 1 + h), a)
                _put(xk, (slot, j), slice(0, 1), b[:1])
                _put(xk, (slot, j), slice(h + 1, h + 2), b[1:])


def _early_gout(sc, co):
    slots, _, h, w, c = co.shape
    return jnp.concatenate(
        [
            jnp.where(s < sc[0], co[s, 0], jnp.zeros_like(co[s, 0])).reshape(h * w, c)
            for s in range(1, slots)
        ],
        axis=0,
    )


def _early_conv_kernel(
    sc, frh, hah, coh, wh, cbh, swh, sbh, pre_ref, gout_ref, sw, sb, fr, ha, co, w_ref, cb, xk, sems
):
    h = fr.shape[2]
    pairs = ((frh, fr), (hah, ha), (coh, co), (wh, w_ref), (cbh, cb), (swh, sw), (sbh, sb))
    copies = [pltpu.make_async_copy(a, b, sems.at[i]) for i, (a, b) in enumerate(pairs)]
    for copy in copies:
        copy.start()
    copies[0].wait()
    copies[1].wait()
    _fill_early(sc, fr, ha, xk)
    copies[2].wait()
    gout_ref[...] = _early_gout(sc, co)
    for copy in copies[3:]:
        copy.wait()
    pre_ref[...] = _conv_bias(xk, w_ref, cb, h)


def _early_act_kernel(sc, pre_ref, gout_ref, sw, sb, lat_ref, g_ref, hid_ref):
    slots, h, w, c = lat_ref.shape
    lat, g, hidden = _activate(pre_ref[...], gout_ref[...], sw, sb)
    for s in range(slots):
        part = lat[s * h * w : (s + 1) * h * w]
        filled = s + 1 < sc[0]
        lat_ref[s] = jnp.where(filled, part, jnp.zeros_like(part)).astype(BF).reshape(h, w, c)
    g_ref[...] = g
    hid_ref[...] = hidden


def _early_sums_kernel(sc, frh, hah, g_ref, hid_ref, gout_ref, acc, xk, fr, ha, sems):
    copies = [
        pltpu.make_async_copy(a, b, sems.at[i]) for i, (a, b) in enumerate(((frh, fr), (hah, ha)))
    ]
    for copy in copies:
        copy.start()
    for copy in copies:
        copy.wait()
    _fill_early(sc, fr, ha, xk)
    _, _, h, _, c = fr.shape
    n9 = 9 * c

    def add(kind, value):
        if kind < 3:
            acc[kind * n9 : (kind + 1) * n9] = value
        elif kind == 3:
            acc[3 * n9 : 3 * n9 + 2 * c] = value
        else:
            at = 3 * n9 + 2 * c + (kind - 4)
            acc[at : at + 1] = value

    acc[3 * n9 + 2 * c :] = jnp.zeros((acc.shape[0] - 3 * n9 - 2 * c, c), F32)
    _weight_grads(xk, g_ref[...], hid_ref[...], gout_ref[...], h, add)


def _late_kernel(
    sc, frs, has, tail, cos, w_ref, cb, sw, sb, early, lat_ref, g_ref, send, keep, xk, acc
):
    fr, ha, co = frs.at[0], has.at[0], cos.at[0]
    _, h, w, c = fr.shape
    on = sc[1] == 0
    for f in range(2):
        _put(xk, (0, f + 2), slice(1, 1 + h), fr[f])
        _put(xk, (0, f + 2), slice(0, 1), ha[f, :1])
        _put(xk, (0, f + 2), slice(h + 1, h + 2), ha[f, 1:])
        a = tail[f * h : (f + 1) * h]
        b = tail[2 * h + 2 * f : 2 * h + 2 * f + 2]
        a = jnp.where(on, a, jnp.zeros_like(a))
        b = jnp.where(on, b, jnp.zeros_like(b))
        _put(xk, (0, f), slice(1, 1 + h), a)
        _put(xk, (0, f), slice(0, 1), b[:1])
        _put(xk, (0, f), slice(h + 1, h + 2), b[1:])
    filled = sc[0] > 0
    gout = jnp.where(filled, co[0], jnp.zeros_like(co[0])).reshape(h * w, c)
    lat, g, hidden = _activate(_conv_bias(xk, w_ref, cb, h), gout, sw, sb)
    lat_ref[...] = jnp.where(filled, lat, jnp.zeros_like(lat)).astype(BF).reshape(h, w, c)
    g_ref[...] = g
    n9 = 9 * c

    def add(kind, value):
        if kind < 3:
            rows = slice(kind * n9, (kind + 1) * n9)
        elif kind == 3:
            rows = slice(3 * n9, 3 * n9 + 2 * c)
        else:
            at = 3 * n9 + 2 * c + (kind - 4)
            rows = slice(at, at + 1)
        acc[rows] = early[rows] + value

    tail_rows = slice(3 * n9 + 2 * c, acc.shape[0])
    acc[tail_rows] = early[tail_rows]

    @pl.when(sc[0] >= 0)
    def _():
        _weight_grads(xk, g, hidden, gout, h, add)

        half = keep.shape[0]
        core = sc[sc.shape[0] - 1]
        send[...] = acc[pl.ds(pl.multiple_of((1 - core) * half, 16), half)].astype(BF)
        keep[...] = acc[pl.ds(pl.multiple_of(core * half, 16), half)]


def _carried_kernel(sc, g_ref, w_ref, out, xk):
    _, _, _, h, w, c = xk.shape
    h = h - 2
    on = sc[1] == 0
    for t in range(2):
        for kw in range(3):
            xk[kw, 0, t, 0:1] = jnp.zeros((1, w, c), BF)
            xk[kw, 0, t, h + 1 : h + 2] = jnp.zeros((1, w, c), BF)
        v = g_ref[:, t * c : (t + 1) * c].reshape(h, w, c)
        _put(xk, (0, t), slice(1, 1 + h), jnp.where(on, v, jnp.zeros_like(v)))
    back = _conv_back(xk, w_ref, h, (2, 3), 2)
    back = jnp.where(sc[0] > 0, back, jnp.full_like(back, EMPTY_GRAD)).astype(BF)
    for t in range(2):
        out[t * h * w : (t + 1) * h * w] = back[:, t * c : (t + 1) * c]


def _back_kernel(sc, g0, g1, w_ref, out_ref, xk):
    slots, _, h, w, c = out_ref.shape
    m = h * w
    zero = jnp.zeros((1, w, c), BF)
    for kw in range(3):
        for j in range(4):
            for s in range(slots):
                xk[kw, s, j, 0:1] = zero
                xk[kw, s, j, h + 1 : h + 2] = zero
    for f in range(2):
        for kw in range(3):
            xk[kw, slots - 1, f + 2, 1 : 1 + h] = jnp.zeros((h, w, c), BF)
        lanes = slice(f * c, (f + 1) * c)
        for s in range(slots):
            v = g0[:, lanes] if s == 0 else g1[(s - 1) * m : s * m, lanes]
            v = v.reshape(h, w, c)
            _put(xk, (s, f), slice(1, 1 + h), v)
            if s > 0:
                on = sc[1 + s] == 0
                _put(xk, (s - 1, f + 2), slice(1, 1 + h), jnp.where(on, v, jnp.zeros_like(v)))
    out = _conv_back(xk, w_ref, h)
    for f in range(2):
        out_ref[:, f] = out[:, f * c : (f + 1) * c].reshape(slots, h, w, c)


def _first_live(a, b):
    return jnp.where(a.astype(F32) < EMPTY_GRAD / 2, a, b)


def _place(sc):
    chip, core = sc[sc.shape[0] - 2], sc[sc.shape[0] - 1]
    return lax.shift_right_logical(chip, 1), lax.bitwise_and(chip, 1), core


def _across_x_kernel(sc, keep, got, send_far, send_near, kept):
    z, x, _ = _place(sc)
    half = keep.shape[0]
    blocks = 4
    rows = half // (2 * blocks)

    def piece(j, side):
        p = 2 * lax.bitwise_xor(z, j) + side
        at = pl.ds(pl.multiple_of(p * rows, 16), rows)
        return keep[at] + got[at].astype(F32)

    for j in range(blocks):
        kept[j * rows : (j + 1) * rows] = piece(j, x)
        send, i = (send_near, j) if j < 2 else (send_far, j - 2)
        send[i * rows : (i + 1) * rows] = piece(j, 1 - x).astype(BF)


def _tail_kernel(sc, fr, ha, out):
    h2 = fr.shape[1] * fr.shape[2]
    live = sc[0] > 0
    for ref, rows in ((fr, slice(0, h2)), (ha, slice(h2, out.shape[0]))):
        v = ref[...].reshape(rows.stop - rows.start, *out.shape[1:])
        out[rows] = jnp.where(live, v, jnp.full_like(v, EMPTY_FRAME))


def _final_kernel(sc, mine, other, got, grad, cw, sw, cb, sb, fg, acc):
    c = mine.shape[1]
    half = acc.shape[0] // 2
    z, x, core = _place(sc)
    blocks = 4
    rows = half // (2 * blocks)
    for ref, at_core in ((mine, core), (other, 1 - core)):
        for k in range(2 * blocks):
            side = x if k < blocks else 1 - x
            chip = 2 * lax.bitwise_xor(z, k % blocks) + side
            at = pl.multiple_of(at_core * half + chip * rows, 16)
            acc[pl.ds(at, rows)] = ref[k * rows : (k + 1) * rows].astype(F32)
    n27, n29 = 27 * c, 29 * c
    cw[...] = acc[:n27]
    sw[...] = acc[n27:n29]
    cb[...] = acc[n29 : n29 + 1]
    sb[...] = acc[n29 + 1 : n29 + 2]
    slots, frames, h, w, _ = grad.shape
    part = mine.shape[0] - half
    for s in range(slots):
        here = sc[0] - 1 == s
        for f in range(frames):
            low = f == 0
            a, b = mine[half:].astype(F32), other[half:].astype(F32)
            beyond = jnp.where(core == 0, a, b) if low else jnp.where(core == 0, b, a)
            beside = got[f * part : (f + 1) * part].astype(F32)
            came = jnp.where(core == 0, _first_live(beside, beyond), beyond)
            came = jnp.where(came < EMPTY_GRAD / 2, came, jnp.zeros_like(came)).reshape(h, w, c)
            fg[s, f] = (grad[s, f] + jnp.where(here, came, jnp.zeros_like(came))).astype(BF)


def _xor(x, k, n, axis):
    return lax.ppermute(x, axis, [(i, i ^ k) for i in range(n)])


def _latest_before(x, empty, axis, n, beside_x, beside_near, beside_far):
    index = lax.axis_index(axis)
    core, pair = index & 1, (index >> 1) & 1

    def newest(early, late):
        return jnp.where(late > empty / 2, early, late)

    def half(v):
        rows = v.shape[0] // 2
        return jnp.where(core == 0, v[:rows], v[rows:])

    other = _xor(x, 1, n, axis)
    a, b = half(x), half(other)
    chip = jnp.where(core == 0, newest(a, b), newest(b, a))
    beside = _xor(chip, 2, n, axis)
    quad = jnp.where(pair == 0, newest(chip, beside), newest(beside, chip))
    quad = beside_x(chip, quad)
    block, before, k = quad, jnp.full_like(quad, empty), 4
    while k < n:
        late = (index & k) > 0
        came = _xor(block, k, n, axis)
        if k == 4:
            came = beside_near(block, came)
        before = jnp.where(late, newest(came, before), before)
        if k == 8:
            before = beside_far(block, before)
        if 2 * k < n:
            block = jnp.where(late, newest(came, block), newest(block, came))
        k *= 2
    before = jnp.where(pair == 0, before, newest(before, beside))
    across = _xor(before, 1, n, axis)
    before = jnp.concatenate(
        [jnp.where(core == 0, before, across), jnp.where(core == 0, across, before)], axis=0
    )
    before = jnp.where(core == 0, before, newest(before, other))
    return jnp.where(before > empty / 2, jnp.zeros_like(before), before)


def _after(value, *earlier):
    return lax.optimization_barrier((value, *earlier))[0]


def body(
    n,
    frames,
    row_halo,
    clip_start,
    slab_counts,
    conv_weight,
    conv_bias,
    stride_weight,
    stride_bias,
    cotangent,
):
    axis = "tm"
    slots, _, h, w, c = frames.shape
    count = slab_counts[0]
    index = lax.axis_index(axis)
    chips = 8
    assert n % (2 * chips) == 0
    sc = jnp.concatenate(
        [
            slab_counts,
            clip_start,
            ((index >> 1) & (chips - 1)).reshape(1).astype(jnp.int32),
            (index & 1).reshape(1).astype(jnp.int32),
        ]
    )
    wt = conv_weight.reshape(27, c, c)
    cb, sb = conv_bias.reshape(1, c), stride_bias.reshape(1, c)
    unit = 16 * 2 * chips
    rows = -(-(29 * c + 2) // unit) * unit
    m = h * w
    conv_flops = 2 * m * 36 * c * 2 * c

    def newest_slot(i, sc):
        return (jnp.maximum(sc[0] - 1, 0), 0, 0, 0, 0)

    tail = pl.pallas_call(
        _tail_kernel,
        out_shape=jax.ShapeDtypeStruct((2 * h + 4, w, c), BF),
        grid_spec=pltpu.PrefetchScalarGridSpec(
            num_scalar_prefetch=1,
            grid=(1,),
            in_specs=[
                pl.BlockSpec((1, 2, h, w, c), newest_slot),
                pl.BlockSpec((1, 2, 2, w, c), newest_slot),
            ],
            out_specs=pl.BlockSpec((2 * h + 4, w, c), lambda i, sc: (0, 0, 0)),
        ),
        compiler_params=pltpu.CompilerParams(vmem_limit_bytes=8 << 20),
    )(
        slab_counts,
        *(pltpu.with_memory_space_constraint(v, pltpu.HBM) for v in (frames, row_halo)),
    )

    held = {}
    wide = ((slots - 1) * m, 2 * c)
    raw = [
        pltpu.with_memory_space_constraint(v, pltpu.HBM)
        for v in (frames, row_halo, cotangent, wt, cb, stride_weight, sb)
    ]
    windows = (3, slots - 1, 4, h + 2, w, c)

    def early_conv(start, follow):
        held["conv"] = _call(
            _early_conv_kernel,
            [
                jax.ShapeDtypeStruct(wide, F32),
                jax.ShapeDtypeStruct((wide[0], c), BF),
                jax.ShapeDtypeStruct(stride_weight.shape, BF),
                jax.ShapeDtypeStruct(sb.shape, F32),
            ],
            [_SMEM] + [_HBM] * len(raw),
            [pltpu.VMEM(v.shape, v.dtype) for v in raw[:5]]
            + [pltpu.VMEM(windows, BF), pltpu.SemaphoreType.DMA((len(raw),))],
            flops=(slots - 1) * conv_flops,
            moved=4 << 20,
        )(_after(sc, start), *raw)
        return _after(follow, held["conv"][0])

    def early_act(start, follow):
        pre, gout1, sw1, sb1 = held["conv"]
        held["early"] = _call(
            _early_act_kernel,
            [
                jax.ShapeDtypeStruct((slots - 1, h, w, c), BF),
                jax.ShapeDtypeStruct(wide, BF),
                jax.ShapeDtypeStruct(wide, BF),
            ],
            [_SMEM] + [_VMEM] * 4,
            moved=2 << 20,
            room=6,
        )(_after(sc, start), pre, gout1, sw1, sb1)
        return _after(follow, held["early"][1])

    def early_sums(start, follow):
        gout1 = held["conv"][1]
        _, g1, hid1 = held["early"]
        held["sums"] = _call(
            _early_sums_kernel,
            jax.ShapeDtypeStruct((rows, c), F32),
            [_SMEM, _HBM, _HBM] + [_VMEM] * 3,
            [pltpu.VMEM(windows, BF)]
            + [pltpu.VMEM(v.shape, BF) for v in raw[:2]]
            + [pltpu.SemaphoreType.DMA((2,))],
            flops=(slots - 1) * conv_flops,
            moved=4 << 20,
        )(_after(sc, start), raw[0], raw[1], g1, hid1, gout1)
        return _after(follow, held["sums"])

    arrived = _latest_before(tail, EMPTY_FRAME, axis, n, early_conv, early_act, early_sums)
    lat1, g1, _ = held["early"]

    def first(*shape):
        return pl.BlockSpec((1, *shape), lambda i: (0,) * (len(shape) + 1))

    half, carried = rows // 2, 2 * m
    lat0, g0, send, keep = _call(
        _late_kernel,
        [
            jax.ShapeDtypeStruct((h, w, c), BF),
            jax.ShapeDtypeStruct((m, 2 * c), BF),
            jax.ShapeDtypeStruct((half, c), BF),
            jax.ShapeDtypeStruct((half, c), F32),
        ],
        [_SMEM, first(2, h, w, c), first(2, 2, w, c), _VMEM, first(1, h, w, c)] + [_VMEM] * 5,
        [pltpu.VMEM((3, 1, 4, h + 2, w, c), BF), pltpu.VMEM((rows, c), F32)],
        flops=2 * conv_flops,
        moved=6 << 20,
        grid=(1,),
    )(sc, frames, row_halo, arrived, cotangent, wt, cb, stride_weight, sb, held["sums"])

    blocks = chips // 2
    piece = half // chips
    got = _xor(send, 1, n, axis)
    first_grad = _call(
        _carried_kernel,
        jax.ShapeDtypeStruct((carried, c), BF),
        [_SMEM, _VMEM, _VMEM],
        [pltpu.VMEM((3, 1, 2, h + 2, w, c), BF)],
        flops=conv_flops // 2,
        moved=1 << 20,
        room=8,
    )(sc, g0, wt)
    keep = _after(keep, first_grad)
    send_far, send_near, kept = _call(
        _across_x_kernel,
        [
            jax.ShapeDtypeStruct((2 * piece, c), BF),
            jax.ShapeDtypeStruct((2 * piece, c), BF),
            jax.ShapeDtypeStruct((blocks * piece, c), F32),
        ],
        [_SMEM] + [_VMEM] * 2,
        room=8,
    )(sc, keep, got)
    got_far = _xor(send_far, 2, n, axis)
    got_near = _xor(send_near, 2, n, axis)
    got_first = _xor(_after(first_grad, kept), 1, n, axis)
    core, pair = index & 1, (index >> 1) & 1

    def by(bit, a, b):
        return jnp.where(bit == 0, a, b)

    def by_half(bit, v):
        rows = v.shape[0] // 2
        return by(bit, v[:rows], v[rows:])

    def ordered(bit, ours, theirs):
        return by(bit, _first_live(ours, theirs), _first_live(theirs, ours))

    chip_first = ordered(core, by_half(core, first_grad), by_half(core, got_first))
    beside_first = _xor(chip_first, 2, n, axis)

    def summed(j, came):
        i = j % 2
        return kept[j * piece : (j + 1) * piece] + came[i * piece : (i + 1) * piece].astype(F32)

    outs = {j: summed(j, got_far).astype(BF) for j in (3, 2)}
    got_near = _after(got_near, outs[3], outs[2])
    outs[1] = summed(1, got_near).astype(BF)
    gots = {j: _xor(outs[j], 4 * j, n, axis) for j in (3, 2, 1)}
    beside_first = _after(beside_first, outs[1])
    lead = ordered(pair, by_half(pair, chip_first), by_half(pair, beside_first))
    grad = _call(
        _back_kernel,
        jax.ShapeDtypeStruct((slots, 2, h, w, c), F32),
        [_SMEM] + [_VMEM] * 3,
        [pltpu.VMEM((3, slots, 4, h + 2, w, c), BF)],
        flops=1,
        moved=1,
        room=24,
    )(_after(sc, outs[1], lead), g0, g1, wt)
    mine = summed(0, _after(got_near, grad))
    for j in (3, 2):
        mine = mine + gots[j].astype(F32)
    gots[1] = _after(gots[1], mine)
    mine = (mine + gots[1].astype(F32)).astype(BF)
    k = 2 * chips
    while k < n:
        mine = (mine.astype(F32) + _xor(mine, k, n, axis).astype(F32)).astype(BF)
        k *= 2
    others = {j: _xor(mine, 4 * j, n, axis) for j in (3, 2, 1)}
    x_own = _xor(mine, 2, n, axis)
    x_near = _xor(others[1], 2, n, axis)
    x_far = _xor(jnp.concatenate([others[2], others[3]], axis=0), 2, n, axis)
    beyond, k = jnp.full_like(lead, EMPTY_GRAD), 4
    while k < n:
        if k == 8:
            lead = _after(lead, others[1])
        came = _xor(lead, k, n, axis)
        beyond = by(index & k, _first_live(beyond, came), beyond)
        if 2 * k < n:
            lead = ordered(index & k, lead, came)
        k *= 2
    theirs = _xor(beyond, 2, n, axis)
    beyond = jnp.concatenate([by(pair, beyond, theirs), by(pair, theirs, beyond)], axis=0)
    beyond = by(pair, _first_live(beside_first, beyond), beyond)
    ours = jnp.concatenate(
        [mine, others[1], others[2], others[3], x_own, x_near, x_far, beyond], axis=0
    )
    other = _xor(ours, 1, n, axis)
    cwg, swg, cbg, sbg, frames_grad = _call(
        _final_kernel,
        [
            jax.ShapeDtypeStruct((27 * c, c), F32),
            jax.ShapeDtypeStruct((2 * c, c), F32),
            jax.ShapeDtypeStruct((1, c), F32),
            jax.ShapeDtypeStruct((1, c), F32),
            jax.ShapeDtypeStruct((slots, 2, h, w, c), BF),
        ],
        [_SMEM] + [_VMEM] * 4,
        [pltpu.VMEM((rows, c), F32)],
        room=12,
    )(sc, ours, other, got_first, grad)
    latents = jnp.concatenate([lat0[None], lat1], axis=0)[:, None]
    return (
        latents,
        frames_grad,
        cwg.reshape(3, 3, 3, c, c),
        cbg[0],
        swg.reshape(2, c, c),
        sbg[0],
    )


def solution(mesh):
    split = P(("groups", "tm"))
    return jax.shard_map(
        functools.partial(body, mesh.shape["tm"]),
        mesh=mesh,
        in_specs=(split, split, split, split, P(), P(), P(), P(), split),
        out_specs=(split, split, P("groups"), P("groups"), P("groups"), P("groups")),
        check_vma=False,
    )
```

```python
import functools

import jax
import jax.numpy as jnp
from jax import lax
from jax.experimental import pallas as pl
from jax.experimental.pallas import tpu as pltpu
from jax.sharding import PartitionSpec as P

BF = jnp.bfloat16
F32 = jnp.float32
EMPTY_FRAME = 100.0
EMPTY_GRAD = 1e30

_VMEM = pl.BlockSpec(memory_space=pltpu.VMEM)
_SMEM = pl.BlockSpec(memory_space=pltpu.SMEM)
_HBM = pl.BlockSpec(memory_space=pltpu.HBM)


def _call(kernel, out_shape, in_specs, scratch=(), flops=0, moved=0, room=16, grid=()):
    return pl.pallas_call(
        kernel,
        out_shape=out_shape,
        grid=grid,
        in_specs=in_specs,
        out_specs=jax.tree.map(lambda _: _VMEM, out_shape),
        scratch_shapes=list(scratch),
        compiler_params=pltpu.CompilerParams(vmem_limit_bytes=room << 20),
        cost_estimate=pl.CostEstimate(flops=flops, bytes_accessed=moved, transcendentals=0),
    )


def _put(xk, at, rows, value):
    n, w, c = value.shape
    flat = value.astype(F32).reshape(n * w, c)
    col = lax.broadcasted_iota(jnp.int32, (n * w, c), 0) % w
    right = jnp.where(col == 0, 0.0, pltpu.roll(flat, 1, 0))
    left = jnp.where(col == w - 1, 0.0, pltpu.roll(flat, n * w - 1, 0))
    for kw, shifted in enumerate((right, flat, left)):
        xk[(kw, *at, rows)] = shifted.astype(BF).reshape(n, w, c)


def _window(xk, kw, j, kh, h):
    v = xk[kw, :, j, kh : kh + h]
    return v.reshape(v.shape[0] * v.shape[1] * v.shape[2], v.shape[3])


def _wide(xk, j, h):
    return jnp.concatenate(
        [_window(xk, kw, j, kh, h) for kh in range(3) for kw in range(3)], axis=1
    )


def _conv(xk, w_ref, h):
    c = w_ref.shape[-1]
    zero = jnp.zeros((c, c), BF)
    lhs = jnp.concatenate([_wide(xk, j, h) for j in range(4)], axis=1)
    rhs = []
    for j in range(4):
        for tap in range(9):
            rhs.append(
                jnp.concatenate(
                    [w_ref[(j - t) * 9 + tap] if 0 <= j - t <= 2 else zero for t in range(2)],
                    axis=1,
                )
            )
    return jnp.dot(lhs, jnp.concatenate(rhs, axis=0), preferred_element_type=F32)


def _conv_back(xk, w_ref, h, frames=range(4), base=0):
    c = w_ref.shape[-1]
    zero = jnp.zeros((c, c), BF)
    lhs = jnp.concatenate([_wide(xk, j - base, h) for j in frames], axis=1)
    rhs = []
    for f in range(2):
        row = []
        for j in frames:
            for tap in range(9):
                kt = 2 - (j - f)
                row.append(w_ref[kt * 9 + 8 - tap] if 0 <= kt <= 2 else zero)
        rhs.append(jnp.concatenate(row, axis=1))
    return lax.dot_general(
        lhs, jnp.concatenate(rhs, axis=0), (((1,), (1,)), ((), ())), preferred_element_type=F32
    )


def _activate(pre, gout, sw_ref, sb_ref):
    s = 1.0 / (1.0 + jnp.exp(-pre))
    hidden = (pre * s).astype(BF)
    sw = jnp.concatenate([sw_ref[0], sw_ref[1]], axis=0)
    lat = jnp.dot(hidden, sw, preferred_element_type=F32) + sb_ref[...]
    gh = lax.dot_general(gout, sw, (((1,), (1,)), ((), ())), preferred_element_type=F32)
    g = (gh * s * (1.0 + pre * (1.0 - s))).astype(BF)
    return lat, g, hidden


def _conv_bias(xk, w_ref, cb_ref, h):
    return _conv(xk, w_ref, h) + jnp.concatenate([cb_ref[...], cb_ref[...]], axis=1)


def _weight_grads(xk, g, hidden, gout, h, add):
    c = gout.shape[-1]
    parts = []
    for j in range(4):
        lhs = _wide(xk, j, h)
        parts.append(
            lax.dot_general(lhs, g, (((0,), (0,)), ((), ())), preferred_element_type=F32)
        )
    for kt in range(3):
        add(kt, parts[kt][:, :c] + parts[kt + 1][:, c:])
    sg = lax.dot_general(hidden, gout, (((0,), (0,)), ((), ())), preferred_element_type=F32)
    g32 = jnp.sum(g.astype(F32), axis=0, keepdims=True)
    add(3, sg)
    add(4, g32[:, :c] + g32[:, c:])
    add(5, jnp.sum(gout.astype(F32), axis=0, keepdims=True))


def _fill_early(sc, fr, ha, xk):
    slots, _, h, w, c = fr.shape
    for s in range(slots):
        for f in range(2):
            spots = [(s - 1, f + 2, None)] if s > 0 else []
            if s + 1 < slots:
                spots.append((s, f, sc[1 + s + 1] == 0))
            for slot, j, keep in spots:
                a, b = fr[s, f], ha[s, f]
                if keep is not None:
                    a = jnp.where(keep, a, jnp.zeros_like(a))
                    b = jnp.where(keep, b, jnp.zeros_like(b))
                _put(xk, (slot, j), slice(1, 1 + h), a)
                _put(xk, (slot, j), slice(0, 1), b[:1])
                _put(xk, (slot, j), slice(h + 1, h + 2), b[1:])


def _early_gout(sc, co):
    slots, _, h, w, c = co.shape
    return jnp.concatenate(
        [
            jnp.where(s < sc[0], co[s, 0], jnp.zeros_like(co[s, 0])).reshape(h * w, c)
            for s in range(1, slots)
        ],
        axis=0,
    )


def _early_conv_kernel(
    sc, frh, hah, coh, wh, cbh, swh, sbh, pre_ref, gout_ref, sw, sb, fr, ha, co, w_ref, cb, xk, sems
):
    h = fr.shape[2]
    pairs = ((frh, fr), (hah, ha), (coh, co), (wh, w_ref), (cbh, cb), (swh, sw), (sbh, sb))
    copies = [pltpu.make_async_copy(a, b, sems.at[i]) for i, (a, b) in enumerate(pairs)]
    for copy in copies:
        copy.start()
    copies[0].wait()
    copies[1].wait()
    _fill_early(sc, fr, ha, xk)
    copies[2].wait()
    gout_ref[...] = _early_gout(sc, co)
    for copy in copies[3:]:
        copy.wait()
    pre_ref[...] = _conv_bias(xk, w_ref, cb, h)


def _early_act_kernel(sc, pre_ref, gout_ref, sw, sb, lat_ref, g_ref, hid_ref):
    slots, h, w, c = lat_ref.shape
    lat, g, hidden = _activate(pre_ref[...], gout_ref[...], sw, sb)
    for s in range(slots):
        part = lat[s * h * w : (s + 1) * h * w]
        filled = s + 1 < sc[0]
        lat_ref[s] = jnp.where(filled, part, jnp.zeros_like(part)).astype(BF).reshape(h, w, c)
    g_ref[...] = g
    hid_ref[...] = hidden


def _early_sums_kernel(sc, frh, hah, g_ref, hid_ref, gout_ref, acc, xk, fr, ha, sems):
    copies = [
        pltpu.make_async_copy(a, b, sems.at[i]) for i, (a, b) in enumerate(((frh, fr), (hah, ha)))
    ]
    for copy in copies:
        copy.start()
    for copy in copies:
        copy.wait()
    _fill_early(sc, fr, ha, xk)
    _, _, h, _, c = fr.shape
    n9 = 9 * c

    def add(kind, value):
        if kind < 3:
            acc[kind * n9 : (kind + 1) * n9] = value
        elif kind == 3:
            acc[3 * n9 : 3 * n9 + 2 * c] = value
        else:
            at = 3 * n9 + 2 * c + (kind - 4)
            acc[at : at + 1] = value

    acc[3 * n9 + 2 * c :] = jnp.zeros((acc.shape[0] - 3 * n9 - 2 * c, c), F32)
    _weight_grads(xk, g_ref[...], hid_ref[...], gout_ref[...], h, add)


def _late_kernel(
    sc, frs, has, tail, cos, w_ref, cb, sw, sb, early, lat_ref, g_ref, send, keep, xk, acc
):
    fr, ha, co = frs.at[0], has.at[0], cos.at[0]
    _, h, w, c = fr.shape
    on = sc[1] == 0
    for f in range(2):
        _put(xk, (0, f + 2), slice(1, 1 + h), fr[f])
        _put(xk, (0, f + 2), slice(0, 1), ha[f, :1])
        _put(xk, (0, f + 2), slice(h + 1, h + 2), ha[f, 1:])
        a = tail[f * h : (f + 1) * h]
        b = tail[2 * h + 2 * f : 2 * h + 2 * f + 2]
        a = jnp.where(on, a, jnp.zeros_like(a))
        b = jnp.where(on, b, jnp.zeros_like(b))
        _put(xk, (0, f), slice(1, 1 + h), a)
        _put(xk, (0, f), slice(0, 1), b[:1])
        _put(xk, (0, f), slice(h + 1, h + 2), b[1:])
    filled = sc[0] > 0
    gout = jnp.where(filled, co[0], jnp.zeros_like(co[0])).reshape(h * w, c)
    lat, g, hidden = _activate(_conv_bias(xk, w_ref, cb, h), gout, sw, sb)
    lat_ref[...] = jnp.where(filled, lat, jnp.zeros_like(lat)).astype(BF).reshape(h, w, c)
    g_ref[...] = g
    n9 = 9 * c

    def add(kind, value):
        if kind < 3:
            rows = slice(kind * n9, (kind + 1) * n9)
        elif kind == 3:
            rows = slice(3 * n9, 3 * n9 + 2 * c)
        else:
            at = 3 * n9 + 2 * c + (kind - 4)
            rows = slice(at, at + 1)
        acc[rows] = early[rows] + value

    tail_rows = slice(3 * n9 + 2 * c, acc.shape[0])
    acc[tail_rows] = early[tail_rows]

    @pl.when(sc[0] >= 0)
    def _():
        _weight_grads(xk, g, hidden, gout, h, add)

        half = keep.shape[0]
        core = sc[sc.shape[0] - 1]
        send[...] = acc[pl.ds(pl.multiple_of((1 - core) * half, 16), half)].astype(BF)
        keep[...] = acc[pl.ds(pl.multiple_of(core * half, 16), half)]


def _carried_kernel(sc, g_ref, w_ref, out, xk):
    _, _, _, h, w, c = xk.shape
    h = h - 2
    on = sc[1] == 0
    for t in range(2):
        for kw in range(3):
            xk[kw, 0, t, 0:1] = jnp.zeros((1, w, c), BF)
            xk[kw, 0, t, h + 1 : h + 2] = jnp.zeros((1, w, c), BF)
        v = g_ref[:, t * c : (t + 1) * c].reshape(h, w, c)
        _put(xk, (0, t), slice(1, 1 + h), jnp.where(on, v, jnp.zeros_like(v)))
    back = _conv_back(xk, w_ref, h, (2, 3), 2)
    back = jnp.where(sc[0] > 0, back, jnp.full_like(back, EMPTY_GRAD)).astype(BF)
    for t in range(2):
        out[t * h * w : (t + 1) * h * w] = back[:, t * c : (t + 1) * c]


def _back_kernel(sc, g0, g1, w_ref, out_ref, xk):
    slots, _, h, w, c = out_ref.shape
    m = h * w
    zero = jnp.zeros((1, w, c), BF)
    for kw in range(3):
        for j in range(4):
            for s in range(slots):
                xk[kw, s, j, 0:1] = zero
                xk[kw, s, j, h + 1 : h + 2] = zero
    for f in range(2):
        for kw in range(3):
            xk[kw, slots - 1, f + 2, 1 : 1 + h] = jnp.zeros((h, w, c), BF)
        lanes = slice(f * c, (f + 1) * c)
        for s in range(slots):
            v = g0[:, lanes] if s == 0 else g1[(s - 1) * m : s * m, lanes]
            v = v.reshape(h, w, c)
            _put(xk, (s, f), slice(1, 1 + h), v)
            if s > 0:
                on = sc[1 + s] == 0
                _put(xk, (s - 1, f + 2), slice(1, 1 + h), jnp.where(on, v, jnp.zeros_like(v)))
    out = _conv_back(xk, w_ref, h)
    for f in range(2):
        out_ref[:, f] = out[:, f * c : (f + 1) * c].reshape(slots, h, w, c)


def _first_live(a, b):
    return jnp.where(a.astype(F32) < EMPTY_GRAD / 2, a, b)


def _place(sc):
    chip, core = sc[sc.shape[0] - 2], sc[sc.shape[0] - 1]
    return lax.shift_right_logical(chip, 1), lax.bitwise_and(chip, 1), core


def _across_x_kernel(sc, keep, got, send_far, send_near, kept):
    z, x, _ = _place(sc)
    half = keep.shape[0]
    blocks = 4
    rows = half // (2 * blocks)

    def piece(j, side):
        p = 2 * lax.bitwise_xor(z, j) + side
        at = pl.ds(pl.multiple_of(p * rows, 16), rows)
        return keep[at] + got[at].astype(F32)

    for j in range(blocks):
        kept[j * rows : (j + 1) * rows] = piece(j, x)
        send, i = (send_near, j) if j < 2 else (send_far, j - 2)
        send[i * rows : (i + 1) * rows] = piece(j, 1 - x).astype(BF)


def _tail_kernel(sc, fr, ha, out):
    h2 = fr.shape[1] * fr.shape[2]
    live = sc[0] > 0
    for ref, rows in ((fr, slice(0, h2)), (ha, slice(h2, out.shape[0]))):
        v = ref[...].reshape(rows.stop - rows.start, *out.shape[1:])
        out[rows] = jnp.where(live, v, jnp.full_like(v, EMPTY_FRAME))


def _final_kernel(sc, mine, other, got, grad, cw, sw, cb, sb, fg, acc):
    c = mine.shape[1]
    half = acc.shape[0] // 2
    z, x, core = _place(sc)
    blocks = 4
    rows = half // (2 * blocks)
    for ref, at_core in ((mine, core), (other, 1 - core)):
        for k in range(2 * blocks):
            side = x if k < blocks else 1 - x
            chip = 2 * lax.bitwise_xor(z, k % blocks) + side
            at = pl.multiple_of(at_core * half + chip * rows, 16)
            acc[pl.ds(at, rows)] = ref[k * rows : (k + 1) * rows].astype(F32)
    n27, n29 = 27 * c, 29 * c
    cw[...] = acc[:n27]
    sw[...] = acc[n27:n29]
    cb[...] = acc[n29 : n29 + 1]
    sb[...] = acc[n29 + 1 : n29 + 2]
    slots, frames, h, w, _ = grad.shape
    part = mine.shape[0] - half
    for s in range(slots):
        here = sc[0] - 1 == s
        for f in range(frames):
            low = f == 0
            a, b = mine[half:].astype(F32), other[half:].astype(F32)
            beyond = jnp.where(core == 0, a, b) if low else jnp.where(core == 0, b, a)
            beside = got[f * part : (f + 1) * part].astype(F32)
            came = jnp.where(core == 0, _first_live(beside, beyond), beyond)
            came = jnp.where(came < EMPTY_GRAD / 2, came, jnp.zeros_like(came)).reshape(h, w, c)
            fg[s, f] = (grad[s, f] + jnp.where(here, came, jnp.zeros_like(came))).astype(BF)


def _xor(x, k, n, axis):
    return lax.ppermute(x, axis, [(i, i ^ k) for i in range(n)])


def _latest_before(x, empty, axis, n, beside_x, beside_near, beside_far):
    index = lax.axis_index(axis)
    core, pair = index & 1, (index >> 1) & 1

    def newest(early, late):
        return jnp.where(late > empty / 2, early, late)

    def half(v):
        rows = v.shape[0] // 2
        return jnp.where(core == 0, v[:rows], v[rows:])

    other = _xor(x, 1, n, axis)
    a, b = half(x), half(other)
    chip = jnp.where(core == 0, newest(a, b), newest(b, a))
    beside = _xor(chip, 2, n, axis)
    quad = jnp.where(pair == 0, newest(chip, beside), newest(beside, chip))
    quad = beside_x(chip, quad)
    block, before, k = quad, jnp.full_like(quad, empty), 4
    while k < n:
        late = (index & k) > 0
        came = _xor(block, k, n, axis)
        if k == 4:
            came = beside_near(block, came)
        before = jnp.where(late, newest(came, before), before)
        if k == 8:
            before = beside_far(block, before)
        if 2 * k < n:
            block = jnp.where(late, newest(came, block), newest(block, came))
        k *= 2
    before = jnp.where(pair == 0, before, newest(before, beside))
    across = _xor(before, 1, n, axis)
    before = jnp.concatenate(
        [jnp.where(core == 0, before, across), jnp.where(core == 0, across, before)], axis=0
    )
    before = jnp.where(core == 0, before, newest(before, other))
    return jnp.where(before > empty / 2, jnp.zeros_like(before), before)


def _after(value, *earlier):
    return lax.optimization_barrier((value, *earlier))[0]


def body(
    n,
    frames,
    row_halo,
    clip_start,
    slab_counts,
    conv_weight,
    conv_bias,
    stride_weight,
    stride_bias,
    cotangent,
):
    axis = "tm"
    slots, _, h, w, c = frames.shape
    count = slab_counts[0]
    index = lax.axis_index(axis)
    chips = 8
    assert n % (2 * chips) == 0
    sc = jnp.concatenate(
        [
            slab_counts,
            clip_start,
            ((index >> 1) & (chips - 1)).reshape(1).astype(jnp.int32),
            (index & 1).reshape(1).astype(jnp.int32),
        ]
    )
    wt = conv_weight.reshape(27, c, c)
    cb, sb = conv_bias.reshape(1, c), stride_bias.reshape(1, c)
    unit = 16 * 2 * chips
    rows = -(-(29 * c + 2) // unit) * unit
    m = h * w
    conv_flops = 2 * m * 36 * c * 2 * c

    def newest_slot(i, sc):
        return (jnp.maximum(sc[0] - 1, 0), 0, 0, 0, 0)

    tail = pl.pallas_call(
        _tail_kernel,
        out_shape=jax.ShapeDtypeStruct((2 * h + 4, w, c), BF),
        grid_spec=pltpu.PrefetchScalarGridSpec(
            num_scalar_prefetch=1,
            grid=(1,),
            in_specs=[
                pl.BlockSpec((1, 2, h, w, c), newest_slot),
                pl.BlockSpec((1, 2, 2, w, c), newest_slot),
            ],
            out_specs=pl.BlockSpec((2 * h + 4, w, c), lambda i, sc: (0, 0, 0)),
        ),
        compiler_params=pltpu.CompilerParams(vmem_limit_bytes=8 << 20),
    )(
        slab_counts,
        *(pltpu.with_memory_space_constraint(v, pltpu.HBM) for v in (frames, row_halo)),
    )

    held = {}
    wide = ((slots - 1) * m, 2 * c)
    raw = [
        pltpu.with_memory_space_constraint(v, pltpu.HBM)
        for v in (frames, row_halo, cotangent, wt, cb, stride_weight, sb)
    ]
    windows = (3, slots - 1, 4, h + 2, w, c)

    def early_conv(start, follow):
        held["conv"] = _call(
            _early_conv_kernel,
            [
                jax.ShapeDtypeStruct(wide, F32),
                jax.ShapeDtypeStruct((wide[0], c), BF),
                jax.ShapeDtypeStruct(stride_weight.shape, BF),
                jax.ShapeDtypeStruct(sb.shape, F32),
            ],
            [_SMEM] + [_HBM] * len(raw),
            [pltpu.VMEM(v.shape, v.dtype) for v in raw[:5]]
            + [pltpu.VMEM(windows, BF), pltpu.SemaphoreType.DMA((len(raw),))],
            flops=(slots - 1) * conv_flops,
            moved=4 << 20,
        )(_after(sc, start), *raw)
        return _after(follow, held["conv"][0])

    def early_act(start, follow):
        pre, gout1, sw1, sb1 = held["conv"]
        held["early"] = _call(
            _early_act_kernel,
            [
                jax.ShapeDtypeStruct((slots - 1, h, w, c), BF),
                jax.ShapeDtypeStruct(wide, BF),
                jax.ShapeDtypeStruct(wide, BF),
            ],
            [_SMEM] + [_VMEM] * 4,
            moved=2 << 20,
            room=6,
        )(_after(sc, start), pre, gout1, sw1, sb1)
        return _after(follow, held["early"][1])

    def early_sums(start, follow):
        gout1 = held["conv"][1]
        _, g1, hid1 = held["early"]
        held["sums"] = _call(
            _early_sums_kernel,
            jax.ShapeDtypeStruct((rows, c), F32),
            [_SMEM, _HBM, _HBM] + [_VMEM] * 3,
            [pltpu.VMEM(windows, BF)]
            + [pltpu.VMEM(v.shape, BF) for v in raw[:2]]
            + [pltpu.SemaphoreType.DMA((2,))],
            flops=(slots - 1) * conv_flops,
            moved=4 << 20,
        )(_after(sc, start), raw[0], raw[1], g1, hid1, gout1)
        return _after(follow, held["sums"])

    arrived = _latest_before(tail, EMPTY_FRAME, axis, n, early_conv, early_act, early_sums)
    lat1, g1, _ = held["early"]

    def first(*shape):
        return pl.BlockSpec((1, *shape), lambda i: (0,) * (len(shape) + 1))

    half, carried = rows // 2, 2 * m
    lat0, g0, send, keep = _call(
        _late_kernel,
        [
            jax.ShapeDtypeStruct((h, w, c), BF),
            jax.ShapeDtypeStruct((m, 2 * c), BF),
            jax.ShapeDtypeStruct((half, c), BF),
            jax.ShapeDtypeStruct((half, c), F32),
        ],
        [_SMEM, first(2, h, w, c), first(2, 2, w, c), _VMEM, first(1, h, w, c)] + [_VMEM] * 5,
        [pltpu.VMEM((3, 1, 4, h + 2, w, c), BF), pltpu.VMEM((rows, c), F32)],
        flops=2 * conv_flops,
        moved=6 << 20,
        grid=(1,),
    )(sc, frames, row_halo, arrived, cotangent, wt, cb, stride_weight, sb, held["sums"])

    blocks = chips // 2
    piece = half // chips
    got = _xor(send, 1, n, axis)
    first_grad = _call(
        _carried_kernel,
        jax.ShapeDtypeStruct((carried, c), BF),
        [_SMEM, _VMEM, _VMEM],
        [pltpu.VMEM((3, 1, 2, h + 2, w, c), BF)],
        flops=conv_flops // 2,
        moved=1 << 20,
        room=8,
    )(sc, g0, wt)
    keep = _after(keep, first_grad)
    send_far, send_near, kept = _call(
        _across_x_kernel,
        [
            jax.ShapeDtypeStruct((2 * piece, c), BF),
            jax.ShapeDtypeStruct((2 * piece, c), BF),
            jax.ShapeDtypeStruct((blocks * piece, c), F32),
        ],
        [_SMEM] + [_VMEM] * 2,
        room=8,
    )(sc, keep, got)
    got_far = _xor(send_far, 2, n, axis)
    got_near = _xor(send_near, 2, n, axis)
    got_first = _xor(_after(first_grad, kept), 1, n, axis)
    core, pair = index & 1, (index >> 1) & 1

    def by(bit, a, b):
        return jnp.where(bit == 0, a, b)

    def by_half(bit, v):
        rows = v.shape[0] // 2
        return by(bit, v[:rows], v[rows:])

    def ordered(bit, ours, theirs):
        return by(bit, _first_live(ours, theirs), _first_live(theirs, ours))

    chip_first = ordered(core, by_half(core, first_grad), by_half(core, got_first))
    beside_first = _xor(chip_first, 2, n, axis)
    got_far = _after(got_far, chip_first)

    def summed(j, came):
        i = j % 2
        return kept[j * piece : (j + 1) * piece] + came[i * piece : (i + 1) * piece].astype(F32)

    outs = {j: summed(j, got_far).astype(BF) for j in (3, 2)}
    got_near = _after(got_near, outs[3], outs[2])
    outs[1] = summed(1, got_near).astype(BF)
    gots = {j: _xor(outs[j], 4 * j, n, axis) for j in (3, 2, 1)}
    lead = ordered(pair, by_half(pair, chip_first), by_half(pair, beside_first))
    near_lead = _xor(lead, 4, n, axis)
    grad = _call(
        _back_kernel,
        jax.ShapeDtypeStruct((slots, 2, h, w, c), F32),
        [_SMEM] + [_VMEM] * 3,
        [pltpu.VMEM((3, slots, 4, h + 2, w, c), BF)],
        flops=1,
        moved=1,
        room=24,
    )(_after(sc, outs[1]), g0, g1, wt)
    mine = summed(0, _after(got_near, grad))
    for j in (3, 2):
        mine = mine + gots[j].astype(F32)
    gots[1] = _after(gots[1], mine)
    mine = (mine + gots[1].astype(F32)).astype(BF)
    k = 2 * chips
    while k < n:
        mine = (mine.astype(F32) + _xor(mine, k, n, axis).astype(F32)).astype(BF)
        k *= 2
    others = {j: _xor(mine, 4 * j, n, axis) for j in (3, 2, 1)}
    x_own = _xor(mine, 2, n, axis)
    x_near = _xor(others[1], 2, n, axis)
    x_far = _xor(jnp.concatenate([others[2], others[3]], axis=0), 2, n, axis)
    beyond = by(index & 4, near_lead, jnp.full_like(lead, EMPTY_GRAD))
    lead, k = _after(ordered(index & 4, lead, near_lead), mine), 8
    while k < n:
        came = _xor(lead, k, n, axis)
        beyond = by(index & k, _first_live(beyond, came), beyond)
        if 2 * k < n:
            lead = ordered(index & k, lead, came)
        k *= 2
    theirs = _xor(beyond, 2, n, axis)
    beyond = jnp.concatenate([by(pair, beyond, theirs), by(pair, theirs, beyond)], axis=0)
    beyond = by(pair, _first_live(beside_first, beyond), beyond)
    ours = jnp.concatenate(
        [mine, others[1], others[2], others[3], x_own, x_near, x_far, beyond], axis=0
    )
    other = _xor(ours, 1, n, axis)
    cwg, swg, cbg, sbg, frames_grad = _call(
        _final_kernel,
        [
            jax.ShapeDtypeStruct((27 * c, c), F32),
            jax.ShapeDtypeStruct((2 * c, c), F32),
            jax.ShapeDtypeStruct((1, c), F32),
            jax.ShapeDtypeStruct((1, c), F32),
            jax.ShapeDtypeStruct((slots, 2, h, w, c), BF),
        ],
        [_SMEM] + [_VMEM] * 4,
        [pltpu.VMEM((rows, c), F32)],
        room=12,
    )(sc, ours, other, got_first, grad)
    latents = jnp.concatenate([lat0[None], lat1], axis=0)[:, None]
    return (
        latents,
        frames_grad,
        cwg.reshape(3, 3, 3, c, c),
        cbg[0],
        swg.reshape(2, c, c),
        sbg[0],
    )


def solution(mesh):
    split = P(("groups", "tm"))
    return jax.shard_map(
        functools.partial(body, mesh.shape["tm"]),
        mesh=mesh,
        in_specs=(split, split, split, split, P(), P(), P(), P(), split),
        out_specs=(split, split, P("groups"), P("groups"), P("groups"), P("groups")),
        check_vma=False,
    )
```

```python
import functools

import jax
import jax.numpy as jnp
from jax import lax
from jax.experimental import pallas as pl
from jax.experimental.pallas import tpu as pltpu
from jax.sharding import PartitionSpec as P

BF = jnp.bfloat16
F32 = jnp.float32
EMPTY_FRAME = 100.0
EMPTY_GRAD = 1e30

_VMEM = pl.BlockSpec(memory_space=pltpu.VMEM)
_SMEM = pl.BlockSpec(memory_space=pltpu.SMEM)
_HBM = pl.BlockSpec(memory_space=pltpu.HBM)


def _call(kernel, out_shape, in_specs, scratch=(), flops=0, moved=0, room=16, grid=(), outs=None, alias=None):
    return pl.pallas_call(
        kernel,
        out_shape=out_shape,
        grid=grid,
        in_specs=in_specs,
        out_specs=jax.tree.map(lambda _: _VMEM, out_shape) if outs is None else outs,
        input_output_aliases=alias or {},
        scratch_shapes=list(scratch),
        compiler_params=pltpu.CompilerParams(vmem_limit_bytes=room << 20),
        cost_estimate=pl.CostEstimate(flops=flops, bytes_accessed=moved, transcendentals=0),
    )


def _put(xk, at, rows, value):
    n, w, c = value.shape
    flat = value.astype(F32).reshape(n * w, c)
    col = lax.broadcasted_iota(jnp.int32, (n * w, c), 0) % w
    right = jnp.where(col == 0, 0.0, pltpu.roll(flat, 1, 0))
    left = jnp.where(col == w - 1, 0.0, pltpu.roll(flat, n * w - 1, 0))
    for kw, shifted in enumerate((right, flat, left)):
        xk[(kw, *at, rows)] = shifted.astype(BF).reshape(n, w, c)


def _window(xk, kw, j, kh, h):
    v = xk[kw, :, j, kh : kh + h]
    return v.reshape(v.shape[0] * v.shape[1] * v.shape[2], v.shape[3])


def _wide(xk, j, h):
    return jnp.concatenate(
        [_window(xk, kw, j, kh, h) for kh in range(3) for kw in range(3)], axis=1
    )


def _conv(xk, w_ref, h):
    c = w_ref.shape[-1]
    zero = jnp.zeros((c, c), BF)
    lhs = jnp.concatenate([_wide(xk, j, h) for j in range(4)], axis=1)
    rhs = []
    for j in range(4):
        for tap in range(9):
            rhs.append(
                jnp.concatenate(
                    [w_ref[(j - t) * 9 + tap] if 0 <= j - t <= 2 else zero for t in range(2)],
                    axis=1,
                )
            )
    return jnp.dot(lhs, jnp.concatenate(rhs, axis=0), preferred_element_type=F32)


def _conv_back(xk, w_ref, h, frames=range(4), base=0):
    c = w_ref.shape[-1]
    zero = jnp.zeros((c, c), BF)
    lhs = jnp.concatenate([_wide(xk, j - base, h) for j in frames], axis=1)
    rhs = []
    for f in range(2):
        row = []
        for j in frames:
            for tap in range(9):
                kt = 2 - (j - f)
                row.append(w_ref[kt * 9 + 8 - tap] if 0 <= kt <= 2 else zero)
        rhs.append(jnp.concatenate(row, axis=1))
    return lax.dot_general(
        lhs, jnp.concatenate(rhs, axis=0), (((1,), (1,)), ((), ())), preferred_element_type=F32
    )


def _activate(pre, gout, sw_ref, sb_ref):
    s = 1.0 / (1.0 + jnp.exp(-pre))
    hidden = (pre * s).astype(BF)
    sw = jnp.concatenate([sw_ref[0], sw_ref[1]], axis=0)
    lat = jnp.dot(hidden, sw, preferred_element_type=F32) + sb_ref[...]
    gh = lax.dot_general(gout, sw, (((1,), (1,)), ((), ())), preferred_element_type=F32)
    g = (gh * s * (1.0 + pre * (1.0 - s))).astype(BF)
    return lat, g, hidden


def _conv_bias(xk, w_ref, cb_ref, h):
    return _conv(xk, w_ref, h) + jnp.concatenate([cb_ref[...], cb_ref[...]], axis=1)


def _weight_grads(xk, g, hidden, gout, h, add):
    c = gout.shape[-1]
    parts = []
    for j in range(4):
        lhs = _wide(xk, j, h)
        parts.append(
            lax.dot_general(lhs, g, (((0,), (0,)), ((), ())), preferred_element_type=F32)
        )
    for kt in range(3):
        add(kt, parts[kt][:, :c] + parts[kt + 1][:, c:])
    sg = lax.dot_general(hidden, gout, (((0,), (0,)), ((), ())), preferred_element_type=F32)
    g32 = jnp.sum(g.astype(F32), axis=0, keepdims=True)
    add(3, sg)
    add(4, g32[:, :c] + g32[:, c:])
    add(5, jnp.sum(gout.astype(F32), axis=0, keepdims=True))


def _fill_early(sc, fr, ha, xk):
    slots, _, h, w, c = fr.shape
    for s in range(slots):
        for f in range(2):
            spots = [(s - 1, f + 2, None)] if s > 0 else []
            if s + 1 < slots:
                spots.append((s, f, sc[1 + s + 1] == 0))
            for slot, j, keep in spots:
                a, b = fr[s, f], ha[s, f]
                if keep is not None:
                    a = jnp.where(keep, a, jnp.zeros_like(a))
                    b = jnp.where(keep, b, jnp.zeros_like(b))
                _put(xk, (slot, j), slice(1, 1 + h), a)
                _put(xk, (slot, j), slice(0, 1), b[:1])
                _put(xk, (slot, j), slice(h + 1, h + 2), b[1:])


def _early_gout(sc, co):
    slots, _, h, w, c = co.shape
    return jnp.concatenate(
        [
            jnp.where(s < sc[0], co[s, 0], jnp.zeros_like(co[s, 0])).reshape(h * w, c)
            for s in range(1, slots)
        ],
        axis=0,
    )


def _early_conv_kernel(
    sc, frh, hah, coh, wh, cbh, swh, sbh, pre_ref, gout_ref, sw, sb, fr, ha, co, w_ref, cb, xk, sems
):
    h = fr.shape[2]
    pairs = ((frh, fr), (hah, ha), (coh, co), (wh, w_ref), (cbh, cb), (swh, sw), (sbh, sb))
    copies = [pltpu.make_async_copy(a, b, sems.at[i]) for i, (a, b) in enumerate(pairs)]
    for copy in copies:
        copy.start()
    copies[0].wait()
    copies[1].wait()
    _fill_early(sc, fr, ha, xk)
    copies[2].wait()
    gout_ref[...] = _early_gout(sc, co)
    for copy in copies[3:]:
        copy.wait()
    pre_ref[...] = _conv_bias(xk, w_ref, cb, h)


def _early_act_kernel(sc, pre_ref, gout_ref, sw, sb, lat_ref, g_ref, hid_ref):
    slots, h, w, c = lat_ref.shape
    lat, g, hidden = _activate(pre_ref[...], gout_ref[...], sw, sb)
    for s in range(slots):
        part = lat[s * h * w : (s + 1) * h * w]
        filled = s + 1 < sc[0]
        lat_ref[s] = jnp.where(filled, part, jnp.zeros_like(part)).astype(BF).reshape(h, w, c)
    g_ref[...] = g
    hid_ref[...] = hidden


def _early_sums_kernel(sc, frh, hah, g_ref, hid_ref, gout_ref, acc, xk, fr, ha, sems):
    copies = [
        pltpu.make_async_copy(a, b, sems.at[i]) for i, (a, b) in enumerate(((frh, fr), (hah, ha)))
    ]
    for copy in copies:
        copy.start()
    for copy in copies:
        copy.wait()
    _fill_early(sc, fr, ha, xk)
    _, _, h, _, c = fr.shape
    n9 = 9 * c

    def add(kind, value):
        if kind < 3:
            acc[kind * n9 : (kind + 1) * n9] = value
        elif kind == 3:
            acc[3 * n9 : 3 * n9 + 2 * c] = value
        else:
            at = 3 * n9 + 2 * c + (kind - 4)
            acc[at : at + 1] = value

    acc[3 * n9 + 2 * c :] = jnp.zeros((acc.shape[0] - 3 * n9 - 2 * c, c), F32)
    _weight_grads(xk, g_ref[...], hid_ref[...], gout_ref[...], h, add)


def _late_kernel(
    sc, frs, has, tail, cos, w_ref, cb, sw, sb, early, lat_ref, g_ref, send, keep, xk, acc
):
    fr, ha, co = frs.at[0], has.at[0], cos.at[0]
    _, h, w, c = fr.shape
    on = sc[1] == 0
    for f in range(2):
        _put(xk, (0, f + 2), slice(1, 1 + h), fr[f])
        _put(xk, (0, f + 2), slice(0, 1), ha[f, :1])
        _put(xk, (0, f + 2), slice(h + 1, h + 2), ha[f, 1:])
        a = tail[f * h : (f + 1) * h]
        b = tail[2 * h + 2 * f : 2 * h + 2 * f + 2]
        a = jnp.where(on, a, jnp.zeros_like(a))
        b = jnp.where(on, b, jnp.zeros_like(b))
        _put(xk, (0, f), slice(1, 1 + h), a)
        _put(xk, (0, f), slice(0, 1), b[:1])
        _put(xk, (0, f), slice(h + 1, h + 2), b[1:])
    filled = sc[0] > 0
    gout = jnp.where(filled, co[0], jnp.zeros_like(co[0])).reshape(h * w, c)
    lat, g, hidden = _activate(_conv_bias(xk, w_ref, cb, h), gout, sw, sb)
    lat_ref[...] = jnp.where(filled, lat, jnp.zeros_like(lat)).astype(BF).reshape(h, w, c)
    g_ref[...] = g
    n9 = 9 * c

    def add(kind, value):
        if kind < 3:
            rows = slice(kind * n9, (kind + 1) * n9)
        elif kind == 3:
            rows = slice(3 * n9, 3 * n9 + 2 * c)
        else:
            at = 3 * n9 + 2 * c + (kind - 4)
            rows = slice(at, at + 1)
        acc[rows] = early[rows] + value

    tail_rows = slice(3 * n9 + 2 * c, acc.shape[0])
    acc[tail_rows] = early[tail_rows]

    @pl.when(sc[0] >= 0)
    def _():
        _weight_grads(xk, g, hidden, gout, h, add)

        half = keep.shape[0]
        core = sc[sc.shape[0] - 1]
        send[...] = acc[pl.ds(pl.multiple_of((1 - core) * half, 16), half)].astype(BF)
        keep[...] = acc[pl.ds(pl.multiple_of(core * half, 16), half)]


def _carried_kernel(sc, g_ref, w_ref, out, xk):
    _, _, _, h, w, c = xk.shape
    h = h - 2
    on = sc[1] == 0
    for t in range(2):
        for kw in range(3):
            xk[kw, 0, t, 0:1] = jnp.zeros((1, w, c), BF)
            xk[kw, 0, t, h + 1 : h + 2] = jnp.zeros((1, w, c), BF)
        v = g_ref[:, t * c : (t + 1) * c].reshape(h, w, c)
        _put(xk, (0, t), slice(1, 1 + h), jnp.where(on, v, jnp.zeros_like(v)))
    back = _conv_back(xk, w_ref, h, (2, 3), 2)
    back = jnp.where(sc[0] > 0, back, jnp.full_like(back, EMPTY_GRAD)).astype(BF)
    for t in range(2):
        out[t * h * w : (t + 1) * h * w] = back[:, t * c : (t + 1) * c]


def _back_kernel(sc, g0, g1, w_ref, out_ref, last_ref, xk, all_ref):
    slots, _, h, w, c = out_ref.shape
    m = h * w
    zero = jnp.zeros((1, w, c), BF)
    for kw in range(3):
        for j in range(4):
            for s in range(slots):
                xk[kw, s, j, 0:1] = zero
                xk[kw, s, j, h + 1 : h + 2] = zero
    for f in range(2):
        for kw in range(3):
            xk[kw, slots - 1, f + 2, 1 : 1 + h] = jnp.zeros((h, w, c), BF)
        lanes = slice(f * c, (f + 1) * c)
        for s in range(slots):
            v = g0[:, lanes] if s == 0 else g1[(s - 1) * m : s * m, lanes]
            v = v.reshape(h, w, c)
            _put(xk, (s, f), slice(1, 1 + h), v)
            if s > 0:
                on = sc[1 + s] == 0
                _put(xk, (s - 1, f + 2), slice(1, 1 + h), jnp.where(on, v, jnp.zeros_like(v)))
    out = _conv_back(xk, w_ref, h)
    for f in range(2):
        lanes = slice(f * c, (f + 1) * c)
        out_ref[:, f] = out[:, lanes].astype(BF).reshape(slots, h, w, c)
        all_ref[:, f] = out[:, lanes].reshape(slots, h, w, c)
    last_ref[...] = all_ref[jnp.maximum(sc[0] - 1, 0)]


def _first_live(a, b):
    return jnp.where(a.astype(F32) < EMPTY_GRAD / 2, a, b)


def _place(sc):
    chip, core = sc[sc.shape[0] - 2], sc[sc.shape[0] - 1]
    return lax.shift_right_logical(chip, 1), lax.bitwise_and(chip, 1), core


def _piece(sc, keep, got, j, side):
    blocks = 4
    rows = keep.shape[0] // (2 * blocks)
    p = 2 * lax.bitwise_xor(_place(sc)[0], j) + side
    at = pl.ds(pl.multiple_of(p * rows, 16), rows)
    return keep[at] + got[at].astype(F32)


def _far_kernel(sc, keep, got, send, kept):
    x = _place(sc)[1]
    rows = kept.shape[0] // 2
    for i, j in enumerate((2, 3)):
        kept[i * rows : (i + 1) * rows] = _piece(sc, keep, got, j, x)
        send[i * rows : (i + 1) * rows] = _piece(sc, keep, got, j, 1 - x).astype(BF)


def _near_kernel(sc, keep, got, mine, theirs, send, kept, chip_first):
    _, x, core = _place(sc)
    rows = kept.shape[0] // 2
    for j in (0, 1):
        kept[j * rows : (j + 1) * rows] = _piece(sc, keep, got, j, x)
        send[j * rows : (j + 1) * rows] = _piece(sc, keep, got, j, 1 - x).astype(BF)
    part = mine.shape[0] // 2
    at = pl.ds(pl.multiple_of(core * part, 16), part)
    a, b = mine[at], theirs[at]
    first = jnp.where(core == 0, _first_live(a, b), _first_live(b, a))
    chip_first[...] = first
    send[2 * rows :] = first


def _tail_kernel(sc, fr, ha, out):
    h2 = fr.shape[1] * fr.shape[2]
    live = sc[0] > 0
    for ref, rows in ((fr, slice(0, h2)), (ha, slice(h2, out.shape[0]))):
        v = ref[...].reshape(rows.stop - rows.start, *out.shape[1:])
        out[rows] = jnp.where(live, v, jnp.full_like(v, EMPTY_FRAME))


def _final_kernel(
    sc, mine, other, beside, last, fg_in, cw, sw, cb, sb, fg, acc, newest, sems
):
    del fg_in
    c = mine.shape[1]
    half = acc.shape[0] // 2
    z, x, core = _place(sc)
    blocks = 4
    rows = half // (2 * blocks)
    n27, n29 = 27 * c, 29 * c
    low = [pltpu.make_async_copy(acc.at[:half], cw.at[:half], sems.at[0])]
    high = [
        pltpu.make_async_copy(acc.at[half:n27], cw.at[half:n27], sems.at[1]),
        pltpu.make_async_copy(acc.at[n27:n29], sw, sems.at[2]),
    ]
    for ref, at_core in ((mine, core), (other, 1 - core)):
        for k in range(2 * blocks):
            side = x if k < blocks else 1 - x
            chip = 2 * lax.bitwise_xor(z, k % blocks) + side
            at = pl.multiple_of(at_core * half + chip * rows, 16)
            acc[pl.ds(at, rows)] = ref[k * rows : (k + 1) * rows].astype(F32)

        @pl.when(at_core == 0)
        def _():
            for copy in low:
                copy.start()

        @pl.when(at_core != 0)
        def _():
            for copy in high:
                copy.start()

    frames, h, w, _ = last.shape
    part = mine.shape[0] - half
    for f in range(frames):
        a, b = mine[half:].astype(F32), other[half:].astype(F32)
        beyond = jnp.where(core == 0, a, b) if f == 0 else jnp.where(core == 0, b, a)
        near = beside[f * part : (f + 1) * part].astype(F32)
        came = jnp.where(core == 0, _first_live(near, beyond), beyond)
        came = jnp.where(came < EMPTY_GRAD / 2, came, jnp.zeros_like(came)).reshape(h, w, c)
        came = jnp.where(sc[0] > 0, came, jnp.zeros_like(came))
        newest[f] = (last[f] + came).astype(BF)
    slab = pltpu.make_async_copy(newest, fg.at[jnp.maximum(sc[0] - 1, 0)], sems.at[3])
    slab.start()
    cb[...] = acc[n29 : n29 + 1]
    sb[...] = acc[n29 + 1 : n29 + 2]
    for copy in (*low, *high, slab):
        copy.wait()


def _xor(x, k, n, axis):
    return lax.ppermute(x, axis, [(i, i ^ k) for i in range(n)])


def _latest_before(x, empty, axis, n, beside_x, beside_near, beside_far):
    index = lax.axis_index(axis)
    core, pair = index & 1, (index >> 1) & 1

    def newest(early, late):
        return jnp.where(late > empty / 2, early, late)

    def half(v):
        rows = v.shape[0] // 2
        return jnp.where(core == 0, v[:rows], v[rows:])

    other = _xor(x, 1, n, axis)
    a, b = half(x), half(other)
    chip = jnp.where(core == 0, newest(a, b), newest(b, a))
    beside = _xor(chip, 2, n, axis)
    quad = jnp.where(pair == 0, newest(chip, beside), newest(beside, chip))
    quad = beside_x(chip, quad)
    block, before, k = quad, jnp.full_like(quad, empty), 4
    while k < n:
        late = (index & k) > 0
        came = _xor(block, k, n, axis)
        if k == 4:
            came = beside_near(block, came)
        before = jnp.where(late, newest(came, before), before)
        if k == 8:
            before = beside_far(block, before)
        if 2 * k < n:
            block = jnp.where(late, newest(came, block), newest(block, came))
        k *= 2
    before = jnp.where(pair == 0, before, newest(before, beside))
    across = _xor(before, 1, n, axis)
    before = jnp.concatenate(
        [jnp.where(core == 0, before, across), jnp.where(core == 0, across, before)], axis=0
    )
    before = jnp.where(core == 0, before, newest(before, other))
    return jnp.where(before > empty / 2, jnp.zeros_like(before), before)


def _after(value, *earlier):
    return lax.optimization_barrier((value, *earlier))[0]


def body(
    n,
    frames,
    row_halo,
    clip_start,
    slab_counts,
    conv_weight,
    conv_bias,
    stride_weight,
    stride_bias,
    cotangent,
):
    axis = "tm"
    slots, _, h, w, c = frames.shape
    count = slab_counts[0]
    index = lax.axis_index(axis)
    chips = 8
    assert n % (2 * chips) == 0
    sc = jnp.concatenate(
        [
            slab_counts,
            clip_start,
            ((index >> 1) & (chips - 1)).reshape(1).astype(jnp.int32),
            (index & 1).reshape(1).astype(jnp.int32),
        ]
    )
    wt = conv_weight.reshape(27, c, c)
    cb, sb = conv_bias.reshape(1, c), stride_bias.reshape(1, c)
    unit = 16 * 2 * chips
    rows = -(-(29 * c + 2) // unit) * unit
    m = h * w
    conv_flops = 2 * m * 36 * c * 2 * c

    def newest_slot(i, sc):
        return (jnp.maximum(sc[0] - 1, 0), 0, 0, 0, 0)

    tail = pl.pallas_call(
        _tail_kernel,
        out_shape=jax.ShapeDtypeStruct((2 * h + 4, w, c), BF),
        grid_spec=pltpu.PrefetchScalarGridSpec(
            num_scalar_prefetch=1,
            grid=(1,),
            in_specs=[
                pl.BlockSpec((1, 2, h, w, c), newest_slot),
                pl.BlockSpec((1, 2, 2, w, c), newest_slot),
            ],
            out_specs=pl.BlockSpec((2 * h + 4, w, c), lambda i, sc: (0, 0, 0)),
        ),
        compiler_params=pltpu.CompilerParams(vmem_limit_bytes=8 << 20),
    )(
        slab_counts,
        *(pltpu.with_memory_space_constraint(v, pltpu.HBM) for v in (frames, row_halo)),
    )

    held = {}
    wide = ((slots - 1) * m, 2 * c)
    raw = [
        pltpu.with_memory_space_constraint(v, pltpu.HBM)
        for v in (frames, row_halo, cotangent, wt, cb, stride_weight, sb)
    ]
    windows = (3, slots - 1, 4, h + 2, w, c)

    def early_conv(start, follow):
        held["conv"] = _call(
            _early_conv_kernel,
            [
                jax.ShapeDtypeStruct(wide, F32),
                jax.ShapeDtypeStruct((wide[0], c), BF),
                jax.ShapeDtypeStruct(stride_weight.shape, BF),
                jax.ShapeDtypeStruct(sb.shape, F32),
            ],
            [_SMEM] + [_HBM] * len(raw),
            [pltpu.VMEM(v.shape, v.dtype) for v in raw[:5]]
            + [pltpu.VMEM(windows, BF), pltpu.SemaphoreType.DMA((len(raw),))],
            flops=(slots - 1) * conv_flops,
            moved=4 << 20,
        )(_after(sc, start), *raw)
        return _after(follow, held["conv"][0])

    def early_act(start, follow):
        pre, gout1, sw1, sb1 = held["conv"]
        held["early"] = _call(
            _early_act_kernel,
            [
                jax.ShapeDtypeStruct((slots - 1, h, w, c), BF),
                jax.ShapeDtypeStruct(wide, BF),
                jax.ShapeDtypeStruct(wide, BF),
            ],
            [_SMEM] + [_VMEM] * 4,
            moved=2 << 20,
            room=6,
        )(_after(sc, start), pre, gout1, sw1, sb1)
        return _after(follow, held["early"][1])

    def early_sums(start, follow):
        gout1 = held["conv"][1]
        _, g1, hid1 = held["early"]
        held["sums"] = _call(
            _early_sums_kernel,
            jax.ShapeDtypeStruct((rows, c), F32),
            [_SMEM, _HBM, _HBM] + [_VMEM] * 3,
            [pltpu.VMEM(windows, BF)]
            + [pltpu.VMEM(v.shape, BF) for v in raw[:2]]
            + [pltpu.SemaphoreType.DMA((2,))],
            flops=(slots - 1) * conv_flops,
            moved=4 << 20,
        )(_after(sc, start), raw[0], raw[1], g1, hid1, gout1)
        return _after(follow, held["sums"])

    arrived = _latest_before(tail, EMPTY_FRAME, axis, n, early_conv, early_act, early_sums)
    lat1, g1, _ = held["early"]

    def first(*shape):
        return pl.BlockSpec((1, *shape), lambda i: (0,) * (len(shape) + 1))

    half, carried = rows // 2, 2 * m
    lat0, g0, send, keep = _call(
        _late_kernel,
        [
            jax.ShapeDtypeStruct((h, w, c), BF),
            jax.ShapeDtypeStruct((m, 2 * c), BF),
            jax.ShapeDtypeStruct((half, c), BF),
            jax.ShapeDtypeStruct((half, c), F32),
        ],
        [_SMEM, first(2, h, w, c), first(2, 2, w, c), _VMEM, first(1, h, w, c)] + [_VMEM] * 5,
        [pltpu.VMEM((3, 1, 4, h + 2, w, c), BF), pltpu.VMEM((rows, c), F32)],
        flops=2 * conv_flops,
        moved=6 << 20,
        grid=(1,),
    )(sc, frames, row_halo, arrived, cotangent, wt, cb, stride_weight, sb, held["sums"])

    blocks = chips // 2
    piece = half // chips
    got = _xor(send, 1, n, axis)
    first_grad = _call(
        _carried_kernel,
        jax.ShapeDtypeStruct((carried, c), BF),
        [_SMEM, _VMEM, _VMEM],
        [pltpu.VMEM((3, 1, 2, h + 2, w, c), BF)],
        flops=conv_flops // 2,
        moved=1 << 20,
        room=8,
    )(sc, g0, wt)
    got_first = _xor(first_grad, 1, n, axis)
    pieces = (
        jax.ShapeDtypeStruct((2 * piece, c), BF),
        jax.ShapeDtypeStruct((2 * piece, c), F32),
    )
    send_far, kept_far = _call(_far_kernel, pieces, [_SMEM] + [_VMEM] * 2, room=4)(
        sc, _after(keep, first_grad), got
    )
    got_far = _xor(send_far, 2, n, axis)
    send_near, kept_near, chip_first = _call(
        _near_kernel,
        (
            jax.ShapeDtypeStruct((2 * piece + carried // 2, c), BF),
            pieces[1],
            jax.ShapeDtypeStruct((carried // 2, c), BF),
        ),
        [_SMEM] + [_VMEM] * 4,
        room=4,
    )(sc, _after(keep, kept_far), got, first_grad, got_first)
    got_near = _xor(send_near, 2, n, axis)
    core, pair = index & 1, (index >> 1) & 1

    def by(bit, a, b):
        return jnp.where(bit == 0, a, b)

    def by_half(bit, v):
        rows = v.shape[0] // 2
        return by(bit, v[:rows], v[rows:])

    def ordered(bit, ours, theirs):
        return by(bit, _first_live(ours, theirs), _first_live(theirs, ours))

    def summed(j, came):
        kept = kept_near if j < 2 else kept_far
        rows = slice((j % 2) * piece, (j % 2 + 1) * piece)
        return kept[rows] + came[rows].astype(F32)

    outs = {j: summed(j, got_far).astype(BF) for j in (3, 2)}
    got_near = _after(got_near, outs[3], outs[2])
    outs[1] = summed(1, got_near).astype(BF)
    gots = {j: _xor(outs[j], 4 * j, n, axis) for j in (3, 2, 1)}
    beside_first = got_near[2 * piece :]
    lead = ordered(pair, by_half(pair, chip_first), by_half(pair, beside_first))
    near_lead = _xor(lead, 4, n, axis)
    slabs, last = _call(
        _back_kernel,
        [
            jax.ShapeDtypeStruct((slots, 2, h, w, c), BF),
            jax.ShapeDtypeStruct((2, h, w, c), F32),
        ],
        [_SMEM] + [_VMEM] * 3,
        [
            pltpu.VMEM((3, slots, 4, h + 2, w, c), BF),
            pltpu.VMEM((slots, 2, h, w, c), F32),
        ],
        flops=1,
        moved=1,
        room=24,
    )(_after(sc, outs[1], lead), g0, g1, wt)
    mine = summed(0, _after(got_near, last))
    for j in (3, 2):
        mine = mine + gots[j].astype(F32)
    gots[1] = _after(gots[1], mine)
    mine = (mine + gots[1].astype(F32)).astype(BF)
    k = 2 * chips
    while k < n:
        mine = (mine.astype(F32) + _xor(mine, k, n, axis).astype(F32)).astype(BF)
        k *= 2
    others = {j: _xor(mine, 4 * j, n, axis) for j in (3, 2, 1)}
    x_own = _xor(mine, 2, n, axis)
    x_near = _xor(others[1], 2, n, axis)
    x_far = _xor(jnp.concatenate([others[2], others[3]], axis=0), 2, n, axis)
    beyond = by(index & 4, near_lead, jnp.full_like(lead, EMPTY_GRAD))
    lead, k = _after(ordered(index & 4, lead, near_lead), x_own), 8
    while k < n:
        came = _xor(lead, k, n, axis)
        beyond = by(index & k, _first_live(beyond, came), beyond)
        if 2 * k < n:
            lead = ordered(index & k, lead, came)
        k *= 2
    theirs = _xor(beyond, 2, n, axis)
    beyond = jnp.concatenate([by(pair, beyond, theirs), by(pair, theirs, beyond)], axis=0)
    beyond = by(pair, _first_live(beside_first, beyond), beyond)
    ours = jnp.concatenate(
        [mine, others[1], others[2], others[3], x_own, x_near, x_far, beyond], axis=0
    )
    other = _xor(ours, 1, n, axis)
    cwg, swg, cbg, sbg, frames_grad = _call(
        _final_kernel,
        [
            jax.ShapeDtypeStruct((27 * c, c), F32),
            jax.ShapeDtypeStruct((2 * c, c), F32),
            jax.ShapeDtypeStruct((1, c), F32),
            jax.ShapeDtypeStruct((1, c), F32),
            jax.ShapeDtypeStruct((slots, 2, h, w, c), BF),
        ],
        [_SMEM] + [_VMEM] * 4 + [_HBM],
        [
            pltpu.VMEM((rows, c), F32),
            pltpu.VMEM((2, h, w, c), BF),
            pltpu.SemaphoreType.DMA((4,)),
        ],
        room=12,
        outs=[_HBM, _HBM, _VMEM, _VMEM, _HBM],
        alias={5: 4},
    )(sc, ours, other, got_first, last, pltpu.with_memory_space_constraint(slabs, pltpu.HBM))
    latents = jnp.concatenate([lat0[None], lat1], axis=0)[:, None]
    return (
        latents,
        frames_grad,
        cwg.reshape(3, 3, 3, c, c),
        cbg[0],
        swg.reshape(2, c, c),
        sbg[0],
    )


def solution(mesh):
    split = P(("groups", "tm"))
    return jax.shard_map(
        functools.partial(body, mesh.shape["tm"]),
        mesh=mesh,
        in_specs=(split, split, split, split, P(), P(), P(), P(), split),
        out_specs=(split, split, P("groups"), P("groups"), P("groups"), P("groups")),
        check_vma=False,
    )
```

```python
import functools

import jax
import jax.numpy as jnp
from jax import lax
from jax.experimental import pallas as pl
from jax.experimental.pallas import tpu as pltpu
from jax.sharding import PartitionSpec as P

BF = jnp.bfloat16
F32 = jnp.float32
EMPTY_FRAME = 100.0
EMPTY_GRAD = 1e30

_VMEM = pl.BlockSpec(memory_space=pltpu.VMEM)
_SMEM = pl.BlockSpec(memory_space=pltpu.SMEM)
_HBM = pl.BlockSpec(memory_space=pltpu.HBM)


def _call(kernel, out_shape, in_specs, scratch=(), flops=0, moved=0, room=16, grid=(), outs=None, alias=None):
    return pl.pallas_call(
        kernel,
        out_shape=out_shape,
        grid=grid,
        in_specs=in_specs,
        out_specs=jax.tree.map(lambda _: _VMEM, out_shape) if outs is None else outs,
        input_output_aliases=alias or {},
        scratch_shapes=list(scratch),
        compiler_params=pltpu.CompilerParams(vmem_limit_bytes=room << 20),
        cost_estimate=pl.CostEstimate(flops=flops, bytes_accessed=moved, transcendentals=0),
    )


def _put(xk, at, rows, value):
    n, w, c = value.shape
    flat = value.astype(F32).reshape(n * w, c)
    col = lax.broadcasted_iota(jnp.int32, (n * w, c), 0) % w
    right = jnp.where(col == 0, 0.0, pltpu.roll(flat, 1, 0))
    left = jnp.where(col == w - 1, 0.0, pltpu.roll(flat, n * w - 1, 0))
    for kw, shifted in enumerate((right, flat, left)):
        xk[(kw, *at, rows)] = shifted.astype(BF).reshape(n, w, c)


def _window(xk, kw, j, kh, h):
    v = xk[kw, :, j, kh : kh + h]
    return v.reshape(v.shape[0] * v.shape[1] * v.shape[2], v.shape[3])


def _wide(xk, j, h):
    return jnp.concatenate(
        [_window(xk, kw, j, kh, h) for kh in range(3) for kw in range(3)], axis=1
    )


def _conv(xk, w_ref, h):
    c = w_ref.shape[-1]
    zero = jnp.zeros((c, c), BF)
    lhs = jnp.concatenate([_wide(xk, j, h) for j in range(4)], axis=1)
    rhs = []
    for j in range(4):
        for tap in range(9):
            rhs.append(
                jnp.concatenate(
                    [w_ref[(j - t) * 9 + tap] if 0 <= j - t <= 2 else zero for t in range(2)],
                    axis=1,
                )
            )
    return jnp.dot(lhs, jnp.concatenate(rhs, axis=0), preferred_element_type=F32)


def _conv_back(xk, w_ref, h, frames=range(4), base=0):
    c = w_ref.shape[-1]
    zero = jnp.zeros((c, c), BF)
    lhs = jnp.concatenate([_wide(xk, j - base, h) for j in frames], axis=1)
    rhs = []
    for f in range(2):
        row = []
        for j in frames:
            for tap in range(9):
                kt = 2 - (j - f)
                row.append(w_ref[kt * 9 + 8 - tap] if 0 <= kt <= 2 else zero)
        rhs.append(jnp.concatenate(row, axis=1))
    return lax.dot_general(
        lhs, jnp.concatenate(rhs, axis=0), (((1,), (1,)), ((), ())), preferred_element_type=F32
    )


def _activate(pre, gout, sw_ref, sb_ref):
    s = 1.0 / (1.0 + jnp.exp(-pre))
    hidden = (pre * s).astype(BF)
    sw = jnp.concatenate([sw_ref[0], sw_ref[1]], axis=0)
    lat = jnp.dot(hidden, sw, preferred_element_type=F32) + sb_ref[...]
    gh = lax.dot_general(gout, sw, (((1,), (1,)), ((), ())), preferred_element_type=F32)
    g = (gh * s * (1.0 + pre * (1.0 - s))).astype(BF)
    return lat, g, hidden


def _conv_bias(xk, w_ref, cb_ref, h):
    return _conv(xk, w_ref, h) + jnp.concatenate([cb_ref[...], cb_ref[...]], axis=1)


def _weight_grads(xk, g, hidden, gout, h, add):
    c = gout.shape[-1]
    parts = []
    for j in range(4):
        lhs = _wide(xk, j, h)
        parts.append(
            lax.dot_general(lhs, g, (((0,), (0,)), ((), ())), preferred_element_type=F32)
        )
    for kt in range(3):
        add(kt, parts[kt][:, :c] + parts[kt + 1][:, c:])
    sg = lax.dot_general(hidden, gout, (((0,), (0,)), ((), ())), preferred_element_type=F32)
    g32 = jnp.sum(g.astype(F32), axis=0, keepdims=True)
    add(3, sg)
    add(4, g32[:, :c] + g32[:, c:])
    add(5, jnp.sum(gout.astype(F32), axis=0, keepdims=True))


def _fill_early(sc, fr, ha, xk):
    slots, _, h, w, c = fr.shape
    for s in range(slots):
        for f in range(2):
            spots = [(s - 1, f + 2, None)] if s > 0 else []
            if s + 1 < slots:
                spots.append((s, f, sc[1 + s + 1] == 0))
            for slot, j, keep in spots:
                a, b = fr[s, f], ha[s, f]
                if keep is not None:
                    a = jnp.where(keep, a, jnp.zeros_like(a))
                    b = jnp.where(keep, b, jnp.zeros_like(b))
                _put(xk, (slot, j), slice(1, 1 + h), a)
                _put(xk, (slot, j), slice(0, 1), b[:1])
                _put(xk, (slot, j), slice(h + 1, h + 2), b[1:])


def _early_gout(sc, co):
    slots, _, h, w, c = co.shape
    return jnp.concatenate(
        [
            jnp.where(s < sc[0], co[s, 0], jnp.zeros_like(co[s, 0])).reshape(h * w, c)
            for s in range(1, slots)
        ],
        axis=0,
    )


def _early_conv_kernel(
    sc, frh, hah, coh, wh, cbh, swh, sbh, pre_ref, gout_ref, sw, sb, fr, ha, co, w_ref, cb, xk, sems
):
    h = fr.shape[2]
    pairs = ((frh, fr), (hah, ha), (coh, co), (wh, w_ref), (cbh, cb), (swh, sw), (sbh, sb))
    copies = [pltpu.make_async_copy(a, b, sems.at[i]) for i, (a, b) in enumerate(pairs)]
    for copy in copies:
        copy.start()
    copies[0].wait()
    copies[1].wait()
    _fill_early(sc, fr, ha, xk)
    copies[2].wait()
    gout_ref[...] = _early_gout(sc, co)
    for copy in copies[3:]:
        copy.wait()
    pre_ref[...] = _conv_bias(xk, w_ref, cb, h)


def _early_act_kernel(sc, pre_ref, gout_ref, sw, sb, lat_ref, g_ref, hid_ref):
    slots, h, w, c = lat_ref.shape
    lat, g, hidden = _activate(pre_ref[...], gout_ref[...], sw, sb)
    for s in range(slots):
        part = lat[s * h * w : (s + 1) * h * w]
        filled = s + 1 < sc[0]
        lat_ref[s] = jnp.where(filled, part, jnp.zeros_like(part)).astype(BF).reshape(h, w, c)
    g_ref[...] = g
    hid_ref[...] = hidden


def _early_sums_kernel(sc, frh, hah, g_ref, hid_ref, gout_ref, acc, xk, fr, ha, sems):
    copies = [
        pltpu.make_async_copy(a, b, sems.at[i]) for i, (a, b) in enumerate(((frh, fr), (hah, ha)))
    ]
    for copy in copies:
        copy.start()
    for copy in copies:
        copy.wait()
    _fill_early(sc, fr, ha, xk)
    _, _, h, _, c = fr.shape
    n9 = 9 * c

    def add(kind, value):
        if kind < 3:
            acc[kind * n9 : (kind + 1) * n9] = value
        elif kind == 3:
            acc[3 * n9 : 3 * n9 + 2 * c] = value
        else:
            at = 3 * n9 + 2 * c + (kind - 4)
            acc[at : at + 1] = value

    acc[3 * n9 + 2 * c :] = jnp.zeros((acc.shape[0] - 3 * n9 - 2 * c, c), F32)
    _weight_grads(xk, g_ref[...], hid_ref[...], gout_ref[...], h, add)


def _late_kernel(
    sc, frs, has, tail, cos, w_ref, cb, sw, sb, early, lat_ref, g_ref, send, keep, xk, acc
):
    fr, ha, co = frs.at[0], has.at[0], cos.at[0]
    _, h, w, c = fr.shape
    on = sc[1] == 0
    for f in range(2):
        _put(xk, (0, f + 2), slice(1, 1 + h), fr[f])
        _put(xk, (0, f + 2), slice(0, 1), ha[f, :1])
        _put(xk, (0, f + 2), slice(h + 1, h + 2), ha[f, 1:])
        a = tail[f * h : (f + 1) * h]
        b = tail[2 * h + 2 * f : 2 * h + 2 * f + 2]
        a = jnp.where(on, a, jnp.zeros_like(a))
        b = jnp.where(on, b, jnp.zeros_like(b))
        _put(xk, (0, f), slice(1, 1 + h), a)
        _put(xk, (0, f), slice(0, 1), b[:1])
        _put(xk, (0, f), slice(h + 1, h + 2), b[1:])
    filled = sc[0] > 0
    gout = jnp.where(filled, co[0], jnp.zeros_like(co[0])).reshape(h * w, c)
    lat, g, hidden = _activate(_conv_bias(xk, w_ref, cb, h), gout, sw, sb)
    lat_ref[...] = jnp.where(filled, lat, jnp.zeros_like(lat)).astype(BF).reshape(h, w, c)
    g_ref[...] = g
    n9 = 9 * c

    def add(kind, value):
        if kind < 3:
            rows = slice(kind * n9, (kind + 1) * n9)
        elif kind == 3:
            rows = slice(3 * n9, 3 * n9 + 2 * c)
        else:
            at = 3 * n9 + 2 * c + (kind - 4)
            rows = slice(at, at + 1)
        acc[rows] = early[rows] + value

    tail_rows = slice(3 * n9 + 2 * c, acc.shape[0])
    acc[tail_rows] = early[tail_rows]

    @pl.when(sc[0] >= 0)
    def _():
        _weight_grads(xk, g, hidden, gout, h, add)

        half = keep.shape[0]
        core = sc[sc.shape[0] - 1]
        send[...] = acc[pl.ds(pl.multiple_of((1 - core) * half, 16), half)].astype(BF)
        keep[...] = acc[pl.ds(pl.multiple_of(core * half, 16), half)]


def _carried_kernel(sc, g_ref, w_ref, out, xk):
    _, _, _, h, w, c = xk.shape
    h = h - 2
    on = sc[1] == 0
    for t in range(2):
        for kw in range(3):
            xk[kw, 0, t, 0:1] = jnp.zeros((1, w, c), BF)
            xk[kw, 0, t, h + 1 : h + 2] = jnp.zeros((1, w, c), BF)
        v = g_ref[:, t * c : (t + 1) * c].reshape(h, w, c)
        _put(xk, (0, t), slice(1, 1 + h), jnp.where(on, v, jnp.zeros_like(v)))
    back = _conv_back(xk, w_ref, h, (2, 3), 2)
    back = jnp.where(sc[0] > 0, back, jnp.full_like(back, EMPTY_GRAD)).astype(BF)
    for t in range(2):
        out[t * h * w : (t + 1) * h * w] = back[:, t * c : (t + 1) * c]


def _back_kernel(sc, g0, g1, w_ref, out_ref, last_ref, xk, all_ref):
    slots, _, h, w, c = out_ref.shape
    m = h * w
    zero = jnp.zeros((1, w, c), BF)
    for kw in range(3):
        for j in range(4):
            for s in range(slots):
                xk[kw, s, j, 0:1] = zero
                xk[kw, s, j, h + 1 : h + 2] = zero
    for f in range(2):
        for kw in range(3):
            xk[kw, slots - 1, f + 2, 1 : 1 + h] = jnp.zeros((h, w, c), BF)
        lanes = slice(f * c, (f + 1) * c)
        for s in range(slots):
            v = g0[:, lanes] if s == 0 else g1[(s - 1) * m : s * m, lanes]
            v = v.reshape(h, w, c)
            _put(xk, (s, f), slice(1, 1 + h), v)
            if s > 0:
                on = sc[1 + s] == 0
                _put(xk, (s - 1, f + 2), slice(1, 1 + h), jnp.where(on, v, jnp.zeros_like(v)))
    out = _conv_back(xk, w_ref, h)
    for f in range(2):
        lanes = slice(f * c, (f + 1) * c)
        out_ref[:, f] = out[:, lanes].astype(BF).reshape(slots, h, w, c)
        all_ref[:, f] = out[:, lanes].reshape(slots, h, w, c)
    last_ref[...] = all_ref[jnp.maximum(sc[0] - 1, 0)]


def _first_live(a, b):
    return jnp.where(a.astype(F32) < EMPTY_GRAD / 2, a, b)


def _place(sc):
    chip, core = sc[sc.shape[0] - 2], sc[sc.shape[0] - 1]
    return lax.shift_right_logical(chip, 1), lax.bitwise_and(chip, 1), core


def _across_x_kernel(sc, keep, got, send_far, send_near, kept):
    z, x, _ = _place(sc)
    half = keep.shape[0]
    blocks = 4
    rows = half // (2 * blocks)

    def piece(j, side):
        p = 2 * lax.bitwise_xor(z, j) + side
        at = pl.ds(pl.multiple_of(p * rows, 16), rows)
        return keep[at] + got[at].astype(F32)

    for j in range(blocks):
        kept[j * rows : (j + 1) * rows] = piece(j, x)
        send, i = (send_near, j) if j < 2 else (send_far, j - 2)
        send[i * rows : (i + 1) * rows] = piece(j, 1 - x).astype(BF)


def _tail_kernel(sc, fr, ha, out):
    h2 = fr.shape[1] * fr.shape[2]
    live = sc[0] > 0
    for ref, rows in ((fr, slice(0, h2)), (ha, slice(h2, out.shape[0]))):
        v = ref[...].reshape(rows.stop - rows.start, *out.shape[1:])
        out[rows] = jnp.where(live, v, jnp.full_like(v, EMPTY_FRAME))


def _final_kernel(
    sc, mine, other, beside, last, fg_in, cw, sw, cb, sb, fg, acc, newest, sems
):
    del fg_in
    c = mine.shape[1]
    half = acc.shape[0] // 2
    z, x, core = _place(sc)
    blocks = 4
    rows = half // (2 * blocks)
    n27, n29 = 27 * c, 29 * c
    low = [pltpu.make_async_copy(acc.at[:half], cw.at[:half], sems.at[0])]
    high = [
        pltpu.make_async_copy(acc.at[half:n27], cw.at[half:n27], sems.at[1]),
        pltpu.make_async_copy(acc.at[n27:n29], sw, sems.at[2]),
    ]
    for ref, at_core in ((mine, core), (other, 1 - core)):
        for k in range(2 * blocks):
            side = x if k < blocks else 1 - x
            chip = 2 * lax.bitwise_xor(z, k % blocks) + side
            at = pl.multiple_of(at_core * half + chip * rows, 16)
            acc[pl.ds(at, rows)] = ref[k * rows : (k + 1) * rows].astype(F32)

        @pl.when(at_core == 0)
        def _():
            for copy in low:
                copy.start()

        @pl.when(at_core != 0)
        def _():
            for copy in high:
                copy.start()

    frames, h, w, _ = last.shape
    part = mine.shape[0] - half
    for f in range(frames):
        a, b = mine[half:].astype(F32), other[half:].astype(F32)
        beyond = jnp.where(core == 0, a, b) if f == 0 else jnp.where(core == 0, b, a)
        near = beside[f * part : (f + 1) * part].astype(F32)
        came = jnp.where(core == 0, _first_live(near, beyond), beyond)
        came = jnp.where(came < EMPTY_GRAD / 2, came, jnp.zeros_like(came)).reshape(h, w, c)
        came = jnp.where(sc[0] > 0, came, jnp.zeros_like(came))
        newest[f] = (last[f] + came).astype(BF)
    slab = pltpu.make_async_copy(newest, fg.at[jnp.maximum(sc[0] - 1, 0)], sems.at[3])
    slab.start()
    cb[...] = acc[n29 : n29 + 1]
    sb[...] = acc[n29 + 1 : n29 + 2]
    for copy in (*low, *high, slab):
        copy.wait()


def _xor(x, k, n, axis):
    return lax.ppermute(x, axis, [(i, i ^ k) for i in range(n)])


def _latest_before(x, empty, axis, n, beside_x, beside_near, beside_far):
    index = lax.axis_index(axis)
    core, pair = index & 1, (index >> 1) & 1

    def newest(early, late):
        return jnp.where(late > empty / 2, early, late)

    def half(v):
        rows = v.shape[0] // 2
        return jnp.where(core == 0, v[:rows], v[rows:])

    other = _xor(x, 1, n, axis)
    a, b = half(x), half(other)
    chip = jnp.where(core == 0, newest(a, b), newest(b, a))
    beside = _xor(chip, 2, n, axis)
    quad = jnp.where(pair == 0, newest(chip, beside), newest(beside, chip))
    quad = beside_x(chip, quad)
    block, before, k = quad, jnp.full_like(quad, empty), 4
    while k < n:
        late = (index & k) > 0
        came = _xor(block, k, n, axis)
        if k == 4:
            came = beside_near(block, came)
        before = jnp.where(late, newest(came, before), before)
        if k == 8:
            before = beside_far(block, before)
        if 2 * k < n:
            block = jnp.where(late, newest(came, block), newest(block, came))
        k *= 2
    before = jnp.where(pair == 0, before, newest(before, beside))
    across = _xor(before, 1, n, axis)
    before = jnp.concatenate(
        [jnp.where(core == 0, before, across), jnp.where(core == 0, across, before)], axis=0
    )
    before = jnp.where(core == 0, before, newest(before, other))
    return jnp.where(before > empty / 2, jnp.zeros_like(before), before)


def _after(value, *earlier):
    return lax.optimization_barrier((value, *earlier))[0]


def body(
    n,
    frames,
    row_halo,
    clip_start,
    slab_counts,
    conv_weight,
    conv_bias,
    stride_weight,
    stride_bias,
    cotangent,
):
    axis = "tm"
    slots, _, h, w, c = frames.shape
    count = slab_counts[0]
    index = lax.axis_index(axis)
    chips = 8
    assert n % (2 * chips) == 0
    sc = jnp.concatenate(
        [
            slab_counts,
            clip_start,
            ((index >> 1) & (chips - 1)).reshape(1).astype(jnp.int32),
            (index & 1).reshape(1).astype(jnp.int32),
        ]
    )
    wt = conv_weight.reshape(27, c, c)
    cb, sb = conv_bias.reshape(1, c), stride_bias.reshape(1, c)
    unit = 16 * 2 * chips
    rows = -(-(29 * c + 2) // unit) * unit
    m = h * w
    conv_flops = 2 * m * 36 * c * 2 * c

    def newest_slot(i, sc):
        return (jnp.maximum(sc[0] - 1, 0), 0, 0, 0, 0)

    tail = pl.pallas_call(
        _tail_kernel,
        out_shape=jax.ShapeDtypeStruct((2 * h + 4, w, c), BF),
        grid_spec=pltpu.PrefetchScalarGridSpec(
            num_scalar_prefetch=1,
            grid=(1,),
            in_specs=[
                pl.BlockSpec((1, 2, h, w, c), newest_slot),
                pl.BlockSpec((1, 2, 2, w, c), newest_slot),
            ],
            out_specs=pl.BlockSpec((2 * h + 4, w, c), lambda i, sc: (0, 0, 0)),
        ),
        compiler_params=pltpu.CompilerParams(vmem_limit_bytes=8 << 20),
    )(
        slab_counts,
        *(pltpu.with_memory_space_constraint(v, pltpu.HBM) for v in (frames, row_halo)),
    )

    held = {}
    wide = ((slots - 1) * m, 2 * c)
    raw = [
        pltpu.with_memory_space_constraint(v, pltpu.HBM)
        for v in (frames, row_halo, cotangent, wt, cb, stride_weight, sb)
    ]
    windows = (3, slots - 1, 4, h + 2, w, c)

    def early_conv(start, follow):
        held["conv"] = _call(
            _early_conv_kernel,
            [
                jax.ShapeDtypeStruct(wide, F32),
                jax.ShapeDtypeStruct((wide[0], c), BF),
                jax.ShapeDtypeStruct(stride_weight.shape, BF),
                jax.ShapeDtypeStruct(sb.shape, F32),
            ],
            [_SMEM] + [_HBM] * len(raw),
            [pltpu.VMEM(v.shape, v.dtype) for v in raw[:5]]
            + [pltpu.VMEM(windows, BF), pltpu.SemaphoreType.DMA((len(raw),))],
            flops=(slots - 1) * conv_flops,
            moved=4 << 20,
        )(_after(sc, start), *raw)
        return _after(follow, held["conv"][0])

    def early_act(start, follow):
        pre, gout1, sw1, sb1 = held["conv"]
        held["early"] = _call(
            _early_act_kernel,
            [
                jax.ShapeDtypeStruct((slots - 1, h, w, c), BF),
                jax.ShapeDtypeStruct(wide, BF),
                jax.ShapeDtypeStruct(wide, BF),
            ],
            [_SMEM] + [_VMEM] * 4,
            moved=2 << 20,
            room=6,
        )(_after(sc, start), pre, gout1, sw1, sb1)
        return _after(follow, held["early"][1])

    def early_sums(start, follow):
        gout1 = held["conv"][1]
        _, g1, hid1 = held["early"]
        held["sums"] = _call(
            _early_sums_kernel,
            jax.ShapeDtypeStruct((rows, c), F32),
            [_SMEM, _HBM, _HBM] + [_VMEM] * 3,
            [pltpu.VMEM(windows, BF)]
            + [pltpu.VMEM(v.shape, BF) for v in raw[:2]]
            + [pltpu.SemaphoreType.DMA((2,))],
            flops=(slots - 1) * conv_flops,
            moved=4 << 20,
        )(_after(sc, start), raw[0], raw[1], g1, hid1, gout1)
        return _after(follow, held["sums"])

    arrived = _latest_before(tail, EMPTY_FRAME, axis, n, early_conv, early_act, early_sums)
    lat1, g1, _ = held["early"]

    def first(*shape):
        return pl.BlockSpec((1, *shape), lambda i: (0,) * (len(shape) + 1))

    half, carried = rows // 2, 2 * m
    lat0, g0, send, keep = _call(
        _late_kernel,
        [
            jax.ShapeDtypeStruct((h, w, c), BF),
            jax.ShapeDtypeStruct((m, 2 * c), BF),
            jax.ShapeDtypeStruct((half, c), BF),
            jax.ShapeDtypeStruct((half, c), F32),
        ],
        [_SMEM, first(2, h, w, c), first(2, 2, w, c), _VMEM, first(1, h, w, c)] + [_VMEM] * 5,
        [pltpu.VMEM((3, 1, 4, h + 2, w, c), BF), pltpu.VMEM((rows, c), F32)],
        flops=2 * conv_flops,
        moved=6 << 20,
        grid=(1,),
    )(sc, frames, row_halo, arrived, cotangent, wt, cb, stride_weight, sb, held["sums"])

    blocks = chips // 2
    piece = half // chips
    got = _xor(send, 1, n, axis)
    first_grad = _call(
        _carried_kernel,
        jax.ShapeDtypeStruct((carried, c), BF),
        [_SMEM, _VMEM, _VMEM],
        [pltpu.VMEM((3, 1, 2, h + 2, w, c), BF)],
        flops=conv_flops // 2,
        moved=1 << 20,
        room=8,
    )(sc, g0, wt)
    send_far, send_near, kept = _call(
        _across_x_kernel,
        [
            jax.ShapeDtypeStruct((2 * piece, c), BF),
            jax.ShapeDtypeStruct((2 * piece, c), BF),
            jax.ShapeDtypeStruct((blocks * piece, c), F32),
        ],
        [_SMEM] + [_VMEM] * 2,
        room=8,
    )(sc, _after(keep, first_grad), got)
    got_far = _xor(send_far, 2, n, axis)
    got_first = _xor(_after(first_grad, kept), 1, n, axis)
    core, pair = index & 1, (index >> 1) & 1

    def by(bit, a, b):
        return jnp.where(bit == 0, a, b)

    def by_half(bit, v):
        rows = v.shape[0] // 2
        return by(bit, v[:rows], v[rows:])

    def ordered(bit, ours, theirs):
        return by(bit, _first_live(ours, theirs), _first_live(theirs, ours))

    chip_first = ordered(core, by_half(core, first_grad), by_half(core, got_first))
    send_near = jnp.concatenate([send_near, chip_first], axis=0)
    got_near = _xor(send_near, 2, n, axis)
    slabs, last = _call(
        _back_kernel,
        [
            jax.ShapeDtypeStruct((slots, 2, h, w, c), BF),
            jax.ShapeDtypeStruct((2, h, w, c), F32),
        ],
        [_SMEM] + [_VMEM] * 3,
        [
            pltpu.VMEM((3, slots, 4, h + 2, w, c), BF),
            pltpu.VMEM((slots, 2, h, w, c), F32),
        ],
        flops=1,
        moved=1,
        room=24,
    )(_after(sc, send_near), g0, g1, wt)
    got_far = _after(got_far, last)

    def summed(j, came):
        i = j % 2
        return kept[j * piece : (j + 1) * piece] + came[i * piece : (i + 1) * piece].astype(F32)

    outs = {j: summed(j, got_far).astype(BF) for j in (3, 2)}
    got_near = _after(got_near, outs[3], outs[2])
    outs[1] = summed(1, got_near).astype(BF)
    gots = {j: _xor(outs[j], 4 * j, n, axis) for j in (3, 2, 1)}
    beside_first = got_near[2 * piece :]
    lead = ordered(pair, by_half(pair, chip_first), by_half(pair, beside_first))
    near_lead = _xor(lead, 4, n, axis)
    mine = summed(0, _after(got_near, outs[1]))
    for j in (3, 2):
        mine = mine + gots[j].astype(F32)
    gots[1] = _after(gots[1], mine)
    mine = (mine + gots[1].astype(F32)).astype(BF)
    k = 2 * chips
    while k < n:
        mine = (mine.astype(F32) + _xor(mine, k, n, axis).astype(F32)).astype(BF)
        k *= 2
    others = {j: _xor(mine, 4 * j, n, axis) for j in (3, 2, 1)}
    x_own = _xor(mine, 2, n, axis)
    x_near = _xor(others[1], 2, n, axis)
    x_far = _xor(jnp.concatenate([others[2], others[3]], axis=0), 2, n, axis)
    beyond = by(index & 4, near_lead, jnp.full_like(lead, EMPTY_GRAD))
    lead, k = _after(ordered(index & 4, lead, near_lead), x_own), 8
    while k < n:
        came = _xor(lead, k, n, axis)
        beyond = by(index & k, _first_live(beyond, came), beyond)
        if 2 * k < n:
            lead = ordered(index & k, lead, came)
        k *= 2
    theirs = _xor(beyond, 2, n, axis)
    beyond = jnp.concatenate([by(pair, beyond, theirs), by(pair, theirs, beyond)], axis=0)
    beyond = by(pair, _first_live(beside_first, beyond), beyond)
    ours = jnp.concatenate(
        [mine, others[1], others[2], others[3], x_own, x_near, x_far, beyond], axis=0
    )
    other = _xor(ours, 1, n, axis)
    cwg, swg, cbg, sbg, frames_grad = _call(
        _final_kernel,
        [
            jax.ShapeDtypeStruct((27 * c, c), F32),
            jax.ShapeDtypeStruct((2 * c, c), F32),
            jax.ShapeDtypeStruct((1, c), F32),
            jax.ShapeDtypeStruct((1, c), F32),
            jax.ShapeDtypeStruct((slots, 2, h, w, c), BF),
        ],
        [_SMEM] + [_VMEM] * 4 + [_HBM],
        [
            pltpu.VMEM((rows, c), F32),
            pltpu.VMEM((2, h, w, c), BF),
            pltpu.SemaphoreType.DMA((4,)),
        ],
        room=12,
        outs=[_HBM, _HBM, _VMEM, _VMEM, _HBM],
        alias={5: 4},
    )(sc, ours, other, got_first, last, pltpu.with_memory_space_constraint(slabs, pltpu.HBM))
    latents = jnp.concatenate([lat0[None], lat1], axis=0)[:, None]
    return (
        latents,
        frames_grad,
        cwg.reshape(3, 3, 3, c, c),
        cbg[0],
        swg.reshape(2, c, c),
        sbg[0],
    )


def solution(mesh):
    split = P(("groups", "tm"))
    return jax.shard_map(
        functools.partial(body, mesh.shape["tm"]),
        mesh=mesh,
        in_specs=(split, split, split, split, P(), P(), P(), P(), split),
        out_specs=(split, split, P("groups"), P("groups"), P("groups"), P("groups")),
        check_vma=False,
    )
```

```python
import functools

import jax
import jax.numpy as jnp
from jax import lax
from jax.experimental import pallas as pl
from jax.experimental.pallas import tpu as pltpu
from jax.sharding import PartitionSpec as P

BF = jnp.bfloat16
F32 = jnp.float32
EMPTY_FRAME = 100.0
EMPTY_GRAD = 1e30

_VMEM = pl.BlockSpec(memory_space=pltpu.VMEM)
_SMEM = pl.BlockSpec(memory_space=pltpu.SMEM)
_HBM = pl.BlockSpec(memory_space=pltpu.HBM)


def _call(kernel, out_shape, in_specs, scratch=(), flops=0, moved=0, room=16, grid=()):
    return pl.pallas_call(
        kernel,
        out_shape=out_shape,
        grid=grid,
        in_specs=in_specs,
        out_specs=jax.tree.map(lambda _: _VMEM, out_shape),
        scratch_shapes=list(scratch),
        compiler_params=pltpu.CompilerParams(vmem_limit_bytes=room << 20),
        cost_estimate=pl.CostEstimate(flops=flops, bytes_accessed=moved, transcendentals=0),
    )


def _put(xk, at, rows, value):
    n, w, c = value.shape
    flat = value.astype(F32).reshape(n * w, c)
    col = lax.broadcasted_iota(jnp.int32, (n * w, c), 0) % w
    right = jnp.where(col == 0, 0.0, pltpu.roll(flat, 1, 0))
    left = jnp.where(col == w - 1, 0.0, pltpu.roll(flat, n * w - 1, 0))
    for kw, shifted in enumerate((right, flat, left)):
        xk[(kw, *at, rows)] = shifted.astype(BF).reshape(n, w, c)


def _window(xk, kw, j, kh, h):
    v = xk[kw, :, j, kh : kh + h]
    return v.reshape(v.shape[0] * v.shape[1] * v.shape[2], v.shape[3])


def _wide(xk, j, h):
    return jnp.concatenate(
        [_window(xk, kw, j, kh, h) for kh in range(3) for kw in range(3)], axis=1
    )


def _conv(xk, w_ref, h):
    c = w_ref.shape[-1]
    zero = jnp.zeros((c, c), BF)
    lhs = jnp.concatenate([_wide(xk, j, h) for j in range(4)], axis=1)
    rhs = []
    for j in range(4):
        for tap in range(9):
            rhs.append(
                jnp.concatenate(
                    [w_ref[(j - t) * 9 + tap] if 0 <= j - t <= 2 else zero for t in range(2)],
                    axis=1,
                )
            )
    return jnp.dot(lhs, jnp.concatenate(rhs, axis=0), preferred_element_type=F32)


def _conv_back(xk, w_ref, h, frames=range(4), base=0):
    c = w_ref.shape[-1]
    zero = jnp.zeros((c, c), BF)
    lhs = jnp.concatenate([_wide(xk, j - base, h) for j in frames], axis=1)
    rhs = []
    for f in range(2):
        row = []
        for j in frames:
            for tap in range(9):
                kt = 2 - (j - f)
                row.append(w_ref[kt * 9 + 8 - tap] if 0 <= kt <= 2 else zero)
        rhs.append(jnp.concatenate(row, axis=1))
    return lax.dot_general(
        lhs, jnp.concatenate(rhs, axis=0), (((1,), (1,)), ((), ())), preferred_element_type=F32
    )


def _activate(pre, gout, sw_ref, sb_ref):
    s = 1.0 / (1.0 + jnp.exp(-pre))
    hidden = (pre * s).astype(BF)
    sw = jnp.concatenate([sw_ref[0], sw_ref[1]], axis=0)
    lat = jnp.dot(hidden, sw, preferred_element_type=F32) + sb_ref[...]
    gh = lax.dot_general(gout, sw, (((1,), (1,)), ((), ())), preferred_element_type=F32)
    g = (gh * s * (1.0 + pre * (1.0 - s))).astype(BF)
    return lat, g, hidden


def _conv_bias(xk, w_ref, cb_ref, h):
    return _conv(xk, w_ref, h) + jnp.concatenate([cb_ref[...], cb_ref[...]], axis=1)


def _weight_grads(xk, g, hidden, gout, h, add):
    c = gout.shape[-1]
    parts = []
    for j in range(4):
        lhs = _wide(xk, j, h)
        parts.append(
            lax.dot_general(lhs, g, (((0,), (0,)), ((), ())), preferred_element_type=F32)
        )
    for kt in range(3):
        add(kt, parts[kt][:, :c] + parts[kt + 1][:, c:])
    sg = lax.dot_general(hidden, gout, (((0,), (0,)), ((), ())), preferred_element_type=F32)
    g32 = jnp.sum(g.astype(F32), axis=0, keepdims=True)
    add(3, sg)
    add(4, g32[:, :c] + g32[:, c:])
    add(5, jnp.sum(gout.astype(F32), axis=0, keepdims=True))


def _fill_early(sc, fr, ha, xk):
    slots, _, h, w, c = fr.shape
    for s in range(slots):
        for f in range(2):
            spots = [(s - 1, f + 2, None)] if s > 0 else []
            if s + 1 < slots:
                spots.append((s, f, sc[1 + s + 1] == 0))
            for slot, j, keep in spots:
                a, b = fr[s, f], ha[s, f]
                if keep is not None:
                    a = jnp.where(keep, a, jnp.zeros_like(a))
                    b = jnp.where(keep, b, jnp.zeros_like(b))
                _put(xk, (slot, j), slice(1, 1 + h), a)
                _put(xk, (slot, j), slice(0, 1), b[:1])
                _put(xk, (slot, j), slice(h + 1, h + 2), b[1:])


def _early_gout(sc, co):
    slots, _, h, w, c = co.shape
    return jnp.concatenate(
        [
            jnp.where(s < sc[0], co[s, 0], jnp.zeros_like(co[s, 0])).reshape(h * w, c)
            for s in range(1, slots)
        ],
        axis=0,
    )


def _early_conv_kernel(
    sc, frh, hah, coh, wh, cbh, swh, sbh, pre_ref, gout_ref, sw, sb, fr, ha, co, w_ref, cb, xk, sems
):
    h = fr.shape[2]
    pairs = ((frh, fr), (hah, ha), (coh, co), (wh, w_ref), (cbh, cb), (swh, sw), (sbh, sb))
    copies = [pltpu.make_async_copy(a, b, sems.at[i]) for i, (a, b) in enumerate(pairs)]
    for copy in copies:
        copy.start()
    copies[0].wait()
    copies[1].wait()
    _fill_early(sc, fr, ha, xk)
    copies[2].wait()
    gout_ref[...] = _early_gout(sc, co)
    for copy in copies[3:]:
        copy.wait()
    pre_ref[...] = _conv_bias(xk, w_ref, cb, h)


def _early_act_kernel(sc, pre_ref, gout_ref, sw, sb, lat_ref, g_ref, hid_ref):
    slots, h, w, c = lat_ref.shape
    lat, g, hidden = _activate(pre_ref[...], gout_ref[...], sw, sb)
    for s in range(slots):
        part = lat[s * h * w : (s + 1) * h * w]
        filled = s + 1 < sc[0]
        lat_ref[s] = jnp.where(filled, part, jnp.zeros_like(part)).astype(BF).reshape(h, w, c)
    g_ref[...] = g
    hid_ref[...] = hidden


def _early_sums_kernel(sc, frh, hah, g_ref, hid_ref, gout_ref, acc, xk, fr, ha, sems):
    copies = [
        pltpu.make_async_copy(a, b, sems.at[i]) for i, (a, b) in enumerate(((frh, fr), (hah, ha)))
    ]
    for copy in copies:
        copy.start()
    for copy in copies:
        copy.wait()
    _fill_early(sc, fr, ha, xk)
    _, _, h, _, c = fr.shape
    n9 = 9 * c

    def add(kind, value):
        if kind < 3:
            acc[kind * n9 : (kind + 1) * n9] = value
        elif kind == 3:
            acc[3 * n9 : 3 * n9 + 2 * c] = value
        else:
            at = 3 * n9 + 2 * c + (kind - 4)
            acc[at : at + 1] = value

    acc[3 * n9 + 2 * c :] = jnp.zeros((acc.shape[0] - 3 * n9 - 2 * c, c), F32)
    _weight_grads(xk, g_ref[...], hid_ref[...], gout_ref[...], h, add)


def _late_kernel(
    sc, frs, has, tail, cos, w_ref, cb, sw, sb, early, lat_ref, g_ref, send, keep, xk, acc
):
    fr, ha, co = frs.at[0], has.at[0], cos.at[0]
    _, h, w, c = fr.shape
    on = sc[1] == 0
    for f in range(2):
        _put(xk, (0, f + 2), slice(1, 1 + h), fr[f])
        _put(xk, (0, f + 2), slice(0, 1), ha[f, :1])
        _put(xk, (0, f + 2), slice(h + 1, h + 2), ha[f, 1:])
        a = tail[f * h : (f + 1) * h]
        b = tail[2 * h + 2 * f : 2 * h + 2 * f + 2]
        a = jnp.where(on, a, jnp.zeros_like(a))
        b = jnp.where(on, b, jnp.zeros_like(b))
        _put(xk, (0, f), slice(1, 1 + h), a)
        _put(xk, (0, f), slice(0, 1), b[:1])
        _put(xk, (0, f), slice(h + 1, h + 2), b[1:])
    filled = sc[0] > 0
    gout = jnp.where(filled, co[0], jnp.zeros_like(co[0])).reshape(h * w, c)
    lat, g, hidden = _activate(_conv_bias(xk, w_ref, cb, h), gout, sw, sb)
    lat_ref[...] = jnp.where(filled, lat, jnp.zeros_like(lat)).astype(BF).reshape(h, w, c)
    g_ref[...] = g
    n9 = 9 * c

    def add(kind, value):
        if kind < 3:
            rows = slice(kind * n9, (kind + 1) * n9)
        elif kind == 3:
            rows = slice(3 * n9, 3 * n9 + 2 * c)
        else:
            at = 3 * n9 + 2 * c + (kind - 4)
            rows = slice(at, at + 1)
        acc[rows] = early[rows] + value

    tail_rows = slice(3 * n9 + 2 * c, acc.shape[0])
    acc[tail_rows] = early[tail_rows]

    @pl.when(sc[0] >= 0)
    def _():
        _weight_grads(xk, g, hidden, gout, h, add)

        half = keep.shape[0]
        core = sc[sc.shape[0] - 1]
        send[...] = acc[pl.ds(pl.multiple_of((1 - core) * half, 16), half)].astype(BF)
        keep[...] = acc[pl.ds(pl.multiple_of(core * half, 16), half)]


def _carried_kernel(sc, g_ref, w_ref, out, xk):
    _, _, _, h, w, c = xk.shape
    h = h - 2
    on = sc[1] == 0
    for t in range(2):
        for kw in range(3):
            xk[kw, 0, t, 0:1] = jnp.zeros((1, w, c), BF)
            xk[kw, 0, t, h + 1 : h + 2] = jnp.zeros((1, w, c), BF)
        v = g_ref[:, t * c : (t + 1) * c].reshape(h, w, c)
        _put(xk, (0, t), slice(1, 1 + h), jnp.where(on, v, jnp.zeros_like(v)))
    back = _conv_back(xk, w_ref, h, (2, 3), 2)
    back = jnp.where(sc[0] > 0, back, jnp.full_like(back, EMPTY_GRAD)).astype(BF)
    for t in range(2):
        out[t * h * w : (t + 1) * h * w] = back[:, t * c : (t + 1) * c]


def _back_kernel(sc, g0, g1, w_ref, out_ref, xk):
    slots, _, h, w, c = out_ref.shape
    m = h * w
    zero = jnp.zeros((1, w, c), BF)
    for kw in range(3):
        for j in range(4):
            for s in range(slots):
                xk[kw, s, j, 0:1] = zero
                xk[kw, s, j, h + 1 : h + 2] = zero
    for f in range(2):
        for kw in range(3):
            xk[kw, slots - 1, f + 2, 1 : 1 + h] = jnp.zeros((h, w, c), BF)
        lanes = slice(f * c, (f + 1) * c)
        for s in range(slots):
            v = g0[:, lanes] if s == 0 else g1[(s - 1) * m : s * m, lanes]
            v = v.reshape(h, w, c)
            _put(xk, (s, f), slice(1, 1 + h), v)
            if s > 0:
                on = sc[1 + s] == 0
                _put(xk, (s - 1, f + 2), slice(1, 1 + h), jnp.where(on, v, jnp.zeros_like(v)))
    out = _conv_back(xk, w_ref, h)
    for f in range(2):
        out_ref[:, f] = out[:, f * c : (f + 1) * c].reshape(slots, h, w, c)


def _first_live(a, b):
    return jnp.where(a.astype(F32) < EMPTY_GRAD / 2, a, b)


def _place(sc):
    chip, core = sc[sc.shape[0] - 2], sc[sc.shape[0] - 1]
    return lax.shift_right_logical(chip, 1), lax.bitwise_and(chip, 1), core


def _across_x_kernel(sc, keep, got, send_far, send_near, kept):
    z, x, _ = _place(sc)
    half = keep.shape[0]
    blocks = 4
    rows = half // (2 * blocks)

    def piece(j, side):
        p = 2 * lax.bitwise_xor(z, j) + side
        at = pl.ds(pl.multiple_of(p * rows, 16), rows)
        return keep[at] + got[at].astype(F32)

    for j in range(blocks):
        kept[j * rows : (j + 1) * rows] = piece(j, x)
        send, i = (send_near, j) if j < 2 else (send_far, j - 2)
        send[i * rows : (i + 1) * rows] = piece(j, 1 - x).astype(BF)


def _tail_kernel(sc, fr, ha, out):
    h2 = fr.shape[1] * fr.shape[2]
    live = sc[0] > 0
    for ref, rows in ((fr, slice(0, h2)), (ha, slice(h2, out.shape[0]))):
        v = ref[...].reshape(rows.stop - rows.start, *out.shape[1:])
        out[rows] = jnp.where(live, v, jnp.full_like(v, EMPTY_FRAME))


def _final_kernel(sc, mine, other, got, grad, cw, sw, cb, sb, fg, acc):
    c = mine.shape[1]
    half = acc.shape[0] // 2
    z, x, core = _place(sc)
    blocks = 4
    rows = half // (2 * blocks)
    for ref, at_core in ((mine, core), (other, 1 - core)):
        for k in range(2 * blocks):
            side = x if k < blocks else 1 - x
            chip = 2 * lax.bitwise_xor(z, k % blocks) + side
            at = pl.multiple_of(at_core * half + chip * rows, 16)
            acc[pl.ds(at, rows)] = ref[k * rows : (k + 1) * rows].astype(F32)
    n27, n29 = 27 * c, 29 * c
    cw[...] = acc[:n27]
    sw[...] = acc[n27:n29]
    cb[...] = acc[n29 : n29 + 1]
    sb[...] = acc[n29 + 1 : n29 + 2]
    slots, frames, h, w, _ = grad.shape
    part = mine.shape[0] - half
    for s in range(slots):
        here = sc[0] - 1 == s
        for f in range(frames):
            low = f == 0
            a, b = mine[half:].astype(F32), other[half:].astype(F32)
            beyond = jnp.where(core == 0, a, b) if low else jnp.where(core == 0, b, a)
            beside = got[f * part : (f + 1) * part].astype(F32)
            came = jnp.where(core == 0, _first_live(beside, beyond), beyond)
            came = jnp.where(came < EMPTY_GRAD / 2, came, jnp.zeros_like(came)).reshape(h, w, c)
            fg[s, f] = (grad[s, f] + jnp.where(here, came, jnp.zeros_like(came))).astype(BF)


def _xor(x, k, n, axis):
    return lax.ppermute(x, axis, [(i, i ^ k) for i in range(n)])


def _latest_before(x, empty, axis, n, beside_x, beside_near, beside_far):
    index = lax.axis_index(axis)
    core, pair = index & 1, (index >> 1) & 1

    def newest(early, late):
        return jnp.where(late > empty / 2, early, late)

    def half(v):
        rows = v.shape[0] // 2
        return jnp.where(core == 0, v[:rows], v[rows:])

    other = _xor(x, 1, n, axis)
    a, b = half(x), half(other)
    chip = jnp.where(core == 0, newest(a, b), newest(b, a))
    beside = _xor(chip, 2, n, axis)
    quad = jnp.where(pair == 0, newest(chip, beside), newest(beside, chip))
    quad = beside_x(chip, quad)
    block, before, k = quad, jnp.full_like(quad, empty), 4
    while k < n:
        late = (index & k) > 0
        came = _xor(block, k, n, axis)
        if k == 4:
            came = beside_near(block, came)
        before = jnp.where(late, newest(came, before), before)
        if k == 8:
            before = beside_far(block, before)
        if 2 * k < n:
            block = jnp.where(late, newest(came, block), newest(block, came))
        k *= 2
    before = jnp.where(pair == 0, before, newest(before, beside))
    across = _xor(before, 1, n, axis)
    before = jnp.concatenate(
        [jnp.where(core == 0, before, across), jnp.where(core == 0, across, before)], axis=0
    )
    before = jnp.where(core == 0, before, newest(before, other))
    return jnp.where(before > empty / 2, jnp.zeros_like(before), before)


def _after(value, *earlier):
    return lax.optimization_barrier((value, *earlier))[0]


def body(
    n,
    frames,
    row_halo,
    clip_start,
    slab_counts,
    conv_weight,
    conv_bias,
    stride_weight,
    stride_bias,
    cotangent,
):
    axis = "tm"
    slots, _, h, w, c = frames.shape
    count = slab_counts[0]
    index = lax.axis_index(axis)
    chips = 8
    assert n % (2 * chips) == 0
    sc = jnp.concatenate(
        [
            slab_counts,
            clip_start,
            ((index >> 1) & (chips - 1)).reshape(1).astype(jnp.int32),
            (index & 1).reshape(1).astype(jnp.int32),
        ]
    )
    wt = conv_weight.reshape(27, c, c)
    cb, sb = conv_bias.reshape(1, c), stride_bias.reshape(1, c)
    unit = 16 * 2 * chips
    rows = -(-(29 * c + 2) // unit) * unit
    m = h * w
    conv_flops = 2 * m * 36 * c * 2 * c

    def newest_slot(i, sc):
        return (jnp.maximum(sc[0] - 1, 0), 0, 0, 0, 0)

    tail = pl.pallas_call(
        _tail_kernel,
        out_shape=jax.ShapeDtypeStruct((2 * h + 4, w, c), BF),
        grid_spec=pltpu.PrefetchScalarGridSpec(
            num_scalar_prefetch=1,
            grid=(1,),
            in_specs=[
                pl.BlockSpec((1, 2, h, w, c), newest_slot),
                pl.BlockSpec((1, 2, 2, w, c), newest_slot),
            ],
            out_specs=pl.BlockSpec((2 * h + 4, w, c), lambda i, sc: (0, 0, 0)),
        ),
        compiler_params=pltpu.CompilerParams(vmem_limit_bytes=8 << 20),
    )(
        slab_counts,
        *(pltpu.with_memory_space_constraint(v, pltpu.HBM) for v in (frames, row_halo)),
    )

    held = {}
    wide = ((slots - 1) * m, 2 * c)
    raw = [
        pltpu.with_memory_space_constraint(v, pltpu.HBM)
        for v in (frames, row_halo, cotangent, wt, cb, stride_weight, sb)
    ]
    windows = (3, slots - 1, 4, h + 2, w, c)

    def early_conv(start, follow):
        held["conv"] = _call(
            _early_conv_kernel,
            [
                jax.ShapeDtypeStruct(wide, F32),
                jax.ShapeDtypeStruct((wide[0], c), BF),
                jax.ShapeDtypeStruct(stride_weight.shape, BF),
                jax.ShapeDtypeStruct(sb.shape, F32),
            ],
            [_SMEM] + [_HBM] * len(raw),
            [pltpu.VMEM(v.shape, v.dtype) for v in raw[:5]]
            + [pltpu.VMEM(windows, BF), pltpu.SemaphoreType.DMA((len(raw),))],
            flops=(slots - 1) * conv_flops,
            moved=4 << 20,
        )(_after(sc, start), *raw)
        return _after(follow, held["conv"][0])

    def early_act(start, follow):
        pre, gout1, sw1, sb1 = held["conv"]
        held["early"] = _call(
            _early_act_kernel,
            [
                jax.ShapeDtypeStruct((slots - 1, h, w, c), BF),
                jax.ShapeDtypeStruct(wide, BF),
                jax.ShapeDtypeStruct(wide, BF),
            ],
            [_SMEM] + [_VMEM] * 4,
            moved=2 << 20,
            room=6,
        )(_after(sc, start), pre, gout1, sw1, sb1)
        return _after(follow, held["early"][1])

    def early_sums(start, follow):
        gout1 = held["conv"][1]
        _, g1, hid1 = held["early"]
        held["sums"] = _call(
            _early_sums_kernel,
            jax.ShapeDtypeStruct((rows, c), F32),
            [_SMEM, _HBM, _HBM] + [_VMEM] * 3,
            [pltpu.VMEM(windows, BF)]
            + [pltpu.VMEM(v.shape, BF) for v in raw[:2]]
            + [pltpu.SemaphoreType.DMA((2,))],
            flops=(slots - 1) * conv_flops,
            moved=4 << 20,
        )(_after(sc, start), raw[0], raw[1], g1, hid1, gout1)
        return _after(follow, held["sums"])

    arrived = _latest_before(tail, EMPTY_FRAME, axis, n, early_conv, early_act, early_sums)
    lat1, g1, _ = held["early"]

    def first(*shape):
        return pl.BlockSpec((1, *shape), lambda i: (0,) * (len(shape) + 1))

    half, carried = rows // 2, 2 * m
    lat0, g0, send, keep = _call(
        _late_kernel,
        [
            jax.ShapeDtypeStruct((h, w, c), BF),
            jax.ShapeDtypeStruct((m, 2 * c), BF),
            jax.ShapeDtypeStruct((half, c), BF),
            jax.ShapeDtypeStruct((half, c), F32),
        ],
        [_SMEM, first(2, h, w, c), first(2, 2, w, c), _VMEM, first(1, h, w, c)] + [_VMEM] * 5,
        [pltpu.VMEM((3, 1, 4, h + 2, w, c), BF), pltpu.VMEM((rows, c), F32)],
        flops=2 * conv_flops,
        moved=6 << 20,
        grid=(1,),
    )(sc, frames, row_halo, arrived, cotangent, wt, cb, stride_weight, sb, held["sums"])

    blocks = chips // 2
    piece = half // chips
    got = _xor(send, 1, n, axis)
    first_grad = _call(
        _carried_kernel,
        jax.ShapeDtypeStruct((carried, c), BF),
        [_SMEM, _VMEM, _VMEM],
        [pltpu.VMEM((3, 1, 2, h + 2, w, c), BF)],
        flops=conv_flops // 2,
        moved=1 << 20,
        room=8,
    )(sc, g0, wt)
    send_far, send_near, kept = _call(
        _across_x_kernel,
        [
            jax.ShapeDtypeStruct((2 * piece, c), BF),
            jax.ShapeDtypeStruct((2 * piece, c), BF),
            jax.ShapeDtypeStruct((blocks * piece, c), F32),
        ],
        [_SMEM] + [_VMEM] * 2,
        room=8,
    )(sc, _after(keep, first_grad), got)
    got_far = _xor(send_far, 2, n, axis)
    got_first = _xor(_after(first_grad, kept), 1, n, axis)
    core, pair = index & 1, (index >> 1) & 1

    def by(bit, a, b):
        return jnp.where(bit == 0, a, b)

    def by_half(bit, v):
        rows = v.shape[0] // 2
        return by(bit, v[:rows], v[rows:])

    def ordered(bit, ours, theirs):
        return by(bit, _first_live(ours, theirs), _first_live(theirs, ours))

    chip_first = ordered(core, by_half(core, first_grad), by_half(core, got_first))
    send_near = jnp.concatenate([send_near, chip_first], axis=0)
    got_near = _xor(send_near, 2, n, axis)
    grad = _call(
        _back_kernel,
        jax.ShapeDtypeStruct((slots, 2, h, w, c), F32),
        [_SMEM] + [_VMEM] * 3,
        [pltpu.VMEM((3, slots, 4, h + 2, w, c), BF)],
        flops=1,
        moved=1,
        room=24,
    )(_after(sc, send_near), g0, g1, wt)
    got_far = _after(got_far, grad)

    def summed(j, came):
        i = j % 2
        return kept[j * piece : (j + 1) * piece] + came[i * piece : (i + 1) * piece].astype(F32)

    outs = {j: summed(j, got_far).astype(BF) for j in (3, 2)}
    got_near = _after(got_near, outs[3], outs[2])
    outs[1] = summed(1, got_near).astype(BF)
    gots = {j: _xor(outs[j], 4 * j, n, axis) for j in (3, 2, 1)}
    beside_first = got_near[2 * piece :]
    lead = ordered(pair, by_half(pair, chip_first), by_half(pair, beside_first))
    near_lead = _xor(lead, 4, n, axis)
    mine = summed(0, _after(got_near, outs[1]))
    for j in (3, 2):
        mine = mine + gots[j].astype(F32)
    gots[1] = _after(gots[1], mine)
    mine = (mine + gots[1].astype(F32)).astype(BF)
    k = 2 * chips
    while k < n:
        mine = (mine.astype(F32) + _xor(mine, k, n, axis).astype(F32)).astype(BF)
        k *= 2
    others = {j: _xor(mine, 4 * j, n, axis) for j in (3, 2, 1)}
    x_own = _xor(mine, 2, n, axis)
    x_near = _xor(others[1], 2, n, axis)
    x_far = _xor(jnp.concatenate([others[2], others[3]], axis=0), 2, n, axis)
    beyond = by(index & 4, near_lead, jnp.full_like(lead, EMPTY_GRAD))
    lead, k = _after(ordered(index & 4, lead, near_lead), x_own), 8
    while k < n:
        came = _xor(lead, k, n, axis)
        beyond = by(index & k, _first_live(beyond, came), beyond)
        if 2 * k < n:
            lead = ordered(index & k, lead, came)
        k *= 2
    theirs = _xor(beyond, 2, n, axis)
    beyond = jnp.concatenate([by(pair, beyond, theirs), by(pair, theirs, beyond)], axis=0)
    beyond = by(pair, _first_live(beside_first, beyond), beyond)
    ours = jnp.concatenate(
        [mine, others[1], others[2], others[3], x_own, x_near, x_far, beyond], axis=0
    )
    other = _xor(ours, 1, n, axis)
    cwg, swg, cbg, sbg, frames_grad = _call(
        _final_kernel,
        [
            jax.ShapeDtypeStruct((27 * c, c), F32),
            jax.ShapeDtypeStruct((2 * c, c), F32),
            jax.ShapeDtypeStruct((1, c), F32),
            jax.ShapeDtypeStruct((1, c), F32),
            jax.ShapeDtypeStruct((slots, 2, h, w, c), BF),
        ],
        [_SMEM] + [_VMEM] * 4,
        [pltpu.VMEM((rows, c), F32)],
        room=12,
    )(sc, ours, other, got_first, grad)
    latents = jnp.concatenate([lat0[None], lat1], axis=0)[:, None]
    return (
        latents,
        frames_grad,
        cwg.reshape(3, 3, 3, c, c),
        cbg[0],
        swg.reshape(2, c, c),
        sbg[0],
    )


def solution(mesh):
    split = P(("groups", "tm"))
    return jax.shard_map(
        functools.partial(body, mesh.shape["tm"]),
        mesh=mesh,
        in_specs=(split, split, split, split, P(), P(), P(), P(), split),
        out_specs=(split, split, P("groups"), P("groups"), P("groups"), P("groups")),
        check_vma=False,
    )
```

```python
import functools

import jax
import jax.numpy as jnp
from jax import lax
from jax.experimental import pallas as pl
from jax.experimental.pallas import tpu as pltpu
from jax.sharding import PartitionSpec as P

BF = jnp.bfloat16
F32 = jnp.float32
EMPTY_FRAME = 100.0
EMPTY_GRAD = 1e30

_VMEM = pl.BlockSpec(memory_space=pltpu.VMEM)
_SMEM = pl.BlockSpec(memory_space=pltpu.SMEM)
_HBM = pl.BlockSpec(memory_space=pltpu.HBM)


def _call(kernel, out_shape, in_specs, scratch=(), flops=0, moved=0, room=16, grid=()):
    return pl.pallas_call(
        kernel,
        out_shape=out_shape,
        grid=grid,
        in_specs=in_specs,
        out_specs=jax.tree.map(lambda _: _VMEM, out_shape),
        scratch_shapes=list(scratch),
        compiler_params=pltpu.CompilerParams(vmem_limit_bytes=room << 20),
        cost_estimate=pl.CostEstimate(flops=flops, bytes_accessed=moved, transcendentals=0),
    )


def _put(xk, at, rows, value):
    n, w, c = value.shape
    flat = value.astype(F32).reshape(n * w, c)
    col = lax.broadcasted_iota(jnp.int32, (n * w, c), 0) % w
    right = jnp.where(col == 0, 0.0, pltpu.roll(flat, 1, 0))
    left = jnp.where(col == w - 1, 0.0, pltpu.roll(flat, n * w - 1, 0))
    for kw, shifted in enumerate((right, flat, left)):
        xk[(kw, *at, rows)] = shifted.astype(BF).reshape(n, w, c)


def _window(xk, kw, j, kh, h):
    v = xk[kw, :, j, kh : kh + h]
    return v.reshape(v.shape[0] * v.shape[1] * v.shape[2], v.shape[3])


def _wide(xk, j, h):
    return jnp.concatenate(
        [_window(xk, kw, j, kh, h) for kh in range(3) for kw in range(3)], axis=1
    )


def _conv(xk, w_ref, h):
    c = w_ref.shape[-1]
    zero = jnp.zeros((c, c), BF)
    lhs = jnp.concatenate([_wide(xk, j, h) for j in range(4)], axis=1)
    rhs = []
    for j in range(4):
        for tap in range(9):
            rhs.append(
                jnp.concatenate(
                    [w_ref[(j - t) * 9 + tap] if 0 <= j - t <= 2 else zero for t in range(2)],
                    axis=1,
                )
            )
    return jnp.dot(lhs, jnp.concatenate(rhs, axis=0), preferred_element_type=F32)


def _conv_back(xk, w_ref, h, frames=range(4), base=0):
    c = w_ref.shape[-1]
    zero = jnp.zeros((c, c), BF)
    lhs = jnp.concatenate([_wide(xk, j - base, h) for j in frames], axis=1)
    rhs = []
    for f in range(2):
        row = []
        for j in frames:
            for tap in range(9):
                kt = 2 - (j - f)
                row.append(w_ref[kt * 9 + 8 - tap] if 0 <= kt <= 2 else zero)
        rhs.append(jnp.concatenate(row, axis=1))
    return lax.dot_general(
        lhs, jnp.concatenate(rhs, axis=0), (((1,), (1,)), ((), ())), preferred_element_type=F32
    )


def _activate(pre, gout, sw_ref, sb_ref):
    s = 1.0 / (1.0 + jnp.exp(-pre))
    hidden = (pre * s).astype(BF)
    sw = jnp.concatenate([sw_ref[0], sw_ref[1]], axis=0)
    lat = jnp.dot(hidden, sw, preferred_element_type=F32) + sb_ref[...]
    gh = lax.dot_general(gout, sw, (((1,), (1,)), ((), ())), preferred_element_type=F32)
    g = (gh * s * (1.0 + pre * (1.0 - s))).astype(BF)
    return lat, g, hidden


def _conv_bias(xk, w_ref, cb_ref, h):
    return _conv(xk, w_ref, h) + jnp.concatenate([cb_ref[...], cb_ref[...]], axis=1)


def _weight_grads(xk, g, hidden, gout, h, add):
    c = gout.shape[-1]
    parts = []
    for j in range(4):
        lhs = _wide(xk, j, h)
        parts.append(
            lax.dot_general(lhs, g, (((0,), (0,)), ((), ())), preferred_element_type=F32)
        )
    for kt in range(3):
        add(kt, parts[kt][:, :c] + parts[kt + 1][:, c:])
    sg = lax.dot_general(hidden, gout, (((0,), (0,)), ((), ())), preferred_element_type=F32)
    g32 = jnp.sum(g.astype(F32), axis=0, keepdims=True)
    add(3, sg)
    add(4, g32[:, :c] + g32[:, c:])
    add(5, jnp.sum(gout.astype(F32), axis=0, keepdims=True))


def _fill_early(sc, fr, ha, xk):
    slots, _, h, w, c = fr.shape
    for s in range(slots):
        for f in range(2):
            spots = [(s - 1, f + 2, None)] if s > 0 else []
            if s + 1 < slots:
                spots.append((s, f, sc[1 + s + 1] == 0))
            for slot, j, keep in spots:
                a, b = fr[s, f], ha[s, f]
                if keep is not None:
                    a = jnp.where(keep, a, jnp.zeros_like(a))
                    b = jnp.where(keep, b, jnp.zeros_like(b))
                _put(xk, (slot, j), slice(1, 1 + h), a)
                _put(xk, (slot, j), slice(0, 1), b[:1])
                _put(xk, (slot, j), slice(h + 1, h + 2), b[1:])


def _early_gout(sc, co):
    slots, _, h, w, c = co.shape
    return jnp.concatenate(
        [
            jnp.where(s < sc[0], co[s, 0], jnp.zeros_like(co[s, 0])).reshape(h * w, c)
            for s in range(1, slots)
        ],
        axis=0,
    )


def _early_conv_kernel(
    sc, frh, hah, coh, wh, cbh, swh, sbh, pre_ref, gout_ref, sw, sb, fr, ha, co, w_ref, cb, xk, sems
):
    h = fr.shape[2]
    pairs = ((frh, fr), (hah, ha), (coh, co), (wh, w_ref), (cbh, cb), (swh, sw), (sbh, sb))
    copies = [pltpu.make_async_copy(a, b, sems.at[i]) for i, (a, b) in enumerate(pairs)]
    for copy in copies:
        copy.start()
    copies[0].wait()
    copies[1].wait()
    _fill_early(sc, fr, ha, xk)
    copies[2].wait()
    gout_ref[...] = _early_gout(sc, co)
    for copy in copies[3:]:
        copy.wait()
    pre_ref[...] = _conv_bias(xk, w_ref, cb, h)


def _early_act_kernel(sc, pre_ref, gout_ref, sw, sb, lat_ref, g_ref, hid_ref):
    slots, h, w, c = lat_ref.shape
    lat, g, hidden = _activate(pre_ref[...], gout_ref[...], sw, sb)
    for s in range(slots):
        part = lat[s * h * w : (s + 1) * h * w]
        filled = s + 1 < sc[0]
        lat_ref[s] = jnp.where(filled, part, jnp.zeros_like(part)).astype(BF).reshape(h, w, c)
    g_ref[...] = g
    hid_ref[...] = hidden


def _early_sums_kernel(sc, frh, hah, g_ref, hid_ref, gout_ref, acc, xk, fr, ha, sems):
    copies = [
        pltpu.make_async_copy(a, b, sems.at[i]) for i, (a, b) in enumerate(((frh, fr), (hah, ha)))
    ]
    for copy in copies:
        copy.start()
    for copy in copies:
        copy.wait()
    _fill_early(sc, fr, ha, xk)
    _, _, h, _, c = fr.shape
    n9 = 9 * c

    def add(kind, value):
        if kind < 3:
            acc[kind * n9 : (kind + 1) * n9] = value
        elif kind == 3:
            acc[3 * n9 : 3 * n9 + 2 * c] = value
        else:
            at = 3 * n9 + 2 * c + (kind - 4)
            acc[at : at + 1] = value

    acc[3 * n9 + 2 * c :] = jnp.zeros((acc.shape[0] - 3 * n9 - 2 * c, c), F32)
    _weight_grads(xk, g_ref[...], hid_ref[...], gout_ref[...], h, add)


def _late_kernel(
    sc, frs, has, tail, cos, w_ref, cb, sw, sb, early, lat_ref, g_ref, send, keep, xk, acc
):
    fr, ha, co = frs.at[0], has.at[0], cos.at[0]
    _, h, w, c = fr.shape
    on = sc[1] == 0
    for f in range(2):
        _put(xk, (0, f + 2), slice(1, 1 + h), fr[f])
        _put(xk, (0, f + 2), slice(0, 1), ha[f, :1])
        _put(xk, (0, f + 2), slice(h + 1, h + 2), ha[f, 1:])
        a = tail[f * h : (f + 1) * h]
        b = tail[2 * h + 2 * f : 2 * h + 2 * f + 2]
        a = jnp.where(on, a, jnp.zeros_like(a))
        b = jnp.where(on, b, jnp.zeros_like(b))
        _put(xk, (0, f), slice(1, 1 + h), a)
        _put(xk, (0, f), slice(0, 1), b[:1])
        _put(xk, (0, f), slice(h + 1, h + 2), b[1:])
    filled = sc[0] > 0
    gout = jnp.where(filled, co[0], jnp.zeros_like(co[0])).reshape(h * w, c)
    lat, g, hidden = _activate(_conv_bias(xk, w_ref, cb, h), gout, sw, sb)
    lat_ref[...] = jnp.where(filled, lat, jnp.zeros_like(lat)).astype(BF).reshape(h, w, c)
    g_ref[...] = g
    n9 = 9 * c

    def add(kind, value):
        if kind < 3:
            rows = slice(kind * n9, (kind + 1) * n9)
        elif kind == 3:
            rows = slice(3 * n9, 3 * n9 + 2 * c)
        else:
            at = 3 * n9 + 2 * c + (kind - 4)
            rows = slice(at, at + 1)
        acc[rows] = early[rows] + value

    tail_rows = slice(3 * n9 + 2 * c, acc.shape[0])
    acc[tail_rows] = early[tail_rows]

    @pl.when(sc[0] >= 0)
    def _():
        _weight_grads(xk, g, hidden, gout, h, add)

        half = keep.shape[0]
        core = sc[sc.shape[0] - 1]
        send[...] = acc[pl.ds(pl.multiple_of((1 - core) * half, 16), half)].astype(BF)
        keep[...] = acc[pl.ds(pl.multiple_of(core * half, 16), half)]


def _carried_kernel(sc, g_ref, w_ref, out, xk):
    _, _, _, h, w, c = xk.shape
    h = h - 2
    on = sc[1] == 0
    for t in range(2):
        for kw in range(3):
            xk[kw, 0, t, 0:1] = jnp.zeros((1, w, c), BF)
            xk[kw, 0, t, h + 1 : h + 2] = jnp.zeros((1, w, c), BF)
        v = g_ref[:, t * c : (t + 1) * c].reshape(h, w, c)
        _put(xk, (0, t), slice(1, 1 + h), jnp.where(on, v, jnp.zeros_like(v)))
    back = _conv_back(xk, w_ref, h, (2, 3), 2)
    back = jnp.where(sc[0] > 0, back, jnp.full_like(back, EMPTY_GRAD)).astype(BF)
    for t in range(2):
        out[t * h * w : (t + 1) * h * w] = back[:, t * c : (t + 1) * c]


def _back_kernel(sc, g0, g1, w_ref, out_ref, xk):
    slots, _, h, w, c = out_ref.shape
    m = h * w
    zero = jnp.zeros((1, w, c), BF)
    for kw in range(3):
        for j in range(4):
            for s in range(slots):
                xk[kw, s, j, 0:1] = zero
                xk[kw, s, j, h + 1 : h + 2] = zero
    for f in range(2):
        for kw in range(3):
            xk[kw, slots - 1, f + 2, 1 : 1 + h] = jnp.zeros((h, w, c), BF)
        lanes = slice(f * c, (f + 1) * c)
        for s in range(slots):
            v = g0[:, lanes] if s == 0 else g1[(s - 1) * m : s * m, lanes]
            v = v.reshape(h, w, c)
            _put(xk, (s, f), slice(1, 1 + h), v)
            if s > 0:
                on = sc[1 + s] == 0
                _put(xk, (s - 1, f + 2), slice(1, 1 + h), jnp.where(on, v, jnp.zeros_like(v)))
    out = _conv_back(xk, w_ref, h)
    for f in range(2):
        out_ref[:, f] = out[:, f * c : (f + 1) * c].reshape(slots, h, w, c)


def _first_live(a, b):
    return jnp.where(a.astype(F32) < EMPTY_GRAD / 2, a, b)


def _place(sc):
    chip, core = sc[sc.shape[0] - 2], sc[sc.shape[0] - 1]
    return lax.shift_right_logical(chip, 1), lax.bitwise_and(chip, 1), core


def _across_x_kernel(sc, keep, got, send_far, send_near, kept):
    z, x, _ = _place(sc)
    half = keep.shape[0]
    blocks = 4
    rows = half // (2 * blocks)

    def piece(j, side):
        p = 2 * lax.bitwise_xor(z, j) + side
        at = pl.ds(pl.multiple_of(p * rows, 16), rows)
        return keep[at] + got[at].astype(F32)

    for j in range(blocks):
        kept[j * rows : (j + 1) * rows] = piece(j, x)
        send, i = (send_near, j) if j < 2 else (send_far, j - 2)
        send[i * rows : (i + 1) * rows] = piece(j, 1 - x).astype(BF)


def _tail_kernel(sc, fr, ha, out):
    h2 = fr.shape[1] * fr.shape[2]
    live = sc[0] > 0
    for ref, rows in ((fr, slice(0, h2)), (ha, slice(h2, out.shape[0]))):
        v = ref[...].reshape(rows.stop - rows.start, *out.shape[1:])
        out[rows] = jnp.where(live, v, jnp.full_like(v, EMPTY_FRAME))


def _final_kernel(sc, mine, other, got, grad, cw, sw, cb, sb, fg, acc):
    c = mine.shape[1]
    half = acc.shape[0] // 2
    z, x, core = _place(sc)
    blocks = 4
    rows = half // (2 * blocks)
    for ref, at_core in ((mine, core), (other, 1 - core)):
        for k in range(2 * blocks):
            side = x if k < blocks else 1 - x
            chip = 2 * lax.bitwise_xor(z, k % blocks) + side
            at = pl.multiple_of(at_core * half + chip * rows, 16)
            acc[pl.ds(at, rows)] = ref[k * rows : (k + 1) * rows].astype(F32)
    n27, n29 = 27 * c, 29 * c
    cw[...] = acc[:n27]
    sw[...] = acc[n27:n29]
    cb[...] = acc[n29 : n29 + 1]
    sb[...] = acc[n29 + 1 : n29 + 2]
    slots, frames, h, w, _ = grad.shape
    part = mine.shape[0] - half
    for s in range(slots):
        here = sc[0] - 1 == s
        for f in range(frames):
            low = f == 0
            a, b = mine[half:].astype(F32), other[half:].astype(F32)
            beyond = jnp.where(core == 0, a, b) if low else jnp.where(core == 0, b, a)
            beside = got[f * part : (f + 1) * part].astype(F32)
            came = jnp.where(core == 0, _first_live(beside, beyond), beyond)
            came = jnp.where(came < EMPTY_GRAD / 2, came, jnp.zeros_like(came)).reshape(h, w, c)
            fg[s, f] = (grad[s, f] + jnp.where(here, came, jnp.zeros_like(came))).astype(BF)


def _xor(x, k, n, axis):
    return lax.ppermute(x, axis, [(i, i ^ k) for i in range(n)])


def _latest_before(x, empty, axis, n, beside_x, beside_near, beside_far):
    index = lax.axis_index(axis)
    core, pair = index & 1, (index >> 1) & 1

    def newest(early, late):
        return jnp.where(late > empty / 2, early, late)

    def half(v):
        rows = v.shape[0] // 2
        return jnp.where(core == 0, v[:rows], v[rows:])

    other = _xor(x, 1, n, axis)
    a, b = half(x), half(other)
    chip = jnp.where(core == 0, newest(a, b), newest(b, a))
    beside = _xor(chip, 2, n, axis)
    quad = jnp.where(pair == 0, newest(chip, beside), newest(beside, chip))
    quad = beside_x(chip, quad)
    block, before, k = quad, jnp.full_like(quad, empty), 4
    while k < n:
        late = (index & k) > 0
        came = _xor(block, k, n, axis)
        if k == 4:
            came = beside_near(block, came)
        before = jnp.where(late, newest(came, before), before)
        if k == 8:
            before = beside_far(block, before)
        if 2 * k < n:
            block = jnp.where(late, newest(came, block), newest(block, came))
        k *= 2
    before = jnp.where(pair == 0, before, newest(before, beside))
    across = _xor(before, 1, n, axis)
    before = jnp.concatenate(
        [jnp.where(core == 0, before, across), jnp.where(core == 0, across, before)], axis=0
    )
    before = jnp.where(core == 0, before, newest(before, other))
    return jnp.where(before > empty / 2, jnp.zeros_like(before), before)


def _after(value, *earlier):
    return lax.optimization_barrier((value, *earlier))[0]


def body(
    n,
    frames,
    row_halo,
    clip_start,
    slab_counts,
    conv_weight,
    conv_bias,
    stride_weight,
    stride_bias,
    cotangent,
):
    axis = "tm"
    slots, _, h, w, c = frames.shape
    count = slab_counts[0]
    index = lax.axis_index(axis)
    chips = 8
    assert n % (2 * chips) == 0
    sc = jnp.concatenate(
        [
            slab_counts,
            clip_start,
            ((index >> 1) & (chips - 1)).reshape(1).astype(jnp.int32),
            (index & 1).reshape(1).astype(jnp.int32),
        ]
    )
    wt = conv_weight.reshape(27, c, c)
    cb, sb = conv_bias.reshape(1, c), stride_bias.reshape(1, c)
    unit = 16 * 2 * chips
    rows = -(-(29 * c + 2) // unit) * unit
    m = h * w
    conv_flops = 2 * m * 36 * c * 2 * c

    def newest_slot(i, sc):
        return (jnp.maximum(sc[0] - 1, 0), 0, 0, 0, 0)

    tail = pl.pallas_call(
        _tail_kernel,
        out_shape=jax.ShapeDtypeStruct((2 * h + 4, w, c), BF),
        grid_spec=pltpu.PrefetchScalarGridSpec(
            num_scalar_prefetch=1,
            grid=(1,),
            in_specs=[
                pl.BlockSpec((1, 2, h, w, c), newest_slot),
                pl.BlockSpec((1, 2, 2, w, c), newest_slot),
            ],
            out_specs=pl.BlockSpec((2 * h + 4, w, c), lambda i, sc: (0, 0, 0)),
        ),
        compiler_params=pltpu.CompilerParams(vmem_limit_bytes=8 << 20),
    )(
        slab_counts,
        *(pltpu.with_memory_space_constraint(v, pltpu.HBM) for v in (frames, row_halo)),
    )

    held = {}
    wide = ((slots - 1) * m, 2 * c)
    raw = [
        pltpu.with_memory_space_constraint(v, pltpu.HBM)
        for v in (frames, row_halo, cotangent, wt, cb, stride_weight, sb)
    ]
    windows = (3, slots - 1, 4, h + 2, w, c)

    def early_conv(start, follow):
        held["conv"] = _call(
            _early_conv_kernel,
            [
                jax.ShapeDtypeStruct(wide, F32),
                jax.ShapeDtypeStruct((wide[0], c), BF),
                jax.ShapeDtypeStruct(stride_weight.shape, BF),
                jax.ShapeDtypeStruct(sb.shape, F32),
            ],
            [_SMEM] + [_HBM] * len(raw),
            [pltpu.VMEM(v.shape, v.dtype) for v in raw[:5]]
            + [pltpu.VMEM(windows, BF), pltpu.SemaphoreType.DMA((len(raw),))],
            flops=(slots - 1) * conv_flops,
            moved=4 << 20,
        )(_after(sc, start), *raw)
        return _after(follow, held["conv"][0])

    def early_act(start, follow):
        pre, gout1, sw1, sb1 = held["conv"]
        held["early"] = _call(
            _early_act_kernel,
            [
                jax.ShapeDtypeStruct((slots - 1, h, w, c), BF),
                jax.ShapeDtypeStruct(wide, BF),
                jax.ShapeDtypeStruct(wide, BF),
            ],
            [_SMEM] + [_VMEM] * 4,
            moved=2 << 20,
            room=6,
        )(_after(sc, start), pre, gout1, sw1, sb1)
        return _after(follow, held["early"][1])

    def early_sums(start, follow):
        gout1 = held["conv"][1]
        _, g1, hid1 = held["early"]
        held["sums"] = _call(
            _early_sums_kernel,
            jax.ShapeDtypeStruct((rows, c), F32),
            [_SMEM, _HBM, _HBM] + [_VMEM] * 3,
            [pltpu.VMEM(windows, BF)]
            + [pltpu.VMEM(v.shape, BF) for v in raw[:2]]
            + [pltpu.SemaphoreType.DMA((2,))],
            flops=(slots - 1) * conv_flops,
            moved=4 << 20,
        )(_after(sc, start), raw[0], raw[1], g1, hid1, gout1)
        return _after(follow, held["sums"])

    arrived = _latest_before(tail, EMPTY_FRAME, axis, n, early_conv, early_act, early_sums)
    lat1, g1, _ = held["early"]

    def first(*shape):
        return pl.BlockSpec((1, *shape), lambda i: (0,) * (len(shape) + 1))

    half, carried = rows // 2, 2 * m
    lat0, g0, send, keep = _call(
        _late_kernel,
        [
            jax.ShapeDtypeStruct((h, w, c), BF),
            jax.ShapeDtypeStruct((m, 2 * c), BF),
            jax.ShapeDtypeStruct((half, c), BF),
            jax.ShapeDtypeStruct((half, c), F32),
        ],
        [_SMEM, first(2, h, w, c), first(2, 2, w, c), _VMEM, first(1, h, w, c)] + [_VMEM] * 5,
        [pltpu.VMEM((3, 1, 4, h + 2, w, c), BF), pltpu.VMEM((rows, c), F32)],
        flops=2 * conv_flops,
        moved=6 << 20,
        grid=(1,),
    )(sc, frames, row_halo, arrived, cotangent, wt, cb, stride_weight, sb, held["sums"])

    blocks = chips // 2
    piece = half // chips
    got = _xor(send, 1, n, axis)
    first_grad = _call(
        _carried_kernel,
        jax.ShapeDtypeStruct((carried, c), BF),
        [_SMEM, _VMEM, _VMEM],
        [pltpu.VMEM((3, 1, 2, h + 2, w, c), BF)],
        flops=conv_flops // 2,
        moved=1 << 20,
        room=8,
    )(sc, g0, wt)
    send_far, send_near, kept = _call(
        _across_x_kernel,
        [
            jax.ShapeDtypeStruct((2 * piece, c), BF),
            jax.ShapeDtypeStruct((2 * piece, c), BF),
            jax.ShapeDtypeStruct((blocks * piece, c), F32),
        ],
        [_SMEM] + [_VMEM] * 2,
        room=8,
    )(sc, _after(keep, first_grad), got)
    got_far = _xor(send_far, 2, n, axis)
    got_first = _xor(_after(first_grad, kept), 1, n, axis)
    core, pair = index & 1, (index >> 1) & 1

    def by(bit, a, b):
        return jnp.where(bit == 0, a, b)

    def by_half(bit, v):
        rows = v.shape[0] // 2
        return by(bit, v[:rows], v[rows:])

    def ordered(bit, ours, theirs):
        return by(bit, _first_live(ours, theirs), _first_live(theirs, ours))

    chip_first = ordered(core, by_half(core, first_grad), by_half(core, got_first))
    send_near = jnp.concatenate([send_near, chip_first], axis=0)
    got_near = _xor(send_near, 2, n, axis)
    grad = _call(
        _back_kernel,
        jax.ShapeDtypeStruct((slots, 2, h, w, c), F32),
        [_SMEM] + [_VMEM] * 3,
        [pltpu.VMEM((3, slots, 4, h + 2, w, c), BF)],
        flops=1,
        moved=1,
        room=24,
    )(_after(sc, send_near), g0, g1, wt)
    got_far = _after(got_far, grad)

    def summed(j, came):
        i = j % 2
        return kept[j * piece : (j + 1) * piece] + came[i * piece : (i + 1) * piece].astype(F32)

    outs = {j: summed(j, got_far).astype(BF) for j in (3, 2)}
    got_near = _after(got_near, outs[3], outs[2])
    outs[1] = summed(1, got_near).astype(BF)
    gots = {j: _xor(outs[j], 4 * j, n, axis) for j in (3, 2, 1)}
    beside_first = got_near[2 * piece :]
    lead = ordered(pair, by_half(pair, chip_first), by_half(pair, beside_first))
    near_lead = _xor(lead, 4, n, axis)
    mine = summed(0, _after(got_near, outs[1]))
    for j in (3, 2):
        mine = mine + gots[j].astype(F32)
    gots[1] = _after(gots[1], mine)
    mine = (mine + gots[1].astype(F32)).astype(BF)
    k = 2 * chips
    while k < n:
        mine = (mine.astype(F32) + _xor(mine, k, n, axis).astype(F32)).astype(BF)
        k *= 2
    others = {j: _xor(mine, 4 * j, n, axis) for j in (1, 3, 2)}
    x_near = _xor(jnp.concatenate([mine, others[1]], axis=0), 2, n, axis)
    x_far = _xor(jnp.concatenate([others[2], others[3]], axis=0), 2, n, axis)
    beyond = by(index & 4, near_lead, jnp.full_like(lead, EMPTY_GRAD))
    lead, k = _after(ordered(index & 4, lead, near_lead), others[1]), 8
    while k < n:
        came = _xor(lead, k, n, axis)
        beyond = by(index & k, _first_live(beyond, came), beyond)
        if 2 * k < n:
            lead = ordered(index & k, lead, came)
        k *= 2
    theirs = _xor(beyond, 2, n, axis)
    beyond = jnp.concatenate([by(pair, beyond, theirs), by(pair, theirs, beyond)], axis=0)
    beyond = by(pair, _first_live(beside_first, beyond), beyond)
    ours = jnp.concatenate(
        [mine, others[1], others[2], others[3], x_near, x_far, beyond], axis=0
    )
    other = _xor(ours, 1, n, axis)
    cwg, swg, cbg, sbg, frames_grad = _call(
        _final_kernel,
        [
            jax.ShapeDtypeStruct((27 * c, c), F32),
            jax.ShapeDtypeStruct((2 * c, c), F32),
            jax.ShapeDtypeStruct((1, c), F32),
            jax.ShapeDtypeStruct((1, c), F32),
            jax.ShapeDtypeStruct((slots, 2, h, w, c), BF),
        ],
        [_SMEM] + [_VMEM] * 4,
        [pltpu.VMEM((rows, c), F32)],
        room=12,
    )(sc, ours, other, got_first, grad)
    latents = jnp.concatenate([lat0[None], lat1], axis=0)[:, None]
    return (
        latents,
        frames_grad,
        cwg.reshape(3, 3, 3, c, c),
        cbg[0],
        swg.reshape(2, c, c),
        sbg[0],
    )


def solution(mesh):
    split = P(("groups", "tm"))
    return jax.shard_map(
        functools.partial(body, mesh.shape["tm"]),
        mesh=mesh,
        in_specs=(split, split, split, split, P(), P(), P(), P(), split),
        out_specs=(split, split, P("groups"), P("groups"), P("groups"), P("groups")),
        check_vma=False,
    )
```

```python
import functools

import jax
import jax.numpy as jnp
from jax import lax
from jax.experimental import pallas as pl
from jax.experimental.pallas import tpu as pltpu
from jax.sharding import PartitionSpec as P

BF = jnp.bfloat16
F32 = jnp.float32
EMPTY_FRAME = 100.0
EMPTY_GRAD = 1e30

_VMEM = pl.BlockSpec(memory_space=pltpu.VMEM)
_SMEM = pl.BlockSpec(memory_space=pltpu.SMEM)
_HBM = pl.BlockSpec(memory_space=pltpu.HBM)


def _call(kernel, out_shape, in_specs, scratch=(), flops=0, moved=0, room=16, grid=()):
    return pl.pallas_call(
        kernel,
        out_shape=out_shape,
        grid=grid,
        in_specs=in_specs,
        out_specs=jax.tree.map(lambda _: _VMEM, out_shape),
        scratch_shapes=list(scratch),
        compiler_params=pltpu.CompilerParams(vmem_limit_bytes=room << 20),
        cost_estimate=pl.CostEstimate(flops=flops, bytes_accessed=moved, transcendentals=0),
    )


def _put(xk, at, rows, value):
    n, w, c = value.shape
    flat = value.astype(F32).reshape(n * w, c)
    col = lax.broadcasted_iota(jnp.int32, (n * w, c), 0) % w
    right = jnp.where(col == 0, 0.0, pltpu.roll(flat, 1, 0))
    left = jnp.where(col == w - 1, 0.0, pltpu.roll(flat, n * w - 1, 0))
    for kw, shifted in enumerate((right, flat, left)):
        xk[(kw, *at, rows)] = shifted.astype(BF).reshape(n, w, c)


def _window(xk, kw, j, kh, h):
    v = xk[kw, :, j, kh : kh + h]
    return v.reshape(v.shape[0] * v.shape[1] * v.shape[2], v.shape[3])


def _wide(xk, j, h):
    return jnp.concatenate(
        [_window(xk, kw, j, kh, h) for kh in range(3) for kw in range(3)], axis=1
    )


def _conv(xk, w_ref, h):
    c = w_ref.shape[-1]
    zero = jnp.zeros((c, c), BF)
    lhs = jnp.concatenate([_wide(xk, j, h) for j in range(4)], axis=1)
    rhs = []
    for j in range(4):
        for tap in range(9):
            rhs.append(
                jnp.concatenate(
                    [w_ref[(j - t) * 9 + tap] if 0 <= j - t <= 2 else zero for t in range(2)],
                    axis=1,
                )
            )
    return jnp.dot(lhs, jnp.concatenate(rhs, axis=0), preferred_element_type=F32)


def _conv_back(xk, w_ref, h, frames=range(4), base=0):
    c = w_ref.shape[-1]
    zero = jnp.zeros((c, c), BF)
    lhs = jnp.concatenate([_wide(xk, j - base, h) for j in frames], axis=1)
    rhs = []
    for f in range(2):
        row = []
        for j in frames:
            for tap in range(9):
                kt = 2 - (j - f)
                row.append(w_ref[kt * 9 + 8 - tap] if 0 <= kt <= 2 else zero)
        rhs.append(jnp.concatenate(row, axis=1))
    return lax.dot_general(
        lhs, jnp.concatenate(rhs, axis=0), (((1,), (1,)), ((), ())), preferred_element_type=F32
    )


def _activate(pre, gout, sw_ref, sb_ref):
    s = 1.0 / (1.0 + jnp.exp(-pre))
    hidden = (pre * s).astype(BF)
    sw = jnp.concatenate([sw_ref[0], sw_ref[1]], axis=0)
    lat = jnp.dot(hidden, sw, preferred_element_type=F32) + sb_ref[...]
    gh = lax.dot_general(gout, sw, (((1,), (1,)), ((), ())), preferred_element_type=F32)
    g = (gh * s * (1.0 + pre * (1.0 - s))).astype(BF)
    return lat, g, hidden


def _conv_bias(xk, w_ref, cb_ref, h):
    return _conv(xk, w_ref, h) + jnp.concatenate([cb_ref[...], cb_ref[...]], axis=1)


def _weight_grads(xk, g, hidden, gout, h, add):
    c = gout.shape[-1]
    parts = []
    for j in range(4):
        lhs = _wide(xk, j, h)
        parts.append(
            lax.dot_general(lhs, g, (((0,), (0,)), ((), ())), preferred_element_type=F32)
        )
    for kt in range(3):
        add(kt, parts[kt][:, :c] + parts[kt + 1][:, c:])
    sg = lax.dot_general(hidden, gout, (((0,), (0,)), ((), ())), preferred_element_type=F32)
    g32 = jnp.sum(g.astype(F32), axis=0, keepdims=True)
    add(3, sg)
    add(4, g32[:, :c] + g32[:, c:])
    add(5, jnp.sum(gout.astype(F32), axis=0, keepdims=True))


def _fill_early(sc, fr, ha, xk):
    slots, _, h, w, c = fr.shape
    for s in range(slots):
        for f in range(2):
            spots = [(s - 1, f + 2, None)] if s > 0 else []
            if s + 1 < slots:
                spots.append((s, f, sc[1 + s + 1] == 0))
            for slot, j, keep in spots:
                a, b = fr[s, f], ha[s, f]
                if keep is not None:
                    a = jnp.where(keep, a, jnp.zeros_like(a))
                    b = jnp.where(keep, b, jnp.zeros_like(b))
                _put(xk, (slot, j), slice(1, 1 + h), a)
                _put(xk, (slot, j), slice(0, 1), b[:1])
                _put(xk, (slot, j), slice(h + 1, h + 2), b[1:])


def _early_gout(sc, co):
    slots, _, h, w, c = co.shape
    return jnp.concatenate(
        [
            jnp.where(s < sc[0], co[s, 0], jnp.zeros_like(co[s, 0])).reshape(h * w, c)
            for s in range(1, slots)
        ],
        axis=0,
    )


def _early_conv_kernel(
    sc, frh, hah, coh, wh, cbh, swh, sbh, pre_ref, gout_ref, sw, sb, fr, ha, co, w_ref, cb, xk, sems
):
    h = fr.shape[2]
    pairs = ((frh, fr), (hah, ha), (coh, co), (wh, w_ref), (cbh, cb), (swh, sw), (sbh, sb))
    copies = [pltpu.make_async_copy(a, b, sems.at[i]) for i, (a, b) in enumerate(pairs)]
    for copy in copies:
        copy.start()
    copies[0].wait()
    copies[1].wait()
    _fill_early(sc, fr, ha, xk)
    copies[2].wait()
    gout_ref[...] = _early_gout(sc, co)
    for copy in copies[3:]:
        copy.wait()
    pre_ref[...] = _conv_bias(xk, w_ref, cb, h)


def _early_act_kernel(sc, pre_ref, gout_ref, sw, sb, lat_ref, g_ref, hid_ref):
    slots, h, w, c = lat_ref.shape
    lat, g, hidden = _activate(pre_ref[...], gout_ref[...], sw, sb)
    for s in range(slots):
        part = lat[s * h * w : (s + 1) * h * w]
        filled = s + 1 < sc[0]
        lat_ref[s] = jnp.where(filled, part, jnp.zeros_like(part)).astype(BF).reshape(h, w, c)
    g_ref[...] = g
    hid_ref[...] = hidden


def _early_sums_kernel(sc, frh, hah, g_ref, hid_ref, gout_ref, acc, xk, fr, ha, sems):
    copies = [
        pltpu.make_async_copy(a, b, sems.at[i]) for i, (a, b) in enumerate(((frh, fr), (hah, ha)))
    ]
    for copy in copies:
        copy.start()
    for copy in copies:
        copy.wait()
    _fill_early(sc, fr, ha, xk)
    _, _, h, _, c = fr.shape
    n9 = 9 * c

    def add(kind, value):
        if kind < 3:
            acc[kind * n9 : (kind + 1) * n9] = value
        elif kind == 3:
            acc[3 * n9 : 3 * n9 + 2 * c] = value
        else:
            at = 3 * n9 + 2 * c + (kind - 4)
            acc[at : at + 1] = value

    acc[3 * n9 + 2 * c :] = jnp.zeros((acc.shape[0] - 3 * n9 - 2 * c, c), F32)
    _weight_grads(xk, g_ref[...], hid_ref[...], gout_ref[...], h, add)


def _late_kernel(
    sc, frs, has, tail, cos, w_ref, cb, sw, sb, early, lat_ref, g_ref, send, keep, xk, acc
):
    fr, ha, co = frs.at[0], has.at[0], cos.at[0]
    _, h, w, c = fr.shape
    on = sc[1] == 0
    for f in range(2):
        _put(xk, (0, f + 2), slice(1, 1 + h), fr[f])
        _put(xk, (0, f + 2), slice(0, 1), ha[f, :1])
        _put(xk, (0, f + 2), slice(h + 1, h + 2), ha[f, 1:])
        a = tail[f * h : (f + 1) * h]
        b = tail[2 * h + 2 * f : 2 * h + 2 * f + 2]
        a = jnp.where(on, a, jnp.zeros_like(a))
        b = jnp.where(on, b, jnp.zeros_like(b))
        _put(xk, (0, f), slice(1, 1 + h), a)
        _put(xk, (0, f), slice(0, 1), b[:1])
        _put(xk, (0, f), slice(h + 1, h + 2), b[1:])
    filled = sc[0] > 0
    gout = jnp.where(filled, co[0], jnp.zeros_like(co[0])).reshape(h * w, c)
    lat, g, hidden = _activate(_conv_bias(xk, w_ref, cb, h), gout, sw, sb)
    lat_ref[...] = jnp.where(filled, lat, jnp.zeros_like(lat)).astype(BF).reshape(h, w, c)
    g_ref[...] = g
    n9 = 9 * c

    def add(kind, value):
        if kind < 3:
            rows = slice(kind * n9, (kind + 1) * n9)
        elif kind == 3:
            rows = slice(3 * n9, 3 * n9 + 2 * c)
        else:
            at = 3 * n9 + 2 * c + (kind - 4)
            rows = slice(at, at + 1)
        acc[rows] = early[rows] + value

    tail_rows = slice(3 * n9 + 2 * c, acc.shape[0])
    acc[tail_rows] = early[tail_rows]

    @pl.when(sc[0] >= 0)
    def _():
        _weight_grads(xk, g, hidden, gout, h, add)

        half = keep.shape[0]
        core = sc[sc.shape[0] - 1]
        send[...] = acc[pl.ds(pl.multiple_of((1 - core) * half, 16), half)].astype(BF)
        keep[...] = acc[pl.ds(pl.multiple_of(core * half, 16), half)]


def _carried_kernel(sc, g_ref, w_ref, out, xk):
    _, _, _, h, w, c = xk.shape
    h = h - 2
    on = sc[1] == 0
    for t in range(2):
        for kw in range(3):
            xk[kw, 0, t, 0:1] = jnp.zeros((1, w, c), BF)
            xk[kw, 0, t, h + 1 : h + 2] = jnp.zeros((1, w, c), BF)
        v = g_ref[:, t * c : (t + 1) * c].reshape(h, w, c)
        _put(xk, (0, t), slice(1, 1 + h), jnp.where(on, v, jnp.zeros_like(v)))
    back = _conv_back(xk, w_ref, h, (2, 3), 2)
    back = jnp.where(sc[0] > 0, back, jnp.full_like(back, EMPTY_GRAD)).astype(BF)
    for t in range(2):
        out[t * h * w : (t + 1) * h * w] = back[:, t * c : (t + 1) * c]


def _back_kernel(sc, g0, g1, w_ref, out_ref, xk):
    slots, _, h, w, c = out_ref.shape
    m = h * w
    zero = jnp.zeros((1, w, c), BF)
    for kw in range(3):
        for j in range(4):
            for s in range(slots):
                xk[kw, s, j, 0:1] = zero
                xk[kw, s, j, h + 1 : h + 2] = zero
    for f in range(2):
        for kw in range(3):
            xk[kw, slots - 1, f + 2, 1 : 1 + h] = jnp.zeros((h, w, c), BF)
        lanes = slice(f * c, (f + 1) * c)
        for s in range(slots):
            v = g0[:, lanes] if s == 0 else g1[(s - 1) * m : s * m, lanes]
            v = v.reshape(h, w, c)
            _put(xk, (s, f), slice(1, 1 + h), v)
            if s > 0:
                on = sc[1 + s] == 0
                _put(xk, (s - 1, f + 2), slice(1, 1 + h), jnp.where(on, v, jnp.zeros_like(v)))
    out = _conv_back(xk, w_ref, h)
    for f in range(2):
        out_ref[:, f] = out[:, f * c : (f + 1) * c].reshape(slots, h, w, c)


def _first_live(a, b):
    return jnp.where(a.astype(F32) < EMPTY_GRAD / 2, a, b)


def _place(sc):
    chip, core = sc[sc.shape[0] - 2], sc[sc.shape[0] - 1]
    return lax.shift_right_logical(chip, 1), lax.bitwise_and(chip, 1), core


def _across_x_kernel(sc, keep, got, send_far, send_near, kept):
    z, x, _ = _place(sc)
    half = keep.shape[0]
    blocks = 4
    rows = half // (2 * blocks)

    def piece(j, side):
        p = 2 * lax.bitwise_xor(z, j) + side
        at = pl.ds(pl.multiple_of(p * rows, 16), rows)
        return keep[at] + got[at].astype(F32)

    for j in range(blocks):
        kept[j * rows : (j + 1) * rows] = piece(j, x)
        send, i = (send_near, j) if j < 2 else (send_far, j - 2)
        send[i * rows : (i + 1) * rows] = piece(j, 1 - x).astype(BF)


def _tail_kernel(sc, fr, ha, out):
    h2 = fr.shape[1] * fr.shape[2]
    live = sc[0] > 0
    for ref, rows in ((fr, slice(0, h2)), (ha, slice(h2, out.shape[0]))):
        v = ref[...].reshape(rows.stop - rows.start, *out.shape[1:])
        out[rows] = jnp.where(live, v, jnp.full_like(v, EMPTY_FRAME))


def _final_kernel(sc, mine, other, got, grad, cw, sw, cb, sb, fg, acc):
    c = mine.shape[1]
    half = acc.shape[0] // 2
    z, x, core = _place(sc)
    blocks = 4
    rows = half // (2 * blocks)
    for ref, at_core in ((mine, core), (other, 1 - core)):
        for k in range(2 * blocks):
            side = x if k < blocks else 1 - x
            chip = 2 * lax.bitwise_xor(z, k % blocks) + side
            at = pl.multiple_of(at_core * half + chip * rows, 16)
            acc[pl.ds(at, rows)] = ref[k * rows : (k + 1) * rows].astype(F32)
    n27, n29 = 27 * c, 29 * c
    cw[...] = acc[:n27]
    sw[...] = acc[n27:n29]
    cb[...] = acc[n29 : n29 + 1]
    sb[...] = acc[n29 + 1 : n29 + 2]
    slots, frames, h, w, _ = grad.shape
    part = mine.shape[0] - half
    for s in range(slots):
        here = sc[0] - 1 == s
        for f in range(frames):
            low = f == 0
            a, b = mine[half:].astype(F32), other[half:].astype(F32)
            beyond = jnp.where(core == 0, a, b) if low else jnp.where(core == 0, b, a)
            beside = got[f * part : (f + 1) * part].astype(F32)
            came = jnp.where(core == 0, _first_live(beside, beyond), beyond)
            came = jnp.where(came < EMPTY_GRAD / 2, came, jnp.zeros_like(came)).reshape(h, w, c)
            fg[s, f] = (grad[s, f] + jnp.where(here, came, jnp.zeros_like(came))).astype(BF)


def _xor(x, k, n, axis):
    return lax.ppermute(x, axis, [(i, i ^ k) for i in range(n)])


def _latest_before(x, empty, axis, n, beside_x, beside_near, beside_far):
    index = lax.axis_index(axis)
    core, pair = index & 1, (index >> 1) & 1

    def newest(early, late):
        return jnp.where(late > empty / 2, early, late)

    def half(v):
        rows = v.shape[0] // 2
        return jnp.where(core == 0, v[:rows], v[rows:])

    other = _xor(x, 1, n, axis)
    a, b = half(x), half(other)
    chip = jnp.where(core == 0, newest(a, b), newest(b, a))
    beside = _xor(chip, 2, n, axis)
    quad = jnp.where(pair == 0, newest(chip, beside), newest(beside, chip))
    quad = beside_x(chip, quad)
    block, before, k = quad, jnp.full_like(quad, empty), 4
    while k < n:
        late = (index & k) > 0
        came = _xor(block, k, n, axis)
        if k == 4:
            came = beside_near(block, came)
        before = jnp.where(late, newest(came, before), before)
        if k == 8:
            before = beside_far(block, before)
        if 2 * k < n:
            block = jnp.where(late, newest(came, block), newest(block, came))
        k *= 2
    before = jnp.where(pair == 0, before, newest(before, beside))
    across = _xor(before, 1, n, axis)
    before = jnp.concatenate(
        [jnp.where(core == 0, before, across), jnp.where(core == 0, across, before)], axis=0
    )
    before = jnp.where(core == 0, before, newest(before, other))
    return jnp.where(before > empty / 2, jnp.zeros_like(before), before)


def _after(value, *earlier):
    return lax.optimization_barrier((value, *earlier))[0]


def body(
    n,
    frames,
    row_halo,
    clip_start,
    slab_counts,
    conv_weight,
    conv_bias,
    stride_weight,
    stride_bias,
    cotangent,
):
    axis = "tm"
    slots, _, h, w, c = frames.shape
    count = slab_counts[0]
    index = lax.axis_index(axis)
    chips = 8
    assert n % (2 * chips) == 0
    sc = jnp.concatenate(
        [
            slab_counts,
            clip_start,
            ((index >> 1) & (chips - 1)).reshape(1).astype(jnp.int32),
            (index & 1).reshape(1).astype(jnp.int32),
        ]
    )
    wt = conv_weight.reshape(27, c, c)
    cb, sb = conv_bias.reshape(1, c), stride_bias.reshape(1, c)
    unit = 16 * 2 * chips
    rows = -(-(29 * c + 2) // unit) * unit
    m = h * w
    conv_flops = 2 * m * 36 * c * 2 * c

    def newest_slot(i, sc):
        return (jnp.maximum(sc[0] - 1, 0), 0, 0, 0, 0)

    tail = pl.pallas_call(
        _tail_kernel,
        out_shape=jax.ShapeDtypeStruct((2 * h + 4, w, c), BF),
        grid_spec=pltpu.PrefetchScalarGridSpec(
            num_scalar_prefetch=1,
            grid=(1,),
            in_specs=[
                pl.BlockSpec((1, 2, h, w, c), newest_slot),
                pl.BlockSpec((1, 2, 2, w, c), newest_slot),
            ],
            out_specs=pl.BlockSpec((2 * h + 4, w, c), lambda i, sc: (0, 0, 0)),
        ),
        compiler_params=pltpu.CompilerParams(vmem_limit_bytes=8 << 20),
    )(
        slab_counts,
        *(pltpu.with_memory_space_constraint(v, pltpu.HBM) for v in (frames, row_halo)),
    )

    held = {}
    wide = ((slots - 1) * m, 2 * c)
    raw = [
        pltpu.with_memory_space_constraint(v, pltpu.HBM)
        for v in (frames, row_halo, cotangent, wt, cb, stride_weight, sb)
    ]
    windows = (3, slots - 1, 4, h + 2, w, c)

    def early_conv(start, follow):
        held["conv"] = _call(
            _early_conv_kernel,
            [
                jax.ShapeDtypeStruct(wide, F32),
                jax.ShapeDtypeStruct((wide[0], c), BF),
                jax.ShapeDtypeStruct(stride_weight.shape, BF),
                jax.ShapeDtypeStruct(sb.shape, F32),
            ],
            [_SMEM] + [_HBM] * len(raw),
            [pltpu.VMEM(v.shape, v.dtype) for v in raw[:5]]
            + [pltpu.VMEM(windows, BF), pltpu.SemaphoreType.DMA((len(raw),))],
            flops=(slots - 1) * conv_flops,
            moved=4 << 20,
        )(_after(sc, start), *raw)
        return _after(follow, held["conv"][0])

    def early_act(start, follow):
        pre, gout1, sw1, sb1 = held["conv"]
        held["early"] = _call(
            _early_act_kernel,
            [
                jax.ShapeDtypeStruct((slots - 1, h, w, c), BF),
                jax.ShapeDtypeStruct(wide, BF),
                jax.ShapeDtypeStruct(wide, BF),
            ],
            [_SMEM] + [_VMEM] * 4,
            moved=2 << 20,
            room=6,
        )(_after(sc, start), pre, gout1, sw1, sb1)
        return _after(follow, held["early"][1])

    def early_sums(start, follow):
        gout1 = held["conv"][1]
        _, g1, hid1 = held["early"]
        held["sums"] = _call(
            _early_sums_kernel,
            jax.ShapeDtypeStruct((rows, c), F32),
            [_SMEM, _HBM, _HBM] + [_VMEM] * 3,
            [pltpu.VMEM(windows, BF)]
            + [pltpu.VMEM(v.shape, BF) for v in raw[:2]]
            + [pltpu.SemaphoreType.DMA((2,))],
            flops=(slots - 1) * conv_flops,
            moved=4 << 20,
        )(_after(sc, start), raw[0], raw[1], g1, hid1, gout1)
        return _after(follow, held["sums"])

    arrived = _latest_before(tail, EMPTY_FRAME, axis, n, early_conv, early_act, early_sums)
    lat1, g1, _ = held["early"]

    def first(*shape):
        return pl.BlockSpec((1, *shape), lambda i: (0,) * (len(shape) + 1))

    half, carried = rows // 2, 2 * m
    lat0, g0, send, keep = _call(
        _late_kernel,
        [
            jax.ShapeDtypeStruct((h, w, c), BF),
            jax.ShapeDtypeStruct((m, 2 * c), BF),
            jax.ShapeDtypeStruct((half, c), BF),
            jax.ShapeDtypeStruct((half, c), F32),
        ],
        [_SMEM, first(2, h, w, c), first(2, 2, w, c), _VMEM, first(1, h, w, c)] + [_VMEM] * 5,
        [pltpu.VMEM((3, 1, 4, h + 2, w, c), BF), pltpu.VMEM((rows, c), F32)],
        flops=2 * conv_flops,
        moved=6 << 20,
        grid=(1,),
    )(sc, frames, row_halo, arrived, cotangent, wt, cb, stride_weight, sb, held["sums"])

    blocks = chips // 2
    piece = half // chips
    got = _xor(send, 1, n, axis)
    first_grad = _call(
        _carried_kernel,
        jax.ShapeDtypeStruct((carried, c), BF),
        [_SMEM, _VMEM, _VMEM],
        [pltpu.VMEM((3, 1, 2, h + 2, w, c), BF)],
        flops=conv_flops // 2,
        moved=1 << 20,
        room=8,
    )(sc, g0, wt)
    send_far, send_near, kept = _call(
        _across_x_kernel,
        [
            jax.ShapeDtypeStruct((2 * piece, c), BF),
            jax.ShapeDtypeStruct((2 * piece, c), BF),
            jax.ShapeDtypeStruct((blocks * piece, c), F32),
        ],
        [_SMEM] + [_VMEM] * 2,
        room=8,
    )(sc, _after(keep, first_grad), got)
    got_far = _xor(send_far, 2, n, axis)
    got_first = _xor(_after(first_grad, kept), 1, n, axis)
    core, pair = index & 1, (index >> 1) & 1

    def by(bit, a, b):
        return jnp.where(bit == 0, a, b)

    def by_half(bit, v):
        rows = v.shape[0] // 2
        return by(bit, v[:rows], v[rows:])

    def ordered(bit, ours, theirs):
        return by(bit, _first_live(ours, theirs), _first_live(theirs, ours))

    chip_first = ordered(core, by_half(core, first_grad), by_half(core, got_first))
    send_near = jnp.concatenate([send_near, chip_first], axis=0)
    got_near = _xor(send_near, 2, n, axis)
    grad = _call(
        _back_kernel,
        jax.ShapeDtypeStruct((slots, 2, h, w, c), F32),
        [_SMEM] + [_VMEM] * 3,
        [pltpu.VMEM((3, slots, 4, h + 2, w, c), BF)],
        flops=1,
        moved=1,
        room=24,
    )(_after(sc, send_near), g0, g1, wt)
    got_far = _after(got_far, grad)

    def summed(j, came):
        i = j % 2
        return kept[j * piece : (j + 1) * piece] + came[i * piece : (i + 1) * piece].astype(F32)

    outs = {j: summed(j, got_far).astype(BF) for j in (3, 2)}
    got_near = _after(got_near, outs[3], outs[2])
    outs[1] = summed(1, got_near).astype(BF)
    gots = {j: _xor(outs[j], 4 * j, n, axis) for j in (3, 2, 1)}
    beside_first = got_near[2 * piece :]
    lead = ordered(pair, by_half(pair, chip_first), by_half(pair, beside_first))
    near_lead = _xor(lead, 4, n, axis)
    mine = summed(0, _after(got_near, outs[1]))
    for j in (3, 2):
        mine = mine + gots[j].astype(F32)
    gots[1] = _after(gots[1], mine)
    mine = (mine + gots[1].astype(F32)).astype(BF)
    k = 2 * chips
    while k < n:
        mine = (mine.astype(F32) + _xor(mine, k, n, axis).astype(F32)).astype(BF)
        k *= 2
    others = {j: _xor(mine, 4 * j, n, axis) for j in (1, 3, 2)}
    x_near = _xor(jnp.concatenate([mine, others[1]], axis=0), 2, n, axis)
    beyond = by(index & 4, near_lead, jnp.full_like(lead, EMPTY_GRAD))
    lead, k = _after(ordered(index & 4, lead, near_lead), others[1]), 8
    while k < n:
        came = _xor(lead, k, n, axis)
        beyond = by(index & k, _first_live(beyond, came), beyond)
        if 2 * k < n:
            lead = ordered(index & k, lead, came)
        k *= 2
    x_far = _xor(jnp.concatenate([others[2], others[3], beyond], axis=0), 2, n, axis)
    theirs = x_far[2 * piece :]
    beyond = jnp.concatenate([by(pair, beyond, theirs), by(pair, theirs, beyond)], axis=0)
    beyond = by(pair, _first_live(beside_first, beyond), beyond)
    ours = jnp.concatenate(
        [mine, others[1], others[2], others[3], x_near, x_far[: 2 * piece], beyond], axis=0
    )
    other = _xor(ours, 1, n, axis)
    cwg, swg, cbg, sbg, frames_grad = _call(
        _final_kernel,
        [
            jax.ShapeDtypeStruct((27 * c, c), F32),
            jax.ShapeDtypeStruct((2 * c, c), F32),
            jax.ShapeDtypeStruct((1, c), F32),
            jax.ShapeDtypeStruct((1, c), F32),
            jax.ShapeDtypeStruct((slots, 2, h, w, c), BF),
        ],
        [_SMEM] + [_VMEM] * 4,
        [pltpu.VMEM((rows, c), F32)],
        room=12,
    )(sc, ours, other, got_first, grad)
    latents = jnp.concatenate([lat0[None], lat1], axis=0)[:, None]
    return (
        latents,
        frames_grad,
        cwg.reshape(3, 3, 3, c, c),
        cbg[0],
        swg.reshape(2, c, c),
        sbg[0],
    )


def solution(mesh):
    split = P(("groups", "tm"))
    return jax.shard_map(
        functools.partial(body, mesh.shape["tm"]),
        mesh=mesh,
        in_specs=(split, split, split, split, P(), P(), P(), P(), split),
        out_specs=(split, split, P("groups"), P("groups"), P("groups"), P("groups")),
        check_vma=False,
    )
```

```python
import functools

import jax
import jax.numpy as jnp
from jax import lax
from jax.experimental import pallas as pl
from jax.experimental.pallas import tpu as pltpu
from jax.sharding import PartitionSpec as P

BF = jnp.bfloat16
F32 = jnp.float32
EMPTY_FRAME = 100.0
EMPTY_GRAD = 1e30

_VMEM = pl.BlockSpec(memory_space=pltpu.VMEM)
_SMEM = pl.BlockSpec(memory_space=pltpu.SMEM)
_HBM = pl.BlockSpec(memory_space=pltpu.HBM)


def _call(kernel, out_shape, in_specs, scratch=(), flops=0, moved=0, room=16, grid=()):
    return pl.pallas_call(
        kernel,
        out_shape=out_shape,
        grid=grid,
        in_specs=in_specs,
        out_specs=jax.tree.map(lambda _: _VMEM, out_shape),
        scratch_shapes=list(scratch),
        compiler_params=pltpu.CompilerParams(vmem_limit_bytes=room << 20),
        cost_estimate=pl.CostEstimate(flops=flops, bytes_accessed=moved, transcendentals=0),
    )


def _put(xk, at, rows, value):
    n, w, c = value.shape
    flat = value.astype(F32).reshape(n * w, c)
    col = lax.broadcasted_iota(jnp.int32, (n * w, c), 0) % w
    right = jnp.where(col == 0, 0.0, pltpu.roll(flat, 1, 0))
    left = jnp.where(col == w - 1, 0.0, pltpu.roll(flat, n * w - 1, 0))
    for kw, shifted in enumerate((right, flat, left)):
        xk[(kw, *at, rows)] = shifted.astype(BF).reshape(n, w, c)


def _window(xk, kw, j, kh, h):
    v = xk[kw, :, j, kh : kh + h]
    return v.reshape(v.shape[0] * v.shape[1] * v.shape[2], v.shape[3])


def _wide(xk, j, h):
    return jnp.concatenate(
        [_window(xk, kw, j, kh, h) for kh in range(3) for kw in range(3)], axis=1
    )


def _conv(xk, w_ref, h):
    c = w_ref.shape[-1]
    zero = jnp.zeros((c, c), BF)
    lhs = jnp.concatenate([_wide(xk, j, h) for j in range(4)], axis=1)
    rhs = []
    for j in range(4):
        for tap in range(9):
            rhs.append(
                jnp.concatenate(
                    [w_ref[(j - t) * 9 + tap] if 0 <= j - t <= 2 else zero for t in range(2)],
                    axis=1,
                )
            )
    return jnp.dot(lhs, jnp.concatenate(rhs, axis=0), preferred_element_type=F32)


def _conv_back(xk, w_ref, h, frames=range(4), base=0):
    c = w_ref.shape[-1]
    zero = jnp.zeros((c, c), BF)
    lhs = jnp.concatenate([_wide(xk, j - base, h) for j in frames], axis=1)
    rhs = []
    for f in range(2):
        row = []
        for j in frames:
            for tap in range(9):
                kt = 2 - (j - f)
                row.append(w_ref[kt * 9 + 8 - tap] if 0 <= kt <= 2 else zero)
        rhs.append(jnp.concatenate(row, axis=1))
    return lax.dot_general(
        lhs, jnp.concatenate(rhs, axis=0), (((1,), (1,)), ((), ())), preferred_element_type=F32
    )


def _activate(pre, gout, sw_ref, sb_ref):
    s = 1.0 / (1.0 + jnp.exp(-pre))
    hidden = (pre * s).astype(BF)
    sw = jnp.concatenate([sw_ref[0], sw_ref[1]], axis=0)
    lat = jnp.dot(hidden, sw, preferred_element_type=F32) + sb_ref[...]
    gh = lax.dot_general(gout, sw, (((1,), (1,)), ((), ())), preferred_element_type=F32)
    g = (gh * s * (1.0 + pre * (1.0 - s))).astype(BF)
    return lat, g, hidden


def _conv_bias(xk, w_ref, cb_ref, h):
    return _conv(xk, w_ref, h) + jnp.concatenate([cb_ref[...], cb_ref[...]], axis=1)


def _weight_grads(xk, g, hidden, gout, h, add):
    c = gout.shape[-1]
    parts = []
    for j in range(4):
        lhs = _wide(xk, j, h)
        parts.append(
            lax.dot_general(lhs, g, (((0,), (0,)), ((), ())), preferred_element_type=F32)
        )
    for kt in range(3):
        add(kt, parts[kt][:, :c] + parts[kt + 1][:, c:])
    sg = lax.dot_general(hidden, gout, (((0,), (0,)), ((), ())), preferred_element_type=F32)
    g32 = jnp.sum(g.astype(F32), axis=0, keepdims=True)
    add(3, sg)
    add(4, g32[:, :c] + g32[:, c:])
    add(5, jnp.sum(gout.astype(F32), axis=0, keepdims=True))


def _fill_early(sc, fr, ha, xk):
    slots, _, h, w, c = fr.shape
    for s in range(slots):
        for f in range(2):
            spots = [(s - 1, f + 2, None)] if s > 0 else []
            if s + 1 < slots:
                spots.append((s, f, sc[1 + s + 1] == 0))
            for slot, j, keep in spots:
                a, b = fr[s, f], ha[s, f]
                if keep is not None:
                    a = jnp.where(keep, a, jnp.zeros_like(a))
                    b = jnp.where(keep, b, jnp.zeros_like(b))
                _put(xk, (slot, j), slice(1, 1 + h), a)
                _put(xk, (slot, j), slice(0, 1), b[:1])
                _put(xk, (slot, j), slice(h + 1, h + 2), b[1:])


def _early_gout(sc, co):
    slots, _, h, w, c = co.shape
    return jnp.concatenate(
        [
            jnp.where(s < sc[0], co[s, 0], jnp.zeros_like(co[s, 0])).reshape(h * w, c)
            for s in range(1, slots)
        ],
        axis=0,
    )


def _early_conv_kernel(
    sc, frh, hah, coh, wh, cbh, swh, sbh, pre_ref, gout_ref, sw, sb, fr, ha, co, w_ref, cb, xk, sems
):
    h = fr.shape[2]
    pairs = ((frh, fr), (hah, ha), (coh, co), (wh, w_ref), (cbh, cb), (swh, sw), (sbh, sb))
    copies = [pltpu.make_async_copy(a, b, sems.at[i]) for i, (a, b) in enumerate(pairs)]
    for copy in copies:
        copy.start()
    copies[0].wait()
    copies[1].wait()
    _fill_early(sc, fr, ha, xk)
    copies[2].wait()
    gout_ref[...] = _early_gout(sc, co)
    for copy in copies[3:]:
        copy.wait()
    pre_ref[...] = _conv_bias(xk, w_ref, cb, h)


def _early_act_kernel(sc, pre_ref, gout_ref, sw, sb, lat_ref, g_ref, hid_ref):
    slots, h, w, c = lat_ref.shape
    lat, g, hidden = _activate(pre_ref[...], gout_ref[...], sw, sb)
    for s in range(slots):
        part = lat[s * h * w : (s + 1) * h * w]
        filled = s + 1 < sc[0]
        lat_ref[s] = jnp.where(filled, part, jnp.zeros_like(part)).astype(BF).reshape(h, w, c)
    g_ref[...] = g
    hid_ref[...] = hidden


def _early_sums_kernel(sc, frh, hah, g_ref, hid_ref, gout_ref, acc, xk, fr, ha, sems):
    copies = [
        pltpu.make_async_copy(a, b, sems.at[i]) for i, (a, b) in enumerate(((frh, fr), (hah, ha)))
    ]
    for copy in copies:
        copy.start()
    for copy in copies:
        copy.wait()
    _fill_early(sc, fr, ha, xk)
    _, _, h, _, c = fr.shape
    n9 = 9 * c

    def add(kind, value):
        if kind < 3:
            acc[kind * n9 : (kind + 1) * n9] = value
        elif kind == 3:
            acc[3 * n9 : 3 * n9 + 2 * c] = value
        else:
            at = 3 * n9 + 2 * c + (kind - 4)
            acc[at : at + 1] = value

    acc[3 * n9 + 2 * c :] = jnp.zeros((acc.shape[0] - 3 * n9 - 2 * c, c), F32)
    _weight_grads(xk, g_ref[...], hid_ref[...], gout_ref[...], h, add)


def _late_kernel(
    sc, frs, has, tail, cos, w_ref, cb, sw, sb, early, lat_ref, g_ref, send, keep, xk, acc
):
    fr, ha, co = frs.at[0], has.at[0], cos.at[0]
    _, h, w, c = fr.shape
    on = sc[1] == 0
    for f in range(2):
        _put(xk, (0, f + 2), slice(1, 1 + h), fr[f])
        _put(xk, (0, f + 2), slice(0, 1), ha[f, :1])
        _put(xk, (0, f + 2), slice(h + 1, h + 2), ha[f, 1:])
        a = tail[f * h : (f + 1) * h]
        b = tail[2 * h + 2 * f : 2 * h + 2 * f + 2]
        a = jnp.where(on, a, jnp.zeros_like(a))
        b = jnp.where(on, b, jnp.zeros_like(b))
        _put(xk, (0, f), slice(1, 1 + h), a)
        _put(xk, (0, f), slice(0, 1), b[:1])
        _put(xk, (0, f), slice(h + 1, h + 2), b[1:])
    filled = sc[0] > 0
    gout = jnp.where(filled, co[0], jnp.zeros_like(co[0])).reshape(h * w, c)
    lat, g, hidden = _activate(_conv_bias(xk, w_ref, cb, h), gout, sw, sb)
    lat_ref[...] = jnp.where(filled, lat, jnp.zeros_like(lat)).astype(BF).reshape(h, w, c)
    g_ref[...] = g
    n9 = 9 * c

    def add(kind, value):
        if kind < 3:
            rows = slice(kind * n9, (kind + 1) * n9)
        elif kind == 3:
            rows = slice(3 * n9, 3 * n9 + 2 * c)
        else:
            at = 3 * n9 + 2 * c + (kind - 4)
            rows = slice(at, at + 1)
        acc[rows] = early[rows] + value

    tail_rows = slice(3 * n9 + 2 * c, acc.shape[0])
    acc[tail_rows] = early[tail_rows]

    @pl.when(sc[0] >= 0)
    def _():
        _weight_grads(xk, g, hidden, gout, h, add)

        half = keep.shape[0]
        core = sc[sc.shape[0] - 1]
        send[...] = acc[pl.ds(pl.multiple_of((1 - core) * half, 16), half)].astype(BF)
        keep[...] = acc[pl.ds(pl.multiple_of(core * half, 16), half)]


def _carried_kernel(sc, g_ref, w_ref, out, xk):
    _, _, _, h, w, c = xk.shape
    h = h - 2
    on = sc[1] == 0
    for t in range(2):
        for kw in range(3):
            xk[kw, 0, t, 0:1] = jnp.zeros((1, w, c), BF)
            xk[kw, 0, t, h + 1 : h + 2] = jnp.zeros((1, w, c), BF)
        v = g_ref[:, t * c : (t + 1) * c].reshape(h, w, c)
        _put(xk, (0, t), slice(1, 1 + h), jnp.where(on, v, jnp.zeros_like(v)))
    back = _conv_back(xk, w_ref, h, (2, 3), 2)
    back = jnp.where(sc[0] > 0, back, jnp.full_like(back, EMPTY_GRAD)).astype(BF)
    for t in range(2):
        out[t * h * w : (t + 1) * h * w] = back[:, t * c : (t + 1) * c]


def _back_kernel(sc, g0, g1, w_ref, out_ref, xk):
    slots, _, h, w, c = out_ref.shape
    m = h * w
    zero = jnp.zeros((1, w, c), BF)
    for kw in range(3):
        for j in range(4):
            for s in range(slots):
                xk[kw, s, j, 0:1] = zero
                xk[kw, s, j, h + 1 : h + 2] = zero
    for f in range(2):
        for kw in range(3):
            xk[kw, slots - 1, f + 2, 1 : 1 + h] = jnp.zeros((h, w, c), BF)
        lanes = slice(f * c, (f + 1) * c)
        for s in range(slots):
            v = g0[:, lanes] if s == 0 else g1[(s - 1) * m : s * m, lanes]
            v = v.reshape(h, w, c)
            _put(xk, (s, f), slice(1, 1 + h), v)
            if s > 0:
                on = sc[1 + s] == 0
                _put(xk, (s - 1, f + 2), slice(1, 1 + h), jnp.where(on, v, jnp.zeros_like(v)))
    out = _conv_back(xk, w_ref, h)
    for f in range(2):
        out_ref[:, f] = out[:, f * c : (f + 1) * c].reshape(slots, h, w, c)


def _first_live(a, b):
    return jnp.where(a.astype(F32) < EMPTY_GRAD / 2, a, b)


def _place(sc):
    chip, core = sc[sc.shape[0] - 2], sc[sc.shape[0] - 1]
    return lax.shift_right_logical(chip, 1), lax.bitwise_and(chip, 1), core


def _across_x_kernel(sc, keep, got, send_far, send_near, kept):
    z, x, _ = _place(sc)
    half = keep.shape[0]
    blocks = 4
    rows = half // (2 * blocks)

    def piece(j, side):
        p = 2 * lax.bitwise_xor(z, j) + side
        at = pl.ds(pl.multiple_of(p * rows, 16), rows)
        return keep[at] + got[at].astype(F32)

    for j in range(blocks):
        kept[j * rows : (j + 1) * rows] = piece(j, x)
        send, i = (send_near, j) if j < 2 else (send_far, j - 2)
        send[i * rows : (i + 1) * rows] = piece(j, 1 - x).astype(BF)


def _tail_kernel(sc, fr, ha, out):
    h2 = fr.shape[1] * fr.shape[2]
    live = sc[0] > 0
    for ref, rows in ((fr, slice(0, h2)), (ha, slice(h2, out.shape[0]))):
        v = ref[...].reshape(rows.stop - rows.start, *out.shape[1:])
        out[rows] = jnp.where(live, v, jnp.full_like(v, EMPTY_FRAME))


def _final_kernel(sc, mine, other, got, grad, cw, sw, cb, sb, fg, acc):
    c = mine.shape[1]
    half = acc.shape[0] // 2
    z, x, core = _place(sc)
    blocks = 4
    rows = half // (2 * blocks)
    for ref, at_core in ((mine, core), (other, 1 - core)):
        for k in range(2 * blocks):
            side = x if k < blocks else 1 - x
            chip = 2 * lax.bitwise_xor(z, k % blocks) + side
            at = pl.multiple_of(at_core * half + chip * rows, 16)
            acc[pl.ds(at, rows)] = ref[k * rows : (k + 1) * rows].astype(F32)
    n27, n29 = 27 * c, 29 * c
    cw[...] = acc[:n27]
    sw[...] = acc[n27:n29]
    cb[...] = acc[n29 : n29 + 1]
    sb[...] = acc[n29 + 1 : n29 + 2]
    slots, frames, h, w, _ = grad.shape
    part = mine.shape[0] - half
    for s in range(slots):
        here = sc[0] - 1 == s
        for f in range(frames):
            low = f == 0
            a, b = mine[half:].astype(F32), other[half:].astype(F32)
            beyond = jnp.where(core == 0, a, b) if low else jnp.where(core == 0, b, a)
            beside = got[f * part : (f + 1) * part].astype(F32)
            came = jnp.where(core == 0, _first_live(beside, beyond), beyond)
            came = jnp.where(came < EMPTY_GRAD / 2, came, jnp.zeros_like(came)).reshape(h, w, c)
            fg[s, f] = (grad[s, f] + jnp.where(here, came, jnp.zeros_like(came))).astype(BF)


def _xor(x, k, n, axis):
    return lax.ppermute(x, axis, [(i, i ^ k) for i in range(n)])


def _latest_before(x, empty, axis, n, beside_x, beside_near, beside_far):
    index = lax.axis_index(axis)
    core, pair = index & 1, (index >> 1) & 1

    def newest(early, late):
        return jnp.where(late > empty / 2, early, late)

    def half(v):
        rows = v.shape[0] // 2
        return jnp.where(core == 0, v[:rows], v[rows:])

    other = _xor(x, 1, n, axis)
    a, b = half(x), half(other)
    chip = jnp.where(core == 0, newest(a, b), newest(b, a))
    beside = _xor(chip, 2, n, axis)
    quad = jnp.where(pair == 0, newest(chip, beside), newest(beside, chip))
    quad = beside_x(chip, quad)
    block, before, k = quad, jnp.full_like(quad, empty), 4
    while k < n:
        late = (index & k) > 0
        came = _xor(block, k, n, axis)
        if k == 4:
            came = beside_near(block, came)
        before = jnp.where(late, newest(came, before), before)
        if k == 8:
            before = beside_far(block, before)
        if 2 * k < n:
            block = jnp.where(late, newest(came, block), newest(block, came))
        k *= 2
    before = jnp.where(pair == 0, before, newest(before, beside))
    across = _xor(before, 1, n, axis)
    before = jnp.concatenate(
        [jnp.where(core == 0, before, across), jnp.where(core == 0, across, before)], axis=0
    )
    before = jnp.where(core == 0, before, newest(before, other))
    return jnp.where(before > empty / 2, jnp.zeros_like(before), before)


def _after(value, *earlier):
    return lax.optimization_barrier((value, *earlier))[0]


def body(
    n,
    frames,
    row_halo,
    clip_start,
    slab_counts,
    conv_weight,
    conv_bias,
    stride_weight,
    stride_bias,
    cotangent,
):
    axis = "tm"
    slots, _, h, w, c = frames.shape
    count = slab_counts[0]
    index = lax.axis_index(axis)
    chips = 8
    assert n % (2 * chips) == 0
    sc = jnp.concatenate(
        [
            slab_counts,
            clip_start,
            ((index >> 1) & (chips - 1)).reshape(1).astype(jnp.int32),
            (index & 1).reshape(1).astype(jnp.int32),
        ]
    )
    wt = conv_weight.reshape(27, c, c)
    cb, sb = conv_bias.reshape(1, c), stride_bias.reshape(1, c)
    unit = 16 * 2 * chips
    rows = -(-(29 * c + 2) // unit) * unit
    m = h * w
    conv_flops = 2 * m * 36 * c * 2 * c

    def newest_slot(i, sc):
        return (jnp.maximum(sc[0] - 1, 0), 0, 0, 0, 0)

    tail = pl.pallas_call(
        _tail_kernel,
        out_shape=jax.ShapeDtypeStruct((2 * h + 4, w, c), BF),
        grid_spec=pltpu.PrefetchScalarGridSpec(
            num_scalar_prefetch=1,
            grid=(1,),
            in_specs=[
                pl.BlockSpec((1, 2, h, w, c), newest_slot),
                pl.BlockSpec((1, 2, 2, w, c), newest_slot),
            ],
            out_specs=pl.BlockSpec((2 * h + 4, w, c), lambda i, sc: (0, 0, 0)),
        ),
        compiler_params=pltpu.CompilerParams(vmem_limit_bytes=8 << 20),
    )(
        slab_counts,
        *(pltpu.with_memory_space_constraint(v, pltpu.HBM) for v in (frames, row_halo)),
    )

    held = {}
    wide = ((slots - 1) * m, 2 * c)
    raw = [
        pltpu.with_memory_space_constraint(v, pltpu.HBM)
        for v in (frames, row_halo, cotangent, wt, cb, stride_weight, sb)
    ]
    windows = (3, slots - 1, 4, h + 2, w, c)

    def early_conv(start, follow):
        held["conv"] = _call(
            _early_conv_kernel,
            [
                jax.ShapeDtypeStruct(wide, F32),
                jax.ShapeDtypeStruct((wide[0], c), BF),
                jax.ShapeDtypeStruct(stride_weight.shape, BF),
                jax.ShapeDtypeStruct(sb.shape, F32),
            ],
            [_SMEM] + [_HBM] * len(raw),
            [pltpu.VMEM(v.shape, v.dtype) for v in raw[:5]]
            + [pltpu.VMEM(windows, BF), pltpu.SemaphoreType.DMA((len(raw),))],
            flops=(slots - 1) * conv_flops,
            moved=4 << 20,
        )(_after(sc, start), *raw)
        return _after(follow, held["conv"][0])

    def early_act(start, follow):
        pre, gout1, sw1, sb1 = held["conv"]
        held["early"] = _call(
            _early_act_kernel,
            [
                jax.ShapeDtypeStruct((slots - 1, h, w, c), BF),
                jax.ShapeDtypeStruct(wide, BF),
                jax.ShapeDtypeStruct(wide, BF),
            ],
            [_SMEM] + [_VMEM] * 4,
            moved=2 << 20,
            room=6,
        )(_after(sc, start), pre, gout1, sw1, sb1)
        return _after(follow, held["early"][1])

    def early_sums(start, follow):
        gout1 = held["conv"][1]
        _, g1, hid1 = held["early"]
        held["sums"] = _call(
            _early_sums_kernel,
            jax.ShapeDtypeStruct((rows, c), F32),
            [_SMEM, _HBM, _HBM] + [_VMEM] * 3,
            [pltpu.VMEM(windows, BF)]
            + [pltpu.VMEM(v.shape, BF) for v in raw[:2]]
            + [pltpu.SemaphoreType.DMA((2,))],
            flops=(slots - 1) * conv_flops,
            moved=4 << 20,
        )(_after(sc, start), raw[0], raw[1], g1, hid1, gout1)
        return _after(follow, held["sums"])

    arrived = _latest_before(tail, EMPTY_FRAME, axis, n, early_conv, early_act, early_sums)
    lat1, g1, _ = held["early"]

    def first(*shape):
        return pl.BlockSpec((1, *shape), lambda i: (0,) * (len(shape) + 1))

    half, carried = rows // 2, 2 * m
    lat0, g0, send, keep = _call(
        _late_kernel,
        [
            jax.ShapeDtypeStruct((h, w, c), BF),
            jax.ShapeDtypeStruct((m, 2 * c), BF),
            jax.ShapeDtypeStruct((half, c), BF),
            jax.ShapeDtypeStruct((half, c), F32),
        ],
        [_SMEM, first(2, h, w, c), first(2, 2, w, c), _VMEM, first(1, h, w, c)] + [_VMEM] * 5,
        [pltpu.VMEM((3, 1, 4, h + 2, w, c), BF), pltpu.VMEM((rows, c), F32)],
        flops=2 * conv_flops,
        moved=6 << 20,
        grid=(1,),
    )(sc, frames, row_halo, arrived, cotangent, wt, cb, stride_weight, sb, held["sums"])

    blocks = chips // 2
    piece = half // chips
    got = _xor(send, 1, n, axis)
    first_grad = _call(
        _carried_kernel,
        jax.ShapeDtypeStruct((carried, c), BF),
        [_SMEM, _VMEM, _VMEM],
        [pltpu.VMEM((3, 1, 2, h + 2, w, c), BF)],
        flops=conv_flops // 2,
        moved=1 << 20,
        room=8,
    )(sc, g0, wt)
    send_far, send_near, kept = _call(
        _across_x_kernel,
        [
            jax.ShapeDtypeStruct((2 * piece, c), BF),
            jax.ShapeDtypeStruct((2 * piece, c), BF),
            jax.ShapeDtypeStruct((blocks * piece, c), F32),
        ],
        [_SMEM] + [_VMEM] * 2,
        room=8,
    )(sc, _after(keep, first_grad), got)
    got_far = _xor(send_far, 2, n, axis)
    got_first = _xor(_after(first_grad, kept), 1, n, axis)
    core, pair = index & 1, (index >> 1) & 1

    def by(bit, a, b):
        return jnp.where(bit == 0, a, b)

    def by_half(bit, v):
        rows = v.shape[0] // 2
        return by(bit, v[:rows], v[rows:])

    def ordered(bit, ours, theirs):
        return by(bit, _first_live(ours, theirs), _first_live(theirs, ours))

    chip_first = ordered(core, by_half(core, first_grad), by_half(core, got_first))
    send_near = jnp.concatenate([send_near, chip_first], axis=0)
    got_near = _xor(send_near, 2, n, axis)
    grad = _call(
        _back_kernel,
        jax.ShapeDtypeStruct((slots, 2, h, w, c), F32),
        [_SMEM] + [_VMEM] * 3,
        [pltpu.VMEM((3, slots, 4, h + 2, w, c), BF)],
        flops=1,
        moved=1,
        room=24,
    )(_after(sc, send_near), g0, g1, wt)
    got_far = _after(got_far, grad)

    def summed(j, came):
        i = j % 2
        return kept[j * piece : (j + 1) * piece] + came[i * piece : (i + 1) * piece].astype(F32)

    outs = {j: summed(j, got_far).astype(BF) for j in (3, 2)}
    got_near = _after(got_near, outs[3], outs[2])
    outs[1] = summed(1, got_near).astype(BF)
    gots = {j: _xor(outs[j], 4 * j, n, axis) for j in (3, 2, 1)}
    beside_first = got_near[2 * piece :]
    lead = ordered(pair, chip_first, beside_first)
    near_lead = _xor(lead, 4, n, axis)
    mine = summed(0, _after(got_near, outs[1]))
    for j in (3, 2):
        mine = mine + gots[j].astype(F32)
    gots[1] = _after(gots[1], mine)
    mine = (mine + gots[1].astype(F32)).astype(BF)
    k = 2 * chips
    while k < n:
        mine = (mine.astype(F32) + _xor(mine, k, n, axis).astype(F32)).astype(BF)
        k *= 2
    others = {j: _xor(mine, 4 * j, n, axis) for j in (1, 3, 2)}
    x_near = _xor(jnp.concatenate([mine, others[1]], axis=0), 2, n, axis)
    x_far = _xor(jnp.concatenate([others[2], others[3]], axis=0), 2, n, axis)
    beyond = by(index & 4, near_lead, jnp.full_like(lead, EMPTY_GRAD))
    lead, k = _after(ordered(index & 4, lead, near_lead), others[1]), 8
    while k < n:
        came = _xor(lead, k, n, axis)
        beyond = by(index & k, _first_live(beyond, came), beyond)
        if 2 * k < n:
            lead = ordered(index & k, lead, came)
        k *= 2
    beyond = by(pair, _first_live(beside_first, beyond), beyond)
    ours = jnp.concatenate(
        [mine, others[1], others[2], others[3], x_near, x_far, beyond], axis=0
    )
    other = _xor(ours, 1, n, axis)
    cwg, swg, cbg, sbg, frames_grad = _call(
        _final_kernel,
        [
            jax.ShapeDtypeStruct((27 * c, c), F32),
            jax.ShapeDtypeStruct((2 * c, c), F32),
            jax.ShapeDtypeStruct((1, c), F32),
            jax.ShapeDtypeStruct((1, c), F32),
            jax.ShapeDtypeStruct((slots, 2, h, w, c), BF),
        ],
        [_SMEM] + [_VMEM] * 4,
        [pltpu.VMEM((rows, c), F32)],
        room=12,
    )(sc, ours, other, got_first, grad)
    latents = jnp.concatenate([lat0[None], lat1], axis=0)[:, None]
    return (
        latents,
        frames_grad,
        cwg.reshape(3, 3, 3, c, c),
        cbg[0],
        swg.reshape(2, c, c),
        sbg[0],
    )


def solution(mesh):
    split = P(("groups", "tm"))
    return jax.shard_map(
        functools.partial(body, mesh.shape["tm"]),
        mesh=mesh,
        in_specs=(split, split, split, split, P(), P(), P(), P(), split),
        out_specs=(split, split, P("groups"), P("groups"), P("groups"), P("groups")),
        check_vma=False,
    )
```
